32 devices in a mesh: fsdp: 8 (over y, x, core), seq: 4 (over z).
Axes of the slice: x: 2, y: 2, z: 4, core: 2. Of those that a mesh axis runs over, the one named last changes fastest.
Arguments:
- tokens: bfloat16 [16384, 512], P(('fsdp', 'seq')), may hold values from -6 to 6
- memory: bfloat16 [16384, 512], P(('fsdp', 'seq')), may hold values from -6 to 6
- targets: bfloat16 [16384, 512], P(('fsdp', 'seq')), may hold values from -21 to 21
- doc_lengths: int32 [8, 4], P('fsdp'), may hold values from 1 to 1024, 2048 in all within a row
- doc_order: int32 [8, 4], P('fsdp'), may hold values from 0 to 3, each once within a row
- memory_lengths: int32 [8, 4], P('fsdp'), may hold values from 1 to 512, 1536 in all within a row
- self_query: bfloat16 [512, 512], P('fsdp'), may hold values from -0.25 to 0.25
- self_query_bias: bfloat16 [512], P('fsdp'), may hold values from -1.75 to 1.75
- self_key: bfloat16 [512, 512], P('fsdp'), may hold values from -0.25 to 0.25
- self_value: bfloat16 [512, 512], P('fsdp'), may hold values from -0.25 to 0.25
- self_value_bias: bfloat16 [512], P('fsdp'), may hold values from -1.75 to 1.75
- self_output: bfloat16 [512, 512], P('fsdp'), may hold values from -2 to 2
- self_output_bias: bfloat16 [512], P('fsdp'), may hold values from -1.75 to 1.75
- first_gain: bfloat16 [512], P('fsdp'), may hold values from 0.5 to 1.5
- first_shift: bfloat16 [512], P('fsdp'), may hold values from -1.75 to 1.75
- cross_query: bfloat16 [512, 512], P('fsdp'), may hold values from -0.25 to 0.25
- cross_query_bias: bfloat16 [512], P('fsdp'), may hold values from -1.75 to 1.75
- cross_key: bfloat16 [512, 512], P('fsdp'), may hold values from -0.25 to 0.25
- cross_value: bfloat16 [512, 512], P('fsdp'), may hold values from -0.25 to 0.25
- cross_value_bias: bfloat16 [512], P('fsdp'), may hold values from -1.75 to 1.75
- cross_output: bfloat16 [512, 512], P('fsdp'), may hold values from -2 to 2
- cross_output_bias: bfloat16 [512], P('fsdp'), may hold values from -1.75 to 1.75
- second_gain: bfloat16 [512], P('fsdp'), may hold values from 0.5 to 1.5
- second_shift: bfloat16 [512], P('fsdp'), may hold values from -1.75 to 1.75
- expand_weight: bfloat16 [512, 2048], P('fsdp'), may hold values from -0.25 to 0.25
- expand_bias: bfloat16 [2048], P('fsdp'), may hold values from -1.75 to 1.75
- contract_weight: bfloat16 [2048, 512], P('fsdp'), may hold values from -0.25 to 0.25
- contract_bias: bfloat16 [512], P('fsdp'), may hold values from -1.75 to 1.75
- third_gain: bfloat16 [512], P('fsdp'), may hold values from 0.5 to 1.5
- third_shift: bfloat16 [512], P('fsdp'), may hold values from -1.75 to 1.75
Outputs:
- block_output: bfloat16 [16384, 512], P(('fsdp', 'seq'))
- loss_value: float32 [], replicated
- input_grad: float32 [16384, 512], P(('fsdp', 'seq'))
- memory_grad: float32 [16384, 512], P(('fsdp', 'seq'))
- self_query_grad: float32 [512, 512], P('fsdp')
- self_query_bias_grad: float32 [512], P('fsdp')
- self_key_grad: float32 [512, 512], P('fsdp')
- self_value_grad: float32 [512, 512], P('fsdp')
- self_value_bias_grad: float32 [512], P('fsdp')
- self_output_grad: float32 [512, 512], P('fsdp')
- self_output_bias_grad: float32 [512], P('fsdp')
- first_gain_grad: float32 [512], P('fsdp')
- first_shift_grad: float32 [512], P('fsdp')
- cross_query_grad: float32 [512, 512], P('fsdp')
- cross_query_bias_grad: float32 [512], P('fsdp')
- cross_key_grad: float32 [512, 512], P('fsdp')
- cross_value_grad: float32 [512, 512], P('fsdp')
- cross_value_bias_grad: float32 [512], P('fsdp')
- cross_output_grad: float32 [512, 512], P('fsdp')
- cross_output_bias_grad: float32 [512], P('fsdp')
- second_gain_grad: float32 [512], P('fsdp')
- second_shift_grad: float32 [512], P('fsdp')
- expand_weight_grad: float32 [512, 2048], P('fsdp')
- expand_bias_grad: float32 [2048], P('fsdp')
- contract_weight_grad: float32 [2048, 512], P('fsdp')
- contract_bias_grad: float32 [512], P('fsdp')
- third_gain_grad: float32 [512], P('fsdp')
- third_shift_grad: float32 [512], P('fsdp')
The draws below stay inside these ranges and needn't reach their ends.
Inputs may be any that keep to these rules, and one draw needn't show every extreme that they name: `doc_lengths`: the 4 lengths of a group sum to 2048; in every group the largest is 1024. `doc_order`: each row holds every slot number once. `memory_lengths`: in every group the largest is 512.
All inputs are finite; a program needn't handle non-finite values.
Results may differ from the reference program's by a relative error of at most 0.025.
Values may be sent and summed in bfloat16 or wider, within the bound.
No kernel may reach another device: no remote copies, remote signals or barrier semaphores. Data moves between devices by JAX's collectives and lax.ppermute only.
A program may use at most 128 MiB of HBM per device.

```python
import math
import jax
import jax.numpy as jnp
import numpy as np
from jax import lax

D = 512
HEADS = 8
HDIM = 64
FF = 2048
DOCS = 4
MEM = 512
GROUP_TOK = 2048
MAXLEN = 1024
TOKENS = 16384
MEM_ROWS = 16384
N_FSDP = 8


def draw_targets(key, part):
    row_place = jnp.arange(TOKENS, dtype=jnp.float32) / max(TOKENS - 1, 1)
    row_scale = 1.0 + 2.5 * row_place
    values = jnp.clip(jax.random.normal(key, (TOKENS, D), jnp.float32), -6.0, 6.0)
    return (values * row_scale[:, None]).astype(jnp.bfloat16)


def level_of(stream_key, extent, pieces, low, top_value):
    loudness, own = 1.0, jax.random.fold_in(stream_key, 6)
    for position, blocks in pieces:
        steps = jnp.exp(jax.random.uniform(jax.random.fold_in(own, position), (blocks,), jnp.float32, low / len(pieces), top_value / len(pieces)))
        loudness = loudness * jnp.repeat(steps, extent[position] // blocks).reshape([-1 if axis == position else 1 for axis in range(len(extent))])
    return loudness


def profile(number_of, total, bound, skew):
    loads = [(1 << 20) // math.isqrt(standing ** skew) + 1 for standing in range(2, number_of + 1)]
    surplus, given = total - bound - (number_of - 1), [1] * (number_of - 1)
    while surplus > 0:
        free = [i for i in range(number_of - 1) if given[i] < bound]
        pool, remaining = sum([loads[i] for i in free]), surplus
        for i in free:
            extra = min(bound - given[i], max(1, remaining * loads[i] // pool), surplus)
            given[i] = given[i] + extra
            surplus = surplus - extra
    return np.array([bound] + given)


def uneven(key, number_of, total, most, skew):
    if number_of == 2:
        one = jax.random.randint(key, (), max(1, total - most), min(most, total - 1) + 1)
        return jnp.stack([one, total - one])
    sizes = jnp.asarray(profile(number_of, total, most, skew), jnp.int32)
    pairs = (number_of - 1) // 2
    source_of, sink = sizes[1:1 + 2 * pairs:2], sizes[2:2 + 2 * pairs:2]
    margin = jnp.minimum(source_of - 1, most - sink)
    moved = jax.random.randint(jax.random.fold_in(key, 1), (pairs,), 0, 1 << 20) % (margin + 1)
    sizes = sizes.at[1:1 + 2 * pairs:2].set(source_of - moved).at[2:2 + 2 * pairs:2].set(sink + moved)
    return sizes[jax.random.permutation(jax.random.fold_in(key, 2), number_of)]


def noise(stream_key, shape, width, most, split=(), kind=jnp.bfloat16):
    entries = jax.random.normal(stream_key, shape, jnp.float32) * width
    if len(split) > 0:
        entries = level_of(stream_key, shape, split, -0.22, 0.18) * entries
    return jnp.clip(entries, min=-most, max=most).astype(kind)


def setup_inputs(seed: int = 0) -> dict:
    keys = jax.random.split(jax.random.key(seed), 31)
    return {
        "tokens": noise(keys[0], (TOKENS, D), 1.0, 6.0, ((0, 32),)),
        "memory": noise(keys[1], (MEM_ROWS, D), 1.0, 6.0, ((0, 32),)),
        "targets": draw_targets(jax.random.fold_in(keys[30], 71), 0),
        "doc_lengths": jax.vmap(lambda own: uneven(own, DOCS, GROUP_TOK, MAXLEN, 1))(jax.random.split(keys[3], N_FSDP)).reshape((N_FSDP, DOCS)).astype(jnp.int32),
        "doc_order": jax.vmap(lambda own: jax.random.permutation(own, DOCS))(jax.random.split(keys[4], N_FSDP)).reshape((N_FSDP, DOCS)).astype(jnp.int32),
        "memory_lengths": jax.vmap(lambda own: uneven(own, DOCS, DOCS * MEM * 3 // 4, MEM, 0))(jax.random.split(keys[5], N_FSDP)).reshape((N_FSDP, DOCS)).astype(jnp.int32),
        "self_query": noise(keys[6], (D, D), D ** -0.5, 0.25, ((0, 8),)),
        "self_query_bias": noise(keys[7], (D,), 0.3, 1.75, ((0, 8),)),
        "self_key": noise(keys[8], (D, D), D ** -0.5, 0.25, ((0, 8),)),
        "self_value": noise(keys[9], (D, D), D ** -0.5, 0.25, ((0, 8),)),
        "self_value_bias": noise(keys[10], (D,), 0.3, 1.75, ((0, 8),)),
        "self_output": noise(keys[11], (D, D), (D // 64) ** -0.5, 2.0, ((0, 8),)),
        "self_output_bias": noise(keys[12], (D,), 0.3, 1.75, ((0, 8),)),
        "first_gain": jnp.clip(1.0 + 0.1 * jax.random.normal(keys[13], (D,), jnp.float32), 0.5, 1.5).astype(jnp.bfloat16),
        "first_shift": noise(keys[14], (D,), 0.3, 1.75, ((0, 8),)),
        "cross_query": noise(keys[15], (D, D), D ** -0.5, 0.25, ((0, 8),)),
        "cross_query_bias": noise(keys[16], (D,), 0.3, 1.75, ((0, 8),)),
        "cross_key": noise(keys[17], (D, D), D ** -0.5, 0.25, ((0, 8),)),
        "cross_value": noise(keys[18], (D, D), D ** -0.5, 0.25, ((0, 8),)),
        "cross_value_bias": noise(keys[19], (D,), 0.3, 1.75, ((0, 8),)),
        "cross_output": noise(keys[20], (D, D), (D // 64) ** -0.5, 2.0, ((0, 8),)),
        "cross_output_bias": noise(keys[21], (D,), 0.3, 1.75, ((0, 8),)),
        "second_gain": jnp.clip(1.0 + 0.1 * jax.random.normal(keys[22], (D,), jnp.float32), 0.5, 1.5).astype(jnp.bfloat16),
        "second_shift": noise(keys[23], (D,), 0.3, 1.75, ((0, 8),)),
        "expand_weight": noise(keys[24], (D, FF), D ** -0.5, 0.25, ((0, 8),)),
        "expand_bias": noise(keys[25], (FF,), 0.3, 1.75, ((0, 8),)),
        "contract_weight": noise(keys[26], (FF, D), (FF // 4) ** -0.5, 0.25, ((0, 8),)),
        "contract_bias": noise(keys[27], (D,), 0.3, 1.75, ((0, 8),)),
        "third_gain": jnp.clip(1.0 + 0.1 * jax.random.normal(keys[28], (D,), jnp.float32), 0.5, 1.5).astype(jnp.bfloat16),
        "third_shift": noise(keys[29], (D,), 0.3, 1.75, ((0, 8),)),
    }


@jax.custom_vjp
def low(v):
    return lax.optimization_barrier(v.astype(jnp.bfloat16)).astype(jnp.float32)

@jax.custom_vjp
def low_back(v):
    return v

def low_keep(v):
    return (low(v), None)

def low_pass(kept, grad):
    return (grad,)

def back_keep(v):
    return (v, None)

def back_low(kept, grad):
    return (low(grad),)
low.defvjp(low_keep, low_pass)
low_back.defvjp(back_keep, back_low)

def rounded(value):
    return low(low_back(value))

def product(left_side, right_side):
    return jnp.dot(left_side, right_side, precision=lax.Precision.HIGHEST)

def layer_norm(values, norm_gain, norm_shift):
    centred = values - lax.optimization_barrier(jnp.mean(values, axis=-1, keepdims=True))
    variance = lax.optimization_barrier(jnp.mean(centred * centred, axis=-1, keepdims=True))
    return centred * lax.rsqrt(variance + 1e-05) * norm_gain + norm_shift

def document_slots(lengths, slot_order):
    slot_range = jnp.arange(DOCS, dtype=jnp.int32)
    matches = (slot_order[:, None] == slot_range[None, :]).astype(jnp.int32)
    placed = lax.optimization_barrier(jnp.sum(matches * lengths[None, :], axis=1))
    slot_ends = jnp.cumsum(placed)
    positions = jnp.arange(GROUP_TOK, dtype=jnp.int32)
    slot_index = lax.optimization_barrier(jnp.sum((positions[:, None] >= slot_ends[None, :]).astype(jnp.int32), axis=1))
    pick_table = (slot_index[:, None] == slot_range[None, :]).astype(jnp.int32)
    return lax.optimization_barrier(jnp.sum(pick_table * slot_order[None, :], axis=1))

def memory_slots(memory_limits):
    key_index = jnp.arange(DOCS * MEM, dtype=jnp.int32)
    key_document = key_index // MEM
    pick_table = (key_document[:, None] == jnp.arange(DOCS, dtype=jnp.int32)[None, :]).astype(jnp.int32)
    key_limit = lax.optimization_barrier(jnp.sum(pick_table * memory_limits[None, :], axis=1))
    return (key_document, key_index % MEM < key_limit)

def attend(queries, key_rows, value_rows, allowed_fn):
    group_rows = queries.shape[0]
    block_rows = min(512, group_rows)
    blocks = group_rows // block_rows
    key_heads = key_rows.reshape(key_rows.shape[0], HEADS, HDIM)
    value_heads = value_rows.reshape(value_rows.shape[0], HEADS, HDIM)
    query_blocks = queries.reshape(blocks, block_rows, HEADS, HDIM)
    block_starts = jnp.arange(blocks, dtype=jnp.int32) * block_rows

    def one_block(inputs_pair):
        block_start, query_part = inputs_pair
        scores = jnp.einsum('qhd,khd->hqk', query_part, key_heads, precision=lax.Precision.HIGHEST) * HDIM ** (-0.5)
        scores = low_back(scores)
        scores = jnp.where(allowed_fn(block_start, block_rows)[None], scores, -1e+30)
        softmax_weights = low(jax.nn.softmax(scores, axis=-1))
        result = jnp.einsum('hqk,khd->qhd', softmax_weights, value_heads, precision=lax.Precision.HIGHEST)
        return result.reshape(block_rows, HEADS * HDIM)
    outputs = lax.map(jax.checkpoint(one_block), (block_starts, query_blocks))
    return outputs.reshape(group_rows, HEADS * HDIM)

def layer_forward(params, inputs, memory_part, document_slot, key_document, key_valid):
    self_query, self_query_bias, self_key, self_value, self_value_bias, self_output, self_output_bias, first_gain, first_shift, cross_query, cross_query_bias, cross_key, cross_value, cross_value_bias, cross_output, cross_output_bias, second_gain, second_shift, expand_weight, expand_bias, contract_weight, contract_bias, third_gain, third_shift = params
    positions = jnp.arange(inputs.shape[0], dtype=jnp.int32)

    def self_allowed(block_start, span_rows):
        query_docs = lax.dynamic_slice_in_dim(document_slot, block_start, span_rows)
        query_pos = block_start + jnp.arange(span_rows, dtype=jnp.int32)
        return (query_docs[:, None] == document_slot[None, :]) & (query_pos[:, None] >= positions[None, :])

    def cross_allowed(block_start, span_rows):
        query_docs = lax.dynamic_slice_in_dim(document_slot, block_start, span_rows)
        return (query_docs[:, None] == key_document[None, :]) & key_valid[None, :]
    queries = rounded(product(inputs, self_query) + self_query_bias)
    key_rows = rounded(product(inputs, self_key))
    value_rows = rounded(product(inputs, self_value) + self_value_bias)
    context = rounded(attend(queries, key_rows, value_rows, self_allowed))
    self_branch = low_back(product(context, self_output) + self_output_bias)
    first_out = layer_norm(inputs + self_branch, first_gain, first_shift)
    first_low = low(first_out)
    cross_queries = rounded(product(first_low, cross_query) + cross_query_bias)
    memory_keys = rounded(product(memory_part, cross_key))
    memory_values = rounded(product(memory_part, cross_value) + cross_value_bias)
    cross_context = rounded(attend(cross_queries, memory_keys, memory_values, cross_allowed))
    cross_branch = low_back(product(cross_context, cross_output) + cross_output_bias)
    second = layer_norm(first_out + cross_branch, second_gain, second_shift)
    second_low = low(second)
    expanded = low_back(product(second_low, expand_weight) + expand_bias)
    hidden = low(jax.nn.silu(expanded))
    feed_out = low_back(product(hidden, contract_weight) + contract_bias)
    return layer_norm(second + feed_out, third_gain, third_shift)

def reference(tokens, memory, targets, doc_lengths, doc_order, memory_lengths, self_query, self_query_bias, self_key, self_value, self_value_bias, self_output, self_output_bias, first_gain, first_shift, cross_query, cross_query_bias, cross_key, cross_value, cross_value_bias, cross_output, cross_output_bias, second_gain, second_shift, expand_weight, expand_bias, contract_weight, contract_bias, third_gain, third_shift):
    params = tuple([weight_item.astype(jnp.float32) for weight_item in (self_query, self_query_bias, self_key, self_value, self_value_bias, self_output, self_output_bias, first_gain, first_shift, cross_query, cross_query_bias, cross_key, cross_value, cross_value_bias, cross_output, cross_output_bias, second_gain, second_shift, expand_weight, expand_bias, contract_weight, contract_bias, third_gain, third_shift)])
    group_inputs = tokens.astype(jnp.float32).reshape(N_FSDP, GROUP_TOK, D)
    group_memory = memory.astype(jnp.float32).reshape(N_FSDP, DOCS * MEM, D)
    group_targets = targets.astype(jnp.float32).reshape(N_FSDP, GROUP_TOK, D)

    def per_group(carried, group_item):
        grad_sums, error_sum, live_count = carried
        inputs, memory_part, target_part, lengths, slot_order, memory_limits = group_item
        document_slot = document_slots(lengths, slot_order)
        key_document, key_valid = memory_slots(memory_limits)
        live_rows = (document_slot != DOCS - 1).astype(jnp.float32)[:, None]

        def forward(weights_all, inputs_all, memory_all):
            return layer_forward(weights_all, inputs_all, memory_all, document_slot, key_document, key_valid)
        output, pullback = jax.vjp(forward, params, inputs, memory_part)
        difference = output - target_part
        grad_params, grad_inputs, grad_memory = pullback(live_rows * difference)
        grad_sums = jax.tree.map(lambda total_grad, new_grad: total_grad + new_grad, grad_sums, grad_params)
        error_sum = error_sum + jnp.sum(live_rows * difference * difference)
        live_count = live_count + jnp.sum(live_rows)
        return ((grad_sums, error_sum, live_count), (output.astype(jnp.bfloat16), grad_inputs, grad_memory))
    start_sums = tuple([jnp.zeros(weight_item.shape, jnp.float32) for weight_item in params])
    start_carry = (start_sums, jnp.zeros((), jnp.float32), jnp.zeros((), jnp.float32))
    (grad_sums, error_sum, live_count), (outputs, grad_inputs, grad_memory) = lax.scan(per_group, start_carry, (group_inputs, group_memory, group_targets, doc_lengths, doc_order, memory_lengths))
    block_output = outputs.reshape(TOKENS, D)
    loss_value = error_sum / (live_count * D)
    input_grad = grad_inputs.reshape(TOKENS, D)
    memory_grad = grad_memory.reshape(MEM_ROWS, D)
    return (block_output, loss_value, input_grad, memory_grad, grad_sums[0], grad_sums[1], grad_sums[2], grad_sums[3], grad_sums[4], grad_sums[5], grad_sums[6], grad_sums[7], grad_sums[8], grad_sums[9], grad_sums[10], grad_sums[11], grad_sums[12], grad_sums[13], grad_sums[14], grad_sums[15], grad_sums[16], grad_sums[17], grad_sums[18], grad_sums[19], grad_sums[20], grad_sums[21], grad_sums[22], grad_sums[23])
```

```python
import jax
import jax.numpy as jnp
from jax import lax
from jax.experimental import pallas as pl
from jax.experimental.pallas import tpu as pltpu
from jax.sharding import PartitionSpec as P

D = 512
HDIM = 64
HEADS = D // HDIM
DOCS = 4
MEM = 512
FFB = 4
TILE = 256
VROWS = 32
NEG = -1e30
BF = jnp.bfloat16
F32 = jnp.float32
VMEM_BYTES = 60 * 1024 * 1024

(
    V_SQB,
    V_SVB,
    V_SOB,
    V_G1,
    V_S1,
    V_CQB,
    V_CVB,
    V_COB,
    V_G2,
    V_S2,
    V_CB,
    V_G3,
    V_S3,
    V_EB,
) = range(14)


def mm(a, b):
    return jnp.dot(a, b, preferred_element_type=F32)


def mm_nt(a, b):
    return lax.dot_general(a, b, (((1,), (1,)), ((), ())), preferred_element_type=F32)


def mm_tn(a, b):
    return lax.dot_general(a, b, (((0,), (0,)), ((), ())), preferred_element_type=F32)


def col_sum(v):
    return jnp.sum(v.astype(F32), axis=0, keepdims=True)


def chip_steps(count):
    bits = []
    bit = 2
    while bit < count:
        bits.append(bit)
        bit *= 2
    return bits, bits[::-1]


def gather_masks(count):
    result = []
    for steps in chip_steps(count):
        masks = [0]
        for step in steps:
            masks = masks + [m ^ step for m in masks]
        result.append(masks)
    own0, own1 = result
    return [own0 + [m ^ 1 for m in own1], own1 + [m ^ 1 for m in own0]]


def reduce_masks(count):
    result = []
    for steps in chip_steps(count):
        masks = [0]
        for step in steps[::-1]:
            masks = masks + [m ^ step for m in masks]
        result.append(masks)
    return result


def step_pairs(count, index):
    orders = chip_steps(count)
    return [(i, i ^ orders[i & 1][index]) for i in range(count)]


def fsdp_gather(own, count):
    have = [own]
    for index in range(len(chip_steps(count)[0])):
        pairs = step_pairs(count, index)
        have = have + [lax.ppermute(a, "fsdp", pairs) for a in have]
    swap = [(i, i ^ 1) for i in range(count)]
    return have + [lax.ppermute(a, "fsdp", swap) for a in have]


def add_low(a, b):
    return (a.astype(F32) + b.astype(F32)).astype(BF)


def fsdp_reduce(send, own, count):
    swap = [(i, i ^ 1) for i in range(count)]
    got = lax.ppermute(send, "fsdp", swap)
    half = own.shape[0]
    for index in range(len(chip_steps(count)[0])):
        half = half // 2
        upper = add_low(own[half:], got[half:])
        lower = add_low(own[:half], got[:half])
        own, got = lower, lax.ppermute(upper, "fsdp", step_pairs(count, index))
    return add_low(own[0], got[0])


def seq_sum(part, count):
    z = lax.axis_index("seq")
    odd = (z % 2) == 1
    half = part.shape[0] // 2
    low, high = part[:half], part[half:]
    pairs = [(i, i ^ 1) for i in range(count)]
    got = lax.ppermute(jnp.where(odd, low, high), "seq", pairs)
    mine = add_low(jnp.where(odd, high, low), got)
    bit = 2
    while bit < count:
        mine = add_low(mine, lax.ppermute(mine, "seq", [(i, i ^ bit) for i in range(count)]))
        bit *= 2
    other = lax.ppermute(mine, "seq", pairs)
    return jnp.where(odd, jnp.concatenate([other, mine]), jnp.concatenate([mine, other]))


def seq_up(a, count):
    return lax.ppermute(a, "seq", [(i, i + 1) for i in range(count - 1)])


def seq_down(a, count):
    return lax.ppermute(a, "seq", [(i + 1, i) for i in range(count - 1)])


def slot_place(index, masks, slot):
    return jnp.where(index % 2 == 0, index ^ masks[0][slot], index ^ masks[1][slot])


class Shard:
    def __init__(self, rows, mem_rows, count, split, piece, wide_piece):
        self.rows = rows
        self.mem_rows = mem_rows
        self.count = count
        self.split = split
        self.piece = piece
        self.wide_piece = wide_piece
        self.group_rows = rows * split
        self.group_mem = mem_rows * split
        self.halo = min(-(-(self.group_rows // 2 - 1) // rows), split - 1)
        self.window = rows * (self.halo + 1)
        self.q_blocks = rows // TILE
        self.k_blocks = self.window // TILE
        self.m_blocks = self.group_mem // TILE
        self.gather = gather_masks(count)
        self.reduce = reduce_masks(count)


def start_weight(sh, slots, row, n, target, sem):
    index = lax.axis_index("fsdp")
    for s, slot in enumerate(slots):
        place = pl.multiple_of(slot_place(index, sh.gather, s) * n, n)
        pltpu.make_async_copy(slot.at[pl.ds(row, n)], target.at[pl.ds(place, n)], sem).start()


def wait_all(target, sem):
    pltpu.make_async_copy(target, target, sem).wait()


def put_grad(sh, full, n, row, send_ref, own_ref):
    index = lax.axis_index("fsdp")
    partner = index ^ 1
    for s in range(sh.count // 2):
        mine = pl.multiple_of(slot_place(index, sh.reduce, s) * n, n)
        theirs = pl.multiple_of(slot_place(partner, sh.reduce, s) * n, n)
        own_ref[s, pl.ds(row, n), :] = full[pl.ds(mine, n), :]
        send_ref[s, pl.ds(row, n), :] = full[pl.ds(theirs, n), :]


def doc_bounds(lens, order):
    starts, ends = [], []
    total = jnp.int32(0)
    for p in range(DOCS):
        starts.append(total)
        total = total + lens[0, order[0, p]]
        ends.append(total)
    return starts, ends


def pick(starts, ends, pos, values):
    out = jnp.zeros_like(pos)
    for p in range(DOCS):
        out = jnp.where((pos >= starts[p]) & (pos < ends[p]), values[p], out)
    return out


def lane_pos(base):
    return base + lax.broadcasted_iota(jnp.int32, (1, TILE), 1)


def norm_stats(v):
    mean = jnp.mean(v, axis=1, keepdims=True)
    c = v - mean
    inv = lax.rsqrt(jnp.mean(c * c, axis=1, keepdims=True) + 1e-05)
    return c * inv, inv


def norm_back(dy, n, inv, gain):
    e = dy * gain
    return inv * (
        e - jnp.mean(e, axis=1, keepdims=True) - n * jnp.mean(e * n, axis=1, keepdims=True)
    )


def head_rows(h):
    return slice(h * HDIM, (h + 1) * HDIM)


def pair_lanes(h):
    j = h // 2
    return slice(j * 2 * HDIM, (j + 1) * 2 * HDIM)


def spread_rows(source, target):
    for h in range(HEADS):
        o = (h % 2) * HDIM
        target[h, pl.ds(o, HDIM), :] = source[head_rows(h), :]


def spread_zero(target):
    for h in range(HEADS):
        o = (1 - h % 2) * HDIM
        target[h, pl.ds(o, HDIM), :] = jnp.zeros((HDIM, TILE), BF)


def spread_lanes(source, target):
    lane = lax.broadcasted_iota(jnp.int32, (TILE, 2 * HDIM), 1)
    for h in range(HEADS):
        part = source[:, pair_lanes(h)]
        keep = (lane >= HDIM) if h % 2 else (lane < HDIM)
        target[h] = jnp.where(keep, part, jnp.zeros_like(part))


def forward_tile(keys, vals_t, bias, q_t, m_ref, l_ref, acc_ref):
    for h in range(HEADS):
        s = mm(keys[:, pair_lanes(h)], q_t[h]) + bias[...]
        m_old = m_ref[h : h + 1, :]
        m_new = jnp.maximum(m_old, jnp.max(s, axis=0, keepdims=True))
        p = jnp.exp(s - m_new)
        alpha = jnp.exp(m_old - m_new)
        m_ref[h : h + 1, :] = m_new
        l_ref[h : h + 1, :] = alpha * l_ref[h : h + 1, :] + jnp.sum(p, axis=0, keepdims=True)
        acc_ref[head_rows(h), :] = acc_ref[head_rows(h), :] * alpha + mm(
            vals_t[head_rows(h), :], p.astype(BF)
        )


def forward_start(m_ref, l_ref, acc_ref):
    m_ref[...] = jnp.full(m_ref.shape, NEG, F32)
    l_ref[...] = jnp.zeros(l_ref.shape, F32)
    acc_ref[...] = jnp.zeros(acc_ref.shape, F32)


def forward_end(b, m_ref, l_ref, acc_ref, ctx_ref, ctx_t_ref, lse_ref):
    lse_ref[b] = m_ref[...] + jnp.log(l_ref[...])
    for h in range(HEADS):
        acc_ref[head_rows(h), :] = acc_ref[head_rows(h), :] / l_ref[h : h + 1, :]
    ctx_t_ref[b] = acc_ref[...]
    ctx_ref[pl.ds(pl.multiple_of(b * TILE, TILE), TILE), :] = acc_ref[...].T.astype(BF)


def backward_tile(keys, vals, keys_t, bias, q_t, g_t, q_m, g_m, lse, delta, dk, dv, dq_t):
    for h in range(0, HEADS, 2):
        dk_sum = dk[:, pair_lanes(h)]
        dv_sum = dv[:, pair_lanes(h)]
        for i in (h, h + 1):
            s = mm(keys[:, pair_lanes(i)], q_t[i]) + bias[...]
            p = jnp.exp(s - lse[i : i + 1, :])
            dp = mm(vals[:, pair_lanes(i)], g_t[i])
            ds = (p * (dp - delta[i : i + 1, :])).astype(BF)
            dv_sum = dv_sum + mm(p.astype(BF), g_m[i])
            dk_sum = dk_sum + mm(ds, q_m[i])
            dq_t[head_rows(i), :] = dq_t[head_rows(i), :] + mm(keys_t[head_rows(i), :], ds)
        dk[:, pair_lanes(h)] = dk_sum
        dv[:, pair_lanes(h)] = dv_sum


def backward_start(b, q_t3, g_t3, q, g, ctx_t3, q_t, g_t, q_m, g_m, delta, dq_t):
    rows = pl.ds(pl.multiple_of(b * TILE, TILE), TILE)
    spread_rows(q_t3.at[b], q_t)
    spread_rows(g_t3.at[b], g_t)
    spread_lanes(q[rows, :], q_m)
    spread_lanes(g[rows, :], g_m)
    prod = g_t3[b].astype(F32) * ctx_t3[b]
    for h in range(HEADS):
        delta[h : h + 1, :] = jnp.sum(prod[head_rows(h), :], axis=0, keepdims=True)
    dq_t[...] = jnp.zeros(dq_t.shape, F32)


def self_tiles(sh, lens, order, b, bias, body):
    z = lax.axis_index("seq")
    starts, ends = doc_bounds(lens, order)
    shift = (z - sh.halo) * sh.rows
    q_base = sh.halo * sh.rows + b * TILE
    first = pick(starts, ends, q_base + shift, starts) - shift
    q_pos = lane_pos(q_base)
    q_start = pick(starts, ends, q_pos + shift, starts) - shift
    last = q_base // TILE
    number = last - first // TILE + 1

    def step(i, carry):
        t = last - i
        k_pos = t * TILE + lax.broadcasted_iota(jnp.int32, (TILE, TILE), 0)
        bias[...] = jnp.where((k_pos >= q_start) & (k_pos <= q_pos), 0.0, NEG)
        body(t)
        return carry

    lax.fori_loop(0, number, step, 0)


def self_forward_kernel(sh, lens, order, *refs):
    halo, count, rows, n = sh.halo, sh.count, sh.rows, sh.piece
    toks = refs[: halo + 1]
    slots = refs[halo + 1 : halo + 1 + count]
    (q_ref, q_t3, k3, v3, k_t3, ctx, ctx_t3, lse, vec) = refs[halo + 1 + count : halo + 10 + count]
    (wq, wk, wv, vec_slots, v_t3, q_t, bias, m_ref, l_ref, acc, sems) = refs[halo + 10 + count :]
    z = lax.axis_index("seq")
    for s, slot in enumerate(slots):
        pltpu.make_async_copy(slot.at[pl.ds(3 * n, VROWS)], vec_slots.at[s], sems.at[3]).start()
    for i, w in enumerate((wq, wk, wv)):
        start_weight(sh, slots, i * n, n, w, sems.at[i])
    spread_zero(q_t)
    wait_all(vec_slots, sems.at[3])
    vec[...] = jnp.sum(vec_slots[...].astype(F32), axis=0)
    wait_all(wq, sems.at[0])
    wait_all(wk, sems.at[1])
    wait_all(wv, sems.at[2])
    tiles = rows // TILE

    def own_rows(i, carry):
        r = pl.ds(pl.multiple_of(i * TILE, TILE), TILE)
        q = (mm(toks[0][r, :], wq[...]) + vec[V_SQB : V_SQB + 1, :]).astype(BF)
        q = q * BF(HDIM**-0.5)
        q_ref[r, :] = q
        q_t3[i] = q.T
        return carry

    lax.fori_loop(0, tiles, own_rows, 0)
    for k in range(halo + 1):

        def window_rows(i, carry, k=k):
            r = pl.ds(pl.multiple_of(i * TILE, TILE), TILE)
            t = (halo - k) * tiles + i
            x = toks[k][r, :]
            key = mm(x, wk[...]).astype(BF)
            val = (mm(x, wv[...]) + vec[V_SVB : V_SVB + 1, :]).astype(BF)
            k3[t] = key
            v3[t] = val
            k_t3[t] = key.T
            v_t3[t] = val.T
            return carry

        @pl.when(z >= k)
        def _(window_rows=window_rows):
            lax.fori_loop(0, tiles, window_rows, 0)

    def block(b, carry):
        spread_rows(q_t3.at[b], q_t)
        forward_start(m_ref, l_ref, acc)
        self_tiles(
            sh,
            lens,
            order,
            b,
            bias,
            lambda t: forward_tile(k3.at[t], v_t3.at[t], bias, q_t, m_ref, l_ref, acc),
        )
        forward_end(b, m_ref, l_ref, acc, ctx, ctx_t3, lse)
        return carry

    lax.fori_loop(0, sh.q_blocks, block, 0)


SMEM_SPEC = pl.BlockSpec(memory_space=pltpu.SMEM)
VMEM_SPEC = pl.BlockSpec(memory_space=pltpu.VMEM)
ANY_SPEC = pl.BlockSpec(memory_space=pl.ANY)


def shape(dims, dtype):
    return jax.ShapeDtypeStruct(dims, dtype)


def call(body, name, inputs, specs, outs, scratch):
    return pl.pallas_call(
        body,
        name=name,
        in_specs=specs,
        out_specs=[VMEM_SPEC] * len(outs),
        out_shape=outs,
        scratch_shapes=scratch,
        compiler_params=pltpu.CompilerParams(vmem_limit_bytes=VMEM_BYTES),
    )(*inputs)


def self_forward(sh, lens, order, toks, slots):
    nb, nq = sh.k_blocks, sh.q_blocks
    outs = [
        shape((sh.rows, D), BF),
        shape((nq, D, TILE), BF),
        shape((nb, TILE, D), BF),
        shape((nb, TILE, D), BF),
        shape((nb, D, TILE), BF),
        shape((sh.rows, D), BF),
        shape((nq, D, TILE), F32),
        shape((nq, HEADS, TILE), F32),
        shape((VROWS, D), F32),
    ]
    scratch = [
        pltpu.VMEM((D, D), BF),
        pltpu.VMEM((D, D), BF),
        pltpu.VMEM((D, D), BF),
        pltpu.VMEM((sh.count, VROWS, D), BF),
        pltpu.VMEM((nb, D, TILE), BF),
        pltpu.VMEM((HEADS, 2 * HDIM, TILE), BF),
        pltpu.VMEM((TILE, TILE), F32),
        pltpu.VMEM((HEADS, TILE), F32),
        pltpu.VMEM((HEADS, TILE), F32),
        pltpu.VMEM((D, TILE), F32),
        pltpu.SemaphoreType.DMA((4,)),
    ]
    specs = [SMEM_SPEC] * 2 + [VMEM_SPEC] * len(toks) + [ANY_SPEC] * len(slots)
    return call(
        lambda *refs: self_forward_kernel(sh, *refs),
        "self_forward",
        (lens, order, *toks, *slots),
        specs,
        outs,
        scratch,
    )


def cross_tiles(sh, lens, order, mlens, b, bias, bounds, skip_pad, body):
    z = lax.axis_index("seq")
    starts, ends = doc_bounds(lens, order)
    for p in range(DOCS):
        bounds[0, p] = starts[p]
        bounds[1, p] = ends[p]
    base = z * sh.rows + b * TILE
    slots = [order[0, p] for p in range(DOCS)]
    pos = lane_pos(base)
    low = pick(starts, ends, pos, [s * MEM for s in slots])
    high = pick(starts, ends, pos, [s * MEM + mlens[0, s] for s in slots])

    def doc(p, carry):
        slot = order[0, p]
        seen = (bounds[0, p] < base + TILE) & (bounds[1, p] > base)
        if skip_pad:
            seen = seen & (slot != DOCS - 1)
        number = jnp.where(seen, (mlens[0, slot] + TILE - 1) // TILE, 0)

        def step(i, inner):
            t = slot * (MEM // TILE) + i
            k_pos = t * TILE + lax.broadcasted_iota(jnp.int32, (TILE, TILE), 0)
            bias[...] = jnp.where((k_pos >= low) & (k_pos < high), 0.0, NEG)
            body(t)
            return inner

        return lax.fori_loop(0, number, step, carry)

    lax.fori_loop(0, DOCS, doc, 0)


def touched_tile(sh, lens, order, mlens, t, bounds, skip_pad):
    z = lax.axis_index("seq")
    slot = t // (MEM // TILE)
    base = z * sh.rows
    seen = (bounds[2, slot] < base + sh.rows) & (bounds[3, slot] > base)
    seen = seen & (t % (MEM // TILE) * TILE < mlens[0, slot])
    if skip_pad:
        seen = seen & (slot != DOCS - 1)
    return seen


def slot_bounds(lens, order, bounds):
    starts, ends = doc_bounds(lens, order)
    for p in range(DOCS):
        bounds[2, order[0, p]] = starts[p]
        bounds[3, order[0, p]] = ends[p]


def cross_forward_kernel(sh, lens, order, mlens, *refs):
    count, rows, n, split = sh.count, sh.rows, sh.piece, sh.split
    tok, ctx, vec = refs[:3]
    mems = refs[3 : 3 + 2 * split - 1]
    slots = refs[2 + 2 * split : 2 + 2 * split + count]
    outs = refs[2 + 2 * split + count :]
    (n1, inv1, first_low, q_ref, q_t3, mk3, mv3, mk_t3, cctx, cctx_t3, lse, mem) = outs[:12]
    (wo, wcq, wck, wcv, mv_t3, q_t, bias, m_ref, l_ref, acc, bounds, sems) = outs[12:]
    z = lax.axis_index("seq")
    for i, w in enumerate((wo, wcq, wck, wcv)):
        start_weight(sh, slots, i * n, n, w, sems.at[i])
    own = mems[0]
    tiles_per = sh.mem_rows // TILE

    def place(source, shard):
        for i in range(tiles_per):
            pltpu.make_async_copy(
                source.at[pl.ds(i * TILE, TILE)], mem.at[shard * tiles_per + i], sems.at[4]
            ).start()

    place(own, z)
    for k in range(1, split):
        up, down = mems[2 * k - 1], mems[2 * k]

        @pl.when(z >= k)
        def _(up=up, k=k):
            place(up, z - k)

        @pl.when(z + k < split)
        def _(down=down, k=k):
            place(down, z + k)

    slot_bounds(lens, order, bounds)
    spread_zero(q_t)
    wait_all(wo, sems.at[0])
    wait_all(wcq, sems.at[1])

    def own_rows(i, carry):
        r = pl.ds(pl.multiple_of(i * TILE, TILE), TILE)
        v = tok[r, :].astype(F32) + (mm(ctx[r, :], wo[...]) + vec[V_SOB : V_SOB + 1, :])
        normal, inv = norm_stats(v)
        n1[r, :] = normal
        inv1[r, :] = inv
        low = (normal * vec[V_G1 : V_G1 + 1, :] + vec[V_S1 : V_S1 + 1, :]).astype(BF)
        first_low[r, :] = low
        q = (mm(low, wcq[...]) + vec[V_CQB : V_CQB + 1, :]).astype(BF)
        q = q * BF(HDIM**-0.5)
        q_ref[r, :] = q
        q_t3[i] = q.T
        return carry

    lax.fori_loop(0, rows // TILE, own_rows, 0)
    wait_all(wck, sems.at[2])
    wait_all(wcv, sems.at[3])
    wait_all(mem, sems.at[4])

    def mem_tile(t, carry):
        @pl.when(touched_tile(sh, lens, order, mlens, t, bounds, False))
        def _():
            x = mem[t]
            key = mm(x, wck[...]).astype(BF)
            val = (mm(x, wcv[...]) + vec[V_CVB : V_CVB + 1, :]).astype(BF)
            mk3[t] = key
            mv3[t] = val
            mk_t3[t] = key.T
            mv_t3[t] = val.T

        return carry

    lax.fori_loop(0, sh.m_blocks, mem_tile, 0)

    def block(b, carry):
        spread_rows(q_t3.at[b], q_t)
        forward_start(m_ref, l_ref, acc)
        cross_tiles(
            sh,
            lens,
            order,
            mlens,
            b,
            bias,
            bounds,
            False,
            lambda t: forward_tile(mk3.at[t], mv_t3.at[t], bias, q_t, m_ref, l_ref, acc),
        )
        forward_end(b, m_ref, l_ref, acc, cctx, cctx_t3, lse)
        return carry

    lax.fori_loop(0, sh.q_blocks, block, 0)


def cross_forward(sh, lens, order, mlens, tok, ctx, vec, mems, slots):
    nm, nq = sh.m_blocks, sh.q_blocks
    outs = [
        shape((sh.rows, D), F32),
        shape((sh.rows, 1), F32),
        shape((sh.rows, D), BF),
        shape((sh.rows, D), BF),
        shape((nq, D, TILE), BF),
        shape((nm, TILE, D), BF),
        shape((nm, TILE, D), BF),
        shape((nm, D, TILE), BF),
        shape((sh.rows, D), BF),
        shape((nq, D, TILE), F32),
        shape((nq, HEADS, TILE), F32),
        shape((nm, TILE, D), BF),
    ]
    scratch = [
        pltpu.VMEM((D, D), BF),
        pltpu.VMEM((D, D), BF),
        pltpu.VMEM((D, D), BF),
        pltpu.VMEM((D, D), BF),
        pltpu.VMEM((nm, D, TILE), BF),
        pltpu.VMEM((HEADS, 2 * HDIM, TILE), BF),
        pltpu.VMEM((TILE, TILE), F32),
        pltpu.VMEM((HEADS, TILE), F32),
        pltpu.VMEM((HEADS, TILE), F32),
        pltpu.VMEM((D, TILE), F32),
        pltpu.SMEM((4, DOCS), jnp.int32),
        pltpu.SemaphoreType.DMA((5,)),
    ]
    specs = [SMEM_SPEC] * 3 + [VMEM_SPEC] * 3 + [ANY_SPEC] * (len(mems) + len(slots))
    return call(
        lambda *refs: cross_forward_kernel(sh, *refs),
        "cross_forward",
        (lens, order, mlens, tok, ctx, vec, *mems, *slots),
        specs,
        outs,
        scratch,
    )


def feed_kernel(sh, lens, order, *refs):
    count, rows, n, wide = sh.count, sh.rows, sh.piece, sh.wide_piece
    n1, cctx, targets, vec = refs[:4]
    slots = refs[4 : 4 + count]
    outs = refs[4 + count :]
    (final_ref, g_second, g_cc, g_cc_t3, g_send, g_own, vec_grad, loss) = outs[:8]
    (wco, w1, w2, n2, sec_low, hid, dact, feed_low, g_exp, g_cross, stage, stage2, sems) = outs[8:]
    z = lax.axis_index("seq")
    start_weight(sh, slots, 4 * n, n, wco, sems.at[0])
    for c in range(FFB):
        start_weight(sh, slots, (5 + c) * n, n, w1.at[c], sems.at[1 + c])
    start_weight(sh, slots, 9 * n, wide, w2, sems.at[5])
    vec_grad[...] = jnp.zeros(vec_grad.shape, F32)
    loss[...] = jnp.zeros(loss.shape, F32)
    starts, ends = doc_bounds(lens, order)
    pad_start, pad_end = jnp.int32(0), jnp.int32(0)
    for p in range(DOCS):
        is_pad = order[0, p] == DOCS - 1
        pad_start = jnp.where(is_pad, starts[p], pad_start)
        pad_end = jnp.where(is_pad, ends[p], pad_end)
    wait_all(wco, sems.at[0])
    for c in range(FFB):
        wait_all(w1.at[c], sems.at[1 + c])
    wait_all(w2, sems.at[5])

    def add_vec(row, value):
        vec_grad[row : row + 1, :] = vec_grad[row : row + 1, :] + value

    def chunk(i, carry):
        r = pl.ds(pl.multiple_of(i * TILE, TILE), TILE)
        first = n1[r, :] * vec[V_G1 : V_G1 + 1, :] + vec[V_S1 : V_S1 + 1, :]
        v = first + (mm(cctx[r, :], wco[...]) + vec[V_COB : V_COB + 1, :])
        normal2, inv2 = norm_stats(v)
        n2[...] = normal2
        second = normal2 * vec[V_G2 : V_G2 + 1, :] + vec[V_S2 : V_S2 + 1, :]
        low = second.astype(BF)
        sec_low[r, :] = low
        feed = second + vec[V_CB : V_CB + 1, :]
        for c in range(FFB):
            e = mm(low, w1[c]) + vec[V_EB + c : V_EB + c + 1, :]
            sg = jax.nn.sigmoid(e)
            h = (e * sg).astype(BF)
            hid[c, r, :] = h
            dact[c] = sg * (1.0 + e * (1.0 - sg))
            feed = feed + mm(h, w2[pl.ds(c * D, D), :])
        normal3, inv3 = norm_stats(feed)
        final = normal3 * vec[V_G3 : V_G3 + 1, :] + vec[V_S3 : V_S3 + 1, :]
        final_ref[r, :] = final.astype(BF)
        diff = final - targets[r, :].astype(F32)
        pos = z * rows + i * TILE + lax.broadcasted_iota(jnp.int32, (TILE, 1), 0)
        live = jnp.where((pos >= pad_start) & (pos < pad_end), 0.0, 1.0)
        g = live * diff
        loss[0:1, :] = loss[0:1, :] + col_sum(g * diff)
        add_vec(V_G3, col_sum(g * normal3))
        add_vec(V_S3, col_sum(g))
        g_third = norm_back(g, normal3, inv3, vec[V_G3 : V_G3 + 1, :])
        g_low = g_third.astype(BF)
        feed_low[r, :] = g_low
        add_vec(V_CB, col_sum(g_low))
        total = g_third
        for c in range(FFB):
            ge = (mm_nt(g_low, w2[pl.ds(c * D, D), :]) * dact[c]).astype(BF)
            g_exp[c, r, :] = ge
            add_vec(V_EB + c, col_sum(ge))
            total = total + mm_nt(ge, w1[c])
        normal2 = n2[...]
        add_vec(V_G2, col_sum(total * normal2))
        add_vec(V_S2, col_sum(total))
        gs = norm_back(total, normal2, inv2, vec[V_G2 : V_G2 + 1, :])
        g_second[r, :] = gs
        gc = gs.astype(BF)
        g_cross[r, :] = gc
        add_vec(V_COB, col_sum(gc))
        gcc = mm_nt(gc, wco[...]).astype(BF)
        g_cc[r, :] = gcc
        g_cc_t3[i] = gcc.T
        return carry

    lax.fori_loop(0, rows // TILE, chunk, 0)
    live_count = jnp.int32(rows) - jnp.maximum(
        jnp.minimum(pad_end, (z + 1) * rows) - jnp.maximum(pad_start, z * rows), 0
    )
    loss[1:2, :] = jnp.full((1, D), live_count.astype(F32))
    stage[...] = mm_tn(cctx[...], g_cross[...]).astype(BF)
    put_grad(sh, stage, n, 0, g_send, g_own)
    for c in range(FFB):
        stage[...] = mm_tn(sec_low[...], g_exp[c]).astype(BF)
        put_grad(sh, stage, n, (1 + c) * n, g_send, g_own)
    for c in range(FFB):
        stage2[pl.ds(c * D, D), :] = mm_tn(hid[c], feed_low[...]).astype(BF)
    put_grad(sh, stage2, wide, 5 * n, g_send, g_own)


def feed(sh, lens, order, n1, cctx, targets, vec, slots):
    rows, nq, n = sh.rows, sh.q_blocks, sh.piece
    block = 5 * n + sh.wide_piece
    outs = [
        shape((rows, D), BF),
        shape((rows, D), F32),
        shape((rows, D), BF),
        shape((nq, D, TILE), BF),
        shape((sh.count // 2, block, D), BF),
        shape((sh.count // 2, block, D), BF),
        shape((VROWS, D), F32),
        shape((8, D), F32),
    ]
    scratch = [
        pltpu.VMEM((D, D), BF),
        pltpu.VMEM((FFB, D, D), BF),
        pltpu.VMEM((FFB * D, D), BF),
        pltpu.VMEM((TILE, D), F32),
        pltpu.VMEM((rows, D), BF),
        pltpu.VMEM((FFB, rows, D), BF),
        pltpu.VMEM((FFB, TILE, D), F32),
        pltpu.VMEM((rows, D), BF),
        pltpu.VMEM((FFB, rows, D), BF),
        pltpu.VMEM((rows, D), BF),
        pltpu.VMEM((D, D), BF),
        pltpu.VMEM((FFB * D, D), BF),
        pltpu.SemaphoreType.DMA((6,)),
    ]
    specs = [SMEM_SPEC] * 2 + [VMEM_SPEC] * 4 + [ANY_SPEC] * len(slots)
    return call(
        lambda *refs: feed_kernel(sh, *refs),
        "feed",
        (lens, order, n1, cctx, targets, vec, *slots),
        specs,
        outs,
        scratch,
    )


def cross_backward_kernel(sh, lens, order, mlens, *refs):
    count, rows, n = sh.count, sh.rows, sh.piece
    (q_ref, q_t3, mk3, mv3, mk_t3, cctx_t3, lse, g_cc, g_cc_t3, g_second, n1, inv1) = refs[:12]
    (first_low, mem, ctx, vec, vec_in) = refs[12:17]
    slots = refs[17 : 17 + count]
    outs = refs[17 + count :]
    (g_send, g_own, mem_grad, g_first, g_ctx, g_ctx_t3, vec_grad) = outs[:7]
    (wo, wcq, wck, wcv, q_t, g_t, q_m, g_m, delta, bias, dk, dv, dq_t, dq, g_self) = outs[7:22]
    (acc_k, acc_v, stage, bounds, sems) = outs[22:]
    for i, w in enumerate((wo, wcq, wck, wcv)):
        start_weight(sh, slots, i * n, n, w, sems.at[i])
    vec_grad[...] = vec_in[...]
    slot_bounds(lens, order, bounds)
    spread_zero(q_t)
    spread_zero(g_t)

    def clear(t, carry):
        @pl.when(touched_tile(sh, lens, order, mlens, t, bounds, True))
        def _():
            dk[t] = jnp.zeros((TILE, D), F32)
            dv[t] = jnp.zeros((TILE, D), F32)

        return carry

    lax.fori_loop(0, sh.m_blocks, clear, 0)

    def block(b, carry):
        backward_start(b, q_t3, g_cc_t3, q_ref, g_cc, cctx_t3, q_t, g_t, q_m, g_m, delta, dq_t)
        cross_tiles(
            sh,
            lens,
            order,
            mlens,
            b,
            bias,
            bounds,
            True,
            lambda t: backward_tile(
                mk3.at[t],
                mv3.at[t],
                mk_t3.at[t],
                bias,
                q_t,
                g_t,
                q_m,
                g_m,
                lse.at[b],
                delta,
                dk.at[t],
                dv.at[t],
                dq_t,
            ),
        )
        r = pl.ds(pl.multiple_of(b * TILE, TILE), TILE)
        dq[r, :] = (dq_t[...] * HDIM**-0.5).T.astype(BF)
        return carry

    lax.fori_loop(0, sh.q_blocks, block, 0)
    for i, w in enumerate((wo, wcq, wck, wcv)):
        wait_all(w, sems.at[i])

    def add_vec(row, value):
        vec_grad[row : row + 1, :] = vec_grad[row : row + 1, :] + value

    acc_k[...] = jnp.zeros(acc_k.shape, F32)
    acc_v[...] = jnp.zeros(acc_v.shape, F32)

    def mem_tile(t, carry):
        seen = touched_tile(sh, lens, order, mlens, t, bounds, True)

        @pl.when(seen)
        def _():
            k_low = dk[t].astype(BF)
            v_low = dv[t].astype(BF)
            x = mem[t]
            acc_k[...] = acc_k[...] + mm_tn(x, k_low)
            acc_v[...] = acc_v[...] + mm_tn(x, v_low)
            add_vec(V_CVB, col_sum(v_low))
            mem_grad[t] = (mm_nt(k_low, wck[...]) + mm_nt(v_low, wcv[...])).astype(BF)

        @pl.when(jnp.logical_not(seen))
        def _():
            mem_grad[t] = jnp.zeros((TILE, D), BF)

        return carry

    lax.fori_loop(0, sh.m_blocks, mem_tile, 0)

    def own_rows(i, carry):
        r = pl.ds(pl.multiple_of(i * TILE, TILE), TILE)
        total = g_second[r, :] + mm_nt(dq[r, :], wcq[...])
        normal = n1[r, :]
        add_vec(V_G1, col_sum(total * normal))
        add_vec(V_S1, col_sum(total))
        gf = norm_back(total, normal, inv1[r, :], vec[V_G1 : V_G1 + 1, :])
        g_first[r, :] = gf
        low = gf.astype(BF)
        g_self[r, :] = low
        add_vec(V_SOB, col_sum(low))
        gc = mm_nt(low, wo[...]).astype(BF)
        g_ctx[r, :] = gc
        g_ctx_t3[i] = gc.T
        return carry

    lax.fori_loop(0, rows // TILE, own_rows, 0)
    add_vec(V_CQB, col_sum(dq[...]))
    stage[...] = mm_tn(ctx[...], g_self[...]).astype(BF)
    put_grad(sh, stage, n, 0, g_send, g_own)
    stage[...] = mm_tn(first_low[...], dq[...]).astype(BF)
    put_grad(sh, stage, n, n, g_send, g_own)
    stage[...] = acc_k[...].astype(BF)
    put_grad(sh, stage, n, 2 * n, g_send, g_own)
    stage[...] = acc_v[...].astype(BF)
    put_grad(sh, stage, n, 3 * n, g_send, g_own)


def cross_backward(sh, lens, order, mlens, arrays, slots):
    rows, nq, nm, n = sh.rows, sh.q_blocks, sh.m_blocks, sh.piece
    outs = [
        shape((sh.count // 2, 4 * n, D), BF),
        shape((sh.count // 2, 4 * n, D), BF),
        shape((nm, TILE, D), BF),
        shape((rows, D), F32),
        shape((rows, D), BF),
        shape((nq, D, TILE), BF),
        shape((VROWS, D), F32),
    ]
    scratch = [
        pltpu.VMEM((D, D), BF),
        pltpu.VMEM((D, D), BF),
        pltpu.VMEM((D, D), BF),
        pltpu.VMEM((D, D), BF),
        pltpu.VMEM((HEADS, 2 * HDIM, TILE), BF),
        pltpu.VMEM((HEADS, 2 * HDIM, TILE), BF),
        pltpu.VMEM((HEADS, TILE, 2 * HDIM), BF),
        pltpu.VMEM((HEADS, TILE, 2 * HDIM), BF),
        pltpu.VMEM((HEADS, TILE), F32),
        pltpu.VMEM((TILE, TILE), F32),
        pltpu.VMEM((nm, TILE, D), F32),
        pltpu.VMEM((nm, TILE, D), F32),
        pltpu.VMEM((D, TILE), F32),
        pltpu.VMEM((rows, D), BF),
        pltpu.VMEM((rows, D), BF),
        pltpu.VMEM((D, D), F32),
        pltpu.VMEM((D, D), F32),
        pltpu.VMEM((D, D), BF),
        pltpu.SMEM((4, DOCS), jnp.int32),
        pltpu.SemaphoreType.DMA((4,)),
    ]
    specs = [SMEM_SPEC] * 3 + [VMEM_SPEC] * len(arrays) + [ANY_SPEC] * len(slots)
    return call(
        lambda *refs: cross_backward_kernel(sh, *refs),
        "cross_backward",
        (lens, order, mlens, *arrays, *slots),
        specs,
        outs,
        scratch,
    )


def self_backward_kernel(sh, lens, order, *refs):
    count, rows, n, halo = sh.count, sh.rows, sh.piece, sh.halo
    (q_ref, q_t3, k3, v3, k_t3, ctx_t3, lse, g_ctx, g_ctx_t3, g_first, vec_in) = refs[:11]
    toks = refs[11 : 12 + halo]
    slots = refs[12 + halo : 12 + halo + count]
    outs = refs[12 + halo + count :]
    (g_send, g_own, grad_own, grad_halo) = outs[:4]
    (wq, wk, wv, q_t, g_t, q_m, g_m, delta, bias, dk, dv, dq_t, dq) = outs[4:17]
    (acc_k, acc_v, vec_grad, stage, sems) = outs[17:]
    z = lax.axis_index("seq")
    for i, w in enumerate((wq, wk, wv)):
        start_weight(sh, slots, i * n, n, w, sems.at[i])
    vec_grad[...] = vec_in[...]
    spread_zero(q_t)
    spread_zero(g_t)

    def clear(t, carry):
        dk[t] = jnp.zeros((TILE, D), F32)
        dv[t] = jnp.zeros((TILE, D), F32)
        return carry

    lax.fori_loop(0, sh.k_blocks, clear, 0)

    def block(b, carry):
        backward_start(b, q_t3, g_ctx_t3, q_ref, g_ctx, ctx_t3, q_t, g_t, q_m, g_m, delta, dq_t)
        self_tiles(
            sh,
            lens,
            order,
            b,
            bias,
            lambda t: backward_tile(
                k3.at[t],
                v3.at[t],
                k_t3.at[t],
                bias,
                q_t,
                g_t,
                q_m,
                g_m,
                lse.at[b],
                delta,
                dk.at[t],
                dv.at[t],
                dq_t,
            ),
        )
        r = pl.ds(pl.multiple_of(b * TILE, TILE), TILE)
        dq[r, :] = (dq_t[...] * HDIM**-0.5).T.astype(BF)
        return carry

    lax.fori_loop(0, sh.q_blocks, block, 0)
    for i, w in enumerate((wq, wk, wv)):
        wait_all(w, sems.at[i])

    def add_vec(row, value):
        vec_grad[row : row + 1, :] = vec_grad[row : row + 1, :] + value

    acc_k[...] = jnp.zeros(acc_k.shape, F32)
    acc_v[...] = jnp.zeros(acc_v.shape, F32)
    tiles = rows // TILE
    for k in range(halo, -1, -1):

        def window_rows(i, carry, k=k):
            r = pl.ds(pl.multiple_of(i * TILE, TILE), TILE)
            t = (halo - k) * tiles + i
            k_low = dk[t].astype(BF)
            v_low = dv[t].astype(BF)
            x = toks[k][r, :]
            acc_k[...] = acc_k[...] + mm_tn(x, k_low)
            acc_v[...] = acc_v[...] + mm_tn(x, v_low)
            add_vec(V_SVB, col_sum(v_low))
            part = mm_nt(k_low, wk[...]) + mm_nt(v_low, wv[...])
            if k == 0:
                grad_own[r, :] = g_first[r, :] + part + mm_nt(dq[r, :], wq[...])
            else:
                grad_halo[k - 1, r, :] = part.astype(BF)
            return carry

        @pl.when(z >= k)
        def _(window_rows=window_rows):
            lax.fori_loop(0, tiles, window_rows, 0)

        if k > 0:

            @pl.when(z < k)
            def _(k=k):
                grad_halo[k - 1] = jnp.zeros((rows, D), BF)

    add_vec(V_SQB, col_sum(dq[...]))
    stage[...] = mm_tn(toks[0][...], dq[...]).astype(BF)
    put_grad(sh, stage, n, 0, g_send, g_own)
    stage[...] = acc_k[...].astype(BF)
    put_grad(sh, stage, n, n, g_send, g_own)
    stage[...] = acc_v[...].astype(BF)
    put_grad(sh, stage, n, 2 * n, g_send, g_own)
    vec_low = vec_grad[...].astype(BF)
    for s in range(count // 2):
        g_send[s, pl.ds(3 * n, VROWS), :] = vec_low
        g_own[s, pl.ds(3 * n, VROWS), :] = vec_low


def self_backward(sh, lens, order, arrays, toks, slots):
    rows, nb, n = sh.rows, sh.k_blocks, sh.piece
    outs = [
        shape((sh.count // 2, 3 * n + VROWS, D), BF),
        shape((sh.count // 2, 3 * n + VROWS, D), BF),
        shape((rows, D), F32),
        shape((sh.halo, rows, D), BF),
    ]
    scratch = [
        pltpu.VMEM((D, D), BF),
        pltpu.VMEM((D, D), BF),
        pltpu.VMEM((D, D), BF),
        pltpu.VMEM((HEADS, 2 * HDIM, TILE), BF),
        pltpu.VMEM((HEADS, 2 * HDIM, TILE), BF),
        pltpu.VMEM((HEADS, TILE, 2 * HDIM), BF),
        pltpu.VMEM((HEADS, TILE, 2 * HDIM), BF),
        pltpu.VMEM((HEADS, TILE), F32),
        pltpu.VMEM((TILE, TILE), F32),
        pltpu.VMEM((nb, TILE, D), F32),
        pltpu.VMEM((nb, TILE, D), F32),
        pltpu.VMEM((D, TILE), F32),
        pltpu.VMEM((rows, D), BF),
        pltpu.VMEM((D, D), F32),
        pltpu.VMEM((D, D), F32),
        pltpu.VMEM((VROWS, D), F32),
        pltpu.VMEM((D, D), BF),
        pltpu.SemaphoreType.DMA((3,)),
    ]
    specs = [SMEM_SPEC] * 2 + [VMEM_SPEC] * (len(arrays) + len(toks)) + [ANY_SPEC] * len(slots)
    return call(
        lambda *refs: self_backward_kernel(sh, *refs),
        "self_backward",
        (lens, order, *arrays, *toks, *slots),
        specs,
        outs,
        scratch,
    )


def shards(
    tokens,
    memory,
    targets,
    doc_lengths,
    doc_order,
    memory_lengths,
    self_query,
    self_query_bias,
    self_key,
    self_value,
    self_value_bias,
    self_output,
    self_output_bias,
    first_gain,
    first_shift,
    cross_query,
    cross_query_bias,
    cross_key,
    cross_value,
    cross_value_bias,
    cross_output,
    cross_output_bias,
    second_gain,
    second_shift,
    expand_weight,
    expand_bias,
    contract_weight,
    contract_bias,
    third_gain,
    third_shift,
):
    split = lax.axis_size("seq")
    count = lax.axis_size("fsdp")
    fsdp = lax.axis_index("fsdp")
    n = self_query.shape[0]
    wide = contract_weight.shape[0]
    sh = Shard(tokens.shape[0], memory.shape[0], count, split, n, wide)

    toks = [tokens]
    for _ in range(sh.halo):
        toks.append(seq_up(toks[-1], split))

    small = jnp.stack(
        [
            self_query_bias,
            self_value_bias,
            self_output_bias,
            first_gain,
            first_shift,
            cross_query_bias,
            cross_value_bias,
            cross_output_bias,
            second_gain,
            second_shift,
            contract_bias,
            third_gain,
            third_shift,
        ]
    )
    block = jnp.zeros((V_EB, D), BF)
    block = lax.dynamic_update_slice(block, small, (jnp.int32(0), fsdp * n))
    wide_bias = jnp.zeros((FFB * D,), BF)
    wide_bias = lax.dynamic_update_slice(wide_bias, expand_bias, (fsdp * expand_bias.shape[0],))
    vec_own = jnp.concatenate(
        [block, wide_bias.reshape(FFB, D), jnp.zeros((VROWS - V_EB - FFB, D), BF)]
    )
    own_a = jnp.concatenate([self_query, self_key, self_value, vec_own])
    own_b = jnp.concatenate(
        [self_output, cross_query, cross_key, cross_value, cross_output]
        + [expand_weight[:, c * D : (c + 1) * D] for c in range(FFB)]
        + [contract_weight]
    )
    slots_a = fsdp_gather(own_a, count)
    slots_b = fsdp_gather(own_b, count)

    mems = [memory]
    up, down = memory, memory
    for _ in range(split - 1):
        up, down = seq_up(up, split), seq_down(down, split)
        mems += [up, down]

    (q, q_t3, k3, v3, k_t3, ctx, ctx_t3, lse, vec) = self_forward(
        sh, doc_lengths, doc_order, toks, slots_a
    )
    (n1, inv1, first_low, cq, cq_t3, mk3, mv3, mk_t3, cctx, cctx_t3, clse, mem) = cross_forward(
        sh, doc_lengths, doc_order, memory_lengths, tokens, ctx, vec, mems, slots_b
    )
    (final_low, g_second, g_cc, g_cc_t3, send_c, own_c, vec_grad, loss) = feed(
        sh, doc_lengths, doc_order, n1, cctx, targets, vec, slots_b
    )
    error_sum, live_count = lax.psum((jnp.sum(loss[0]), loss[1, 0]), ("fsdp", "seq"))
    loss_value = error_sum / (live_count * D)
    red_c = seq_sum(fsdp_reduce(send_c, own_c, count), split)
    (send_b, own_b2, mem_part, g_first, g_ctx, g_ctx_t3, vec_grad) = cross_backward(
        sh,
        doc_lengths,
        doc_order,
        memory_lengths,
        (
            cq,
            cq_t3,
            mk3,
            mv3,
            mk_t3,
            cctx_t3,
            clse,
            g_cc,
            g_cc_t3,
            g_second,
            n1,
            inv1,
            first_low,
            mem,
            ctx,
            vec,
            vec_grad,
        ),
        slots_b,
    )
    red_b = seq_sum(fsdp_reduce(send_b, own_b2, count), split)
    z = lax.axis_index("seq")
    parts = mem_part.reshape(split, sh.mem_rows, D)

    def mem_shard(k):
        index = jnp.clip(z + k, 0, split - 1)
        return lax.dynamic_index_in_dim(parts, index, 0, keepdims=False)

    memory_grad = mem_shard(0).astype(F32)
    up = down = None
    for k in range(split - 1, 0, -1):
        mine_up, mine_down = mem_shard(k), mem_shard(-k)
        up = seq_up(mine_up if up is None else add_low(mine_up, up), split)
        down = seq_down(mine_down if down is None else add_low(mine_down, down), split)
    memory_grad = memory_grad + up.astype(F32) + down.astype(F32)

    (send_a, own_a2, grad_own, grad_halo) = self_backward(
        sh,
        doc_lengths,
        doc_order,
        (q, q_t3, k3, v3, k_t3, ctx_t3, lse, g_ctx, g_ctx_t3, g_first, vec_grad),
        toks,
        slots_a,
    )
    red_a = seq_sum(fsdp_reduce(send_a, own_a2, count), split)
    back = None
    for k in range(sh.halo, 0, -1):
        mine = grad_halo[k - 1]
        back = seq_down(mine if back is None else add_low(mine, back), split)
    input_grad = grad_own + back.astype(F32)

    def rows_of(array, start, size):
        return array[start : start + size].astype(F32)

    vec_rows = red_a[3 * n : 3 * n + VROWS].astype(F32)
    small_grad = lax.dynamic_slice(vec_rows, (jnp.int32(0), fsdp * n), (V_EB, n))
    flat = vec_rows[V_EB : V_EB + FFB].reshape(FFB * D)
    expand_bias_grad = lax.dynamic_slice(
        flat, (fsdp * expand_bias.shape[0],), (expand_bias.shape[0],)
    )
    expand_grad = jnp.concatenate(
        [rows_of(red_c, (1 + c) * n, n) for c in range(FFB)], axis=1
    )
    return (
        final_low,
        loss_value,
        input_grad,
        memory_grad,
        rows_of(red_a, 0, n),
        small_grad[V_SQB],
        rows_of(red_a, n, n),
        rows_of(red_a, 2 * n, n),
        small_grad[V_SVB],
        rows_of(red_b, 0, n),
        small_grad[V_SOB],
        small_grad[V_G1],
        small_grad[V_S1],
        rows_of(red_b, n, n),
        small_grad[V_CQB],
        rows_of(red_b, 2 * n, n),
        rows_of(red_b, 3 * n, n),
        small_grad[V_CVB],
        rows_of(red_c, 0, n),
        small_grad[V_COB],
        small_grad[V_G2],
        small_grad[V_S2],
        expand_grad,
        expand_bias_grad,
        rows_of(red_c, 5 * n, wide),
        small_grad[V_CB],
        small_grad[V_G3],
        small_grad[V_S3],
    )


def solution(mesh):
    rows = P(("fsdp", "seq"), None)
    matrix = P("fsdp", None)
    vector = P("fsdp")
    kinds = (
        "mvmmvmvvvmvmmvmvvvmvmvvv"
    )
    weights = tuple(matrix if kind == "m" else vector for kind in kinds)
    return jax.shard_map(
        shards,
        mesh=mesh,
        in_specs=(rows, rows, rows, matrix, matrix, matrix) + weights,
        out_specs=(rows, P(), rows, rows) + weights,
        check_vma=False,
    )
```

```python
import jax
import jax.numpy as jnp
from jax import lax
from jax.experimental import pallas as pl
from jax.experimental.pallas import tpu as pltpu
from jax.sharding import PartitionSpec as P

D = 512
HDIM = 64
HEADS = D // HDIM
DOCS = 4
MEM = 512
FFB = 4
TILE = 256
GROUP = 4
VROWS = 32
NEG = -1e30
BF = jnp.bfloat16
F32 = jnp.float32
VMEM_BYTES = 60 * 1024 * 1024
SHARED_BYTES = 36 * 1024 * 1024
FLOPS_RATE = 3e13

(
    V_SQB,
    V_SVB,
    V_SOB,
    V_G1,
    V_S1,
    V_CQB,
    V_CVB,
    V_COB,
    V_G2,
    V_S2,
    V_CB,
    V_G3,
    V_S3,
    V_EB,
) = range(14)
V_LOSS = V_EB + FFB
V_LIVE = V_LOSS + 1
LOW_BITS = 36
HIGH_BITS = 36


def mm(a, b):
    return jnp.dot(a, b, preferred_element_type=F32)


def mm_nt(a, b):
    return lax.dot_general(a, b, (((1,), (1,)), ((), ())), preferred_element_type=F32)


def mm_tn(a, b):
    return lax.dot_general(a, b, (((0,), (0,)), ((), ())), preferred_element_type=F32)


def col_sum(v):
    return jnp.sum(v.astype(F32), axis=0, keepdims=True)


def chip_steps(count):
    bits = []
    bit = 2
    while bit < count:
        bits.append(bit)
        bit *= 2
    return bits, bits[::-1]


def gather_masks(count):
    result = []
    for steps in chip_steps(count):
        masks = [0]
        for step in steps:
            masks = masks + [m ^ step for m in masks]
        result.append(masks)
    own0, own1 = result
    return [own0 + [m ^ 1 for m in own1], own1 + [m ^ 1 for m in own0]]


def reduce_masks(count):
    result = []
    for steps in chip_steps(count):
        masks = [0]
        for step in steps[::-1]:
            masks = masks + [m ^ step for m in masks]
        result.append(masks)
    return result


def step_pairs(count, index):
    orders = chip_steps(count)
    return [(i, i ^ orders[i & 1][index]) for i in range(count)]


def fsdp_gather(own, count):
    have = [own]
    for index in range(len(chip_steps(count)[0])):
        pairs = step_pairs(count, index)
        have = have + [lax.ppermute(a, "fsdp", pairs) for a in have]
    swap = [(i, i ^ 1) for i in range(count)]
    return have + [lax.ppermute(a, "fsdp", swap) for a in have]


def add_low(a, b):
    return (a.astype(F32) + b.astype(F32)).astype(BF)


def after(value, *others):
    return lax.optimization_barrier((value, *others))[0]


class Reduction:
    def __init__(self, send, own, count, split, halves):
        self.count, self.split, self.halves = count, split, halves
        self.send, self.own = send, own
        self.odd = (lax.axis_index("seq") % 2) == 1
        self.got = None
        self.plan = [("fsdp", [(i, i ^ 1) for i in range(count)])]
        for index in range(len(chip_steps(count)[0])):
            self.plan.append(("fsdp", step_pairs(count, index)))
        bits = [1 << k for k in range(split.bit_length() - 1)]
        for bit in bits + [1] * halves:
            self.plan.append(("seq", [(i, i ^ bit) for i in range(split)]))

    def step(self, *others):
        send = after(self.send, *others) if others else self.send
        axis, pairs = self.plan.pop(0)
        got = self.got = lax.ppermute(send, axis, pairs)
        left = sum(1 for a, _ in self.plan if a == "fsdp")
        if axis == "fsdp" and left > 0:
            half = self.own.shape[0] // 2
            self.send = add_low(self.own[half:], got[half:])
            self.own = add_low(self.own[:half], got[:half])
        elif axis == "fsdp":
            total = add_low(self.own[0], got[0])
            if self.halves:
                half = total.shape[0] // 2
                self.send = jnp.where(self.odd, total[:half], total[half:])
                self.own = jnp.where(self.odd, total[half:], total[:half])
            else:
                self.send = self.own = total
        elif self.halves and not self.plan:
            self.send = jnp.where(
                self.odd, jnp.concatenate([got, self.own]), jnp.concatenate([self.own, got])
            )
        else:
            self.send = self.own = add_low(self.own, got)
        return self

    def finish(self):
        while self.plan:
            self.step()
        return self.send


def seq_rest(parts, split):
    z = lax.axis_index("seq")
    bit = 4
    while bit < split:
        pairs = parts.reshape(parts.shape[0] // 2, 2, *parts.shape[1:])
        odd = (z // bit) % 2 == 1
        got = lax.ppermute(
            jnp.where(odd, pairs[:, 0], pairs[:, 1]), "seq", [(i, i ^ bit) for i in range(split)]
        )
        parts = jnp.where(odd, pairs[:, 1], pairs[:, 0]) + got
        bit *= 2
    return parts


def seq_up(a, count):
    return lax.ppermute(a, "seq", [(i, i + 1) for i in range(count - 1)])


def seq_down(a, count):
    return lax.ppermute(a, "seq", [(i + 1, i) for i in range(count - 1)])


def slot_place(index, masks, slot):
    return jnp.where(index % 2 == 0, index ^ masks[0][slot], index ^ masks[1][slot])


class Shard:
    def __init__(self, rows, mem_rows, count, split, piece, wide_piece):
        self.rows = rows
        self.mem_rows = mem_rows
        self.count = count
        self.split = split
        self.piece = piece
        self.wide_piece = wide_piece
        self.group_rows = rows * split
        self.group_mem = mem_rows * split
        self.halo = min(-(-(self.group_rows // 2 - 1) // rows), split - 1)
        self.window = rows * (self.halo + 1)
        self.q_blocks = rows // TILE
        self.k_blocks = self.window // TILE
        self.m_blocks = self.group_mem // TILE
        self.gather = gather_masks(count)
        self.reduce = reduce_masks(count)


def start_weight(sh, slots, row, n, target, sem):
    index = lax.axis_index("fsdp")
    for s, slot in enumerate(slots):
        place = pl.multiple_of(slot_place(index, sh.gather, s) * n, n)
        pltpu.make_async_copy(slot.at[pl.ds(row, n)], target.at[pl.ds(place, n)], sem).start()


def wait_all(target, sem):
    pltpu.make_async_copy(target, target, sem).wait()


def put_grad(sh, full, n, row, send_ref, own_ref):
    index = lax.axis_index("fsdp")
    partner = index ^ 1
    for s in range(sh.count // 2):
        mine = pl.multiple_of(slot_place(index, sh.reduce, s) * n, n)
        theirs = pl.multiple_of(slot_place(partner, sh.reduce, s) * n, n)
        own_ref[s, pl.ds(row, n), :] = full[pl.ds(mine, n), :]
        send_ref[s, pl.ds(row, n), :] = full[pl.ds(theirs, n), :]


def doc_bounds(lens, order):
    starts, ends = [], []
    total = jnp.int32(0)
    for p in range(DOCS):
        starts.append(total)
        total = total + lens[0, order[0, p]]
        ends.append(total)
    return starts, ends


def pick(starts, ends, pos, values):
    out = jnp.zeros_like(pos)
    for p in range(DOCS):
        out = jnp.where((pos >= starts[p]) & (pos < ends[p]), values[p], out)
    return out


def lane_pos(base):
    return base + lax.broadcasted_iota(jnp.int32, (1, TILE), 1)


def norm_stats(v):
    mean = jnp.mean(v, axis=1, keepdims=True)
    c = v - mean
    inv = lax.rsqrt(jnp.mean(c * c, axis=1, keepdims=True) + 1e-05)
    return c * inv, inv


def norm_back(dy, n, inv, gain):
    e = dy * gain
    return inv * (
        e - jnp.mean(e, axis=1, keepdims=True) - n * jnp.mean(e * n, axis=1, keepdims=True)
    )


def head_rows(h):
    return slice(h * HDIM, (h + 1) * HDIM)


def pair_lanes(h):
    j = h // 2
    return slice(j * 2 * HDIM, (j + 1) * 2 * HDIM)


def spread_rows(source, target):
    for h in range(HEADS):
        o = (h % 2) * HDIM
        target[h, pl.ds(o, HDIM), :] = source[head_rows(h), :]


def spread_zero(target):
    for h in range(HEADS):
        o = (1 - h % 2) * HDIM
        target[h, pl.ds(o, HDIM), :] = jnp.zeros((HDIM, TILE), BF)


def spread_lanes(source, target):
    lane = lax.broadcasted_iota(jnp.int32, (TILE, 2 * HDIM), 1)
    for h in range(HEADS):
        part = source[:, pair_lanes(h)]
        keep = (lane >= HDIM) if h % 2 else (lane < HDIM)
        target[h] = jnp.where(keep, part, jnp.zeros_like(part))


def forward_tile(keys, vals_t, bias, q_t, m_ref, l_ref, acc_ref):
    heads = range(HEADS)
    mask = bias[...]
    m_old, l_old = m_ref[...], l_ref[...]
    scores = [mm(keys[:, pair_lanes(h)], q_t[h]) + mask for h in heads]
    tops = [
        jnp.maximum(m_old[h : h + 1], jnp.max(scores[h], axis=0, keepdims=True)) for h in heads
    ]
    probs = [jnp.exp(scores[h] - tops[h]) for h in heads]
    alphas = [jnp.exp(m_old[h : h + 1] - tops[h]) for h in heads]
    sums = [
        alphas[h] * l_old[h : h + 1] + jnp.sum(probs[h], axis=0, keepdims=True) for h in heads
    ]
    outs = [mm(vals_t[head_rows(h), :], probs[h].astype(BF)) for h in heads]
    for h in heads:
        acc_ref[head_rows(h), :] = acc_ref[head_rows(h), :] * alphas[h] + outs[h]
    m_ref[...] = jnp.concatenate(tops, axis=0)
    l_ref[...] = jnp.concatenate(sums, axis=0)


def forward_start(m_ref, l_ref, acc_ref):
    m_ref[...] = jnp.full(m_ref.shape, NEG, F32)
    l_ref[...] = jnp.zeros(l_ref.shape, F32)
    acc_ref[...] = jnp.zeros(acc_ref.shape, F32)


def forward_end(b, m_ref, l_ref, acc_ref, ctx_ref, ctx_t_ref, lse_ref):
    lse_ref[b] = m_ref[...] + jnp.log(l_ref[...])
    for h in range(HEADS):
        acc_ref[head_rows(h), :] = acc_ref[head_rows(h), :] / l_ref[h : h + 1, :]
    ctx_t_ref[b] = acc_ref[...]
    ctx_ref[pl.ds(pl.multiple_of(b * TILE, TILE), TILE), :] = acc_ref[...].T.astype(BF)


def backward_tile(keys, vals, keys_t, bias, q_t, g_t, q_m, g_m, lse, delta, dk, dv, dq_t):
    mask = bias[...]
    for first in range(0, HEADS, GROUP):
        heads = range(first, first + GROUP)
        scores = [mm(keys[:, pair_lanes(h)], q_t[h]) for h in heads]
        probs = [jnp.exp(s + mask - lse[h : h + 1, :]) for h, s in zip(heads, scores)]
        dvs = [mm(p.astype(BF), g_m[h]) for h, p in zip(heads, probs)]
        dps = [mm(vals[:, pair_lanes(h)], g_t[h]) for h in heads]
        dss = [
            (p * (dp - delta[h : h + 1, :])).astype(BF) for h, p, dp in zip(heads, probs, dps)
        ]
        dks = [mm(ds, q_m[h]) for h, ds in zip(heads, dss)]
        dqs = [mm(keys_t[head_rows(h), :], ds) for h, ds in zip(heads, dss)]
        for i in range(0, GROUP, 2):
            lanes = pair_lanes(first + i)
            dv[:, lanes] = dv[:, lanes] + dvs[i] + dvs[i + 1]
            dk[:, lanes] = dk[:, lanes] + dks[i] + dks[i + 1]
        for h, dq in zip(heads, dqs):
            dq_t[head_rows(h), :] = dq_t[head_rows(h), :] + dq


def backward_start(b, q_t3, g_t3, q, g, ctx_t3, q_t, g_t, q_m, g_m, delta, dq_t):
    rows = pl.ds(pl.multiple_of(b * TILE, TILE), TILE)
    spread_rows(q_t3.at[b], q_t)
    spread_rows(g_t3.at[b], g_t)
    spread_lanes(q[rows, :], q_m)
    spread_lanes(g[rows, :], g_m)
    prod = g_t3[b].astype(F32) * ctx_t3[b]
    for h in range(HEADS):
        delta[h : h + 1, :] = jnp.sum(prod[head_rows(h), :], axis=0, keepdims=True)
    dq_t[...] = jnp.zeros(dq_t.shape, F32)


def self_tiles(sh, lens, order, b, bias, body):
    z = lax.axis_index("seq")
    starts, ends = doc_bounds(lens, order)
    shift = (z - sh.halo) * sh.rows
    q_base = sh.halo * sh.rows + b * TILE
    first = pick(starts, ends, q_base + shift, starts) - shift
    q_pos = lane_pos(q_base)
    q_start = pick(starts, ends, q_pos + shift, starts) - shift
    last = q_base // TILE
    number = last - first // TILE + 1

    def step(i, carry):
        t = last - i
        k_pos = t * TILE + lax.broadcasted_iota(jnp.int32, (TILE, TILE), 0)
        bias[...] = jnp.where((k_pos >= q_start) & (k_pos <= q_pos), 0.0, NEG)
        body(t)
        return carry

    lax.fori_loop(0, number, step, 0)


def self_forward_kernel(sh, lens, order, *refs):
    halo, count, rows, n = sh.halo, sh.count, sh.rows, sh.piece
    toks = refs[: halo + 1]
    slots = refs[halo + 1 : halo + 1 + count]
    (q_ref, q_t3, k3, v3, k_t3, ctx, ctx_t3, lse, vec) = refs[halo + 1 + count : halo + 10 + count]
    (wq, wk, wv, vec_slots, v_t3, q_t, bias, m_ref, l_ref, acc, sems) = refs[halo + 10 + count :]
    z = lax.axis_index("seq")
    for s, slot in enumerate(slots):
        pltpu.make_async_copy(slot.at[pl.ds(3 * n, VROWS)], vec_slots.at[s], sems.at[3]).start()
    for i, w in enumerate((wq, wk, wv)):
        start_weight(sh, slots, i * n, n, w, sems.at[i])
    spread_zero(q_t)
    wait_all(vec_slots, sems.at[3])
    vec[...] = jnp.sum(vec_slots[...].astype(F32), axis=0)
    wait_all(wq, sems.at[0])
    wait_all(wk, sems.at[1])
    wait_all(wv, sems.at[2])
    tiles = rows // TILE

    def own_rows(i, carry):
        r = pl.ds(pl.multiple_of(i * TILE, TILE), TILE)
        q = (mm(toks[0][r, :], wq[...]) + vec[V_SQB : V_SQB + 1, :]).astype(BF)
        q = q * BF(HDIM**-0.5)
        q_ref[r, :] = q
        q_t3[i] = q.T
        return carry

    lax.fori_loop(0, tiles, own_rows, 0)
    for k in range(halo + 1):

        def window_rows(i, carry, k=k):
            r = pl.ds(pl.multiple_of(i * TILE, TILE), TILE)
            t = (halo - k) * tiles + i
            x = toks[k][r, :]
            key = mm(x, wk[...]).astype(BF)
            val = (mm(x, wv[...]) + vec[V_SVB : V_SVB + 1, :]).astype(BF)
            k3[t] = key
            v3[t] = val
            k_t3[t] = key.T
            v_t3[t] = val.T
            return carry

        @pl.when(z >= k)
        def _(window_rows=window_rows):
            lax.fori_loop(0, tiles, window_rows, 0)

    def block(b, carry):
        spread_rows(q_t3.at[b], q_t)
        forward_start(m_ref, l_ref, acc)
        self_tiles(
            sh,
            lens,
            order,
            b,
            bias,
            lambda t: forward_tile(k3.at[t], v_t3.at[t], bias, q_t, m_ref, l_ref, acc),
        )
        forward_end(b, m_ref, l_ref, acc, ctx, ctx_t3, lse)
        return carry

    lax.fori_loop(0, sh.q_blocks, block, 0)


SMEM_SPEC = pl.BlockSpec(memory_space=pltpu.SMEM)
VMEM_SPEC = pl.BlockSpec(memory_space=pltpu.VMEM)
ANY_SPEC = pl.BlockSpec(memory_space=pl.ANY)


def shape(dims, dtype):
    return jax.ShapeDtypeStruct(dims, dtype)


def call(body, name, inputs, specs, outs, scratch, micros, vmem=VMEM_BYTES):
    moved = sum(a.size * a.dtype.itemsize for a in (*inputs, *outs))
    cost = pl.CostEstimate(
        flops=int(micros * 1e-6 * FLOPS_RATE), transcendentals=0, bytes_accessed=moved // 50
    )
    return pl.pallas_call(
        body,
        name=name,
        in_specs=specs,
        out_specs=[VMEM_SPEC] * len(outs),
        out_shape=outs,
        scratch_shapes=scratch,
        cost_estimate=cost,
        compiler_params=pltpu.CompilerParams(vmem_limit_bytes=vmem),
    )(*inputs)


def pack_kernel(sh, *refs):
    small = refs[:V_EB]
    wide_bias = refs[V_EB]
    mats = refs[V_EB + 1 : V_EB + 11]
    own_a, own_b = refs[V_EB + 11 :]
    n, wide = sh.piece, sh.wide_piece
    (sq, sk, sv, so, cq, ck, cv, co, w1, w2) = mats
    for i, m in enumerate((sq, sk, sv)):
        own_a[pl.ds(i * n, n), :] = m[...]
    for i, m in enumerate((so, cq, ck, cv, co)):
        own_b[pl.ds(i * n, n), :] = m[...]
    for c in range(FFB):
        own_b[pl.ds((5 + c) * n, n), :] = w1[:, c * D : (c + 1) * D]
    own_b[pl.ds(9 * n, wide), :] = w2[...]
    index = lax.axis_index("fsdp")

    def spread(piece, size, offset):
        hot = lax.broadcasted_iota(jnp.int32, (size, D), 1) == offset + lax.broadcasted_iota(
            jnp.int32, (size, D), 0
        )
        return mm(piece, hot.astype(BF)).astype(BF)

    rows = jnp.concatenate([r[...].reshape(1, n) for r in small], axis=0)
    size = wide_bias.shape[0]
    flat = index * size
    line = spread(wide_bias[...].reshape(1, size), size, flat % D)
    row = lax.broadcasted_iota(jnp.int32, (FFB, D), 0)
    own_a[pl.ds(3 * n, VROWS), :] = jnp.concatenate(
        [
            spread(rows, n, index * n),
            jnp.where(row == flat // D, line, jnp.zeros((FFB, D), BF)),
            jnp.zeros((VROWS - V_EB - FFB, D), BF),
        ],
        axis=0,
    )


def pack(sh, small, wide_bias, mats):
    n, wide = sh.piece, sh.wide_piece
    outs = [shape((3 * n + VROWS, D), BF), shape((9 * n + wide, D), BF)]
    return call(
        lambda *refs: pack_kernel(sh, *refs),
        "pack",
        (*small, wide_bias, *mats),
        [VMEM_SPEC] * (V_EB + 1 + len(mats)),
        outs,
        [],
        2,
    )


def digit_bits(devices):
    return 3 if 7 * devices <= 256 else 1


def digits(value, bits):
    lane = lax.broadcasted_iota(jnp.int32, (1, D), 1)
    scale = jnp.full((1, D), 2.0**LOW_BITS, F32)
    for i in range(9):
        scale = scale * jnp.where((lane // 2**i) % 2 == 1, 2.0 ** -min(bits * 2**i, 140), 1.0)
    whole = jnp.floor(value * scale)
    return whole - 2.0**bits * jnp.floor(value * scale * 2.0**-bits)


def undigits(row, bits):
    lane = lax.broadcasted_iota(jnp.int32, (1, D), 1)
    scale = jnp.full((1, D), 2.0**-LOW_BITS, F32)
    for i in range(7):
        scale = scale * jnp.where(
            (lane // 2**i) % 2 == 1, 2.0 ** min(bits * 2**i, LOW_BITS + HIGH_BITS), 1.0
        )
    used = lane < (LOW_BITS + HIGH_BITS) // bits
    return jnp.sum(jnp.where(used, row * jnp.where(used, scale, 0.0), 0.0), axis=1, keepdims=True)


def finish_kernel(sh, red, *outs):
    n = sh.piece
    mats, small, wide_bias, loss = outs[:3], outs[3 : 3 + V_EB], outs[3 + V_EB], outs[4 + V_EB]
    for i, m in enumerate(mats):
        m[...] = red[pl.ds(i * n, n), :].astype(F32)
    index = lax.axis_index("fsdp")
    vec = red[pl.ds(3 * n, VROWS), :]

    def cut(rows, size, offset):
        hot = lax.broadcasted_iota(jnp.int32, (D, size), 0) == offset + lax.broadcasted_iota(
            jnp.int32, (D, size), 1
        )
        return mm(rows, hot.astype(BF))

    parts = cut(vec, n, index * n)
    for i in range(V_EB):
        small[i][...] = parts[i : i + 1, :].reshape(n)
    size = wide_bias.shape[0]
    flat = index * size
    row = lax.broadcasted_iota(jnp.int32, (VROWS, D), 0)
    lines = jnp.where(row == V_EB + flat // D, vec.astype(F32), 0.0).astype(BF)
    wide_bias[...] = jnp.sum(cut(lines, size, flat % D), axis=0, keepdims=True).reshape(size)
    bits = digit_bits(sh.count * sh.split)
    error_sum = undigits(vec[V_LOSS : V_LOSS + 1, :].astype(F32), bits)
    live = undigits(vec[V_LIVE : V_LIVE + 1, :].astype(F32), bits)
    loss[...] = error_sum / (live * D)


def finish(sh, red, bias_size):
    n = sh.piece
    outs = [shape((n, D), F32)] * 3 + [shape((n,), F32)] * V_EB
    outs += [shape((bias_size,), F32), shape((1, 1), F32)]
    return call(
        lambda *refs: finish_kernel(sh, *refs), "finish", (red,), [VMEM_SPEC], outs, [], 2
    )


def self_forward(sh, lens, order, toks, slots):
    nb, nq = sh.k_blocks, sh.q_blocks
    outs = [
        shape((sh.rows, D), BF),
        shape((nq, D, TILE), BF),
        shape((nb, TILE, D), BF),
        shape((nb, TILE, D), BF),
        shape((nb, D, TILE), BF),
        shape((sh.rows, D), BF),
        shape((nq, D, TILE), F32),
        shape((nq, HEADS, TILE), F32),
        shape((VROWS, D), F32),
    ]
    scratch = [
        pltpu.VMEM((D, D), BF),
        pltpu.VMEM((D, D), BF),
        pltpu.VMEM((D, D), BF),
        pltpu.VMEM((sh.count, VROWS, D), BF),
        pltpu.VMEM((nb, D, TILE), BF),
        pltpu.VMEM((HEADS, 2 * HDIM, TILE), BF),
        pltpu.VMEM((TILE, TILE), F32),
        pltpu.VMEM((HEADS, TILE), F32),
        pltpu.VMEM((HEADS, TILE), F32),
        pltpu.VMEM((D, TILE), F32),
        pltpu.SemaphoreType.DMA((4,)),
    ]
    specs = [SMEM_SPEC] * 2 + [VMEM_SPEC] * len(toks) + [ANY_SPEC] * len(slots)
    return call(
        lambda *refs: self_forward_kernel(sh, *refs),
        "self_forward",
        (lens, order, *toks, *slots),
        specs,
        outs,
        scratch,
        16,
    )


def cross_tiles(sh, lens, order, mlens, b, bias, bounds, skip_pad, body):
    z = lax.axis_index("seq")
    starts, ends = doc_bounds(lens, order)
    for p in range(DOCS):
        bounds[0, p] = starts[p]
        bounds[1, p] = ends[p]
    base = z * sh.rows + b * TILE
    slots = [order[0, p] for p in range(DOCS)]
    pos = lane_pos(base)
    low = pick(starts, ends, pos, [s * MEM for s in slots])
    high = pick(starts, ends, pos, [s * MEM + mlens[0, s] for s in slots])

    def doc(p, carry):
        slot = order[0, p]
        seen = (bounds[0, p] < base + TILE) & (bounds[1, p] > base)
        if skip_pad:
            seen = seen & (slot != DOCS - 1)
        number = jnp.where(seen, (mlens[0, slot] + TILE - 1) // TILE, 0)

        def step(i, inner):
            t = slot * (MEM // TILE) + i
            k_pos = t * TILE + lax.broadcasted_iota(jnp.int32, (TILE, TILE), 0)
            bias[...] = jnp.where((k_pos >= low) & (k_pos < high), 0.0, NEG)
            body(t)
            return inner

        return lax.fori_loop(0, number, step, carry)

    lax.fori_loop(0, DOCS, doc, 0)


def touched_tile(sh, lens, order, mlens, t, bounds, skip_pad):
    z = lax.axis_index("seq")
    slot = t // (MEM // TILE)
    base = z * sh.rows
    seen = (bounds[2, slot] < base + sh.rows) & (bounds[3, slot] > base)
    seen = seen & (t % (MEM // TILE) * TILE < mlens[0, slot])
    if skip_pad:
        seen = seen & (slot != DOCS - 1)
    return seen


def slot_bounds(lens, order, bounds):
    starts, ends = doc_bounds(lens, order)
    for p in range(DOCS):
        bounds[2, order[0, p]] = starts[p]
        bounds[3, order[0, p]] = ends[p]


def cross_forward_kernel(sh, lens, order, mlens, *refs):
    count, rows, n, split = sh.count, sh.rows, sh.piece, sh.split
    tok, ctx, vec = refs[:3]
    mems = refs[3 : 3 + 2 * split - 1]
    slots = refs[2 + 2 * split : 2 + 2 * split + count]
    outs = refs[2 + 2 * split + count :]
    (n1, inv1, first_low, q_ref, q_t3, mk3, mv3, mk_t3, cctx, cctx_t3, lse, mem) = outs[:12]
    (wo, wcq, wck, wcv, mv_t3, q_t, bias, m_ref, l_ref, acc, bounds, sems) = outs[12:]
    z = lax.axis_index("seq")
    for i, w in enumerate((wo, wcq, wck, wcv)):
        start_weight(sh, slots, i * n, n, w, sems.at[i])
    own = mems[0]
    tiles_per = sh.mem_rows // TILE

    def place(source, shard):
        for i in range(tiles_per):
            pltpu.make_async_copy(
                source.at[pl.ds(i * TILE, TILE)], mem.at[shard * tiles_per + i], sems.at[4]
            ).start()

    place(own, z)
    for k in range(1, split):
        up, down = mems[2 * k - 1], mems[2 * k]

        @pl.when(z >= k)
        def _(up=up, k=k):
            place(up, z - k)

        @pl.when(z + k < split)
        def _(down=down, k=k):
            place(down, z + k)

    slot_bounds(lens, order, bounds)
    spread_zero(q_t)
    wait_all(wo, sems.at[0])
    wait_all(wcq, sems.at[1])

    def own_rows(i, carry):
        r = pl.ds(pl.multiple_of(i * TILE, TILE), TILE)
        v = tok[r, :].astype(F32) + (mm(ctx[r, :], wo[...]) + vec[V_SOB : V_SOB + 1, :])
        normal, inv = norm_stats(v)
        n1[r, :] = normal
        inv1[r, :] = inv
        low = (normal * vec[V_G1 : V_G1 + 1, :] + vec[V_S1 : V_S1 + 1, :]).astype(BF)
        first_low[r, :] = low
        q = (mm(low, wcq[...]) + vec[V_CQB : V_CQB + 1, :]).astype(BF)
        q = q * BF(HDIM**-0.5)
        q_ref[r, :] = q
        q_t3[i] = q.T
        return carry

    lax.fori_loop(0, rows // TILE, own_rows, 0)
    wait_all(wck, sems.at[2])
    wait_all(wcv, sems.at[3])
    wait_all(mem, sems.at[4])

    def mem_tile(t, carry):
        @pl.when(touched_tile(sh, lens, order, mlens, t, bounds, False))
        def _():
            x = mem[t]
            key = mm(x, wck[...]).astype(BF)
            val = (mm(x, wcv[...]) + vec[V_CVB : V_CVB + 1, :]).astype(BF)
            mk3[t] = key
            mv3[t] = val
            mk_t3[t] = key.T
            mv_t3[t] = val.T

        return carry

    lax.fori_loop(0, sh.m_blocks, mem_tile, 0)

    def block(b, carry):
        spread_rows(q_t3.at[b], q_t)
        forward_start(m_ref, l_ref, acc)
        cross_tiles(
            sh,
            lens,
            order,
            mlens,
            b,
            bias,
            bounds,
            False,
            lambda t: forward_tile(mk3.at[t], mv_t3.at[t], bias, q_t, m_ref, l_ref, acc),
        )
        forward_end(b, m_ref, l_ref, acc, cctx, cctx_t3, lse)
        return carry

    lax.fori_loop(0, sh.q_blocks, block, 0)


def cross_forward(sh, lens, order, mlens, tok, ctx, vec, mems, slots):
    nm, nq = sh.m_blocks, sh.q_blocks
    outs = [
        shape((sh.rows, D), F32),
        shape((sh.rows, 1), F32),
        shape((sh.rows, D), BF),
        shape((sh.rows, D), BF),
        shape((nq, D, TILE), BF),
        shape((nm, TILE, D), BF),
        shape((nm, TILE, D), BF),
        shape((nm, D, TILE), BF),
        shape((sh.rows, D), BF),
        shape((nq, D, TILE), F32),
        shape((nq, HEADS, TILE), F32),
        shape((nm, TILE, D), BF),
    ]
    scratch = [
        pltpu.VMEM((D, D), BF),
        pltpu.VMEM((D, D), BF),
        pltpu.VMEM((D, D), BF),
        pltpu.VMEM((D, D), BF),
        pltpu.VMEM((nm, D, TILE), BF),
        pltpu.VMEM((HEADS, 2 * HDIM, TILE), BF),
        pltpu.VMEM((TILE, TILE), F32),
        pltpu.VMEM((HEADS, TILE), F32),
        pltpu.VMEM((HEADS, TILE), F32),
        pltpu.VMEM((D, TILE), F32),
        pltpu.SMEM((4, DOCS), jnp.int32),
        pltpu.SemaphoreType.DMA((5,)),
    ]
    specs = [SMEM_SPEC] * 3 + [VMEM_SPEC] * 3 + [ANY_SPEC] * (len(mems) + len(slots))
    return call(
        lambda *refs: cross_forward_kernel(sh, *refs),
        "cross_forward",
        (lens, order, mlens, tok, ctx, vec, *mems, *slots),
        specs,
        outs,
        scratch,
        21,
    )


def feed_kernel(sh, lens, order, *refs):
    count, rows, n, wide = sh.count, sh.rows, sh.piece, sh.wide_piece
    n1, cctx, targets, vec = refs[:4]
    slots = refs[4 : 4 + count]
    outs = refs[4 + count :]
    (final_ref, g_second, g_cc, g_cc_t3, vec_grad) = outs[:5]
    (sec_low, hid, feed_low, g_exp, g_cross) = outs[5:10]
    (wco, w1, w2, n2, dact, loss, sems) = outs[10:]
    z = lax.axis_index("seq")
    start_weight(sh, slots, 4 * n, n, wco, sems.at[0])
    for c in range(FFB):
        start_weight(sh, slots, (5 + c) * n, n, w1.at[c], sems.at[1 + c])
    start_weight(sh, slots, 9 * n, wide, w2, sems.at[5])
    vec_grad[...] = jnp.zeros(vec_grad.shape, F32)
    loss[...] = jnp.zeros(loss.shape, F32)
    starts, ends = doc_bounds(lens, order)
    pad_start, pad_end = jnp.int32(0), jnp.int32(0)
    for p in range(DOCS):
        is_pad = order[0, p] == DOCS - 1
        pad_start = jnp.where(is_pad, starts[p], pad_start)
        pad_end = jnp.where(is_pad, ends[p], pad_end)
    wait_all(wco, sems.at[0])
    for c in range(FFB):
        wait_all(w1.at[c], sems.at[1 + c])
    wait_all(w2, sems.at[5])

    def add_vec(row, value):
        vec_grad[row : row + 1, :] = vec_grad[row : row + 1, :] + value

    def chunk(i, carry):
        r = pl.ds(pl.multiple_of(i * TILE, TILE), TILE)
        first = n1[r, :] * vec[V_G1 : V_G1 + 1, :] + vec[V_S1 : V_S1 + 1, :]
        v = first + (mm(cctx[r, :], wco[...]) + vec[V_COB : V_COB + 1, :])
        normal2, inv2 = norm_stats(v)
        n2[...] = normal2
        second = normal2 * vec[V_G2 : V_G2 + 1, :] + vec[V_S2 : V_S2 + 1, :]
        low = second.astype(BF)
        sec_low[r, :] = low
        feed = second + vec[V_CB : V_CB + 1, :]
        for c in range(FFB):
            e = mm(low, w1[c]) + vec[V_EB + c : V_EB + c + 1, :]
            sg = jax.nn.sigmoid(e)
            h = (e * sg).astype(BF)
            hid[c, r, :] = h
            dact[c] = sg * (1.0 + e * (1.0 - sg))
            feed = feed + mm(h, w2[pl.ds(c * D, D), :])
        normal3, inv3 = norm_stats(feed)
        final = normal3 * vec[V_G3 : V_G3 + 1, :] + vec[V_S3 : V_S3 + 1, :]
        final_ref[r, :] = final.astype(BF)
        diff = final - targets[r, :].astype(F32)
        pos = z * rows + i * TILE + lax.broadcasted_iota(jnp.int32, (TILE, 1), 0)
        live = jnp.where((pos >= pad_start) & (pos < pad_end), 0.0, 1.0)
        g = live * diff
        loss[0:1, :] = loss[0:1, :] + col_sum(g * diff)
        add_vec(V_G3, col_sum(g * normal3))
        add_vec(V_S3, col_sum(g))
        g_third = norm_back(g, normal3, inv3, vec[V_G3 : V_G3 + 1, :])
        g_low = g_third.astype(BF)
        feed_low[r, :] = g_low
        add_vec(V_CB, col_sum(g_low))
        total = g_third
        for c in range(FFB):
            ge = (mm_nt(g_low, w2[pl.ds(c * D, D), :]) * dact[c]).astype(BF)
            g_exp[c, r, :] = ge
            add_vec(V_EB + c, col_sum(ge))
            total = total + mm_nt(ge, w1[c])
        normal2 = n2[...]
        add_vec(V_G2, col_sum(total * normal2))
        add_vec(V_S2, col_sum(total))
        gs = norm_back(total, normal2, inv2, vec[V_G2 : V_G2 + 1, :])
        g_second[r, :] = gs
        gc = gs.astype(BF)
        g_cross[r, :] = gc
        add_vec(V_COB, col_sum(gc))
        gcc = mm_nt(gc, wco[...]).astype(BF)
        g_cc[r, :] = gcc
        g_cc_t3[i] = gcc.T
        return carry

    lax.fori_loop(0, rows // TILE, chunk, 0)
    live_count = jnp.int32(rows) - jnp.maximum(
        jnp.minimum(pad_end, (z + 1) * rows) - jnp.maximum(pad_start, z * rows), 0
    )
    bits = digit_bits(count * sh.split)
    error_sum = jnp.sum(loss[0:1, :], axis=1, keepdims=True)
    vec_grad[V_LOSS : V_LOSS + 1, :] = digits(error_sum, bits)
    vec_grad[V_LIVE : V_LIVE + 1, :] = digits(jnp.full((1, 1), live_count.astype(F32)), bits)


def feed_weights_kernel(sh, cctx, sec_low, hid, feed_low, g_exp, g_cross, *outs):
    n, wide = sh.piece, sh.wide_piece
    (g_send, g_own, stage, stage2) = outs
    stage[...] = mm_tn(cctx[...], g_cross[...]).astype(BF)
    put_grad(sh, stage, n, 0, g_send, g_own)
    for c in range(FFB):
        stage[...] = mm_tn(sec_low[...], g_exp[c]).astype(BF)
        put_grad(sh, stage, n, (1 + c) * n, g_send, g_own)
    for c in range(FFB):
        stage2[pl.ds(c * D, D), :] = mm_tn(hid[c], feed_low[...]).astype(BF)
    put_grad(sh, stage2, wide, 5 * n, g_send, g_own)


def feed_weights(sh, arrays):
    block = 5 * sh.piece + sh.wide_piece
    outs = [
        shape((sh.count // 2, block, D), BF),
        shape((sh.count // 2, block, D), BF),
    ]
    return call(
        lambda *refs: feed_weights_kernel(sh, *refs),
        "feed_weights",
        arrays,
        [VMEM_SPEC] * len(arrays),
        outs,
        [pltpu.VMEM((D, D), BF), pltpu.VMEM((FFB * D, D), BF)],
        6,
        SHARED_BYTES,
    )


def feed(sh, lens, order, n1, cctx, targets, vec, slots):
    rows, nq = sh.rows, sh.q_blocks
    outs = [
        shape((rows, D), BF),
        shape((rows, D), F32),
        shape((rows, D), BF),
        shape((nq, D, TILE), BF),
        shape((VROWS, D), F32),
        shape((rows, D), BF),
        shape((FFB, rows, D), BF),
        shape((rows, D), BF),
        shape((FFB, rows, D), BF),
        shape((rows, D), BF),
    ]
    scratch = [
        pltpu.VMEM((D, D), BF),
        pltpu.VMEM((FFB, D, D), BF),
        pltpu.VMEM((FFB * D, D), BF),
        pltpu.VMEM((TILE, D), F32),
        pltpu.VMEM((FFB, TILE, D), F32),
        pltpu.VMEM((8, D), F32),
        pltpu.SemaphoreType.DMA((6,)),
    ]
    specs = [SMEM_SPEC] * 2 + [VMEM_SPEC] * 4 + [ANY_SPEC] * len(slots)
    return call(
        lambda *refs: feed_kernel(sh, *refs),
        "feed",
        (lens, order, n1, cctx, targets, vec, *slots),
        specs,
        outs,
        scratch,
        14,
        SHARED_BYTES,
    )


def mem_shard(z, slot, high):
    low, mid = z % 2, (z // 2) % 2
    low = low if slot % 2 else 1 - low
    mid = mid if slot >= 2 else 1 - mid
    return 4 * high + 2 * mid + low


def cross_backward_kernel(sh, lens, order, mlens, *refs):
    count, n = sh.count, sh.piece
    (q_ref, q_t3, mk3, mv3, mk_t3, cctx_t3, lse, g_cc, g_cc_t3) = refs[:9]
    slots = refs[9 : 9 + count]
    outs = refs[9 + count :]
    mem_parts = outs[:4]
    (dq, k_low3, v_low3) = outs[4:7]
    (wck, wcv, q_t, g_t, q_m, g_m, delta, bias, dk, dv, dq_t, bounds, sems) = outs[7:]
    for i, w in enumerate((wck, wcv)):
        start_weight(sh, slots, (2 + i) * n, n, w, sems.at[i])
    slot_bounds(lens, order, bounds)
    spread_zero(q_t)
    spread_zero(g_t)

    def clear(t, carry):
        @pl.when(touched_tile(sh, lens, order, mlens, t, bounds, True))
        def _():
            dk[t] = jnp.zeros((TILE, D), F32)
            dv[t] = jnp.zeros((TILE, D), F32)

        return carry

    lax.fori_loop(0, sh.m_blocks, clear, 0)

    def block(b, carry):
        backward_start(b, q_t3, g_cc_t3, q_ref, g_cc, cctx_t3, q_t, g_t, q_m, g_m, delta, dq_t)
        cross_tiles(
            sh,
            lens,
            order,
            mlens,
            b,
            bias,
            bounds,
            True,
            lambda t: backward_tile(
                mk3.at[t],
                mv3.at[t],
                mk_t3.at[t],
                bias,
                q_t,
                g_t,
                q_m,
                g_m,
                lse.at[b],
                delta,
                dk.at[t],
                dv.at[t],
                dq_t,
            ),
        )
        r = pl.ds(pl.multiple_of(b * TILE, TILE), TILE)
        dq[r, :] = (dq_t[...] * HDIM**-0.5).T.astype(BF)
        return carry

    lax.fori_loop(0, sh.q_blocks, block, 0)
    wait_all(wck, sems.at[0])
    wait_all(wcv, sems.at[1])

    z = lax.axis_index("seq")
    tiles_per = sh.mem_rows // TILE

    def mem_tile(i, carry, slot, out):
        shard = mem_shard(z, slot, i // tiles_per)
        t = shard * tiles_per + i % tiles_per
        seen = touched_tile(sh, lens, order, mlens, t, bounds, True)

        @pl.when(seen)
        def _():
            k_low = dk[t].astype(BF)
            v_low = dv[t].astype(BF)
            k_low3[t] = k_low
            v_low3[t] = v_low
            out[i] = (mm_nt(k_low, wck[...]) + mm_nt(v_low, wcv[...])).astype(BF)

        @pl.when(jnp.logical_not(seen))
        def _():
            out[i] = jnp.zeros((TILE, D), BF)

        return carry

    for slot, out in enumerate(mem_parts):
        lax.fori_loop(
            0, sh.m_blocks // 4, lambda i, c, slot=slot, out=out: mem_tile(i, c, slot, out), 0
        )


def cross_backward(sh, lens, order, mlens, arrays, slots):
    rows, nm = sh.rows, sh.m_blocks
    outs = [shape((nm // 4, TILE, D), BF)] * 4 + [
        shape((rows, D), BF),
        shape((nm, TILE, D), BF),
        shape((nm, TILE, D), BF),
    ]
    scratch = [
        pltpu.VMEM((D, D), BF),
        pltpu.VMEM((D, D), BF),
        pltpu.VMEM((HEADS, 2 * HDIM, TILE), BF),
        pltpu.VMEM((HEADS, 2 * HDIM, TILE), BF),
        pltpu.VMEM((HEADS, TILE, 2 * HDIM), BF),
        pltpu.VMEM((HEADS, TILE, 2 * HDIM), BF),
        pltpu.VMEM((HEADS, TILE), F32),
        pltpu.VMEM((TILE, TILE), F32),
        pltpu.VMEM((nm, TILE, D), F32),
        pltpu.VMEM((nm, TILE, D), F32),
        pltpu.VMEM((D, TILE), F32),
        pltpu.SMEM((4, DOCS), jnp.int32),
        pltpu.SemaphoreType.DMA((2,)),
    ]
    specs = [SMEM_SPEC] * 3 + [VMEM_SPEC] * len(arrays) + [ANY_SPEC] * len(slots)
    return call(
        lambda *refs: cross_backward_kernel(sh, *refs),
        "cross_backward",
        (lens, order, mlens, *arrays, *slots),
        specs,
        outs,
        scratch,
        15,
    )


def first_backward_kernel(sh, lens, order, mlens, *refs):
    count, rows, n = sh.count, sh.rows, sh.piece
    (dq, k_low3, v_low3, g_second, n1, inv1, first_low, mem, ctx, vec, vec_in) = refs[:11]
    slots = refs[11 : 11 + count]
    outs = refs[11 + count :]
    (g_send, g_own, g_first, g_ctx, g_ctx_t3, vec_grad) = outs[:6]
    (wo, wcq, g_self, acc_k, acc_v, stage, bounds, sems) = outs[6:]
    for i, w in enumerate((wo, wcq)):
        start_weight(sh, slots, i * n, n, w, sems.at[i])
    vec_grad[...] = vec_in[...]
    slot_bounds(lens, order, bounds)
    wait_all(wo, sems.at[0])
    wait_all(wcq, sems.at[1])

    def add_vec(row, value):
        vec_grad[row : row + 1, :] = vec_grad[row : row + 1, :] + value

    acc_k[...] = jnp.zeros(acc_k.shape, F32)
    acc_v[...] = jnp.zeros(acc_v.shape, F32)

    def mem_tile(t, carry):
        @pl.when(touched_tile(sh, lens, order, mlens, t, bounds, True))
        def _():
            k_low = k_low3[t]
            v_low = v_low3[t]
            x = mem[t]
            acc_k[...] = acc_k[...] + mm_tn(x, k_low)
            acc_v[...] = acc_v[...] + mm_tn(x, v_low)
            add_vec(V_CVB, col_sum(v_low))

        return carry

    lax.fori_loop(0, sh.m_blocks, mem_tile, 0)

    def own_rows(i, carry):
        r = pl.ds(pl.multiple_of(i * TILE, TILE), TILE)
        total = g_second[r, :] + mm_nt(dq[r, :], wcq[...])
        normal = n1[r, :]
        add_vec(V_G1, col_sum(total * normal))
        add_vec(V_S1, col_sum(total))
        gf = norm_back(total, normal, inv1[r, :], vec[V_G1 : V_G1 + 1, :])
        g_first[r, :] = gf
        low = gf.astype(BF)
        g_self[r, :] = low
        add_vec(V_SOB, col_sum(low))
        gc = mm_nt(low, wo[...]).astype(BF)
        g_ctx[r, :] = gc
        g_ctx_t3[i] = gc.T
        return carry

    lax.fori_loop(0, rows // TILE, own_rows, 0)
    add_vec(V_CQB, col_sum(dq[...]))
    stage[...] = mm_tn(ctx[...], g_self[...]).astype(BF)
    put_grad(sh, stage, n, 0, g_send, g_own)
    stage[...] = mm_tn(first_low[...], dq[...]).astype(BF)
    put_grad(sh, stage, n, n, g_send, g_own)
    stage[...] = acc_k[...].astype(BF)
    put_grad(sh, stage, n, 2 * n, g_send, g_own)
    stage[...] = acc_v[...].astype(BF)
    put_grad(sh, stage, n, 3 * n, g_send, g_own)


def first_backward(sh, lens, order, mlens, arrays, slots):
    rows, nq, n = sh.rows, sh.q_blocks, sh.piece
    outs = [
        shape((sh.count // 2, 4 * n, D), BF),
        shape((sh.count // 2, 4 * n, D), BF),
        shape((rows, D), F32),
        shape((rows, D), BF),
        shape((nq, D, TILE), BF),
        shape((VROWS, D), F32),
    ]
    scratch = [
        pltpu.VMEM((D, D), BF),
        pltpu.VMEM((D, D), BF),
        pltpu.VMEM((rows, D), BF),
        pltpu.VMEM((D, D), F32),
        pltpu.VMEM((D, D), F32),
        pltpu.VMEM((D, D), BF),
        pltpu.SMEM((4, DOCS), jnp.int32),
        pltpu.SemaphoreType.DMA((2,)),
    ]
    specs = [SMEM_SPEC] * 3 + [VMEM_SPEC] * len(arrays) + [ANY_SPEC] * len(slots)
    return call(
        lambda *refs: first_backward_kernel(sh, *refs),
        "first_backward",
        (lens, order, mlens, *arrays, *slots),
        specs,
        outs,
        scratch,
        6,
    )


def self_backward_kernel(sh, lens, order, *refs):
    count, rows, n, halo = sh.count, sh.rows, sh.piece, sh.halo
    (q_ref, q_t3, k3, v3, k_t3, ctx_t3, lse, g_ctx, g_ctx_t3) = refs[:9]
    slots = refs[9 : 9 + count]
    outs = refs[9 + count :]
    (grad_halo, dq, k_low3, v_low3) = outs[:4]
    (wk, wv, q_t, g_t, q_m, g_m, delta, bias, dk, dv, dq_t, sems) = outs[4:]
    z = lax.axis_index("seq")
    for i, w in enumerate((wk, wv)):
        start_weight(sh, slots, (1 + i) * n, n, w, sems.at[i])
    spread_zero(q_t)
    spread_zero(g_t)

    def clear(t, carry):
        dk[t] = jnp.zeros((TILE, D), F32)
        dv[t] = jnp.zeros((TILE, D), F32)
        return carry

    lax.fori_loop(0, sh.k_blocks, clear, 0)

    def block(b, carry):
        backward_start(b, q_t3, g_ctx_t3, q_ref, g_ctx, ctx_t3, q_t, g_t, q_m, g_m, delta, dq_t)
        self_tiles(
            sh,
            lens,
            order,
            b,
            bias,
            lambda t: backward_tile(
                k3.at[t],
                v3.at[t],
                k_t3.at[t],
                bias,
                q_t,
                g_t,
                q_m,
                g_m,
                lse.at[b],
                delta,
                dk.at[t],
                dv.at[t],
                dq_t,
            ),
        )
        r = pl.ds(pl.multiple_of(b * TILE, TILE), TILE)
        dq[r, :] = (dq_t[...] * HDIM**-0.5).T.astype(BF)
        return carry

    lax.fori_loop(0, sh.q_blocks, block, 0)
    wait_all(wk, sems.at[0])
    wait_all(wv, sems.at[1])
    tiles = rows // TILE

    def lower(t, carry):
        k_low3[t] = dk[t].astype(BF)
        v_low3[t] = dv[t].astype(BF)
        return carry

    lax.fori_loop(0, sh.k_blocks, lower, 0)
    for k in range(halo, 0, -1):

        def window_rows(i, carry, k=k):
            r = pl.ds(pl.multiple_of(i * TILE, TILE), TILE)
            t = (halo - k) * tiles + i
            part = mm_nt(k_low3[t], wk[...]) + mm_nt(v_low3[t], wv[...])
            grad_halo[k - 1, r, :] = part.astype(BF)
            return carry

        @pl.when(z >= k)
        def _(window_rows=window_rows):
            lax.fori_loop(0, tiles, window_rows, 0)

        @pl.when(z < k)
        def _(k=k):
            grad_halo[k - 1] = jnp.zeros((rows, D), BF)


def self_backward(sh, lens, order, arrays, slots):
    rows, nb = sh.rows, sh.k_blocks
    outs = [
        shape((sh.halo, rows, D), BF),
        shape((rows, D), BF),
        shape((nb, TILE, D), BF),
        shape((nb, TILE, D), BF),
    ]
    scratch = [
        pltpu.VMEM((D, D), BF),
        pltpu.VMEM((D, D), BF),
        pltpu.VMEM((HEADS, 2 * HDIM, TILE), BF),
        pltpu.VMEM((HEADS, 2 * HDIM, TILE), BF),
        pltpu.VMEM((HEADS, TILE, 2 * HDIM), BF),
        pltpu.VMEM((HEADS, TILE, 2 * HDIM), BF),
        pltpu.VMEM((HEADS, TILE), F32),
        pltpu.VMEM((TILE, TILE), F32),
        pltpu.VMEM((nb, TILE, D), F32),
        pltpu.VMEM((nb, TILE, D), F32),
        pltpu.VMEM((D, TILE), F32),
        pltpu.SemaphoreType.DMA((2,)),
    ]
    specs = [SMEM_SPEC] * 2 + [VMEM_SPEC] * len(arrays) + [ANY_SPEC] * len(slots)
    return call(
        lambda *refs: self_backward_kernel(sh, *refs),
        "self_backward",
        (lens, order, *arrays, *slots),
        specs,
        outs,
        scratch,
        14,
    )


def self_weights_kernel(sh, *refs):
    count, rows, n, halo = sh.count, sh.rows, sh.piece, sh.halo
    (dq, k_low3, v_low3, g_first, vec_in) = refs[:5]
    toks = refs[5 : 6 + halo]
    slots = refs[6 + halo : 6 + halo + count]
    outs = refs[6 + halo + count :]
    (g_send, g_own, grad_own) = outs[:3]
    (wq, wk, wv, acc_k, acc_v, vec_grad, stage, sems) = outs[3:]
    z = lax.axis_index("seq")
    for i, w in enumerate((wq, wk, wv)):
        start_weight(sh, slots, i * n, n, w, sems.at[i])
    vec_grad[...] = vec_in[...]
    tiles = rows // TILE

    def add_vec(row, value):
        vec_grad[row : row + 1, :] = vec_grad[row : row + 1, :] + value

    acc_k[...] = jnp.zeros(acc_k.shape, F32)
    acc_v[...] = jnp.zeros(acc_v.shape, F32)
    for k in range(halo, -1, -1):

        def window_rows(i, carry, k=k):
            r = pl.ds(pl.multiple_of(i * TILE, TILE), TILE)
            t = (halo - k) * tiles + i
            x = toks[k][r, :]
            acc_k[...] = acc_k[...] + mm_tn(x, k_low3[t])
            acc_v[...] = acc_v[...] + mm_tn(x, v_low3[t])
            add_vec(V_SVB, col_sum(v_low3[t]))
            return carry

        @pl.when(z >= k)
        def _(window_rows=window_rows):
            lax.fori_loop(0, tiles, window_rows, 0)

    add_vec(V_SQB, col_sum(dq[...]))
    stage[...] = mm_tn(toks[0][...], dq[...]).astype(BF)
    put_grad(sh, stage, n, 0, g_send, g_own)
    stage[...] = acc_k[...].astype(BF)
    put_grad(sh, stage, n, n, g_send, g_own)
    stage[...] = acc_v[...].astype(BF)
    put_grad(sh, stage, n, 2 * n, g_send, g_own)
    vec_low = vec_grad[...].astype(BF)
    for s in range(count // 2):
        g_send[s, pl.ds(3 * n, VROWS), :] = vec_low
        g_own[s, pl.ds(3 * n, VROWS), :] = vec_low
    for i, w in enumerate((wq, wk, wv)):
        wait_all(w, sems.at[i])

    def own_rows(i, carry):
        r = pl.ds(pl.multiple_of(i * TILE, TILE), TILE)
        t = halo * tiles + i
        part = mm_nt(k_low3[t], wk[...]) + mm_nt(v_low3[t], wv[...])
        grad_own[r, :] = g_first[r, :] + part + mm_nt(dq[r, :], wq[...])
        return carry

    lax.fori_loop(0, tiles, own_rows, 0)


def self_weights(sh, arrays, toks, slots):
    rows, n = sh.rows, sh.piece
    outs = [
        shape((sh.count // 2, 3 * n + VROWS, D), BF),
        shape((sh.count // 2, 3 * n + VROWS, D), BF),
        shape((rows, D), F32),
    ]
    scratch = [
        pltpu.VMEM((D, D), BF),
        pltpu.VMEM((D, D), BF),
        pltpu.VMEM((D, D), BF),
        pltpu.VMEM((D, D), F32),
        pltpu.VMEM((D, D), F32),
        pltpu.VMEM((VROWS, D), F32),
        pltpu.VMEM((D, D), BF),
        pltpu.SemaphoreType.DMA((3,)),
    ]
    specs = [VMEM_SPEC] * (len(arrays) + len(toks)) + [ANY_SPEC] * len(slots)
    return call(
        lambda *refs: self_weights_kernel(sh, *refs),
        "self_weights",
        (*arrays, *toks, *slots),
        specs,
        outs,
        scratch,
        7,
    )


def shards(
    tokens,
    memory,
    targets,
    doc_lengths,
    doc_order,
    memory_lengths,
    self_query,
    self_query_bias,
    self_key,
    self_value,
    self_value_bias,
    self_output,
    self_output_bias,
    first_gain,
    first_shift,
    cross_query,
    cross_query_bias,
    cross_key,
    cross_value,
    cross_value_bias,
    cross_output,
    cross_output_bias,
    second_gain,
    second_shift,
    expand_weight,
    expand_bias,
    contract_weight,
    contract_bias,
    third_gain,
    third_shift,
):
    split = lax.axis_size("seq")
    count = lax.axis_size("fsdp")
    n = self_query.shape[0]
    wide = contract_weight.shape[0]
    sh = Shard(tokens.shape[0], memory.shape[0], count, split, n, wide)

    own_a, own_b = pack(
        sh,
        (
            self_query_bias,
            self_value_bias,
            self_output_bias,
            first_gain,
            first_shift,
            cross_query_bias,
            cross_value_bias,
            cross_output_bias,
            second_gain,
            second_shift,
            contract_bias,
            third_gain,
            third_shift,
        ),
        expand_bias,
        (
            self_query,
            self_key,
            self_value,
            self_output,
            cross_query,
            cross_key,
            cross_value,
            cross_output,
            expand_weight,
            contract_weight,
        ),
    )
    toks = [tokens]
    for _ in range(sh.halo):
        toks.append(seq_up(toks[-1], split))
    slots_a = fsdp_gather(own_a, count)
    near = slots_a[count // 2 - 1]
    slots_b = fsdp_gather(after(own_b, toks[1], near), count)
    ups, downs = [seq_up(after(memory, toks[1]), split)], [seq_down(after(memory, toks[1]), split)]
    for k in range(2, split):
        if k == split - 1:
            last = after(memory, ups[0])
            ups.append(lax.ppermute(last, "seq", [(0, split - 1)]))
            downs.append(lax.ppermute(last, "seq", [(split - 1, 0)]))
        else:
            ups.append(seq_up(ups[-1], split))
            downs.append(seq_down(downs[-1], split))
    mems = [memory]
    for up, down in zip(ups, downs):
        mems += [up, down]

    first_tok = after(tokens, ups[0], downs[0], slots_b[1], slots_b[2])
    (q, q_t3, k3, v3, k_t3, ctx, ctx_t3, lse, vec) = self_forward(
        sh, doc_lengths, doc_order, [first_tok] + toks[1:], slots_a
    )
    (n1, inv1, first_low, cq, cq_t3, mk3, mv3, mk_t3, cctx, cctx_t3, clse, mem) = cross_forward(
        sh, doc_lengths, doc_order, memory_lengths, tokens, ctx, vec, mems, slots_b
    )
    feed_out = feed(sh, doc_lengths, doc_order, n1, cctx, targets, vec, slots_b)
    (final_low, g_second, g_cc, g_cc_t3, vec_grad, sec_low, hid, feed_low, g_exp, g_cross) = (
        feed_out
    )
    (send_c, own_c) = feed_weights(sh, (cctx, sec_low, hid, feed_low, g_exp, g_cross))
    sum_c = Reduction(send_c, own_c, count, split, True)
    sum_c.step()
    cq = after(cq, sum_c.send)
    sum_c.step()
    *mem_parts, dcq, k_low3, v_low3 = cross_backward(
        sh,
        doc_lengths,
        doc_order,
        memory_lengths,
        (cq, cq_t3, mk3, mv3, mk_t3, cctx_t3, clse, g_cc, g_cc_t3),
        slots_b,
    )
    dcq = after(dcq, sum_c.send)
    sum_c.step(dcq)
    swap = [(i, i ^ 1) for i in range(split)]
    mem_got = lax.ppermute(mem_parts[0], "seq", swap)
    (send_b, own_b, g_first, g_ctx, g_ctx_t3, vec_grad) = first_backward(
        sh,
        doc_lengths,
        doc_order,
        memory_lengths,
        (dcq, k_low3, v_low3, g_second, n1, inv1, first_low, mem, ctx, vec, vec_grad),
        slots_b,
    )
    mem_away = add_low(after(mem_parts[1], g_first), mem_got)
    sum_b = Reduction(send_b, own_b, count, split, True)
    g_ctx = after(g_ctx, sum_c.send, mem_away)
    sum_c.step(g_ctx)
    sum_b.step(g_ctx)
    mem_got = lax.ppermute(after(mem_parts[2], g_ctx), "seq", swap)
    mem_far = lax.ppermute(after(mem_away, g_ctx), "seq", [(i, i ^ 2) for i in range(split)])
    mem_here = mem_parts[3].astype(F32) + mem_got.astype(F32) + mem_far.astype(F32)
    (grad_halo, dq, sk_low3, sv_low3) = self_backward(
        sh,
        doc_lengths,
        doc_order,
        (q, q_t3, k3, v3, k_t3, ctx_t3, lse, g_ctx, g_ctx_t3),
        slots_a,
    )
    dq = after(dq, mem_here, sum_c.send, sum_b.send)
    back = seq_down(after(grad_halo[sh.halo - 1], dq), split)
    sum_b.step(dq)
    sum_c.step(dq)
    (send_a, own_a, grad_own) = self_weights(
        sh,
        (dq, sk_low3, sv_low3, g_first, vec_grad),
        toks,
        slots_a,
    )
    send_a = after(send_a, sum_b.send, sum_c.send)
    sum_a = Reduction(send_a, own_a, count, split, True)
    sum_a.step()
    sum_b.step(send_a)
    sum_c.step(send_a)
    for k in range(sh.halo - 1, 0, -1):
        back = seq_down(after(add_low(grad_halo[k - 1], back), send_a), split)
    sum_a.step()
    ready, held = sum_a.send, (sum_b.send, sum_c.send)
    while [a for a, _ in sum_a.plan].count("fsdp"):
        sum_a.step()
    sum_b.step(ready)
    ready = sum_a.send
    sum_a.step(back, *held)
    sum_b.step(ready)
    red_a = sum_a.finish()
    red_b = sum_b.finish()
    red_c = sum_c.finish()
    input_grad = grad_own + back.astype(F32)
    memory_grad = seq_rest(mem_here.reshape(split // 4, sh.mem_rows, D), split)[0]

    def rows_of(array, start, size):
        return array[start : start + size].astype(F32)

    done = finish(sh, red_a, expand_bias.shape[0])
    small_grad = done[3 : 3 + V_EB]
    expand_bias_grad = done[3 + V_EB]
    loss_value = done[4 + V_EB].reshape(())
    expand_grad = jnp.concatenate(
        [rows_of(red_c, (1 + c) * n, n) for c in range(FFB)], axis=1
    )
    return (
        final_low,
        loss_value,
        input_grad,
        memory_grad,
        done[0],
        small_grad[V_SQB],
        done[1],
        done[2],
        small_grad[V_SVB],
        rows_of(red_b, 0, n),
        small_grad[V_SOB],
        small_grad[V_G1],
        small_grad[V_S1],
        rows_of(red_b, n, n),
        small_grad[V_CQB],
        rows_of(red_b, 2 * n, n),
        rows_of(red_b, 3 * n, n),
        small_grad[V_CVB],
        rows_of(red_c, 0, n),
        small_grad[V_COB],
        small_grad[V_G2],
        small_grad[V_S2],
        expand_grad,
        expand_bias_grad,
        rows_of(red_c, 5 * n, wide),
        small_grad[V_CB],
        small_grad[V_G3],
        small_grad[V_S3],
    )


def solution(mesh):
    rows = P(("fsdp", "seq"), None)
    matrix = P("fsdp", None)
    vector = P("fsdp")
    kinds = (
        "mvmmvmvvvmvmmvmvvvmvmvvv"
    )
    weights = tuple(matrix if kind == "m" else vector for kind in kinds)
    return jax.shard_map(
        shards,
        mesh=mesh,
        in_specs=(rows, rows, rows, matrix, matrix, matrix) + weights,
        out_specs=(rows, P(), rows, rows) + weights,
        check_vma=False,
    )
```

```python
import jax
import jax.numpy as jnp
from jax import lax
from jax.experimental import pallas as pl
from jax.experimental.pallas import tpu as pltpu
from jax.sharding import PartitionSpec as P

D = 512
HDIM = 64
HEADS = D // HDIM
DOCS = 4
MEM = 512
FFB = 4
TILE = 256
GROUP = 4
VROWS = 32
NEG = -1e30
BF = jnp.bfloat16
F32 = jnp.float32
VMEM_BYTES = 60 * 1024 * 1024
FLOPS_RATE = 3e13

(
    V_SQB,
    V_SVB,
    V_SOB,
    V_G1,
    V_S1,
    V_CQB,
    V_CVB,
    V_COB,
    V_G2,
    V_S2,
    V_CB,
    V_G3,
    V_S3,
    V_EB,
) = range(14)
V_LOSS = V_EB + FFB
V_LIVE = V_LOSS + 1
LOW_BITS = 36
HIGH_BITS = 36


def mm(a, b):
    return jnp.dot(a, b, preferred_element_type=F32)


def mm_nt(a, b):
    return lax.dot_general(a, b, (((1,), (1,)), ((), ())), preferred_element_type=F32)


def mm_tn(a, b):
    return lax.dot_general(a, b, (((0,), (0,)), ((), ())), preferred_element_type=F32)


def col_sum(v):
    return jnp.sum(v.astype(F32), axis=0, keepdims=True)


def chip_steps(count):
    bits = []
    bit = 2
    while bit < count:
        bits.append(bit)
        bit *= 2
    return bits, bits[::-1]


def gather_masks(count):
    result = []
    for steps in chip_steps(count):
        masks = [0]
        for step in steps:
            masks = masks + [m ^ step for m in masks]
        result.append(masks)
    own0, own1 = result
    return [own0 + [m ^ 1 for m in own1], own1 + [m ^ 1 for m in own0]]


def reduce_masks(count):
    result = []
    for steps in chip_steps(count):
        masks = [0]
        for step in steps[::-1]:
            masks = masks + [m ^ step for m in masks]
        result.append(masks)
    return result


def step_pairs(count, index):
    orders = chip_steps(count)
    return [(i, i ^ orders[i & 1][index]) for i in range(count)]


def fsdp_gather_parts(own, count):
    have = [own]
    for index in range(len(chip_steps(count)[0])):
        pairs = step_pairs(count, index)
        have = have + [lax.ppermute(a, "fsdp", pairs) for a in have]
    return have, [(i, i ^ 1) for i in range(count)]


def fsdp_gather(own, count):
    have, swap = fsdp_gather_parts(own, count)
    return have + [lax.ppermute(a, "fsdp", swap) for a in have]


def add_low(a, b):
    return (a.astype(F32) + b.astype(F32)).astype(BF)


def after(value, *others):
    return lax.optimization_barrier((value, *others))[0]


def sum_low(parts):
    total = parts[0].astype(F32)
    for part in parts[1:]:
        total = total + part.astype(F32)
    return total.astype(BF)


class Reduction:
    def __init__(self, send, own, count, split):
        self.send, self.parts = send, [own]
        self.odd = (lax.axis_index("seq") % 2) == 1
        self.got = None
        self.plan = [("fsdp", [(i, i ^ 1) for i in range(count)])]
        for index in range(len(chip_steps(count)[0])):
            self.plan.append(("fsdp", step_pairs(count, index)))
        bits = [1 << k for k in range(split.bit_length() - 1)]
        for bit in bits + [1]:
            self.plan.append(("seq", [(i, i ^ bit) for i in range(split)]))

    def start(self, *others):
        send = after(self.send, *others) if others else self.send
        self.axis, pairs = self.plan.pop(0)
        self.got = lax.ppermute(send, self.axis, pairs)

    def end(self, *others):
        if others:
            self.parts[0] = after(self.parts[0], *others)
        left = sum(1 for axis, _ in self.plan if axis == "fsdp")
        if self.axis == "fsdp":
            self.parts.append(self.got)
            if left > 0:
                half = self.got.shape[0] // 2
                self.send = sum_low([part[half:] for part in self.parts])
                self.parts = [part[:half] for part in self.parts]
            else:
                total = sum_low([part[0] for part in self.parts])
                half = total.shape[0] // 2
                self.send = jnp.where(self.odd, total[:half], total[half:])
                self.parts = [jnp.where(self.odd, total[half:], total[:half])]
        elif self.plan:
            self.send = sum_low([self.parts[0], self.got])
            self.parts = [self.send]
        else:
            mine, got = self.parts[0], self.got
            self.send = jnp.where(
                self.odd, jnp.concatenate([got, mine]), jnp.concatenate([mine, got])
            )

    def step(self, *others):
        self.start(*others)
        self.end()

    def finish(self):
        while self.plan:
            self.step()
        return self.send


def seq_rest(parts, split):
    z = lax.axis_index("seq")
    bit = 4
    while bit < split:
        pairs = parts.reshape(parts.shape[0] // 2, 2, *parts.shape[1:])
        odd = (z // bit) % 2 == 1
        got = lax.ppermute(
            jnp.where(odd, pairs[:, 0], pairs[:, 1]), "seq", [(i, i ^ bit) for i in range(split)]
        )
        parts = jnp.where(odd, pairs[:, 1], pairs[:, 0]) + got
        bit *= 2
    return parts


def seq_up(a, count):
    return lax.ppermute(a, "seq", [(i, i + 1) for i in range(count - 1)])


def seq_down(a, count):
    return lax.ppermute(a, "seq", [(i + 1, i) for i in range(count - 1)])


def slot_place(index, masks, slot):
    return jnp.where(index % 2 == 0, index ^ masks[0][slot], index ^ masks[1][slot])


class Shard:
    def __init__(self, rows, mem_rows, count, split, piece, wide_piece):
        self.rows = rows
        self.mem_rows = mem_rows
        self.count = count
        self.split = split
        self.piece = piece
        self.wide_piece = wide_piece
        self.group_rows = rows * split
        self.group_mem = mem_rows * split
        self.halo = min(-(-(self.group_rows // 2 - 1) // rows), split - 1)
        self.window = rows * (self.halo + 1)
        self.q_blocks = rows // TILE
        self.k_blocks = self.window // TILE
        self.m_blocks = self.group_mem // TILE
        self.gather = gather_masks(count)
        self.reduce = reduce_masks(count)


def start_weight(sh, slots, row, n, target, sem):
    index = lax.axis_index("fsdp")
    for s, slot in enumerate(slots):
        place = pl.multiple_of(slot_place(index, sh.gather, s) * n, n)
        pltpu.make_async_copy(slot.at[pl.ds(row, n)], target.at[pl.ds(place, n)], sem).start()


def wait_all(target, sem):
    pltpu.make_async_copy(target, target, sem).wait()


def tile_copies(t, sources, targets, sems):
    return [
        pltpu.make_async_copy(source.at[t], target.at[t], sems.at[i, t])
        for i, (source, target) in enumerate(zip(sources, targets))
    ]


def start_mems(sh, mems, target, sems, wanted):
    z = lax.axis_index("seq")
    tiles_per = sh.mem_rows // TILE

    def place(source, shard):
        for i in range(tiles_per):
            t = shard * tiles_per + i

            @pl.when(wanted(t))
            def _(i=i, t=t):
                pltpu.make_async_copy(
                    source.at[pl.ds(i * TILE, TILE)], target.at[t], sems.at[t]
                ).start()

    place(mems[0], z)
    for k in range(1, sh.split):
        up, down = mems[2 * k - 1], mems[2 * k]

        @pl.when(z >= k)
        def _(up=up, k=k):
            place(up, z - k)

        @pl.when(z + k < sh.split)
        def _(down=down, k=k):
            place(down, z + k)


def wait_mem(target, t, sems):
    pltpu.make_async_copy(target.at[t], target.at[t], sems.at[t]).wait()


def put_grad(sh, full, n, row, send_ref, own_ref):
    index = lax.axis_index("fsdp")
    partner = index ^ 1
    for s in range(sh.count // 2):
        mine = pl.multiple_of(slot_place(index, sh.reduce, s) * n, n)
        theirs = pl.multiple_of(slot_place(partner, sh.reduce, s) * n, n)
        own_ref[s, pl.ds(row, n), :] = full[pl.ds(mine, n), :]
        send_ref[s, pl.ds(row, n), :] = full[pl.ds(theirs, n), :]


def doc_bounds(lens, order):
    starts, ends = [], []
    total = jnp.int32(0)
    for p in range(DOCS):
        starts.append(total)
        total = total + lens[0, order[0, p]]
        ends.append(total)
    return starts, ends


def pick(starts, ends, pos, values):
    out = jnp.zeros_like(pos)
    for p in range(DOCS):
        out = jnp.where((pos >= starts[p]) & (pos < ends[p]), values[p], out)
    return out


def lane_pos(base):
    return base + lax.broadcasted_iota(jnp.int32, (1, TILE), 1)


def norm_stats(v):
    mean = jnp.mean(v, axis=1, keepdims=True)
    c = v - mean
    inv = lax.rsqrt(jnp.mean(c * c, axis=1, keepdims=True) + 1e-05)
    return c * inv, inv


def norm_back(dy, n, inv, gain):
    e = dy * gain
    return inv * (
        e - jnp.mean(e, axis=1, keepdims=True) - n * jnp.mean(e * n, axis=1, keepdims=True)
    )


def head_rows(h):
    return slice(h * HDIM, (h + 1) * HDIM)


def pair_lanes(h):
    j = h // 2
    return slice(j * 2 * HDIM, (j + 1) * 2 * HDIM)


def spread_rows(source, target):
    for h in range(HEADS):
        o = (h % 2) * HDIM
        target[h, pl.ds(o, HDIM), :] = source[head_rows(h), :]


def spread_zero(target):
    for h in range(HEADS):
        o = (1 - h % 2) * HDIM
        target[h, pl.ds(o, HDIM), :] = jnp.zeros((HDIM, TILE), BF)


def spread_lanes(source, target):
    lane = lax.broadcasted_iota(jnp.int32, (TILE, 2 * HDIM), 1)
    for h in range(HEADS):
        part = source[:, pair_lanes(h)]
        keep = (lane >= HDIM) if h % 2 else (lane < HDIM)
        target[h] = jnp.where(keep, part, jnp.zeros_like(part))


def forward_tile(keys, vals_t, bias, q_t, m_ref, l_ref, acc_ref):
    heads = range(HEADS)
    mask = bias[...]
    m_old, l_old = m_ref[...], l_ref[...]
    scores = [mm(keys[:, pair_lanes(h)], q_t[h]) + mask for h in heads]
    tops = [
        jnp.maximum(m_old[h : h + 1], jnp.max(scores[h], axis=0, keepdims=True)) for h in heads
    ]
    probs = [jnp.exp(scores[h] - tops[h]) for h in heads]
    alphas = [jnp.exp(m_old[h : h + 1] - tops[h]) for h in heads]
    sums = [
        alphas[h] * l_old[h : h + 1] + jnp.sum(probs[h], axis=0, keepdims=True) for h in heads
    ]
    outs = [mm(vals_t[head_rows(h), :], probs[h].astype(BF)) for h in heads]
    for h in heads:
        acc_ref[head_rows(h), :] = acc_ref[head_rows(h), :] * alphas[h] + outs[h]
    m_ref[...] = jnp.concatenate(tops, axis=0)
    l_ref[...] = jnp.concatenate(sums, axis=0)


def forward_start(m_ref, l_ref, acc_ref):
    m_ref[...] = jnp.full(m_ref.shape, NEG, F32)
    l_ref[...] = jnp.zeros(l_ref.shape, F32)
    acc_ref[...] = jnp.zeros(acc_ref.shape, F32)


def forward_end(b, m_ref, l_ref, acc_ref, ctx_ref, ctx_t_ref, lse_ref):
    lse_ref[b] = m_ref[...] + jnp.log(l_ref[...])
    for h in range(HEADS):
        acc_ref[head_rows(h), :] = acc_ref[head_rows(h), :] / l_ref[h : h + 1, :]
    ctx_t_ref[b] = acc_ref[...]
    ctx_ref[pl.ds(pl.multiple_of(b * TILE, TILE), TILE), :] = acc_ref[...].T.astype(BF)


def backward_tile(keys, vals, keys_t, bias, q_t, g_t, q_m, g_m, lse, delta, dk, dv, dq_t):
    mask = bias[...]
    for first in range(0, HEADS, GROUP):
        heads = range(first, first + GROUP)
        scores = [mm(keys[:, pair_lanes(h)], q_t[h]) for h in heads]
        probs = [jnp.exp(s + mask - lse[h : h + 1, :]) for h, s in zip(heads, scores)]
        dvs = [mm(p.astype(BF), g_m[h]) for h, p in zip(heads, probs)]
        dps = [mm(vals[:, pair_lanes(h)], g_t[h]) for h in heads]
        dss = [
            (p * (dp - delta[h : h + 1, :])).astype(BF) for h, p, dp in zip(heads, probs, dps)
        ]
        dks = [mm(ds, q_m[h]) for h, ds in zip(heads, dss)]
        dqs = [mm(keys_t[head_rows(h), :], ds) for h, ds in zip(heads, dss)]
        for i in range(0, GROUP, 2):
            lanes = pair_lanes(first + i)
            dv[:, lanes] = dv[:, lanes] + dvs[i] + dvs[i + 1]
            dk[:, lanes] = dk[:, lanes] + dks[i] + dks[i + 1]
        for h, dq in zip(heads, dqs):
            dq_t[head_rows(h), :] = dq_t[head_rows(h), :] + dq


def backward_start(b, q_t3, g_t3, q, g, ctx_t3, q_t, g_t, q_m, g_m, delta, dq_t):
    rows = pl.ds(pl.multiple_of(b * TILE, TILE), TILE)
    spread_rows(q_t3.at[b], q_t)
    spread_rows(g_t3.at[b], g_t)
    spread_lanes(q[rows, :], q_m)
    spread_lanes(g[rows, :], g_m)
    prod = g_t3[b].astype(F32) * ctx_t3[b]
    for h in range(HEADS):
        delta[h : h + 1, :] = jnp.sum(prod[head_rows(h), :], axis=0, keepdims=True)
    dq_t[...] = jnp.zeros(dq_t.shape, F32)


def self_tiles(sh, lens, order, b, bias, body):
    z = lax.axis_index("seq")
    starts, ends = doc_bounds(lens, order)
    shift = (z - sh.halo) * sh.rows
    q_base = sh.halo * sh.rows + b * TILE
    first = pick(starts, ends, q_base + shift, starts) - shift
    q_pos = lane_pos(q_base)
    q_start = pick(starts, ends, q_pos + shift, starts) - shift
    last = q_base // TILE
    number = last - first // TILE + 1

    def step(i, carry):
        t = last - i
        k_pos = t * TILE + lax.broadcasted_iota(jnp.int32, (TILE, TILE), 0)
        bias[...] = jnp.where((k_pos >= q_start) & (k_pos <= q_pos), 0.0, NEG)
        body(t)
        return carry

    lax.fori_loop(0, number, step, 0)


def self_forward_kernel(sh, lens, order, *refs):
    halo, count, rows, n = sh.halo, sh.count, sh.rows, sh.piece
    toks = refs[: halo + 1]
    slots = refs[halo + 1 : halo + 1 + count]
    (q_ref, q_t3, k3, v3, k_t3, ctx, ctx_t3, lse, vec) = refs[halo + 1 + count : halo + 10 + count]
    (wq, wk, wv, vec_slots, v_t3, q_t, bias, m_ref, l_ref, acc, sems) = refs[halo + 10 + count :]
    z = lax.axis_index("seq")
    for s, slot in enumerate(slots):
        pltpu.make_async_copy(slot.at[pl.ds(3 * n, VROWS)], vec_slots.at[s], sems.at[3]).start()
    for i, w in enumerate((wq, wk, wv)):
        start_weight(sh, slots, i * n, n, w, sems.at[i])
    spread_zero(q_t)
    wait_all(vec_slots, sems.at[3])
    vec[...] = jnp.sum(vec_slots[...].astype(F32), axis=0)
    wait_all(wq, sems.at[0])
    wait_all(wk, sems.at[1])
    wait_all(wv, sems.at[2])
    tiles = rows // TILE

    def own_rows(i, carry):
        r = pl.ds(pl.multiple_of(i * TILE, TILE), TILE)
        q = (mm(toks[0][r, :], wq[...]) + vec[V_SQB : V_SQB + 1, :]).astype(BF)
        q = q * BF(HDIM**-0.5)
        q_ref[r, :] = q
        q_t3[i] = q.T
        return carry

    lax.fori_loop(0, tiles, own_rows, 0)
    for k in range(halo + 1):

        def window_rows(i, carry, k=k):
            r = pl.ds(pl.multiple_of(i * TILE, TILE), TILE)
            t = (halo - k) * tiles + i
            x = toks[k][r, :]
            key = mm(x, wk[...]).astype(BF)
            val = (mm(x, wv[...]) + vec[V_SVB : V_SVB + 1, :]).astype(BF)
            k3[t] = key
            v3[t] = val
            k_t3[t] = key.T
            v_t3[t] = val.T
            return carry

        @pl.when(z >= k)
        def _(window_rows=window_rows):
            lax.fori_loop(0, tiles, window_rows, 0)

    def block(b, carry):
        spread_rows(q_t3.at[b], q_t)
        forward_start(m_ref, l_ref, acc)
        self_tiles(
            sh,
            lens,
            order,
            b,
            bias,
            lambda t: forward_tile(k3.at[t], v_t3.at[t], bias, q_t, m_ref, l_ref, acc),
        )
        forward_end(b, m_ref, l_ref, acc, ctx, ctx_t3, lse)
        return carry

    lax.fori_loop(0, sh.q_blocks, block, 0)


SMEM_SPEC = pl.BlockSpec(memory_space=pltpu.SMEM)
VMEM_SPEC = pl.BlockSpec(memory_space=pltpu.VMEM)
ANY_SPEC = pl.BlockSpec(memory_space=pl.ANY)


def shape(dims, dtype):
    return jax.ShapeDtypeStruct(dims, dtype)


def call(body, name, inputs, specs, outs, scratch, micros, vmem=VMEM_BYTES, out_specs=None):
    moved = sum(a.size * a.dtype.itemsize for a in (*inputs, *outs))
    cost = pl.CostEstimate(
        flops=int(micros * 1e-6 * FLOPS_RATE), transcendentals=0, bytes_accessed=moved // 50
    )
    return pl.pallas_call(
        body,
        name=name,
        in_specs=specs,
        out_specs=out_specs or [VMEM_SPEC] * len(outs),
        out_shape=outs,
        scratch_shapes=scratch,
        cost_estimate=cost,
        compiler_params=pltpu.CompilerParams(vmem_limit_bytes=vmem),
    )(*inputs)


def pack_kernel(sh, *refs):
    small = refs[:V_EB]
    wide_bias = refs[V_EB]
    mats = refs[V_EB + 1 : V_EB + 11]
    own_a, own_b = refs[V_EB + 11 :]
    n, wide = sh.piece, sh.wide_piece
    (sq, sk, sv, so, cq, ck, cv, co, w1, w2) = mats
    for i, m in enumerate((sq, sk, sv)):
        own_a[pl.ds(i * n, n), :] = m[...]
    for i, m in enumerate((so, cq, ck, cv, co)):
        own_b[pl.ds(i * n, n), :] = m[...]
    for c in range(FFB):
        own_b[pl.ds((5 + c) * n, n), :] = w1[:, c * D : (c + 1) * D]
    own_b[pl.ds(9 * n, wide), :] = w2[...]
    index = lax.axis_index("fsdp")

    def spread(piece, size, offset):
        hot = lax.broadcasted_iota(jnp.int32, (size, D), 1) == offset + lax.broadcasted_iota(
            jnp.int32, (size, D), 0
        )
        return mm(piece, hot.astype(BF)).astype(BF)

    rows = jnp.concatenate([r[...].reshape(1, n) for r in small], axis=0)
    size = wide_bias.shape[0]
    flat = index * size
    line = spread(wide_bias[...].reshape(1, size), size, flat % D)
    row = lax.broadcasted_iota(jnp.int32, (FFB, D), 0)
    own_a[pl.ds(3 * n, VROWS), :] = jnp.concatenate(
        [
            spread(rows, n, index * n),
            jnp.where(row == flat // D, line, jnp.zeros((FFB, D), BF)),
            jnp.zeros((VROWS - V_EB - FFB, D), BF),
        ],
        axis=0,
    )


def pack(sh, small, wide_bias, mats):
    n, wide = sh.piece, sh.wide_piece
    outs = [shape((3 * n + VROWS, D), BF), shape((9 * n + wide, D), BF)]
    return call(
        lambda *refs: pack_kernel(sh, *refs),
        "pack",
        (*small, wide_bias, *mats),
        [VMEM_SPEC] * (V_EB + 1 + len(mats)),
        outs,
        [],
        2,
    )


def digit_bits(devices):
    return 3 if 7 * devices <= 256 else 1


def digits(value, bits):
    lane = lax.broadcasted_iota(jnp.int32, (1, D), 1)
    scale = jnp.full((1, D), 2.0**LOW_BITS, F32)
    for i in range(9):
        scale = scale * jnp.where((lane // 2**i) % 2 == 1, 2.0 ** -min(bits * 2**i, 140), 1.0)
    whole = jnp.floor(value * scale)
    return whole - 2.0**bits * jnp.floor(value * scale * 2.0**-bits)


def undigits(row, bits):
    lane = lax.broadcasted_iota(jnp.int32, (1, D), 1)
    scale = jnp.full((1, D), 2.0**-LOW_BITS, F32)
    for i in range(7):
        scale = scale * jnp.where(
            (lane // 2**i) % 2 == 1, 2.0 ** min(bits * 2**i, LOW_BITS + HIGH_BITS), 1.0
        )
    used = lane < (LOW_BITS + HIGH_BITS) // bits
    return jnp.sum(jnp.where(used, row * jnp.where(used, scale, 0.0), 0.0), axis=1, keepdims=True)


def finish_kernel(sh, red, *outs):
    n = sh.piece
    mats, small, wide_bias, loss = outs[:3], outs[3 : 3 + V_EB], outs[3 + V_EB], outs[4 + V_EB]
    for i, m in enumerate(mats):
        m[...] = red[pl.ds(i * n, n), :].astype(F32)
    index = lax.axis_index("fsdp")
    vec = red[pl.ds(3 * n, VROWS), :]

    def cut(rows, size, offset):
        hot = lax.broadcasted_iota(jnp.int32, (D, size), 0) == offset + lax.broadcasted_iota(
            jnp.int32, (D, size), 1
        )
        return mm(rows, hot.astype(BF))

    parts = cut(vec, n, index * n)
    for i in range(V_EB):
        small[i][...] = parts[i : i + 1, :].reshape(n)
    size = wide_bias.shape[0]
    flat = index * size
    row = lax.broadcasted_iota(jnp.int32, (VROWS, D), 0)
    lines = jnp.where(row == V_EB + flat // D, vec.astype(F32), 0.0).astype(BF)
    wide_bias[...] = jnp.sum(cut(lines, size, flat % D), axis=0, keepdims=True).reshape(size)
    bits = digit_bits(sh.count * sh.split)
    error_sum = undigits(vec[V_LOSS : V_LOSS + 1, :].astype(F32), bits)
    live = undigits(vec[V_LIVE : V_LIVE + 1, :].astype(F32), bits)
    loss[...] = error_sum / (live * D)


def finish(sh, red, bias_size):
    n = sh.piece
    outs = [shape((n, D), F32)] * 3 + [shape((n,), F32)] * V_EB
    outs += [shape((bias_size,), F32), shape((1, 1), F32)]
    return call(
        lambda *refs: finish_kernel(sh, *refs), "finish", (red,), [VMEM_SPEC], outs, [], 2
    )


def self_forward(sh, lens, order, toks, slots):
    nb, nq = sh.k_blocks, sh.q_blocks
    outs = [
        shape((sh.rows, D), BF),
        shape((nq, D, TILE), BF),
        shape((nb, TILE, D), BF),
        shape((nb, TILE, D), BF),
        shape((nb, D, TILE), BF),
        shape((sh.rows, D), BF),
        shape((nq, D, TILE), F32),
        shape((nq, HEADS, TILE), F32),
        shape((VROWS, D), F32),
    ]
    scratch = [
        pltpu.VMEM((D, D), BF),
        pltpu.VMEM((D, D), BF),
        pltpu.VMEM((D, D), BF),
        pltpu.VMEM((sh.count, VROWS, D), BF),
        pltpu.VMEM((nb, D, TILE), BF),
        pltpu.VMEM((HEADS, 2 * HDIM, TILE), BF),
        pltpu.VMEM((TILE, TILE), F32),
        pltpu.VMEM((HEADS, TILE), F32),
        pltpu.VMEM((HEADS, TILE), F32),
        pltpu.VMEM((D, TILE), F32),
        pltpu.SemaphoreType.DMA((4,)),
    ]
    specs = [SMEM_SPEC] * 2 + [VMEM_SPEC] * len(toks) + [ANY_SPEC] * len(slots)
    return call(
        lambda *refs: self_forward_kernel(sh, *refs),
        "self_forward",
        (lens, order, *toks, *slots),
        specs,
        outs,
        scratch,
        16,
    )


def cross_tiles(sh, lens, order, mlens, b, bias, bounds, skip_pad, body):
    z = lax.axis_index("seq")
    starts, ends = doc_bounds(lens, order)
    for p in range(DOCS):
        bounds[0, p] = starts[p]
        bounds[1, p] = ends[p]
    base = z * sh.rows + b * TILE
    slots = [order[0, p] for p in range(DOCS)]
    pos = lane_pos(base)
    low = pick(starts, ends, pos, [s * MEM for s in slots])
    high = pick(starts, ends, pos, [s * MEM + mlens[0, s] for s in slots])

    def doc(p, carry):
        slot = order[0, p]
        seen = (bounds[0, p] < base + TILE) & (bounds[1, p] > base)
        if skip_pad:
            seen = seen & (slot != DOCS - 1)
        number = jnp.where(seen, (mlens[0, slot] + TILE - 1) // TILE, 0)

        def step(i, inner):
            t = slot * (MEM // TILE) + i
            k_pos = t * TILE + lax.broadcasted_iota(jnp.int32, (TILE, TILE), 0)
            bias[...] = jnp.where((k_pos >= low) & (k_pos < high), 0.0, NEG)
            body(t)
            return inner

        return lax.fori_loop(0, number, step, carry)

    lax.fori_loop(0, DOCS, doc, 0)


def touched_tile(sh, lens, order, mlens, t, bounds, skip_pad):
    z = lax.axis_index("seq")
    slot = t // (MEM // TILE)
    base = z * sh.rows
    seen = (bounds[2, slot] < base + sh.rows) & (bounds[3, slot] > base)
    seen = seen & (t % (MEM // TILE) * TILE < mlens[0, slot])
    if skip_pad:
        seen = seen & (slot != DOCS - 1)
    return seen


def slot_bounds(lens, order, bounds):
    starts, ends = doc_bounds(lens, order)
    for p in range(DOCS):
        bounds[2, order[0, p]] = starts[p]
        bounds[3, order[0, p]] = ends[p]


def cross_forward_kernel(sh, lens, order, mlens, *refs):
    count, rows, n, split = sh.count, sh.rows, sh.piece, sh.split
    tok, ctx, vec = refs[:3]
    mems = refs[3 : 3 + 2 * split - 1]
    slots = refs[2 + 2 * split : 2 + 2 * split + count]
    outs = refs[2 + 2 * split + count :]
    (n1, inv1, first_low, q_ref, q_t3, *kept, cctx, cctx_t3, lse) = outs[:11]
    (wo, wcq, wck, wcv, mem, mk3, mv3, mk_t3, mv_t3, q_t, bias, m_ref, l_ref, acc) = outs[11:25]
    (bounds, sems, mem_sems, tile_sems) = outs[25:]
    for i, w in enumerate((wo, wcq, wck, wcv)):
        start_weight(sh, slots, i * n, n, w, sems.at[i])

    def wanted(t):
        return touched_tile(sh, lens, order, mlens, t, bounds, False)

    slot_bounds(lens, order, bounds)
    start_mems(sh, mems, mem, mem_sems, wanted)
    spread_zero(q_t)
    wait_all(wo, sems.at[0])
    wait_all(wcq, sems.at[1])

    def own_rows(i, carry):
        r = pl.ds(pl.multiple_of(i * TILE, TILE), TILE)
        v = tok[r, :].astype(F32) + (mm(ctx[r, :], wo[...]) + vec[V_SOB : V_SOB + 1, :])
        normal, inv = norm_stats(v)
        n1[r, :] = normal
        inv1[r, :] = inv
        low = (normal * vec[V_G1 : V_G1 + 1, :] + vec[V_S1 : V_S1 + 1, :]).astype(BF)
        first_low[r, :] = low
        q = (mm(low, wcq[...]) + vec[V_CQB : V_CQB + 1, :]).astype(BF)
        q = q * BF(HDIM**-0.5)
        q_ref[r, :] = q
        q_t3[i] = q.T
        return carry

    lax.fori_loop(0, rows // TILE, own_rows, 0)
    wait_all(wck, sems.at[2])
    wait_all(wcv, sems.at[3])

    def mem_tile(t, carry):
        @pl.when(wanted(t))
        def _():
            wait_mem(mem, t, mem_sems)
            x = mem[t]
            key = mm(x, wck[...]).astype(BF)
            val = (mm(x, wcv[...]) + vec[V_CVB : V_CVB + 1, :]).astype(BF)
            mk3[t] = key
            mv3[t] = val
            mk_t3[t] = key.T
            mv_t3[t] = val.T
            for copy in tile_copies(t, (mk3, mv3, mk_t3), kept, tile_sems):
                copy.start()

        return carry

    lax.fori_loop(0, sh.m_blocks, mem_tile, 0)

    def block(b, carry):
        spread_rows(q_t3.at[b], q_t)
        forward_start(m_ref, l_ref, acc)
        cross_tiles(
            sh,
            lens,
            order,
            mlens,
            b,
            bias,
            bounds,
            False,
            lambda t: forward_tile(mk3.at[t], mv_t3.at[t], bias, q_t, m_ref, l_ref, acc),
        )
        forward_end(b, m_ref, l_ref, acc, cctx, cctx_t3, lse)
        return carry

    lax.fori_loop(0, sh.q_blocks, block, 0)

    def settle(t, carry):
        @pl.when(wanted(t))
        def _():
            for copy in tile_copies(t, (mk3, mv3, mk_t3), kept, tile_sems):
                copy.wait()

        return carry

    lax.fori_loop(0, sh.m_blocks, settle, 0)


def cross_forward(sh, lens, order, mlens, tok, ctx, vec, mems, slots):
    nm, nq = sh.m_blocks, sh.q_blocks
    outs = [
        shape((sh.rows, D), F32),
        shape((sh.rows, 1), F32),
        shape((sh.rows, D), BF),
        shape((sh.rows, D), BF),
        shape((nq, D, TILE), BF),
        shape((nm, TILE, D), BF),
        shape((nm, TILE, D), BF),
        shape((nm, D, TILE), BF),
        shape((sh.rows, D), BF),
        shape((nq, D, TILE), F32),
        shape((nq, HEADS, TILE), F32),
    ]
    scratch = [
        pltpu.VMEM((D, D), BF),
        pltpu.VMEM((D, D), BF),
        pltpu.VMEM((D, D), BF),
        pltpu.VMEM((D, D), BF),
        pltpu.VMEM((nm, TILE, D), BF),
        pltpu.VMEM((nm, TILE, D), BF),
        pltpu.VMEM((nm, TILE, D), BF),
        pltpu.VMEM((nm, D, TILE), BF),
        pltpu.VMEM((nm, D, TILE), BF),
        pltpu.VMEM((HEADS, 2 * HDIM, TILE), BF),
        pltpu.VMEM((TILE, TILE), F32),
        pltpu.VMEM((HEADS, TILE), F32),
        pltpu.VMEM((HEADS, TILE), F32),
        pltpu.VMEM((D, TILE), F32),
        pltpu.SMEM((4, DOCS), jnp.int32),
        pltpu.SemaphoreType.DMA((4,)),
        pltpu.SemaphoreType.DMA((nm,)),
        pltpu.SemaphoreType.DMA((3, nm)),
    ]
    specs = [SMEM_SPEC] * 3 + [VMEM_SPEC] * 3 + [ANY_SPEC] * (len(mems) + len(slots))
    return call(
        lambda *refs: cross_forward_kernel(sh, *refs),
        "cross_forward",
        (lens, order, mlens, tok, ctx, vec, *mems, *slots),
        specs,
        outs,
        scratch,
        21,
        out_specs=[VMEM_SPEC] * 5 + [ANY_SPEC] * 3 + [VMEM_SPEC] * 3,
    )


def feed_kernel(sh, lens, order, *refs):
    count, rows, n, wide = sh.count, sh.rows, sh.piece, sh.wide_piece
    n1, cctx, targets, vec = refs[:4]
    slots = refs[4 : 4 + count]
    outs = refs[4 + count :]
    (final_ref, g_second, g_cc, g_cc_t3, vec_grad, g_send, g_own) = outs[:7]
    (sec_low, hid, feed_low, g_exp, g_cross) = outs[7:12]
    (wco, w1, w2, n2, dact, loss, stage, stage2, sems) = outs[12:]
    z = lax.axis_index("seq")
    start_weight(sh, slots, 4 * n, n, wco, sems.at[0])
    for c in range(FFB):
        start_weight(sh, slots, (5 + c) * n, n, w1.at[c], sems.at[1 + c])
    start_weight(sh, slots, 9 * n, wide, w2, sems.at[5])
    vec_grad[...] = jnp.zeros(vec_grad.shape, F32)
    loss[...] = jnp.zeros(loss.shape, F32)
    starts, ends = doc_bounds(lens, order)
    pad_start, pad_end = jnp.int32(0), jnp.int32(0)
    for p in range(DOCS):
        is_pad = order[0, p] == DOCS - 1
        pad_start = jnp.where(is_pad, starts[p], pad_start)
        pad_end = jnp.where(is_pad, ends[p], pad_end)
    wait_all(wco, sems.at[0])
    for c in range(FFB):
        wait_all(w1.at[c], sems.at[1 + c])
    wait_all(w2, sems.at[5])

    def add_vec(row, value):
        vec_grad[row : row + 1, :] = vec_grad[row : row + 1, :] + value

    def chunk(i, carry):
        r = pl.ds(pl.multiple_of(i * TILE, TILE), TILE)
        first = n1[r, :] * vec[V_G1 : V_G1 + 1, :] + vec[V_S1 : V_S1 + 1, :]
        v = first + (mm(cctx[r, :], wco[...]) + vec[V_COB : V_COB + 1, :])
        normal2, inv2 = norm_stats(v)
        n2[...] = normal2
        second = normal2 * vec[V_G2 : V_G2 + 1, :] + vec[V_S2 : V_S2 + 1, :]
        low = second.astype(BF)
        sec_low[r, :] = low
        feed = second + vec[V_CB : V_CB + 1, :]
        wide = range(FFB)
        es = [mm(low, w1[c]) + vec[V_EB + c : V_EB + c + 1, :] for c in wide]
        sgs = [jax.nn.sigmoid(e) for e in es]
        hs = [(e * sg).astype(BF) for e, sg in zip(es, sgs)]
        for c in wide:
            hid[c, r, :] = hs[c]
            dact[c] = sgs[c] * (1.0 + es[c] * (1.0 - sgs[c]))
        for c in wide:
            feed = feed + mm(hs[c], w2[pl.ds(c * D, D), :])
        normal3, inv3 = norm_stats(feed)
        final = normal3 * vec[V_G3 : V_G3 + 1, :] + vec[V_S3 : V_S3 + 1, :]
        final_ref[r, :] = final.astype(BF)
        diff = final - targets[r, :].astype(F32)
        pos = z * rows + i * TILE + lax.broadcasted_iota(jnp.int32, (TILE, 1), 0)
        live = jnp.where((pos >= pad_start) & (pos < pad_end), 0.0, 1.0)
        g = live * diff
        loss[0:1, :] = loss[0:1, :] + col_sum(g * diff)
        add_vec(V_G3, col_sum(g * normal3))
        add_vec(V_S3, col_sum(g))
        g_third = norm_back(g, normal3, inv3, vec[V_G3 : V_G3 + 1, :])
        g_low = g_third.astype(BF)
        feed_low[r, :] = g_low
        add_vec(V_CB, col_sum(g_low))
        total = g_third
        ges = [(mm_nt(g_low, w2[pl.ds(c * D, D), :]) * dact[c]).astype(BF) for c in wide]
        for c in wide:
            total = total + mm_nt(ges[c], w1[c])
        for c in wide:
            g_exp[c, r, :] = ges[c]
            add_vec(V_EB + c, col_sum(ges[c]))
        normal2 = n2[...]
        add_vec(V_G2, col_sum(total * normal2))
        add_vec(V_S2, col_sum(total))
        gs = norm_back(total, normal2, inv2, vec[V_G2 : V_G2 + 1, :])
        g_second[r, :] = gs
        gc = gs.astype(BF)
        g_cross[r, :] = gc
        add_vec(V_COB, col_sum(gc))
        gcc = mm_nt(gc, wco[...]).astype(BF)
        g_cc[r, :] = gcc
        g_cc_t3[i] = gcc.T
        return carry

    lax.fori_loop(0, rows // TILE, chunk, 0)
    live_count = jnp.int32(rows) - jnp.maximum(
        jnp.minimum(pad_end, (z + 1) * rows) - jnp.maximum(pad_start, z * rows), 0
    )
    bits = digit_bits(count * sh.split)
    error_sum = jnp.sum(loss[0:1, :], axis=1, keepdims=True)
    vec_grad[V_LOSS : V_LOSS + 1, :] = digits(error_sum, bits)
    vec_grad[V_LIVE : V_LIVE + 1, :] = digits(jnp.full((1, 1), live_count.astype(F32)), bits)
    stage[...] = mm_tn(cctx[...], g_cross[...]).astype(BF)
    put_grad(sh, stage, n, 0, g_send, g_own)
    for c in range(FFB):
        stage[...] = mm_tn(sec_low[...], g_exp[c]).astype(BF)
        put_grad(sh, stage, n, (1 + c) * n, g_send, g_own)
    for c in range(FFB):
        stage2[pl.ds(c * D, D), :] = mm_tn(hid[c], feed_low[...]).astype(BF)
    put_grad(sh, stage2, wide, 5 * n, g_send, g_own)


def feed(sh, lens, order, n1, cctx, targets, vec, slots):
    rows, nq = sh.rows, sh.q_blocks
    block = 5 * sh.piece + sh.wide_piece
    outs = [
        shape((rows, D), BF),
        shape((rows, D), F32),
        shape((rows, D), BF),
        shape((nq, D, TILE), BF),
        shape((VROWS, D), F32),
        shape((sh.count // 2, block, D), BF),
        shape((sh.count // 2, block, D), BF),
    ]
    scratch = [
        pltpu.VMEM((rows, D), BF),
        pltpu.VMEM((FFB, rows, D), BF),
        pltpu.VMEM((rows, D), BF),
        pltpu.VMEM((FFB, rows, D), BF),
        pltpu.VMEM((rows, D), BF),
        pltpu.VMEM((D, D), BF),
        pltpu.VMEM((FFB, D, D), BF),
        pltpu.VMEM((FFB * D, D), BF),
        pltpu.VMEM((TILE, D), F32),
        pltpu.VMEM((FFB, TILE, D), F32),
        pltpu.VMEM((8, D), F32),
        pltpu.VMEM((D, D), BF),
        pltpu.VMEM((FFB * D, D), BF),
        pltpu.SemaphoreType.DMA((6,)),
    ]
    specs = [SMEM_SPEC] * 2 + [VMEM_SPEC] * 4 + [ANY_SPEC] * len(slots)
    return call(
        lambda *refs: feed_kernel(sh, *refs),
        "feed",
        (lens, order, n1, cctx, targets, vec, *slots),
        specs,
        outs,
        scratch,
        17,
    )


def mem_shard(z, slot, high):
    low, mid = z % 2, (z // 2) % 2
    low = low if slot % 2 else 1 - low
    mid = mid if slot >= 2 else 1 - mid
    return 4 * high + 2 * mid + low


def cross_backward_kernel(sh, lens, order, mlens, *refs):
    count, n = sh.count, sh.piece
    (q_ref, q_t3, *kept, cctx_t3, lse, g_cc, g_cc_t3) = refs[:9]
    slots = refs[9 : 9 + count]
    outs = refs[9 + count :]
    mem_parts = outs[:4]
    (dq, *low_out) = outs[4:7]
    (wck, wcv, q_t, g_t, q_m, g_m, delta, bias, dk, dv, dq_t) = outs[7:18]
    (mk3, mv3, mk_t3, k_low3, v_low3, bounds, sems, tile_sems, low_sems) = outs[18:]
    for i, w in enumerate((wck, wcv)):
        start_weight(sh, slots, (2 + i) * n, n, w, sems.at[i])
    slot_bounds(lens, order, bounds)
    spread_zero(q_t)
    spread_zero(g_t)

    def each_wanted(body):
        def one(t, carry):
            @pl.when(touched_tile(sh, lens, order, mlens, t, bounds, True))
            def _():
                body(t)

            return carry

        lax.fori_loop(0, sh.m_blocks, one, 0)

    def fetch(t):
        for copy in tile_copies(t, kept, (mk3, mv3, mk_t3), tile_sems):
            copy.start()

    def clear(t):
        dk[t] = jnp.zeros((TILE, D), F32)
        dv[t] = jnp.zeros((TILE, D), F32)
        for copy in tile_copies(t, kept, (mk3, mv3, mk_t3), tile_sems):
            copy.wait()

    def low_copies(t):
        return tile_copies(t, (k_low3, v_low3), low_out, low_sems)

    each_wanted(fetch)
    each_wanted(clear)

    def block(b, carry):
        backward_start(b, q_t3, g_cc_t3, q_ref, g_cc, cctx_t3, q_t, g_t, q_m, g_m, delta, dq_t)
        cross_tiles(
            sh,
            lens,
            order,
            mlens,
            b,
            bias,
            bounds,
            True,
            lambda t: backward_tile(
                mk3.at[t],
                mv3.at[t],
                mk_t3.at[t],
                bias,
                q_t,
                g_t,
                q_m,
                g_m,
                lse.at[b],
                delta,
                dk.at[t],
                dv.at[t],
                dq_t,
            ),
        )
        r = pl.ds(pl.multiple_of(b * TILE, TILE), TILE)
        dq[r, :] = (dq_t[...] * HDIM**-0.5).T.astype(BF)
        return carry

    lax.fori_loop(0, sh.q_blocks, block, 0)
    wait_all(wck, sems.at[0])
    wait_all(wcv, sems.at[1])

    z = lax.axis_index("seq")
    tiles_per = sh.mem_rows // TILE

    def mem_tile(i, carry, slot, out):
        shard = mem_shard(z, slot, i // tiles_per)
        t = shard * tiles_per + i % tiles_per
        seen = touched_tile(sh, lens, order, mlens, t, bounds, True)

        @pl.when(seen)
        def _():
            k_low = dk[t].astype(BF)
            v_low = dv[t].astype(BF)
            k_low3[t] = k_low
            v_low3[t] = v_low
            for copy in low_copies(t):
                copy.start()
            out[i] = (mm_nt(k_low, wck[...]) + mm_nt(v_low, wcv[...])).astype(BF)

        @pl.when(jnp.logical_not(seen))
        def _():
            out[i] = jnp.zeros((TILE, D), BF)

        return carry

    for slot, out in enumerate(mem_parts):
        lax.fori_loop(
            0, sh.m_blocks // 4, lambda i, c, slot=slot, out=out: mem_tile(i, c, slot, out), 0
        )

    def settle(t):
        for copy in low_copies(t):
            copy.wait()

    each_wanted(settle)


def cross_backward(sh, lens, order, mlens, arrays, slots):
    rows, nm = sh.rows, sh.m_blocks
    outs = [shape((nm // 4, TILE, D), BF)] * 4 + [
        shape((rows, D), BF),
        shape((nm, TILE, D), BF),
        shape((nm, TILE, D), BF),
    ]
    scratch = [
        pltpu.VMEM((D, D), BF),
        pltpu.VMEM((D, D), BF),
        pltpu.VMEM((HEADS, 2 * HDIM, TILE), BF),
        pltpu.VMEM((HEADS, 2 * HDIM, TILE), BF),
        pltpu.VMEM((HEADS, TILE, 2 * HDIM), BF),
        pltpu.VMEM((HEADS, TILE, 2 * HDIM), BF),
        pltpu.VMEM((HEADS, TILE), F32),
        pltpu.VMEM((TILE, TILE), F32),
        pltpu.VMEM((nm, TILE, D), F32),
        pltpu.VMEM((nm, TILE, D), F32),
        pltpu.VMEM((D, TILE), F32),
        pltpu.VMEM((nm, TILE, D), BF),
        pltpu.VMEM((nm, TILE, D), BF),
        pltpu.VMEM((nm, D, TILE), BF),
        pltpu.VMEM((nm, TILE, D), BF),
        pltpu.VMEM((nm, TILE, D), BF),
        pltpu.SMEM((4, DOCS), jnp.int32),
        pltpu.SemaphoreType.DMA((2,)),
        pltpu.SemaphoreType.DMA((3, nm)),
        pltpu.SemaphoreType.DMA((2, nm)),
    ]
    specs = [SMEM_SPEC] * 3 + [VMEM_SPEC] * 2 + [ANY_SPEC] * 3 + [VMEM_SPEC] * 4
    specs += [ANY_SPEC] * len(slots)
    return call(
        lambda *refs: cross_backward_kernel(sh, *refs),
        "cross_backward",
        (lens, order, mlens, *arrays, *slots),
        specs,
        outs,
        scratch,
        15,
        out_specs=[VMEM_SPEC] * 5 + [ANY_SPEC] * 2,
    )


def first_backward_kernel(sh, lens, order, mlens, *refs):
    count, rows, n = sh.count, sh.rows, sh.piece
    (dq, *low_in, g_second, n1, inv1, first_low, ctx, vec, vec_in) = refs[:10]
    mems = refs[10 : 9 + 2 * sh.split]
    slots = refs[9 + 2 * sh.split : 9 + 2 * sh.split + count]
    outs = refs[9 + 2 * sh.split + count :]
    (g_send, g_own, g_first, g_ctx, g_ctx_t3, vec_grad) = outs[:6]
    (wo, wcq, g_self, acc_k, acc_v, stage, mem, k_low3, v_low3, bounds) = outs[6:16]
    (sems, mem_sems, low_sems) = outs[16:]
    for i, w in enumerate((wo, wcq)):
        start_weight(sh, slots, i * n, n, w, sems.at[i])
    vec_grad[...] = vec_in[...]
    slot_bounds(lens, order, bounds)

    def wanted(t):
        return touched_tile(sh, lens, order, mlens, t, bounds, True)

    def fetch(t, carry):
        @pl.when(wanted(t))
        def _():
            for copy in tile_copies(t, low_in, (k_low3, v_low3), low_sems):
                copy.start()

        return carry

    lax.fori_loop(0, sh.m_blocks, fetch, 0)
    start_mems(sh, mems, mem, mem_sems, wanted)
    wait_all(wo, sems.at[0])
    wait_all(wcq, sems.at[1])

    def add_vec(row, value):
        vec_grad[row : row + 1, :] = vec_grad[row : row + 1, :] + value

    def own_rows(i, carry):
        r = pl.ds(pl.multiple_of(i * TILE, TILE), TILE)
        total = g_second[r, :] + mm_nt(dq[r, :], wcq[...])
        normal = n1[r, :]
        add_vec(V_G1, col_sum(total * normal))
        add_vec(V_S1, col_sum(total))
        gf = norm_back(total, normal, inv1[r, :], vec[V_G1 : V_G1 + 1, :])
        g_first[r, :] = gf
        low = gf.astype(BF)
        g_self[r, :] = low
        add_vec(V_SOB, col_sum(low))
        gc = mm_nt(low, wo[...]).astype(BF)
        g_ctx[r, :] = gc
        g_ctx_t3[i] = gc.T
        return carry

    lax.fori_loop(0, rows // TILE, own_rows, 0)
    acc_k[...] = jnp.zeros(acc_k.shape, F32)
    acc_v[...] = jnp.zeros(acc_v.shape, F32)

    def mem_tile(t, carry):
        @pl.when(wanted(t))
        def _():
            wait_mem(mem, t, mem_sems)
            for copy in tile_copies(t, low_in, (k_low3, v_low3), low_sems):
                copy.wait()
            k_low = k_low3[t]
            v_low = v_low3[t]
            x = mem[t]
            acc_k[...] = acc_k[...] + mm_tn(x, k_low)
            acc_v[...] = acc_v[...] + mm_tn(x, v_low)
            add_vec(V_CVB, col_sum(v_low))

        return carry

    lax.fori_loop(0, sh.m_blocks, mem_tile, 0)

    add_vec(V_CQB, col_sum(dq[...]))
    stage[...] = mm_tn(ctx[...], g_self[...]).astype(BF)
    put_grad(sh, stage, n, 0, g_send, g_own)
    stage[...] = mm_tn(first_low[...], dq[...]).astype(BF)
    put_grad(sh, stage, n, n, g_send, g_own)
    stage[...] = acc_k[...].astype(BF)
    put_grad(sh, stage, n, 2 * n, g_send, g_own)
    stage[...] = acc_v[...].astype(BF)
    put_grad(sh, stage, n, 3 * n, g_send, g_own)


def first_backward(sh, lens, order, mlens, arrays, mems, slots):
    rows, nq, n, nm = sh.rows, sh.q_blocks, sh.piece, sh.m_blocks
    outs = [
        shape((sh.count // 2, 4 * n, D), BF),
        shape((sh.count // 2, 4 * n, D), BF),
        shape((rows, D), F32),
        shape((rows, D), BF),
        shape((nq, D, TILE), BF),
        shape((VROWS, D), F32),
    ]
    scratch = [
        pltpu.VMEM((D, D), BF),
        pltpu.VMEM((D, D), BF),
        pltpu.VMEM((rows, D), BF),
        pltpu.VMEM((D, D), F32),
        pltpu.VMEM((D, D), F32),
        pltpu.VMEM((D, D), BF),
        pltpu.VMEM((nm, TILE, D), BF),
        pltpu.VMEM((nm, TILE, D), BF),
        pltpu.VMEM((nm, TILE, D), BF),
        pltpu.SMEM((4, DOCS), jnp.int32),
        pltpu.SemaphoreType.DMA((2,)),
        pltpu.SemaphoreType.DMA((nm,)),
        pltpu.SemaphoreType.DMA((2, nm)),
    ]
    specs = [SMEM_SPEC] * 3 + [VMEM_SPEC] + [ANY_SPEC] * 2 + [VMEM_SPEC] * 7
    specs += [ANY_SPEC] * (len(mems) + len(slots))
    return call(
        lambda *refs: first_backward_kernel(sh, *refs),
        "first_backward",
        (lens, order, mlens, *arrays, *mems, *slots),
        specs,
        outs,
        scratch,
        6,
    )


def self_backward_kernel(sh, lens, order, *refs):
    count, rows, n, halo = sh.count, sh.rows, sh.piece, sh.halo
    (q_ref, q_t3, k3, v3, k_t3, ctx_t3, lse, g_ctx, g_ctx_t3) = refs[:9]
    slots = refs[9 : 9 + count]
    outs = refs[9 + count :]
    (grad_halo, dq, k_low3, v_low3) = outs[:4]
    (wk, wv, q_t, g_t, q_m, g_m, delta, bias, dk, dv, dq_t, sems) = outs[4:]
    z = lax.axis_index("seq")
    for i, w in enumerate((wk, wv)):
        start_weight(sh, slots, (1 + i) * n, n, w, sems.at[i])
    spread_zero(q_t)
    spread_zero(g_t)

    def clear(t, carry):
        dk[t] = jnp.zeros((TILE, D), F32)
        dv[t] = jnp.zeros((TILE, D), F32)
        return carry

    lax.fori_loop(0, sh.k_blocks, clear, 0)

    def block(b, carry):
        backward_start(b, q_t3, g_ctx_t3, q_ref, g_ctx, ctx_t3, q_t, g_t, q_m, g_m, delta, dq_t)
        self_tiles(
            sh,
            lens,
            order,
            b,
            bias,
            lambda t: backward_tile(
                k3.at[t],
                v3.at[t],
                k_t3.at[t],
                bias,
                q_t,
                g_t,
                q_m,
                g_m,
                lse.at[b],
                delta,
                dk.at[t],
                dv.at[t],
                dq_t,
            ),
        )
        r = pl.ds(pl.multiple_of(b * TILE, TILE), TILE)
        dq[r, :] = (dq_t[...] * HDIM**-0.5).T.astype(BF)
        return carry

    lax.fori_loop(0, sh.q_blocks, block, 0)
    wait_all(wk, sems.at[0])
    wait_all(wv, sems.at[1])
    tiles = rows // TILE

    def lower(t, carry):
        k_low3[t] = dk[t].astype(BF)
        v_low3[t] = dv[t].astype(BF)
        return carry

    lax.fori_loop(0, sh.k_blocks, lower, 0)
    for k in range(halo, 0, -1):

        def window_rows(i, carry, k=k):
            r = pl.ds(pl.multiple_of(i * TILE, TILE), TILE)
            t = (halo - k) * tiles + i
            part = mm_nt(k_low3[t], wk[...]) + mm_nt(v_low3[t], wv[...])
            grad_halo[k - 1, r, :] = part.astype(BF)
            return carry

        @pl.when(z >= k)
        def _(window_rows=window_rows):
            lax.fori_loop(0, tiles, window_rows, 0)

        @pl.when(z < k)
        def _(k=k):
            grad_halo[k - 1] = jnp.zeros((rows, D), BF)


def self_backward(sh, lens, order, arrays, slots):
    rows, nb = sh.rows, sh.k_blocks
    outs = [
        shape((sh.halo, rows, D), BF),
        shape((rows, D), BF),
        shape((nb, TILE, D), BF),
        shape((nb, TILE, D), BF),
    ]
    scratch = [
        pltpu.VMEM((D, D), BF),
        pltpu.VMEM((D, D), BF),
        pltpu.VMEM((HEADS, 2 * HDIM, TILE), BF),
        pltpu.VMEM((HEADS, 2 * HDIM, TILE), BF),
        pltpu.VMEM((HEADS, TILE, 2 * HDIM), BF),
        pltpu.VMEM((HEADS, TILE, 2 * HDIM), BF),
        pltpu.VMEM((HEADS, TILE), F32),
        pltpu.VMEM((TILE, TILE), F32),
        pltpu.VMEM((nb, TILE, D), F32),
        pltpu.VMEM((nb, TILE, D), F32),
        pltpu.VMEM((D, TILE), F32),
        pltpu.SemaphoreType.DMA((2,)),
    ]
    specs = [SMEM_SPEC] * 2 + [VMEM_SPEC] * len(arrays) + [ANY_SPEC] * len(slots)
    return call(
        lambda *refs: self_backward_kernel(sh, *refs),
        "self_backward",
        (lens, order, *arrays, *slots),
        specs,
        outs,
        scratch,
        14,
    )


def self_weights_kernel(sh, *refs):
    count, rows, n, halo = sh.count, sh.rows, sh.piece, sh.halo
    (dq, k_low3, v_low3, g_first, vec_in) = refs[:5]
    toks = refs[5 : 6 + halo]
    slots = refs[6 + halo : 6 + halo + count]
    outs = refs[6 + halo + count :]
    (g_send, g_own, grad_own) = outs[:3]
    (wq, wk, wv, acc_k, acc_v, vec_grad, stage, sems) = outs[3:]
    z = lax.axis_index("seq")
    for i, w in enumerate((wq, wk, wv)):
        start_weight(sh, slots, i * n, n, w, sems.at[i])
    vec_grad[...] = vec_in[...]
    tiles = rows // TILE

    def add_vec(row, value):
        vec_grad[row : row + 1, :] = vec_grad[row : row + 1, :] + value

    acc_k[...] = jnp.zeros(acc_k.shape, F32)
    acc_v[...] = jnp.zeros(acc_v.shape, F32)
    for k in range(halo, -1, -1):

        def window_rows(i, carry, k=k):
            r = pl.ds(pl.multiple_of(i * TILE, TILE), TILE)
            t = (halo - k) * tiles + i
            x = toks[k][r, :]
            acc_k[...] = acc_k[...] + mm_tn(x, k_low3[t])
            acc_v[...] = acc_v[...] + mm_tn(x, v_low3[t])
            add_vec(V_SVB, col_sum(v_low3[t]))
            return carry

        @pl.when(z >= k)
        def _(window_rows=window_rows):
            lax.fori_loop(0, tiles, window_rows, 0)

    add_vec(V_SQB, col_sum(dq[...]))
    stage[...] = mm_tn(toks[0][...], dq[...]).astype(BF)
    put_grad(sh, stage, n, 0, g_send, g_own)
    stage[...] = acc_k[...].astype(BF)
    put_grad(sh, stage, n, n, g_send, g_own)
    stage[...] = acc_v[...].astype(BF)
    put_grad(sh, stage, n, 2 * n, g_send, g_own)
    vec_low = vec_grad[...].astype(BF)
    for s in range(count // 2):
        g_send[s, pl.ds(3 * n, VROWS), :] = vec_low
        g_own[s, pl.ds(3 * n, VROWS), :] = vec_low
    for i, w in enumerate((wq, wk, wv)):
        wait_all(w, sems.at[i])

    def own_rows(i, carry):
        r = pl.ds(pl.multiple_of(i * TILE, TILE), TILE)
        t = halo * tiles + i
        part = mm_nt(k_low3[t], wk[...]) + mm_nt(v_low3[t], wv[...])
        grad_own[r, :] = g_first[r, :] + part + mm_nt(dq[r, :], wq[...])
        return carry

    lax.fori_loop(0, tiles, own_rows, 0)


def self_weights(sh, arrays, toks, slots):
    rows, n = sh.rows, sh.piece
    outs = [
        shape((sh.count // 2, 3 * n + VROWS, D), BF),
        shape((sh.count // 2, 3 * n + VROWS, D), BF),
        shape((rows, D), F32),
    ]
    scratch = [
        pltpu.VMEM((D, D), BF),
        pltpu.VMEM((D, D), BF),
        pltpu.VMEM((D, D), BF),
        pltpu.VMEM((D, D), F32),
        pltpu.VMEM((D, D), F32),
        pltpu.VMEM((VROWS, D), F32),
        pltpu.VMEM((D, D), BF),
        pltpu.SemaphoreType.DMA((3,)),
    ]
    specs = [VMEM_SPEC] * (len(arrays) + len(toks)) + [ANY_SPEC] * len(slots)
    return call(
        lambda *refs: self_weights_kernel(sh, *refs),
        "self_weights",
        (*arrays, *toks, *slots),
        specs,
        outs,
        scratch,
        7,
    )


def shards(
    tokens,
    memory,
    targets,
    doc_lengths,
    doc_order,
    memory_lengths,
    self_query,
    self_query_bias,
    self_key,
    self_value,
    self_value_bias,
    self_output,
    self_output_bias,
    first_gain,
    first_shift,
    cross_query,
    cross_query_bias,
    cross_key,
    cross_value,
    cross_value_bias,
    cross_output,
    cross_output_bias,
    second_gain,
    second_shift,
    expand_weight,
    expand_bias,
    contract_weight,
    contract_bias,
    third_gain,
    third_shift,
):
    split = lax.axis_size("seq")
    count = lax.axis_size("fsdp")
    n = self_query.shape[0]
    wide = contract_weight.shape[0]
    sh = Shard(tokens.shape[0], memory.shape[0], count, split, n, wide)

    own_a, own_b = pack(
        sh,
        (
            self_query_bias,
            self_value_bias,
            self_output_bias,
            first_gain,
            first_shift,
            cross_query_bias,
            cross_value_bias,
            cross_output_bias,
            second_gain,
            second_shift,
            contract_bias,
            third_gain,
            third_shift,
        ),
        expand_bias,
        (
            self_query,
            self_key,
            self_value,
            self_output,
            cross_query,
            cross_key,
            cross_value,
            cross_output,
            expand_weight,
            contract_weight,
        ),
    )
    toks, downs = [tokens, seq_up(tokens, split)], [seq_down(memory, split)]
    swaps = [(i, i ^ 1) for i in range(count)]
    pairs = [step_pairs(count, index) for index in range(len(chip_steps(count)[0]))]
    slots_a, slots_b = [own_a], [own_b]
    own_b_first = [own_b]
    other_b = [lax.ppermute(own_b, "fsdp", swaps)]
    first = [lax.ppermute(own_a, "fsdp", p) for p in pairs]
    hold = (toks[1], downs[0], *first, *other_b)
    for _ in range(1, sh.halo):
        toks.append(seq_up(after(toks[-1], *hold), split))
    ups = [seq_up(after(memory, *hold), split)]
    held_b = after(own_b, *hold)
    second = [lax.ppermute(held_b, "fsdp", p) for p in pairs]
    for index, p in enumerate(pairs):
        slots_a += [first[index]] + [lax.ppermute(after(a, *hold), "fsdp", p) for a in slots_a[1:]]
    hold = (toks[-1], ups[0], *second, *slots_a[3:])
    for index, p in enumerate(pairs):
        slots_b += [second[index]] + [lax.ppermute(after(a, *hold), "fsdp", p) for a in slots_b[1:]]
    slots_a = slots_a + [lax.ppermute(after(a, *hold), "fsdp", swaps) for a in slots_a]
    for k in range(2, split):
        if k == split - 1:
            last = after(memory, *hold)
            ups.append(lax.ppermute(last, "seq", [(0, split - 1)]))
            downs.append(lax.ppermute(last, "seq", [(split - 1, 0)]))
        else:
            ups.append(seq_up(after(ups[-1], *hold), split))
            downs.append(seq_down(after(downs[-1], *hold), split))
    mems = [memory]
    for up, down in zip(ups, downs):
        mems += [up, down]

    near = [lax.ppermute(after(a, *hold), "fsdp", swaps) for a in second]
    first_tok = after(tokens, *hold, *near)
    (q, q_t3, k3, v3, k_t3, ctx, ctx_t3, lse, vec) = self_forward(
        sh, doc_lengths, doc_order, [first_tok] + toks[1:], slots_a
    )
    swapped = {id(a): b for a, b in zip(own_b_first + second, other_b + near)}
    late = (ctx, *ups, *downs)
    slots_b = slots_b + [
        swapped[id(a)] if id(a) in swapped else lax.ppermute(after(a, *late), "fsdp", swaps)
        for a in slots_b
    ]
    (n1, inv1, first_low, cq, cq_t3, mk3, mv3, mk_t3, cctx, cctx_t3, clse) = cross_forward(
        sh, doc_lengths, doc_order, memory_lengths, tokens, ctx, vec, mems, slots_b
    )
    feed_out = feed(sh, doc_lengths, doc_order, n1, cctx, targets, vec, slots_b)
    (final_low, g_second, g_cc, g_cc_t3, vec_grad, send_c, own_c) = feed_out
    sum_c = Reduction(send_c, own_c, count, split)
    sum_c.step()
    cq = after(cq, sum_c.send)
    sum_c.step()
    *mem_parts, dcq, k_low3, v_low3 = cross_backward(
        sh,
        doc_lengths,
        doc_order,
        memory_lengths,
        (cq, cq_t3, mk3, mv3, mk_t3, cctx_t3, clse, g_cc, g_cc_t3),
        slots_b,
    )
    dcq = after(dcq, sum_c.send)
    sum_c.step(dcq)
    swap = [(i, i ^ 1) for i in range(split)]
    mem_got = lax.ppermute(mem_parts[0], "seq", swap)
    (send_b, own_b, g_first, g_ctx, g_ctx_t3, vec_grad) = first_backward(
        sh,
        doc_lengths,
        doc_order,
        memory_lengths,
        (dcq, k_low3, v_low3, g_second, n1, inv1, first_low, ctx, vec, vec_grad),
        mems,
        slots_b,
    )
    mem_away = add_low(after(mem_parts[1], g_first), mem_got)
    sum_b = Reduction(send_b, own_b, count, split)
    g_ctx = after(g_ctx, sum_c.send, mem_away)
    sum_c.step(g_ctx)
    sum_b.step(g_ctx)
    mem_got = lax.ppermute(after(mem_parts[2], g_ctx), "seq", swap)
    mem_far = lax.ppermute(after(mem_away, g_ctx), "seq", [(i, i ^ 2) for i in range(split)])
    (grad_halo, dq, sk_low3, sv_low3) = self_backward(
        sh,
        doc_lengths,
        doc_order,
        (q, q_t3, k3, v3, k_t3, ctx_t3, lse, g_ctx, g_ctx_t3),
        slots_a,
    )
    dq = after(dq, mem_got, mem_far, sum_c.send, sum_b.send)
    back = seq_down(after(grad_halo[sh.halo - 1], dq), split)
    sum_b.step(dq)
    sum_c.step(dq)
    (send_a, own_a, grad_own) = self_weights(
        sh,
        (dq, sk_low3, sv_low3, g_first, vec_grad),
        toks,
        slots_a,
    )
    send_a = after(send_a, sum_b.send, sum_c.send)
    sum_a = Reduction(send_a, own_a, count, split)
    sum_a.step()
    sum_b.step(send_a)
    sum_c.step(send_a)
    for k in range(sh.halo - 1, 0, -1):
        back = seq_down(after(add_low(grad_halo[k - 1], back), send_a), split)
    sum_a.step()
    ready, held = sum_a.send, (sum_b.send, sum_c.send)
    while [a for a, _ in sum_a.plan].count("fsdp"):
        sum_a.step()
    sum_b.step(ready)
    ready = sum_a.send
    sum_a.step(back, *held)
    sum_b.step(ready)
    input_grad = grad_own + back.astype(F32)
    mem_last = after(mem_parts[3], sum_a.send)
    mem_here = mem_last.astype(F32) + mem_got.astype(F32) + mem_far.astype(F32)
    memory_grad = seq_rest(mem_here.reshape(split // 4, sh.mem_rows, D), split)[0]
    red_a, red_b, red_c = sum_a.finish(), sum_b.finish(), sum_c.finish()

    def rows_of(array, start, size):
        return array[start : start + size].astype(F32)

    done = finish(sh, red_a, expand_bias.shape[0])
    small_grad = done[3 : 3 + V_EB]
    expand_bias_grad = done[3 + V_EB]
    loss_value = done[4 + V_EB].reshape(())
    expand_grad = jnp.concatenate(
        [rows_of(red_c, (1 + c) * n, n) for c in range(FFB)], axis=1
    )
    return (
        final_low,
        loss_value,
        input_grad,
        memory_grad,
        done[0],
        small_grad[V_SQB],
        done[1],
        done[2],
        small_grad[V_SVB],
        rows_of(red_b, 0, n),
        small_grad[V_SOB],
        small_grad[V_G1],
        small_grad[V_S1],
        rows_of(red_b, n, n),
        small_grad[V_CQB],
        rows_of(red_b, 2 * n, n),
        rows_of(red_b, 3 * n, n),
        small_grad[V_CVB],
        rows_of(red_c, 0, n),
        small_grad[V_COB],
        small_grad[V_G2],
        small_grad[V_S2],
        expand_grad,
        expand_bias_grad,
        rows_of(red_c, 5 * n, wide),
        small_grad[V_CB],
        small_grad[V_G3],
        small_grad[V_S3],
    )


def solution(mesh):
    rows = P(("fsdp", "seq"), None)
    matrix = P("fsdp", None)
    vector = P("fsdp")
    kinds = (
        "mvmmvmvvvmvmmvmvvvmvmvvv"
    )
    weights = tuple(matrix if kind == "m" else vector for kind in kinds)
    return jax.shard_map(
        shards,
        mesh=mesh,
        in_specs=(rows, rows, rows, matrix, matrix, matrix) + weights,
        out_specs=(rows, P(), rows, rows) + weights,
        check_vma=False,
    )
```

```python
import jax
import jax.numpy as jnp
from jax import lax
from jax.experimental import pallas as pl
from jax.experimental.pallas import tpu as pltpu
from jax.sharding import PartitionSpec as P

D = 512
HDIM = 64
HEADS = D // HDIM
DOCS = 4
MEM = 512
FFB = 4
TILE = 256
GROUP = 4
VROWS = 32
NEG = -1e30
BF = jnp.bfloat16
F32 = jnp.float32
VMEM_BYTES = 60 * 1024 * 1024
FLOPS_RATE = 3e13

(
    V_SQB,
    V_SVB,
    V_SOB,
    V_G1,
    V_S1,
    V_CQB,
    V_CVB,
    V_COB,
    V_G2,
    V_S2,
    V_CB,
    V_G3,
    V_S3,
    V_EB,
) = range(14)
V_LOSS = V_EB + FFB
V_LIVE = V_LOSS + 1
LOW_BITS = 36
HIGH_BITS = 36


def mm(a, b):
    return jnp.dot(a, b, preferred_element_type=F32)


def mm_nt(a, b):
    return lax.dot_general(a, b, (((1,), (1,)), ((), ())), preferred_element_type=F32)


def mm_tn(a, b):
    return lax.dot_general(a, b, (((0,), (0,)), ((), ())), preferred_element_type=F32)


def col_sum(v):
    return jnp.sum(v.astype(F32), axis=0, keepdims=True)


def chip_steps(count):
    bits = []
    bit = 2
    while bit < count:
        bits.append(bit)
        bit *= 2
    return bits, bits[::-1]


def gather_masks(count):
    result = []
    for steps in chip_steps(count):
        masks = [0]
        for step in steps:
            masks = masks + [m ^ step for m in masks]
        result.append(masks)
    own0, own1 = result
    return [own0 + [m ^ 1 for m in own1], own1 + [m ^ 1 for m in own0]]


def reduce_masks(count):
    result = []
    for steps in chip_steps(count):
        masks = [0]
        for step in steps[::-1]:
            masks = masks + [m ^ step for m in masks]
        result.append(masks)
    return result


def step_pairs(count, index):
    orders = chip_steps(count)
    return [(i, i ^ orders[i & 1][index]) for i in range(count)]


def fsdp_gather_parts(own, count):
    have = [own]
    for index in range(len(chip_steps(count)[0])):
        pairs = step_pairs(count, index)
        have = have + [lax.ppermute(a, "fsdp", pairs) for a in have]
    return have, [(i, i ^ 1) for i in range(count)]


def fsdp_gather(own, count):
    have, swap = fsdp_gather_parts(own, count)
    return have + [lax.ppermute(a, "fsdp", swap) for a in have]


def add_low(a, b):
    return (a.astype(F32) + b.astype(F32)).astype(BF)


def after(value, *others):
    return lax.optimization_barrier((value, *others))[0]


def sum_low(parts):
    total = parts[0].astype(F32)
    for part in parts[1:]:
        total = total + part.astype(F32)
    return total.astype(BF)


class Reduction:
    def __init__(self, send, own, count, split):
        self.send, self.parts = send, [own]
        self.odd = (lax.axis_index("seq") % 2) == 1
        self.got = None
        self.plan = [("fsdp", [(i, i ^ 1) for i in range(count)])]
        for index in range(len(chip_steps(count)[0])):
            self.plan.append(("fsdp", step_pairs(count, index)))
        bits = [1 << k for k in range(split.bit_length() - 1)]
        for bit in bits + [1]:
            self.plan.append(("seq", [(i, i ^ bit) for i in range(split)]))

    def start(self, *others):
        send = after(self.send, *others) if others else self.send
        self.axis, pairs = self.plan.pop(0)
        self.got = lax.ppermute(send, self.axis, pairs)

    def end(self, *others):
        if others:
            self.parts[0] = after(self.parts[0], *others)
        left = sum(1 for axis, _ in self.plan if axis == "fsdp")
        if self.axis == "fsdp":
            self.parts.append(self.got)
            if left > 0:
                half = self.got.shape[0] // 2
                self.send = sum_low([part[half:] for part in self.parts])
                self.parts = [part[:half] for part in self.parts]
            else:
                total = sum_low([part[0] for part in self.parts])
                half = total.shape[0] // 2
                self.send = jnp.where(self.odd, total[:half], total[half:])
                self.parts = [jnp.where(self.odd, total[half:], total[:half])]
        elif self.plan:
            self.send = sum_low([self.parts[0], self.got])
            self.parts = [self.send]
        else:
            mine, got = self.parts[0], self.got
            self.send = jnp.where(
                self.odd, jnp.concatenate([got, mine]), jnp.concatenate([mine, got])
            )

    def step(self, *others):
        self.start(*others)
        self.end()

    def finish(self):
        while self.plan:
            self.step()
        return self.send


def seq_rest(parts, split):
    z = lax.axis_index("seq")
    bit = 4
    while bit < split:
        pairs = parts.reshape(parts.shape[0] // 2, 2, *parts.shape[1:])
        odd = (z // bit) % 2 == 1
        got = lax.ppermute(
            jnp.where(odd, pairs[:, 0], pairs[:, 1]), "seq", [(i, i ^ bit) for i in range(split)]
        )
        parts = jnp.where(odd, pairs[:, 1], pairs[:, 0]) + got
        bit *= 2
    return parts


def seq_up(a, count):
    return lax.ppermute(a, "seq", [(i, i + 1) for i in range(count - 1)])


def seq_down(a, count):
    return lax.ppermute(a, "seq", [(i + 1, i) for i in range(count - 1)])


def slot_place(index, masks, slot):
    return jnp.where(index % 2 == 0, index ^ masks[0][slot], index ^ masks[1][slot])


class Shard:
    def __init__(self, rows, mem_rows, count, split, piece, wide_piece):
        self.rows = rows
        self.mem_rows = mem_rows
        self.count = count
        self.split = split
        self.piece = piece
        self.wide_piece = wide_piece
        self.group_rows = rows * split
        self.group_mem = mem_rows * split
        self.halo = min(-(-(self.group_rows // 2 - 1) // rows), split - 1)
        self.window = rows * (self.halo + 1)
        self.q_blocks = rows // TILE
        self.k_blocks = self.window // TILE
        self.m_blocks = self.group_mem // TILE
        self.gather = gather_masks(count)
        self.reduce = reduce_masks(count)


def start_weight(sh, slots, row, n, target, sem):
    index = lax.axis_index("fsdp")
    for s, slot in enumerate(slots):
        place = pl.multiple_of(slot_place(index, sh.gather, s) * n, n)
        pltpu.make_async_copy(slot.at[pl.ds(row, n)], target.at[pl.ds(place, n)], sem).start()


def wait_all(target, sem):
    pltpu.make_async_copy(target, target, sem).wait()


def send_all(sources, targets, sems, first=0):
    copies = [
        pltpu.make_async_copy(source, target, sems.at[first + i])
        for i, (source, target) in enumerate(zip(sources, targets))
    ]
    for copy in copies:
        copy.start()
    return copies


def tile_copies(t, sources, targets, sems):
    return [
        pltpu.make_async_copy(source.at[t], target.at[t], sems.at[i, t])
        for i, (source, target) in enumerate(zip(sources, targets))
    ]


def start_mems(sh, mems, target, sems, wanted):
    z = lax.axis_index("seq")
    tiles_per = sh.mem_rows // TILE

    def place(source, shard):
        for i in range(tiles_per):
            t = shard * tiles_per + i

            @pl.when(wanted(t))
            def _(i=i, t=t):
                pltpu.make_async_copy(
                    source.at[pl.ds(i * TILE, TILE)], target.at[t], sems.at[t]
                ).start()

    place(mems[0], z)
    for k in range(1, sh.split):
        up, down = mems[2 * k - 1], mems[2 * k]

        @pl.when(z >= k)
        def _(up=up, k=k):
            place(up, z - k)

        @pl.when(z + k < sh.split)
        def _(down=down, k=k):
            place(down, z + k)


def wait_mem(target, t, sems):
    pltpu.make_async_copy(target.at[t], target.at[t], sems.at[t]).wait()


def put_grad(sh, full, n, row, send_ref, own_ref):
    index = lax.axis_index("fsdp")
    partner = index ^ 1
    for s in range(sh.count // 2):
        mine = pl.multiple_of(slot_place(index, sh.reduce, s) * n, n)
        theirs = pl.multiple_of(slot_place(partner, sh.reduce, s) * n, n)
        own_ref[s, pl.ds(row, n), :] = full[pl.ds(mine, n), :]
        send_ref[s, pl.ds(row, n), :] = full[pl.ds(theirs, n), :]


def doc_bounds(lens, order):
    starts, ends = [], []
    total = jnp.int32(0)
    for p in range(DOCS):
        starts.append(total)
        total = total + lens[0, order[0, p]]
        ends.append(total)
    return starts, ends


def pick(starts, ends, pos, values):
    out = jnp.zeros_like(pos)
    for p in range(DOCS):
        out = jnp.where((pos >= starts[p]) & (pos < ends[p]), values[p], out)
    return out


def lane_pos(base):
    return base + lax.broadcasted_iota(jnp.int32, (1, TILE), 1)


def norm_stats(v):
    mean = jnp.mean(v, axis=1, keepdims=True)
    c = v - mean
    inv = lax.rsqrt(jnp.mean(c * c, axis=1, keepdims=True) + 1e-05)
    return c * inv, inv


def norm_back(dy, n, inv, gain):
    e = dy * gain
    return inv * (
        e - jnp.mean(e, axis=1, keepdims=True) - n * jnp.mean(e * n, axis=1, keepdims=True)
    )


def head_rows(h):
    return slice(h * HDIM, (h + 1) * HDIM)


def pair_lanes(h):
    j = h // 2
    return slice(j * 2 * HDIM, (j + 1) * 2 * HDIM)


def spread_rows(source, target):
    for h in range(HEADS):
        o = (h % 2) * HDIM
        target[h, pl.ds(o, HDIM), :] = source[head_rows(h), :]


def spread_zero(target):
    for h in range(HEADS):
        o = (1 - h % 2) * HDIM
        target[h, pl.ds(o, HDIM), :] = jnp.zeros((HDIM, TILE), BF)


def spread_lanes(source, target):
    lane = lax.broadcasted_iota(jnp.int32, (TILE, 2 * HDIM), 1)
    for h in range(HEADS):
        part = source[:, pair_lanes(h)]
        keep = (lane >= HDIM) if h % 2 else (lane < HDIM)
        target[h] = jnp.where(keep, part, jnp.zeros_like(part))


def forward_tile(keys, vals_t, bias, q_t, m_ref, l_ref, acc_ref):
    heads = range(HEADS)
    mask = bias[...]
    m_old, l_old = m_ref[...], l_ref[...]
    scores = [mm(keys[:, pair_lanes(h)], q_t[h]) + mask for h in heads]
    tops = [
        jnp.maximum(m_old[h : h + 1], jnp.max(scores[h], axis=0, keepdims=True)) for h in heads
    ]
    probs = [jnp.exp(scores[h] - tops[h]) for h in heads]
    alphas = [jnp.exp(m_old[h : h + 1] - tops[h]) for h in heads]
    sums = [
        alphas[h] * l_old[h : h + 1] + jnp.sum(probs[h], axis=0, keepdims=True) for h in heads
    ]
    outs = [mm(vals_t[head_rows(h), :], probs[h].astype(BF)) for h in heads]
    for h in heads:
        acc_ref[head_rows(h), :] = acc_ref[head_rows(h), :] * alphas[h] + outs[h]
    m_ref[...] = jnp.concatenate(tops, axis=0)
    l_ref[...] = jnp.concatenate(sums, axis=0)


def forward_start(m_ref, l_ref, acc_ref):
    m_ref[...] = jnp.full(m_ref.shape, NEG, F32)
    l_ref[...] = jnp.zeros(l_ref.shape, F32)
    acc_ref[...] = jnp.zeros(acc_ref.shape, F32)


def forward_end(b, m_ref, l_ref, acc_ref, ctx_ref, ctx_t_ref, lse_ref):
    lse_ref[b] = m_ref[...] + jnp.log(l_ref[...])
    for h in range(HEADS):
        acc_ref[head_rows(h), :] = acc_ref[head_rows(h), :] / l_ref[h : h + 1, :]
    ctx_t_ref[b] = acc_ref[...]
    ctx_ref[pl.ds(pl.multiple_of(b * TILE, TILE), TILE), :] = acc_ref[...].T.astype(BF)


def backward_tile(keys, vals, keys_t, bias, q_t, g_t, q_m, g_m, lse, delta, dk, dv, dq_t):
    mask = bias[...]
    for first in range(0, HEADS, GROUP):
        heads = range(first, first + GROUP)
        scores = [mm(keys[:, pair_lanes(h)], q_t[h]) for h in heads]
        probs = [jnp.exp(s + mask - lse[h : h + 1, :]) for h, s in zip(heads, scores)]
        dvs = [mm(p.astype(BF), g_m[h]) for h, p in zip(heads, probs)]
        dps = [mm(vals[:, pair_lanes(h)], g_t[h]) for h in heads]
        dss = [
            (p * (dp - delta[h : h + 1, :])).astype(BF) for h, p, dp in zip(heads, probs, dps)
        ]
        dks = [mm(ds, q_m[h]) for h, ds in zip(heads, dss)]
        dqs = [mm(keys_t[head_rows(h), :], ds) for h, ds in zip(heads, dss)]
        for i in range(0, GROUP, 2):
            lanes = pair_lanes(first + i)
            dv[:, lanes] = dv[:, lanes] + dvs[i] + dvs[i + 1]
            dk[:, lanes] = dk[:, lanes] + dks[i] + dks[i + 1]
        for h, dq in zip(heads, dqs):
            dq_t[head_rows(h), :] = dq_t[head_rows(h), :] + dq


def backward_start(b, q_t3, g_t3, q, g, ctx_t3, q_t, g_t, q_m, g_m, delta, dq_t):
    rows = pl.ds(pl.multiple_of(b * TILE, TILE), TILE)
    spread_rows(q_t3.at[b], q_t)
    spread_rows(g_t3.at[b], g_t)
    spread_lanes(q[rows, :], q_m)
    spread_lanes(g[rows, :], g_m)
    prod = g_t3[b].astype(F32) * ctx_t3[b]
    for h in range(HEADS):
        delta[h : h + 1, :] = jnp.sum(prod[head_rows(h), :], axis=0, keepdims=True)
    dq_t[...] = jnp.zeros(dq_t.shape, F32)


def self_tiles(sh, lens, order, b, bias, body):
    z = lax.axis_index("seq")
    starts, ends = doc_bounds(lens, order)
    shift = (z - sh.halo) * sh.rows
    q_base = sh.halo * sh.rows + b * TILE
    first = pick(starts, ends, q_base + shift, starts) - shift
    q_pos = lane_pos(q_base)
    q_start = pick(starts, ends, q_pos + shift, starts) - shift
    last = q_base // TILE
    number = last - first // TILE + 1

    def step(i, carry):
        t = last - i
        k_pos = t * TILE + lax.broadcasted_iota(jnp.int32, (TILE, TILE), 0)
        bias[...] = jnp.where((k_pos >= q_start) & (k_pos <= q_pos), 0.0, NEG)
        body(t)
        return carry

    lax.fori_loop(0, number, step, 0)


def self_forward_kernel(sh, lens, order, *refs):
    halo, count, rows, n = sh.halo, sh.count, sh.rows, sh.piece
    toks = refs[: halo + 1]
    slots = refs[halo + 1 : halo + 1 + count]
    (*kept, ctx, ctx_t3, lse, vec) = refs[halo + 1 + count : halo + 10 + count]
    outs = refs[halo + 10 + count :]
    (q_ref, q_t3, k3, v3, k_t3, wq, wk, wv, vec_slots, v_t3, q_t, bias) = outs[:12]
    (m_ref, l_ref, acc, sems, q_sems, tile_sems) = outs[12:]
    z = lax.axis_index("seq")
    for s, slot in enumerate(slots):
        pltpu.make_async_copy(slot.at[pl.ds(3 * n, VROWS)], vec_slots.at[s], sems.at[3]).start()
    for i, w in enumerate((wq, wk, wv)):
        start_weight(sh, slots, i * n, n, w, sems.at[i])
    spread_zero(q_t)
    wait_all(vec_slots, sems.at[3])
    vec[...] = jnp.sum(vec_slots[...].astype(F32), axis=0)
    wait_all(wq, sems.at[0])
    tiles = rows // TILE

    def own_rows(i, carry):
        r = pl.ds(pl.multiple_of(i * TILE, TILE), TILE)
        q = (mm(toks[0][r, :], wq[...]) + vec[V_SQB : V_SQB + 1, :]).astype(BF)
        q = q * BF(HDIM**-0.5)
        q_ref[r, :] = q
        q_t3[i] = q.T
        return carry

    lax.fori_loop(0, tiles, own_rows, 0)
    q_copies = send_all((q_ref, q_t3), kept[:2], q_sems)
    wait_all(wk, sems.at[1])
    wait_all(wv, sems.at[2])

    def window_copies(t):
        return tile_copies(t, (k3, v3, k_t3), kept[2:], tile_sems)

    for k in range(halo + 1):

        def window_rows(i, carry, k=k):
            r = pl.ds(pl.multiple_of(i * TILE, TILE), TILE)
            t = (halo - k) * tiles + i
            x = toks[k][r, :]
            key = mm(x, wk[...]).astype(BF)
            val = (mm(x, wv[...]) + vec[V_SVB : V_SVB + 1, :]).astype(BF)
            k3[t] = key
            v3[t] = val
            k_t3[t] = key.T
            v_t3[t] = val.T
            for copy in window_copies(t):
                copy.start()
            return carry

        @pl.when(z >= k)
        def _(window_rows=window_rows):
            lax.fori_loop(0, tiles, window_rows, 0)

    def block(b, carry):
        spread_rows(q_t3.at[b], q_t)
        forward_start(m_ref, l_ref, acc)
        self_tiles(
            sh,
            lens,
            order,
            b,
            bias,
            lambda t: forward_tile(k3.at[t], v_t3.at[t], bias, q_t, m_ref, l_ref, acc),
        )
        forward_end(b, m_ref, l_ref, acc, ctx, ctx_t3, lse)
        return carry

    lax.fori_loop(0, sh.q_blocks, block, 0)
    for copy in q_copies:
        copy.wait()
    for k in range(halo + 1):

        @pl.when(z >= k)
        def _(k=k):
            for i in range(tiles):
                for copy in window_copies((halo - k) * tiles + i):
                    copy.wait()


SMEM_SPEC = pl.BlockSpec(memory_space=pltpu.SMEM)
VMEM_SPEC = pl.BlockSpec(memory_space=pltpu.VMEM)
ANY_SPEC = pl.BlockSpec(memory_space=pl.ANY)


def shape(dims, dtype):
    return jax.ShapeDtypeStruct(dims, dtype)


def call(body, name, inputs, specs, outs, scratch, micros, vmem=VMEM_BYTES, out_specs=None):
    moved = sum(a.size * a.dtype.itemsize for a in (*inputs, *outs))
    cost = pl.CostEstimate(
        flops=int(micros * 1e-6 * FLOPS_RATE), transcendentals=0, bytes_accessed=moved // 50
    )
    return pl.pallas_call(
        body,
        name=name,
        in_specs=specs,
        out_specs=out_specs or [VMEM_SPEC] * len(outs),
        out_shape=outs,
        scratch_shapes=scratch,
        cost_estimate=cost,
        compiler_params=pltpu.CompilerParams(vmem_limit_bytes=vmem),
    )(*inputs)


def pack_kernel(sh, *refs):
    small = refs[:V_EB]
    wide_bias = refs[V_EB]
    mats = refs[V_EB + 1 : V_EB + 11]
    own_a, own_b = refs[V_EB + 11 :]
    n, wide = sh.piece, sh.wide_piece
    (sq, sk, sv, so, cq, ck, cv, co, w1, w2) = mats
    for i, m in enumerate((sq, sk, sv)):
        own_a[pl.ds(i * n, n), :] = m[...]
    for i, m in enumerate((so, cq, ck, cv, co)):
        own_b[pl.ds(i * n, n), :] = m[...]
    for c in range(FFB):
        own_b[pl.ds((5 + c) * n, n), :] = w1[:, c * D : (c + 1) * D]
    own_b[pl.ds(9 * n, wide), :] = w2[...]
    index = lax.axis_index("fsdp")

    def spread(piece, size, offset):
        hot = lax.broadcasted_iota(jnp.int32, (size, D), 1) == offset + lax.broadcasted_iota(
            jnp.int32, (size, D), 0
        )
        return mm(piece, hot.astype(BF)).astype(BF)

    rows = jnp.concatenate([r[...].reshape(1, n) for r in small], axis=0)
    size = wide_bias.shape[0]
    flat = index * size
    line = spread(wide_bias[...].reshape(1, size), size, flat % D)
    row = lax.broadcasted_iota(jnp.int32, (FFB, D), 0)
    own_a[pl.ds(3 * n, VROWS), :] = jnp.concatenate(
        [
            spread(rows, n, index * n),
            jnp.where(row == flat // D, line, jnp.zeros((FFB, D), BF)),
            jnp.zeros((VROWS - V_EB - FFB, D), BF),
        ],
        axis=0,
    )


def pack(sh, small, wide_bias, mats):
    n, wide = sh.piece, sh.wide_piece
    outs = [shape((3 * n + VROWS, D), BF), shape((9 * n + wide, D), BF)]
    return call(
        lambda *refs: pack_kernel(sh, *refs),
        "pack",
        (*small, wide_bias, *mats),
        [VMEM_SPEC] * (V_EB + 1 + len(mats)),
        outs,
        [],
        2,
    )


def digit_bits(devices):
    return 3 if 7 * devices <= 256 else 1


def digits(value, bits):
    lane = lax.broadcasted_iota(jnp.int32, (1, D), 1)
    scale = jnp.full((1, D), 2.0**LOW_BITS, F32)
    for i in range(9):
        scale = scale * jnp.where((lane // 2**i) % 2 == 1, 2.0 ** -min(bits * 2**i, 140), 1.0)
    whole = jnp.floor(value * scale)
    return whole - 2.0**bits * jnp.floor(value * scale * 2.0**-bits)


def undigits(row, bits):
    lane = lax.broadcasted_iota(jnp.int32, (1, D), 1)
    scale = jnp.full((1, D), 2.0**-LOW_BITS, F32)
    for i in range(7):
        scale = scale * jnp.where(
            (lane // 2**i) % 2 == 1, 2.0 ** min(bits * 2**i, LOW_BITS + HIGH_BITS), 1.0
        )
    used = lane < (LOW_BITS + HIGH_BITS) // bits
    return jnp.sum(jnp.where(used, row * jnp.where(used, scale, 0.0), 0.0), axis=1, keepdims=True)


def finish_kernel(sh, mine, got, *outs):
    n = sh.piece
    mats, small, wide_bias, loss = outs[:3], outs[3 : 3 + V_EB], outs[3 + V_EB], outs[4 + V_EB]
    red = outs[5 + V_EB]
    odd = lax.axis_index("seq") % 2 == 1
    half = mine.shape[0]
    red[pl.ds(0, half), :] = jnp.where(odd, got[...], mine[...])
    red[pl.ds(half, half), :] = jnp.where(odd, mine[...], got[...])
    for i, m in enumerate(mats):
        m[...] = red[pl.ds(i * n, n), :].astype(F32)
    index = lax.axis_index("fsdp")
    vec = red[pl.ds(3 * n, VROWS), :]

    def cut(rows, size, offset):
        hot = lax.broadcasted_iota(jnp.int32, (D, size), 0) == offset + lax.broadcasted_iota(
            jnp.int32, (D, size), 1
        )
        return mm(rows, hot.astype(BF))

    parts = cut(vec, n, index * n)
    for i in range(V_EB):
        small[i][...] = parts[i : i + 1, :].reshape(n)
    size = wide_bias.shape[0]
    flat = index * size
    row = lax.broadcasted_iota(jnp.int32, (VROWS, D), 0)
    lines = jnp.where(row == V_EB + flat // D, vec.astype(F32), 0.0).astype(BF)
    wide_bias[...] = jnp.sum(cut(lines, size, flat % D), axis=0, keepdims=True).reshape(size)
    bits = digit_bits(sh.count * sh.split)
    error_sum = undigits(vec[V_LOSS : V_LOSS + 1, :].astype(F32), bits)
    live = undigits(vec[V_LIVE : V_LIVE + 1, :].astype(F32), bits)
    loss[...] = error_sum / (live * D)


def finish(sh, mine, got, bias_size):
    n = sh.piece
    outs = [shape((n, D), F32)] * 3 + [shape((n,), F32)] * V_EB
    outs += [shape((bias_size,), F32), shape((1, 1), F32)]
    return call(
        lambda *refs: finish_kernel(sh, *refs),
        "finish",
        (mine, got),
        [VMEM_SPEC] * 2,
        outs,
        [pltpu.VMEM((3 * n + VROWS, D), BF)],
        2,
    )


def self_forward(sh, lens, order, toks, slots):
    nb, nq = sh.k_blocks, sh.q_blocks
    outs = [
        shape((sh.rows, D), BF),
        shape((nq, D, TILE), BF),
        shape((nb, TILE, D), BF),
        shape((nb, TILE, D), BF),
        shape((nb, D, TILE), BF),
        shape((sh.rows, D), BF),
        shape((nq, D, TILE), F32),
        shape((nq, HEADS, TILE), F32),
        shape((VROWS, D), F32),
    ]
    scratch = [
        pltpu.VMEM((sh.rows, D), BF),
        pltpu.VMEM((nq, D, TILE), BF),
        pltpu.VMEM((nb, TILE, D), BF),
        pltpu.VMEM((nb, TILE, D), BF),
        pltpu.VMEM((nb, D, TILE), BF),
        pltpu.VMEM((D, D), BF),
        pltpu.VMEM((D, D), BF),
        pltpu.VMEM((D, D), BF),
        pltpu.VMEM((sh.count, VROWS, D), BF),
        pltpu.VMEM((nb, D, TILE), BF),
        pltpu.VMEM((HEADS, 2 * HDIM, TILE), BF),
        pltpu.VMEM((TILE, TILE), F32),
        pltpu.VMEM((HEADS, TILE), F32),
        pltpu.VMEM((HEADS, TILE), F32),
        pltpu.VMEM((D, TILE), F32),
        pltpu.SemaphoreType.DMA((4,)),
        pltpu.SemaphoreType.DMA((2,)),
        pltpu.SemaphoreType.DMA((3, nb)),
    ]
    specs = [SMEM_SPEC] * 2 + [VMEM_SPEC] * len(toks) + [ANY_SPEC] * len(slots)
    return call(
        lambda *refs: self_forward_kernel(sh, *refs),
        "self_forward",
        (lens, order, *toks, *slots),
        specs,
        outs,
        scratch,
        16,
        out_specs=[ANY_SPEC] * 5 + [VMEM_SPEC] * 4,
    )


def cross_tiles(sh, lens, order, mlens, b, bias, bounds, skip_pad, body):
    z = lax.axis_index("seq")
    starts, ends = doc_bounds(lens, order)
    for p in range(DOCS):
        bounds[0, p] = starts[p]
        bounds[1, p] = ends[p]
    base = z * sh.rows + b * TILE
    slots = [order[0, p] for p in range(DOCS)]
    pos = lane_pos(base)
    low = pick(starts, ends, pos, [s * MEM for s in slots])
    high = pick(starts, ends, pos, [s * MEM + mlens[0, s] for s in slots])

    def doc(p, carry):
        slot = order[0, p]
        seen = (bounds[0, p] < base + TILE) & (bounds[1, p] > base)
        if skip_pad:
            seen = seen & (slot != DOCS - 1)
        number = jnp.where(seen, (mlens[0, slot] + TILE - 1) // TILE, 0)

        def step(i, inner):
            t = slot * (MEM // TILE) + i
            k_pos = t * TILE + lax.broadcasted_iota(jnp.int32, (TILE, TILE), 0)
            bias[...] = jnp.where((k_pos >= low) & (k_pos < high), 0.0, NEG)
            body(t)
            return inner

        return lax.fori_loop(0, number, step, carry)

    lax.fori_loop(0, DOCS, doc, 0)


def touched_tile(sh, lens, order, mlens, t, bounds, skip_pad):
    z = lax.axis_index("seq")
    slot = t // (MEM // TILE)
    base = z * sh.rows
    seen = (bounds[2, slot] < base + sh.rows) & (bounds[3, slot] > base)
    seen = seen & (t % (MEM // TILE) * TILE < mlens[0, slot])
    if skip_pad:
        seen = seen & (slot != DOCS - 1)
    return seen


def slot_bounds(lens, order, bounds):
    starts, ends = doc_bounds(lens, order)
    for p in range(DOCS):
        bounds[2, order[0, p]] = starts[p]
        bounds[3, order[0, p]] = ends[p]


def cross_forward_kernel(sh, lens, order, mlens, *refs):
    count, rows, n, split = sh.count, sh.rows, sh.piece, sh.split
    tok, ctx, vec = refs[:3]
    mems = refs[3 : 3 + 2 * split - 1]
    slots = refs[2 + 2 * split : 2 + 2 * split + count]
    outs = refs[2 + 2 * split + count :]
    (n1_out, inv1, *early, mk_out, mv_out, mk_t_out, cctx, cctx_t3, lse) = outs[:11]
    kept = (mk_out, mv_out, mk_t_out)
    (n1, first_low, q_ref, q_t3) = outs[11:15]
    outs = outs[4:]
    (wo, wcq, wck, wcv, mem, mk3, mv3, mk_t3, mv_t3, q_t, bias, m_ref, l_ref, acc) = outs[11:25]
    (bounds, sems, mem_sems, tile_sems, row_sems) = outs[25:]
    for i, w in enumerate((wo, wcq, wck, wcv)):
        start_weight(sh, slots, i * n, n, w, sems.at[i])

    def wanted(t):
        return touched_tile(sh, lens, order, mlens, t, bounds, False)

    slot_bounds(lens, order, bounds)
    start_mems(sh, mems, mem, mem_sems, wanted)
    spread_zero(q_t)
    wait_all(wo, sems.at[0])
    wait_all(wcq, sems.at[1])

    def own_rows(i, carry):
        r = pl.ds(pl.multiple_of(i * TILE, TILE), TILE)
        v = tok[r, :].astype(F32) + (mm(ctx[r, :], wo[...]) + vec[V_SOB : V_SOB + 1, :])
        normal, inv = norm_stats(v)
        n1[r, :] = normal
        inv1[r, :] = inv
        low = (normal * vec[V_G1 : V_G1 + 1, :] + vec[V_S1 : V_S1 + 1, :]).astype(BF)
        first_low[r, :] = low
        q = (mm(low, wcq[...]) + vec[V_CQB : V_CQB + 1, :]).astype(BF)
        q = q * BF(HDIM**-0.5)
        q_ref[r, :] = q
        q_t3[i] = q.T
        return carry

    lax.fori_loop(0, rows // TILE, own_rows, 0)
    row_copies = send_all((n1, first_low, q_ref, q_t3), (n1_out, *early), row_sems)
    wait_all(wck, sems.at[2])
    wait_all(wcv, sems.at[3])

    def mem_tile(t, carry):
        @pl.when(wanted(t))
        def _():
            wait_mem(mem, t, mem_sems)
            x = mem[t]
            key = mm(x, wck[...]).astype(BF)
            val = (mm(x, wcv[...]) + vec[V_CVB : V_CVB + 1, :]).astype(BF)
            mk3[t] = key
            mv3[t] = val
            mk_t3[t] = key.T
            mv_t3[t] = val.T
            for copy in tile_copies(t, (mk3, mv3, mk_t3), kept, tile_sems):
                copy.start()

        return carry

    lax.fori_loop(0, sh.m_blocks, mem_tile, 0)

    def block(b, carry):
        spread_rows(q_t3.at[b], q_t)
        forward_start(m_ref, l_ref, acc)
        cross_tiles(
            sh,
            lens,
            order,
            mlens,
            b,
            bias,
            bounds,
            False,
            lambda t: forward_tile(mk3.at[t], mv_t3.at[t], bias, q_t, m_ref, l_ref, acc),
        )
        forward_end(b, m_ref, l_ref, acc, cctx, cctx_t3, lse)
        return carry

    lax.fori_loop(0, sh.q_blocks, block, 0)

    def settle(t, carry):
        @pl.when(wanted(t))
        def _():
            for copy in tile_copies(t, (mk3, mv3, mk_t3), kept, tile_sems):
                copy.wait()

        return carry

    lax.fori_loop(0, sh.m_blocks, settle, 0)
    for copy in row_copies:
        copy.wait()


def cross_forward(sh, lens, order, mlens, tok, ctx, vec, mems, slots):
    nm, nq = sh.m_blocks, sh.q_blocks
    outs = [
        shape((sh.rows, D), F32),
        shape((sh.rows, 1), F32),
        shape((sh.rows, D), BF),
        shape((sh.rows, D), BF),
        shape((nq, D, TILE), BF),
        shape((nm, TILE, D), BF),
        shape((nm, TILE, D), BF),
        shape((nm, D, TILE), BF),
        shape((sh.rows, D), BF),
        shape((nq, D, TILE), F32),
        shape((nq, HEADS, TILE), F32),
    ]
    scratch = [
        pltpu.VMEM((sh.rows, D), F32),
        pltpu.VMEM((sh.rows, D), BF),
        pltpu.VMEM((sh.rows, D), BF),
        pltpu.VMEM((nq, D, TILE), BF),
        pltpu.VMEM((D, D), BF),
        pltpu.VMEM((D, D), BF),
        pltpu.VMEM((D, D), BF),
        pltpu.VMEM((D, D), BF),
        pltpu.VMEM((nm, TILE, D), BF),
        pltpu.VMEM((nm, TILE, D), BF),
        pltpu.VMEM((nm, TILE, D), BF),
        pltpu.VMEM((nm, D, TILE), BF),
        pltpu.VMEM((nm, D, TILE), BF),
        pltpu.VMEM((HEADS, 2 * HDIM, TILE), BF),
        pltpu.VMEM((TILE, TILE), F32),
        pltpu.VMEM((HEADS, TILE), F32),
        pltpu.VMEM((HEADS, TILE), F32),
        pltpu.VMEM((D, TILE), F32),
        pltpu.SMEM((4, DOCS), jnp.int32),
        pltpu.SemaphoreType.DMA((4,)),
        pltpu.SemaphoreType.DMA((nm,)),
        pltpu.SemaphoreType.DMA((3, nm)),
        pltpu.SemaphoreType.DMA((4,)),
    ]
    specs = [SMEM_SPEC] * 3 + [VMEM_SPEC] * 3 + [ANY_SPEC] * (len(mems) + len(slots))
    return call(
        lambda *refs: cross_forward_kernel(sh, *refs),
        "cross_forward",
        (lens, order, mlens, tok, ctx, vec, *mems, *slots),
        specs,
        outs,
        scratch,
        21,
        out_specs=[ANY_SPEC, VMEM_SPEC] + [ANY_SPEC] * 6 + [VMEM_SPEC] * 3,
    )


def feed_kernel(sh, lens, order, *refs):
    count, rows, n, wide = sh.count, sh.rows, sh.piece, sh.wide_piece
    n1, cctx, targets, vec = refs[:4]
    slots = refs[4 : 4 + count]
    outs = refs[4 + count :]
    row_outs, vec_grad, grad_outs = outs[:4], outs[4], outs[5:7]
    (final_ref, g_second, g_cc, g_cc_t3, g_send, g_own) = outs[7:13]
    (sec_low, hid, feed_low, g_exp, g_cross) = outs[13:18]
    (wco, w1, w2, n2, dact, loss, stage, stage2, sems, out_sems) = outs[18:]
    z = lax.axis_index("seq")
    start_weight(sh, slots, 4 * n, n, wco, sems.at[0])
    for c in range(FFB):
        start_weight(sh, slots, (5 + c) * n, n, w1.at[c], sems.at[1 + c])
    start_weight(sh, slots, 9 * n, wide, w2, sems.at[5])
    vec_grad[...] = jnp.zeros(vec_grad.shape, F32)
    loss[...] = jnp.zeros(loss.shape, F32)
    starts, ends = doc_bounds(lens, order)
    pad_start, pad_end = jnp.int32(0), jnp.int32(0)
    for p in range(DOCS):
        is_pad = order[0, p] == DOCS - 1
        pad_start = jnp.where(is_pad, starts[p], pad_start)
        pad_end = jnp.where(is_pad, ends[p], pad_end)
    wait_all(wco, sems.at[0])

    def add_vec(row, value):
        vec_grad[row : row + 1, :] = vec_grad[row : row + 1, :] + value

    def chunk(i, carry):
        r = pl.ds(pl.multiple_of(i * TILE, TILE), TILE)
        first = n1[r, :] * vec[V_G1 : V_G1 + 1, :] + vec[V_S1 : V_S1 + 1, :]
        v = first + (mm(cctx[r, :], wco[...]) + vec[V_COB : V_COB + 1, :])
        normal2, inv2 = norm_stats(v)
        n2[...] = normal2
        second = normal2 * vec[V_G2 : V_G2 + 1, :] + vec[V_S2 : V_S2 + 1, :]
        low = second.astype(BF)
        sec_low[r, :] = low
        feed = second + vec[V_CB : V_CB + 1, :]
        wide = range(FFB)

        @pl.when(i == 0)
        def _():
            for c in wide:
                wait_all(w1.at[c], sems.at[1 + c])
            wait_all(w2, sems.at[5])

        es = [mm(low, w1[c]) + vec[V_EB + c : V_EB + c + 1, :] for c in wide]
        sgs = [jax.nn.sigmoid(e) for e in es]
        hs = [(e * sg).astype(BF) for e, sg in zip(es, sgs)]
        for c in wide:
            hid[c, r, :] = hs[c]
            dact[c] = sgs[c] * (1.0 + es[c] * (1.0 - sgs[c]))
        for c in wide:
            feed = feed + mm(hs[c], w2[pl.ds(c * D, D), :])
        normal3, inv3 = norm_stats(feed)
        final = normal3 * vec[V_G3 : V_G3 + 1, :] + vec[V_S3 : V_S3 + 1, :]
        final_ref[r, :] = final.astype(BF)
        diff = final - targets[r, :].astype(F32)
        pos = z * rows + i * TILE + lax.broadcasted_iota(jnp.int32, (TILE, 1), 0)
        live = jnp.where((pos >= pad_start) & (pos < pad_end), 0.0, 1.0)
        g = live * diff
        loss[0:1, :] = loss[0:1, :] + col_sum(g * diff)
        add_vec(V_G3, col_sum(g * normal3))
        add_vec(V_S3, col_sum(g))
        g_third = norm_back(g, normal3, inv3, vec[V_G3 : V_G3 + 1, :])
        g_low = g_third.astype(BF)
        feed_low[r, :] = g_low
        add_vec(V_CB, col_sum(g_low))
        total = g_third
        ges = [(mm_nt(g_low, w2[pl.ds(c * D, D), :]) * dact[c]).astype(BF) for c in wide]
        for c in wide:
            total = total + mm_nt(ges[c], w1[c])
        for c in wide:
            g_exp[c, r, :] = ges[c]
            add_vec(V_EB + c, col_sum(ges[c]))
        normal2 = n2[...]
        add_vec(V_G2, col_sum(total * normal2))
        add_vec(V_S2, col_sum(total))
        gs = norm_back(total, normal2, inv2, vec[V_G2 : V_G2 + 1, :])
        g_second[r, :] = gs
        gc = gs.astype(BF)
        g_cross[r, :] = gc
        add_vec(V_COB, col_sum(gc))
        gcc = mm_nt(gc, wco[...]).astype(BF)
        g_cc[r, :] = gcc
        g_cc_t3[i] = gcc.T
        return carry

    lax.fori_loop(0, rows // TILE, chunk, 0)
    live_count = jnp.int32(rows) - jnp.maximum(
        jnp.minimum(pad_end, (z + 1) * rows) - jnp.maximum(pad_start, z * rows), 0
    )
    bits = digit_bits(count * sh.split)
    error_sum = jnp.sum(loss[0:1, :], axis=1, keepdims=True)
    vec_grad[V_LOSS : V_LOSS + 1, :] = digits(error_sum, bits)
    vec_grad[V_LIVE : V_LIVE + 1, :] = digits(jnp.full((1, 1), live_count.astype(F32)), bits)
    copies = send_all((final_ref, g_second, g_cc, g_cc_t3), row_outs, out_sems)

    def send_grad(full, size, row):
        put_grad(sh, full, size, row, g_send, g_own)
        copies.extend(
            send_all(
                [ref.at[:, pl.ds(row, size)] for ref in (g_send, g_own)],
                [ref.at[:, pl.ds(row, size)] for ref in grad_outs],
                out_sems,
                len(copies),
            )
        )

    for c in range(FFB):
        stage2[pl.ds(c * D, D), :] = mm_tn(hid[c], feed_low[...]).astype(BF)
    send_grad(stage2, wide, 5 * n)
    for c in range(FFB):
        stage[...] = mm_tn(sec_low[...], g_exp[c]).astype(BF)
        send_grad(stage, n, (1 + c) * n)
    stage[...] = mm_tn(cctx[...], g_cross[...]).astype(BF)
    send_grad(stage, n, 0)
    for copy in copies:
        copy.wait()


def feed(sh, lens, order, n1, cctx, targets, vec, slots):
    rows, nq = sh.rows, sh.q_blocks
    block = 5 * sh.piece + sh.wide_piece
    outs = [
        shape((rows, D), BF),
        shape((rows, D), F32),
        shape((rows, D), BF),
        shape((nq, D, TILE), BF),
        shape((VROWS, D), F32),
        shape((sh.count // 2, block, D), BF),
        shape((sh.count // 2, block, D), BF),
    ]
    scratch = [
        pltpu.VMEM((rows, D), BF),
        pltpu.VMEM((rows, D), F32),
        pltpu.VMEM((rows, D), BF),
        pltpu.VMEM((nq, D, TILE), BF),
        pltpu.VMEM((sh.count // 2, block, D), BF),
        pltpu.VMEM((sh.count // 2, block, D), BF),
        pltpu.VMEM((rows, D), BF),
        pltpu.VMEM((FFB, rows, D), BF),
        pltpu.VMEM((rows, D), BF),
        pltpu.VMEM((FFB, rows, D), BF),
        pltpu.VMEM((rows, D), BF),
        pltpu.VMEM((D, D), BF),
        pltpu.VMEM((FFB, D, D), BF),
        pltpu.VMEM((FFB * D, D), BF),
        pltpu.VMEM((TILE, D), F32),
        pltpu.VMEM((FFB, TILE, D), F32),
        pltpu.VMEM((8, D), F32),
        pltpu.VMEM((D, D), BF),
        pltpu.VMEM((FFB * D, D), BF),
        pltpu.SemaphoreType.DMA((6,)),
        pltpu.SemaphoreType.DMA((4 + 2 * (FFB + 2),)),
    ]
    specs = [SMEM_SPEC] * 2 + [VMEM_SPEC] * 4 + [ANY_SPEC] * len(slots)
    return call(
        lambda *refs: feed_kernel(sh, *refs),
        "feed",
        (lens, order, n1, cctx, targets, vec, *slots),
        specs,
        outs,
        scratch,
        17,
        out_specs=[ANY_SPEC] * 4 + [VMEM_SPEC] + [ANY_SPEC] * 2,
    )


def mem_shard(z, slot, high):
    low, mid = z % 2, (z // 2) % 2
    low = low if slot % 2 else 1 - low
    mid = mid if slot >= 2 else 1 - mid
    return 4 * high + 2 * mid + low


def cross_backward_kernel(sh, lens, order, mlens, *refs):
    count, n = sh.count, sh.piece
    (q_ref, q_t3, *kept, cctx_t3, lse, g_cc, g_cc_t3) = refs[:9]
    slots = refs[9 : 9 + count]
    outs = refs[9 + count :]
    mem_parts = outs[:4]
    (dq, *low_out) = outs[4:7]
    (wck, wcv, q_t, g_t, q_m, g_m, delta, bias, dk, dv, dq_t) = outs[7:18]
    (mk3, mv3, mk_t3, k_low3, v_low3, bounds, sems, tile_sems, low_sems) = outs[18:]
    for i, w in enumerate((wck, wcv)):
        start_weight(sh, slots, (2 + i) * n, n, w, sems.at[i])
    slot_bounds(lens, order, bounds)
    spread_zero(q_t)
    spread_zero(g_t)

    def each_wanted(body):
        def one(t, carry):
            @pl.when(touched_tile(sh, lens, order, mlens, t, bounds, True))
            def _():
                body(t)

            return carry

        lax.fori_loop(0, sh.m_blocks, one, 0)

    def fetch(t):
        for copy in tile_copies(t, kept, (mk3, mv3, mk_t3), tile_sems):
            copy.start()

    def clear(t):
        dk[t] = jnp.zeros((TILE, D), F32)
        dv[t] = jnp.zeros((TILE, D), F32)
        for copy in tile_copies(t, kept, (mk3, mv3, mk_t3), tile_sems):
            copy.wait()

    def low_copies(t):
        return tile_copies(t, (k_low3, v_low3), low_out, low_sems)

    each_wanted(fetch)
    each_wanted(clear)

    def block(b, carry):
        backward_start(b, q_t3, g_cc_t3, q_ref, g_cc, cctx_t3, q_t, g_t, q_m, g_m, delta, dq_t)
        cross_tiles(
            sh,
            lens,
            order,
            mlens,
            b,
            bias,
            bounds,
            True,
            lambda t: backward_tile(
                mk3.at[t],
                mv3.at[t],
                mk_t3.at[t],
                bias,
                q_t,
                g_t,
                q_m,
                g_m,
                lse.at[b],
                delta,
                dk.at[t],
                dv.at[t],
                dq_t,
            ),
        )
        r = pl.ds(pl.multiple_of(b * TILE, TILE), TILE)
        dq[r, :] = (dq_t[...] * HDIM**-0.5).T.astype(BF)
        return carry

    lax.fori_loop(0, sh.q_blocks, block, 0)
    wait_all(wck, sems.at[0])
    wait_all(wcv, sems.at[1])

    z = lax.axis_index("seq")
    tiles_per = sh.mem_rows // TILE

    def mem_tile(i, carry, slot, out):
        shard = mem_shard(z, slot, i // tiles_per)
        t = shard * tiles_per + i % tiles_per
        seen = touched_tile(sh, lens, order, mlens, t, bounds, True)

        @pl.when(seen)
        def _():
            k_low = dk[t].astype(BF)
            v_low = dv[t].astype(BF)
            k_low3[t] = k_low
            v_low3[t] = v_low
            for copy in low_copies(t):
                copy.start()
            out[i] = (mm_nt(k_low, wck[...]) + mm_nt(v_low, wcv[...])).astype(BF)

        @pl.when(jnp.logical_not(seen))
        def _():
            out[i] = jnp.zeros((TILE, D), BF)

        return carry

    for slot, out in enumerate(mem_parts):
        lax.fori_loop(
            0, sh.m_blocks // 4, lambda i, c, slot=slot, out=out: mem_tile(i, c, slot, out), 0
        )

    def settle(t):
        for copy in low_copies(t):
            copy.wait()

    each_wanted(settle)


def cross_backward(sh, lens, order, mlens, arrays, slots):
    rows, nm = sh.rows, sh.m_blocks
    outs = [shape((nm // 4, TILE, D), BF)] * 4 + [
        shape((rows, D), BF),
        shape((nm, TILE, D), BF),
        shape((nm, TILE, D), BF),
    ]
    scratch = [
        pltpu.VMEM((D, D), BF),
        pltpu.VMEM((D, D), BF),
        pltpu.VMEM((HEADS, 2 * HDIM, TILE), BF),
        pltpu.VMEM((HEADS, 2 * HDIM, TILE), BF),
        pltpu.VMEM((HEADS, TILE, 2 * HDIM), BF),
        pltpu.VMEM((HEADS, TILE, 2 * HDIM), BF),
        pltpu.VMEM((HEADS, TILE), F32),
        pltpu.VMEM((TILE, TILE), F32),
        pltpu.VMEM((nm, TILE, D), F32),
        pltpu.VMEM((nm, TILE, D), F32),
        pltpu.VMEM((D, TILE), F32),
        pltpu.VMEM((nm, TILE, D), BF),
        pltpu.VMEM((nm, TILE, D), BF),
        pltpu.VMEM((nm, D, TILE), BF),
        pltpu.VMEM((nm, TILE, D), BF),
        pltpu.VMEM((nm, TILE, D), BF),
        pltpu.SMEM((4, DOCS), jnp.int32),
        pltpu.SemaphoreType.DMA((2,)),
        pltpu.SemaphoreType.DMA((3, nm)),
        pltpu.SemaphoreType.DMA((2, nm)),
    ]
    specs = [SMEM_SPEC] * 3 + [VMEM_SPEC] * 2 + [ANY_SPEC] * 3 + [VMEM_SPEC] * 4
    specs += [ANY_SPEC] * len(slots)
    return call(
        lambda *refs: cross_backward_kernel(sh, *refs),
        "cross_backward",
        (lens, order, mlens, *arrays, *slots),
        specs,
        outs,
        scratch,
        15,
        out_specs=[VMEM_SPEC] * 5 + [ANY_SPEC] * 2,
    )


def first_backward_kernel(sh, lens, order, mlens, *refs):
    count, rows, n = sh.count, sh.rows, sh.piece
    (dq, *low_in, g_second, n1, inv1, first_low, ctx, vec, vec_in) = refs[:10]
    mems = refs[10 : 9 + 2 * sh.split]
    slots = refs[9 + 2 * sh.split : 9 + 2 * sh.split + count]
    outs = refs[9 + 2 * sh.split + count :]
    (g_send, g_own, g_first, g_ctx, g_ctx_t3, vec_grad) = outs[:6]
    (wo, wcq, g_self, acc_k, acc_v, stage, mem, k_low3, v_low3, bounds) = outs[6:16]
    (sems, mem_sems, low_sems) = outs[16:]
    for i, w in enumerate((wo, wcq)):
        start_weight(sh, slots, i * n, n, w, sems.at[i])
    vec_grad[...] = vec_in[...]
    slot_bounds(lens, order, bounds)

    def wanted(t):
        return touched_tile(sh, lens, order, mlens, t, bounds, True)

    def fetch(t, carry):
        @pl.when(wanted(t))
        def _():
            for copy in tile_copies(t, low_in, (k_low3, v_low3), low_sems):
                copy.start()

        return carry

    lax.fori_loop(0, sh.m_blocks, fetch, 0)
    start_mems(sh, mems, mem, mem_sems, wanted)
    wait_all(wo, sems.at[0])
    wait_all(wcq, sems.at[1])

    def add_vec(row, value):
        vec_grad[row : row + 1, :] = vec_grad[row : row + 1, :] + value

    def own_rows(i, carry):
        r = pl.ds(pl.multiple_of(i * TILE, TILE), TILE)
        total = g_second[r, :] + mm_nt(dq[r, :], wcq[...])
        normal = n1[r, :]
        add_vec(V_G1, col_sum(total * normal))
        add_vec(V_S1, col_sum(total))
        gf = norm_back(total, normal, inv1[r, :], vec[V_G1 : V_G1 + 1, :])
        g_first[r, :] = gf
        low = gf.astype(BF)
        g_self[r, :] = low
        add_vec(V_SOB, col_sum(low))
        gc = mm_nt(low, wo[...]).astype(BF)
        g_ctx[r, :] = gc
        g_ctx_t3[i] = gc.T
        return carry

    lax.fori_loop(0, rows // TILE, own_rows, 0)
    acc_k[...] = jnp.zeros(acc_k.shape, F32)
    acc_v[...] = jnp.zeros(acc_v.shape, F32)

    def mem_tile(t, carry):
        @pl.when(wanted(t))
        def _():
            wait_mem(mem, t, mem_sems)
            for copy in tile_copies(t, low_in, (k_low3, v_low3), low_sems):
                copy.wait()
            k_low = k_low3[t]
            v_low = v_low3[t]
            x = mem[t]
            acc_k[...] = acc_k[...] + mm_tn(x, k_low)
            acc_v[...] = acc_v[...] + mm_tn(x, v_low)
            add_vec(V_CVB, col_sum(v_low))

        return carry

    lax.fori_loop(0, sh.m_blocks, mem_tile, 0)

    add_vec(V_CQB, col_sum(dq[...]))
    stage[...] = mm_tn(ctx[...], g_self[...]).astype(BF)
    put_grad(sh, stage, n, 0, g_send, g_own)
    stage[...] = mm_tn(first_low[...], dq[...]).astype(BF)
    put_grad(sh, stage, n, n, g_send, g_own)
    stage[...] = acc_k[...].astype(BF)
    put_grad(sh, stage, n, 2 * n, g_send, g_own)
    stage[...] = acc_v[...].astype(BF)
    put_grad(sh, stage, n, 3 * n, g_send, g_own)


def first_backward(sh, lens, order, mlens, arrays, mems, slots):
    rows, nq, n, nm = sh.rows, sh.q_blocks, sh.piece, sh.m_blocks
    outs = [
        shape((sh.count // 2, 4 * n, D), BF),
        shape((sh.count // 2, 4 * n, D), BF),
        shape((rows, D), F32),
        shape((rows, D), BF),
        shape((nq, D, TILE), BF),
        shape((VROWS, D), F32),
    ]
    scratch = [
        pltpu.VMEM((D, D), BF),
        pltpu.VMEM((D, D), BF),
        pltpu.VMEM((rows, D), BF),
        pltpu.VMEM((D, D), F32),
        pltpu.VMEM((D, D), F32),
        pltpu.VMEM((D, D), BF),
        pltpu.VMEM((nm, TILE, D), BF),
        pltpu.VMEM((nm, TILE, D), BF),
        pltpu.VMEM((nm, TILE, D), BF),
        pltpu.SMEM((4, DOCS), jnp.int32),
        pltpu.SemaphoreType.DMA((2,)),
        pltpu.SemaphoreType.DMA((nm,)),
        pltpu.SemaphoreType.DMA((2, nm)),
    ]
    specs = [SMEM_SPEC] * 3 + [VMEM_SPEC] + [ANY_SPEC] * 2 + [VMEM_SPEC] * 7
    specs += [ANY_SPEC] * (len(mems) + len(slots))
    return call(
        lambda *refs: first_backward_kernel(sh, *refs),
        "first_backward",
        (lens, order, mlens, *arrays, *mems, *slots),
        specs,
        outs,
        scratch,
        6,
    )


def self_backward_kernel(sh, lens, order, *refs):
    count, rows, n, halo = sh.count, sh.rows, sh.piece, sh.halo
    (q_ref, q_t3, k3, v3, k_t3, ctx_t3, lse, g_ctx, g_ctx_t3) = refs[:9]
    slots = refs[9 : 9 + count]
    outs = refs[9 + count :]
    (grad_halo, dq, k_low3, v_low3) = outs[:4]
    (wk, wv, q_t, g_t, q_m, g_m, delta, bias, dk, dv, dq_t, sems) = outs[4:]
    z = lax.axis_index("seq")
    for i, w in enumerate((wk, wv)):
        start_weight(sh, slots, (1 + i) * n, n, w, sems.at[i])
    spread_zero(q_t)
    spread_zero(g_t)

    def clear(t, carry):
        dk[t] = jnp.zeros((TILE, D), F32)
        dv[t] = jnp.zeros((TILE, D), F32)
        return carry

    lax.fori_loop(0, sh.k_blocks, clear, 0)

    def block(b, carry):
        backward_start(b, q_t3, g_ctx_t3, q_ref, g_ctx, ctx_t3, q_t, g_t, q_m, g_m, delta, dq_t)
        self_tiles(
            sh,
            lens,
            order,
            b,
            bias,
            lambda t: backward_tile(
                k3.at[t],
                v3.at[t],
                k_t3.at[t],
                bias,
                q_t,
                g_t,
                q_m,
                g_m,
                lse.at[b],
                delta,
                dk.at[t],
                dv.at[t],
                dq_t,
            ),
        )
        r = pl.ds(pl.multiple_of(b * TILE, TILE), TILE)
        dq[r, :] = (dq_t[...] * HDIM**-0.5).T.astype(BF)
        return carry

    lax.fori_loop(0, sh.q_blocks, block, 0)
    wait_all(wk, sems.at[0])
    wait_all(wv, sems.at[1])
    tiles = rows // TILE

    def lower(t, carry):
        k_low3[t] = dk[t].astype(BF)
        v_low3[t] = dv[t].astype(BF)
        return carry

    lax.fori_loop(0, sh.k_blocks, lower, 0)
    for k in range(halo, 0, -1):

        def window_rows(i, carry, k=k):
            r = pl.ds(pl.multiple_of(i * TILE, TILE), TILE)
            t = (halo - k) * tiles + i
            part = mm_nt(k_low3[t], wk[...]) + mm_nt(v_low3[t], wv[...])
            grad_halo[k - 1, r, :] = part.astype(BF)
            return carry

        @pl.when(z >= k)
        def _(window_rows=window_rows):
            lax.fori_loop(0, tiles, window_rows, 0)

        @pl.when(z < k)
        def _(k=k):
            grad_halo[k - 1] = jnp.zeros((rows, D), BF)


def self_backward(sh, lens, order, arrays, slots):
    rows, nb = sh.rows, sh.k_blocks
    outs = [
        shape((sh.halo, rows, D), BF),
        shape((rows, D), BF),
        shape((nb, TILE, D), BF),
        shape((nb, TILE, D), BF),
    ]
    scratch = [
        pltpu.VMEM((D, D), BF),
        pltpu.VMEM((D, D), BF),
        pltpu.VMEM((HEADS, 2 * HDIM, TILE), BF),
        pltpu.VMEM((HEADS, 2 * HDIM, TILE), BF),
        pltpu.VMEM((HEADS, TILE, 2 * HDIM), BF),
        pltpu.VMEM((HEADS, TILE, 2 * HDIM), BF),
        pltpu.VMEM((HEADS, TILE), F32),
        pltpu.VMEM((TILE, TILE), F32),
        pltpu.VMEM((nb, TILE, D), F32),
        pltpu.VMEM((nb, TILE, D), F32),
        pltpu.VMEM((D, TILE), F32),
        pltpu.SemaphoreType.DMA((2,)),
    ]
    specs = [SMEM_SPEC] * 2 + [VMEM_SPEC] * len(arrays) + [ANY_SPEC] * len(slots)
    return call(
        lambda *refs: self_backward_kernel(sh, *refs),
        "self_backward",
        (lens, order, *arrays, *slots),
        specs,
        outs,
        scratch,
        14,
    )


def self_weights_kernel(sh, *refs):
    count, rows, n, halo = sh.count, sh.rows, sh.piece, sh.halo
    (dq, k_low3, v_low3, g_first, vec_in) = refs[:5]
    toks = refs[5 : 6 + halo]
    slots = refs[6 + halo : 6 + halo + count]
    outs = refs[6 + halo + count :]
    (g_send, g_own, grad_own) = outs[:3]
    (wq, wk, wv, acc_k, acc_v, vec_grad, stage, sems) = outs[3:]
    z = lax.axis_index("seq")
    for i, w in enumerate((wq, wk, wv)):
        start_weight(sh, slots, i * n, n, w, sems.at[i])
    vec_grad[...] = vec_in[...]
    tiles = rows // TILE

    def add_vec(row, value):
        vec_grad[row : row + 1, :] = vec_grad[row : row + 1, :] + value

    acc_k[...] = jnp.zeros(acc_k.shape, F32)
    acc_v[...] = jnp.zeros(acc_v.shape, F32)
    for k in range(halo, -1, -1):

        def window_rows(i, carry, k=k):
            r = pl.ds(pl.multiple_of(i * TILE, TILE), TILE)
            t = (halo - k) * tiles + i
            x = toks[k][r, :]
            acc_k[...] = acc_k[...] + mm_tn(x, k_low3[t])
            acc_v[...] = acc_v[...] + mm_tn(x, v_low3[t])
            add_vec(V_SVB, col_sum(v_low3[t]))
            return carry

        @pl.when(z >= k)
        def _(window_rows=window_rows):
            lax.fori_loop(0, tiles, window_rows, 0)

    add_vec(V_SQB, col_sum(dq[...]))
    stage[...] = mm_tn(toks[0][...], dq[...]).astype(BF)
    put_grad(sh, stage, n, 0, g_send, g_own)
    stage[...] = acc_k[...].astype(BF)
    put_grad(sh, stage, n, n, g_send, g_own)
    stage[...] = acc_v[...].astype(BF)
    put_grad(sh, stage, n, 2 * n, g_send, g_own)
    vec_low = vec_grad[...].astype(BF)
    for s in range(count // 2):
        g_send[s, pl.ds(3 * n, VROWS), :] = vec_low
        g_own[s, pl.ds(3 * n, VROWS), :] = vec_low
    for i, w in enumerate((wq, wk, wv)):
        wait_all(w, sems.at[i])

    def own_rows(i, carry):
        r = pl.ds(pl.multiple_of(i * TILE, TILE), TILE)
        t = halo * tiles + i
        part = mm_nt(k_low3[t], wk[...]) + mm_nt(v_low3[t], wv[...])
        grad_own[r, :] = g_first[r, :] + part + mm_nt(dq[r, :], wq[...])
        return carry

    lax.fori_loop(0, tiles, own_rows, 0)


def self_weights(sh, arrays, toks, slots):
    rows, n = sh.rows, sh.piece
    outs = [
        shape((sh.count // 2, 3 * n + VROWS, D), BF),
        shape((sh.count // 2, 3 * n + VROWS, D), BF),
        shape((rows, D), F32),
    ]
    scratch = [
        pltpu.VMEM((D, D), BF),
        pltpu.VMEM((D, D), BF),
        pltpu.VMEM((D, D), BF),
        pltpu.VMEM((D, D), F32),
        pltpu.VMEM((D, D), F32),
        pltpu.VMEM((VROWS, D), F32),
        pltpu.VMEM((D, D), BF),
        pltpu.SemaphoreType.DMA((3,)),
    ]
    specs = [VMEM_SPEC] * (len(arrays) + len(toks)) + [ANY_SPEC] * len(slots)
    return call(
        lambda *refs: self_weights_kernel(sh, *refs),
        "self_weights",
        (*arrays, *toks, *slots),
        specs,
        outs,
        scratch,
        7,
    )


def shards(
    tokens,
    memory,
    targets,
    doc_lengths,
    doc_order,
    memory_lengths,
    self_query,
    self_query_bias,
    self_key,
    self_value,
    self_value_bias,
    self_output,
    self_output_bias,
    first_gain,
    first_shift,
    cross_query,
    cross_query_bias,
    cross_key,
    cross_value,
    cross_value_bias,
    cross_output,
    cross_output_bias,
    second_gain,
    second_shift,
    expand_weight,
    expand_bias,
    contract_weight,
    contract_bias,
    third_gain,
    third_shift,
):
    split = lax.axis_size("seq")
    count = lax.axis_size("fsdp")
    n = self_query.shape[0]
    wide = contract_weight.shape[0]
    sh = Shard(tokens.shape[0], memory.shape[0], count, split, n, wide)

    own_a, own_b = pack(
        sh,
        (
            self_query_bias,
            self_value_bias,
            self_output_bias,
            first_gain,
            first_shift,
            cross_query_bias,
            cross_value_bias,
            cross_output_bias,
            second_gain,
            second_shift,
            contract_bias,
            third_gain,
            third_shift,
        ),
        expand_bias,
        (
            self_query,
            self_key,
            self_value,
            self_output,
            cross_query,
            cross_key,
            cross_value,
            cross_output,
            expand_weight,
            contract_weight,
        ),
    )
    toks, downs = [tokens, seq_up(tokens, split)], [seq_down(memory, split)]
    swaps = [(i, i ^ 1) for i in range(count)]
    pairs = [step_pairs(count, index) for index in range(len(chip_steps(count)[0]))]
    slots_a, slots_b = [own_a], [own_b]
    own_b_first = [own_b]
    other_b = [lax.ppermute(own_b, "fsdp", swaps)]
    first = [lax.ppermute(own_a, "fsdp", p) for p in pairs]
    hold = (toks[1], downs[0], *first, *other_b)
    for _ in range(1, sh.halo):
        toks.append(seq_up(after(toks[-1], *hold), split))
    ups = [seq_up(after(memory, *hold), split)]
    held_b = after(own_b, *hold)
    second = [lax.ppermute(held_b, "fsdp", p) for p in pairs]
    for index, p in enumerate(pairs):
        slots_a += [first[index]] + [lax.ppermute(after(a, *hold), "fsdp", p) for a in slots_a[1:]]
    hold = (toks[-1], ups[0], *second, *slots_a[3:])
    for index, p in enumerate(pairs):
        slots_b += [second[index]] + [lax.ppermute(after(a, *hold), "fsdp", p) for a in slots_b[1:]]
    slots_a = slots_a + [lax.ppermute(after(a, *hold), "fsdp", swaps) for a in slots_a]
    for k in range(2, split):
        if k == split - 1:
            last = after(memory, *hold)
            ends = lax.ppermute(last, "seq", [(0, split - 1), (split - 1, 0)])
            ups.append(ends)
            downs.append(ends)
        else:
            ups.append(seq_up(after(ups[-1], *hold), split))
            downs.append(seq_down(after(downs[-1], *hold), split))
    mems = [memory]
    for up, down in zip(ups, downs):
        mems += [up, down]

    near = [lax.ppermute(after(a, *hold), "fsdp", swaps) for a in second]
    first_tok = after(tokens, *hold, *near)
    (q, q_t3, k3, v3, k_t3, ctx, ctx_t3, lse, vec) = self_forward(
        sh, doc_lengths, doc_order, [first_tok] + toks[1:], slots_a
    )
    swapped = {id(a): b for a, b in zip(own_b_first + second, other_b + near)}
    late = (ctx, *ups, *downs)
    slots_b = slots_b + [
        swapped[id(a)] if id(a) in swapped else lax.ppermute(after(a, *late), "fsdp", swaps)
        for a in slots_b
    ]
    (n1, inv1, first_low, cq, cq_t3, mk3, mv3, mk_t3, cctx, cctx_t3, clse) = cross_forward(
        sh, doc_lengths, doc_order, memory_lengths, tokens, ctx, vec, mems, slots_b
    )
    feed_out = feed(sh, doc_lengths, doc_order, n1, cctx, targets, vec, slots_b)
    (final_low, g_second, g_cc, g_cc_t3, vec_grad, send_c, own_c) = feed_out
    sum_c = Reduction(send_c, own_c, count, split)
    sum_c.step()
    cq = after(cq, sum_c.send)
    sum_c.step()
    *mem_parts, dcq, k_low3, v_low3 = cross_backward(
        sh,
        doc_lengths,
        doc_order,
        memory_lengths,
        (cq, cq_t3, mk3, mv3, mk_t3, cctx_t3, clse, g_cc, g_cc_t3),
        slots_b,
    )
    dcq = after(dcq, sum_c.send)
    sum_c.step(dcq)
    swap = [(i, i ^ 1) for i in range(split)]
    mem_got = lax.ppermute(mem_parts[0], "seq", swap)
    (send_b, own_b, g_first, g_ctx, g_ctx_t3, vec_grad) = first_backward(
        sh,
        doc_lengths,
        doc_order,
        memory_lengths,
        (dcq, k_low3, v_low3, g_second, n1, inv1, first_low, ctx, vec, vec_grad),
        mems,
        slots_b,
    )
    mem_away = add_low(after(mem_parts[1], g_first), mem_got)
    sum_b = Reduction(send_b, own_b, count, split)
    g_ctx = after(g_ctx, sum_c.send, mem_away)
    sum_c.step(g_ctx)
    sum_b.step(g_ctx)
    mem_got = lax.ppermute(after(mem_parts[2], g_ctx), "seq", swap)
    mem_far = lax.ppermute(after(mem_away, g_ctx), "seq", [(i, i ^ 2) for i in range(split)])
    (grad_halo, dq, sk_low3, sv_low3) = self_backward(
        sh,
        doc_lengths,
        doc_order,
        (q, q_t3, k3, v3, k_t3, ctx_t3, lse, g_ctx, g_ctx_t3),
        slots_a,
    )
    dq = after(dq, mem_got, mem_far, sum_c.send, sum_b.send)
    back = seq_down(after(grad_halo[sh.halo - 1], dq), split)
    sum_b.step(dq)
    sum_c.step(dq)
    (send_a, own_a, grad_own) = self_weights(
        sh,
        (dq, sk_low3, sv_low3, g_first, vec_grad),
        toks,
        slots_a,
    )
    send_a = after(send_a, sum_b.send, sum_c.send)
    sum_a = Reduction(send_a, own_a, count, split)
    sum_a.step()
    sum_b.step(send_a)
    sum_c.step(send_a)
    for k in range(sh.halo - 1, 0, -1):
        back = seq_down(after(add_low(grad_halo[k - 1], back), send_a), split)
    sum_a.step()
    ready, held = sum_a.send, (sum_b.send, sum_c.send)
    while [a for a, _ in sum_a.plan].count("fsdp"):
        sum_a.step()
    sum_b.step(ready)
    ready = sum_a.send
    sum_a.step(back, *held)
    sum_b.step(ready)
    input_grad = grad_own + back.astype(F32)
    mem_last = after(mem_parts[3], sum_a.send)
    mem_here = mem_last.astype(F32) + mem_got.astype(F32) + mem_far.astype(F32)
    memory_grad = seq_rest(mem_here.reshape(split // 4, sh.mem_rows, D), split)[0]
    sum_a.finish()
    red_b, red_c = sum_b.finish(), sum_c.finish()

    def rows_of(array, start, size):
        return array[start : start + size].astype(F32)

    done = finish(sh, sum_a.parts[0], sum_a.got, expand_bias.shape[0])
    small_grad = done[3 : 3 + V_EB]
    expand_bias_grad = done[3 + V_EB]
    loss_value = done[4 + V_EB].reshape(())
    expand_grad = jnp.concatenate(
        [rows_of(red_c, (1 + c) * n, n) for c in range(FFB)], axis=1
    )
    return (
        final_low,
        loss_value,
        input_grad,
        memory_grad,
        done[0],
        small_grad[V_SQB],
        done[1],
        done[2],
        small_grad[V_SVB],
        rows_of(red_b, 0, n),
        small_grad[V_SOB],
        small_grad[V_G1],
        small_grad[V_S1],
        rows_of(red_b, n, n),
        small_grad[V_CQB],
        rows_of(red_b, 2 * n, n),
        rows_of(red_b, 3 * n, n),
        small_grad[V_CVB],
        rows_of(red_c, 0, n),
        small_grad[V_COB],
        small_grad[V_G2],
        small_grad[V_S2],
        expand_grad,
        expand_bias_grad,
        rows_of(red_c, 5 * n, wide),
        small_grad[V_CB],
        small_grad[V_G3],
        small_grad[V_S3],
    )


def solution(mesh):
    rows = P(("fsdp", "seq"), None)
    matrix = P("fsdp", None)
    vector = P("fsdp")
    kinds = (
        "mvmmvmvvvmvmmvmvvvmvmvvv"
    )
    weights = tuple(matrix if kind == "m" else vector for kind in kinds)
    return jax.shard_map(
        shards,
        mesh=mesh,
        in_specs=(rows, rows, rows, matrix, matrix, matrix) + weights,
        out_specs=(rows, P(), rows, rows) + weights,
        check_vma=False,
    )
```

```python
import jax
import jax.numpy as jnp
from jax import lax
from jax.experimental import pallas as pl
from jax.experimental.pallas import tpu as pltpu
from jax.sharding import PartitionSpec as P

D = 512
HDIM = 64
HEADS = D // HDIM
DOCS = 4
MEM = 512
FFB = 4
TILE = 256
GROUP = 4
VROWS = 32
NEG = -1e30
BF = jnp.bfloat16
F32 = jnp.float32
VMEM_BYTES = 60 * 1024 * 1024
FLOPS_RATE = 3e13

(
    V_SQB,
    V_SVB,
    V_SOB,
    V_G1,
    V_S1,
    V_CQB,
    V_CVB,
    V_COB,
    V_G2,
    V_S2,
    V_CB,
    V_G3,
    V_S3,
    V_EB,
) = range(14)
V_LOSS = V_EB + FFB
V_LIVE = V_LOSS + 1
LOW_BITS = 36
HIGH_BITS = 36


def mm(a, b):
    return jnp.dot(a, b, preferred_element_type=F32)


def mm_nt(a, b):
    return lax.dot_general(a, b, (((1,), (1,)), ((), ())), preferred_element_type=F32)


def mm_tn(a, b):
    return lax.dot_general(a, b, (((0,), (0,)), ((), ())), preferred_element_type=F32)


def col_sum(v):
    return jnp.sum(v.astype(F32), axis=0, keepdims=True)


def chip_steps(count):
    bits = []
    bit = 2
    while bit < count:
        bits.append(bit)
        bit *= 2
    return bits, bits[::-1]


def gather_masks(count):
    result = []
    for steps in chip_steps(count):
        masks = [0]
        for step in steps:
            masks = masks + [m ^ step for m in masks]
        result.append(masks)
    own0, own1 = result
    return [own0 + [m ^ 1 for m in own1], own1 + [m ^ 1 for m in own0]]


def reduce_masks(count):
    result = []
    for steps in chip_steps(count):
        masks = [0]
        for step in steps[::-1]:
            masks = masks + [m ^ step for m in masks]
        result.append(masks)
    return result


def step_pairs(count, index):
    orders = chip_steps(count)
    return [(i, i ^ orders[i & 1][index]) for i in range(count)]


def fsdp_gather_parts(own, count):
    have = [own]
    for index in range(len(chip_steps(count)[0])):
        pairs = step_pairs(count, index)
        have = have + [lax.ppermute(a, "fsdp", pairs) for a in have]
    return have, [(i, i ^ 1) for i in range(count)]


def fsdp_gather(own, count):
    have, swap = fsdp_gather_parts(own, count)
    return have + [lax.ppermute(a, "fsdp", swap) for a in have]


def add_low(a, b):
    return (a.astype(F32) + b.astype(F32)).astype(BF)


def after(value, *others):
    return lax.optimization_barrier((value, *others))[0]


def sum_low(parts):
    total = parts[0].astype(F32)
    for part in parts[1:]:
        total = total + part.astype(F32)
    return total.astype(BF)


class Reduction:
    def __init__(self, send, own, count, split):
        self.send, self.parts = send, [own]
        self.odd = (lax.axis_index("seq") % 2) == 1
        self.got = None
        self.plan = [("fsdp", [(i, i ^ 1) for i in range(count)])]
        for index in range(len(chip_steps(count)[0])):
            self.plan.append(("fsdp", step_pairs(count, index)))
        bits = [1 << k for k in range(split.bit_length() - 1)]
        for bit in bits + [1]:
            self.plan.append(("seq", [(i, i ^ bit) for i in range(split)]))

    def start(self, *others):
        send = after(self.send, *others) if others else self.send
        self.axis, pairs = self.plan.pop(0)
        self.got = lax.ppermute(send, self.axis, pairs)

    def end(self, *others):
        if others:
            self.parts[0] = after(self.parts[0], *others)
        left = sum(1 for axis, _ in self.plan if axis == "fsdp")
        if self.axis == "fsdp":
            self.parts.append(self.got)
            if left > 0:
                half = self.got.shape[0] // 2
                self.send = sum_low([part[half:] for part in self.parts])
                self.parts = [part[:half] for part in self.parts]
            else:
                total = sum_low([part[0] for part in self.parts])
                half = total.shape[0] // 2
                self.send = jnp.where(self.odd, total[:half], total[half:])
                self.parts = [jnp.where(self.odd, total[half:], total[:half])]
        elif self.plan:
            self.send = sum_low([self.parts[0], self.got])
            self.parts = [self.send]
        else:
            mine, got = self.parts[0], self.got
            self.send = jnp.where(
                self.odd, jnp.concatenate([got, mine]), jnp.concatenate([mine, got])
            )

    def step(self, *others):
        self.start(*others)
        self.end()

    def finish(self):
        while self.plan:
            self.step()
        return self.send


def seq_rest(parts, split):
    z = lax.axis_index("seq")
    bit = 4
    while bit < split:
        pairs = parts.reshape(parts.shape[0] // 2, 2, *parts.shape[1:])
        odd = (z // bit) % 2 == 1
        got = lax.ppermute(
            jnp.where(odd, pairs[:, 0], pairs[:, 1]), "seq", [(i, i ^ bit) for i in range(split)]
        )
        parts = jnp.where(odd, pairs[:, 1], pairs[:, 0]) + got
        bit *= 2
    return parts


def seq_up(a, count):
    return lax.ppermute(a, "seq", [(i, i + 1) for i in range(count - 1)])


def seq_down(a, count):
    return lax.ppermute(a, "seq", [(i + 1, i) for i in range(count - 1)])


def slot_place(index, masks, slot):
    return jnp.where(index % 2 == 0, index ^ masks[0][slot], index ^ masks[1][slot])


class Shard:
    def __init__(self, rows, mem_rows, count, split, piece, wide_piece):
        self.rows = rows
        self.mem_rows = mem_rows
        self.count = count
        self.split = split
        self.piece = piece
        self.wide_piece = wide_piece
        self.group_rows = rows * split
        self.group_mem = mem_rows * split
        self.halo = min(-(-(self.group_rows // 2 - 1) // rows), split - 1)
        self.window = rows * (self.halo + 1)
        self.q_blocks = rows // TILE
        self.k_blocks = self.window // TILE
        self.m_blocks = self.group_mem // TILE
        self.gather = gather_masks(count)
        self.reduce = reduce_masks(count)


def start_weight(sh, slots, row, n, target, sem):
    index = lax.axis_index("fsdp")
    for s, slot in enumerate(slots):
        place = pl.multiple_of(slot_place(index, sh.gather, s) * n, n)
        pltpu.make_async_copy(slot.at[pl.ds(row, n)], target.at[pl.ds(place, n)], sem).start()


def wait_all(target, sem):
    pltpu.make_async_copy(target, target, sem).wait()


def send_all(sources, targets, sems, first=0):
    copies = [
        pltpu.make_async_copy(source, target, sems.at[first + i])
        for i, (source, target) in enumerate(zip(sources, targets))
    ]
    for copy in copies:
        copy.start()
    return copies


def tile_copies(t, sources, targets, sems):
    return [
        pltpu.make_async_copy(source.at[t], target.at[t], sems.at[i, t])
        for i, (source, target) in enumerate(zip(sources, targets))
    ]


def start_mems(sh, mems, target, sems, wanted):
    z = lax.axis_index("seq")
    tiles_per = sh.mem_rows // TILE

    def place(source, shard):
        for i in range(tiles_per):
            t = shard * tiles_per + i

            @pl.when(wanted(t))
            def _(i=i, t=t):
                pltpu.make_async_copy(
                    source.at[pl.ds(i * TILE, TILE)], target.at[t], sems.at[t]
                ).start()

    place(mems[0], z)
    for k in range(1, sh.split):
        up, down = mems[2 * k - 1], mems[2 * k]

        @pl.when(z >= k)
        def _(up=up, k=k):
            place(up, z - k)

        @pl.when(z + k < sh.split)
        def _(down=down, k=k):
            place(down, z + k)


def wait_mem(target, t, sems):
    pltpu.make_async_copy(target.at[t], target.at[t], sems.at[t]).wait()


def put_grad(sh, full, n, row, send_ref, own_ref):
    index = lax.axis_index("fsdp")
    partner = index ^ 1
    for s in range(sh.count // 2):
        mine = pl.multiple_of(slot_place(index, sh.reduce, s) * n, n)
        theirs = pl.multiple_of(slot_place(partner, sh.reduce, s) * n, n)
        own_ref[s, pl.ds(row, n), :] = full[pl.ds(mine, n), :]
        send_ref[s, pl.ds(row, n), :] = full[pl.ds(theirs, n), :]


def doc_bounds(lens, order):
    starts, ends = [], []
    total = jnp.int32(0)
    for p in range(DOCS):
        starts.append(total)
        total = total + lens[0, order[0, p]]
        ends.append(total)
    return starts, ends


def pick(starts, ends, pos, values):
    out = jnp.zeros_like(pos)
    for p in range(DOCS):
        out = jnp.where((pos >= starts[p]) & (pos < ends[p]), values[p], out)
    return out


def lane_pos(base):
    return base + lax.broadcasted_iota(jnp.int32, (1, TILE), 1)


def norm_stats(v):
    mean = jnp.mean(v, axis=1, keepdims=True)
    c = v - mean
    inv = lax.rsqrt(jnp.mean(c * c, axis=1, keepdims=True) + 1e-05)
    return c * inv, inv


def norm_back(dy, n, inv, gain):
    e = dy * gain
    return inv * (
        e - jnp.mean(e, axis=1, keepdims=True) - n * jnp.mean(e * n, axis=1, keepdims=True)
    )


def head_rows(h):
    return slice(h * HDIM, (h + 1) * HDIM)


def pair_lanes(h):
    j = h // 2
    return slice(j * 2 * HDIM, (j + 1) * 2 * HDIM)


def spread_rows(source, target):
    for h in range(HEADS):
        o = (h % 2) * HDIM
        target[h, pl.ds(o, HDIM), :] = source[head_rows(h), :]


def spread_zero(target):
    for h in range(HEADS):
        o = (1 - h % 2) * HDIM
        target[h, pl.ds(o, HDIM), :] = jnp.zeros((HDIM, TILE), BF)


def spread_lanes(source, target):
    lane = lax.broadcasted_iota(jnp.int32, (TILE, 2 * HDIM), 1)
    for h in range(HEADS):
        part = source[:, pair_lanes(h)]
        keep = (lane >= HDIM) if h % 2 else (lane < HDIM)
        target[h] = jnp.where(keep, part, jnp.zeros_like(part))


def forward_tile(keys, vals_t, bias, q_t, m_ref, l_ref, acc_ref):
    heads = range(HEADS)
    mask = bias[...]
    m_old, l_old = m_ref[...], l_ref[...]
    scores = [mm(keys[:, pair_lanes(h)], q_t[h]) + mask for h in heads]
    tops = [
        jnp.maximum(m_old[h : h + 1], jnp.max(scores[h], axis=0, keepdims=True)) for h in heads
    ]
    probs = [jnp.exp(scores[h] - tops[h]) for h in heads]
    alphas = [jnp.exp(m_old[h : h + 1] - tops[h]) for h in heads]
    sums = [
        alphas[h] * l_old[h : h + 1] + jnp.sum(probs[h], axis=0, keepdims=True) for h in heads
    ]
    outs = [mm(vals_t[head_rows(h), :], probs[h].astype(BF)) for h in heads]
    for h in heads:
        acc_ref[head_rows(h), :] = acc_ref[head_rows(h), :] * alphas[h] + outs[h]
    m_ref[...] = jnp.concatenate(tops, axis=0)
    l_ref[...] = jnp.concatenate(sums, axis=0)


def forward_start(m_ref, l_ref, acc_ref):
    m_ref[...] = jnp.full(m_ref.shape, NEG, F32)
    l_ref[...] = jnp.zeros(l_ref.shape, F32)
    acc_ref[...] = jnp.zeros(acc_ref.shape, F32)


def forward_end(b, m_ref, l_ref, acc_ref, ctx_ref, ctx_t_ref, lse_ref):
    lse_ref[b] = m_ref[...] + jnp.log(l_ref[...])
    for h in range(HEADS):
        acc_ref[head_rows(h), :] = acc_ref[head_rows(h), :] / l_ref[h : h + 1, :]
    ctx_t_ref[b] = acc_ref[...]
    ctx_ref[pl.ds(pl.multiple_of(b * TILE, TILE), TILE), :] = acc_ref[...].T.astype(BF)


def backward_tile(keys, vals, keys_t, bias, q_t, g_t, q_m, g_m, lse, delta, dk, dv, dq_t):
    mask = bias[...]
    for first in range(0, HEADS, GROUP):
        heads = range(first, first + GROUP)
        scores = [mm(keys[:, pair_lanes(h)], q_t[h]) for h in heads]
        probs = [jnp.exp(s + mask - lse[h : h + 1, :]) for h, s in zip(heads, scores)]
        dvs = [mm(p.astype(BF), g_m[h]) for h, p in zip(heads, probs)]
        dps = [mm(vals[:, pair_lanes(h)], g_t[h]) for h in heads]
        dss = [
            (p * (dp - delta[h : h + 1, :])).astype(BF) for h, p, dp in zip(heads, probs, dps)
        ]
        dks = [mm(ds, q_m[h]) for h, ds in zip(heads, dss)]
        dqs = [mm(keys_t[head_rows(h), :], ds) for h, ds in zip(heads, dss)]
        for i in range(0, GROUP, 2):
            lanes = pair_lanes(first + i)
            dv[:, lanes] = dv[:, lanes] + dvs[i] + dvs[i + 1]
            dk[:, lanes] = dk[:, lanes] + dks[i] + dks[i + 1]
        for h, dq in zip(heads, dqs):
            dq_t[head_rows(h), :] = dq_t[head_rows(h), :] + dq


def backward_start(b, q_t3, g_t3, q, g, ctx_t3, q_t, g_t, q_m, g_m, delta, dq_t):
    rows = pl.ds(pl.multiple_of(b * TILE, TILE), TILE)
    spread_rows(q_t3.at[b], q_t)
    spread_rows(g_t3.at[b], g_t)
    spread_lanes(q[rows, :], q_m)
    spread_lanes(g[rows, :], g_m)
    prod = g_t3[b].astype(F32) * ctx_t3[b]
    for h in range(HEADS):
        delta[h : h + 1, :] = jnp.sum(prod[head_rows(h), :], axis=0, keepdims=True)
    dq_t[...] = jnp.zeros(dq_t.shape, F32)


def self_tiles(sh, lens, order, b, bias, body):
    z = lax.axis_index("seq")
    starts, ends = doc_bounds(lens, order)
    shift = (z - sh.halo) * sh.rows
    q_base = sh.halo * sh.rows + b * TILE
    first = pick(starts, ends, q_base + shift, starts) - shift
    q_pos = lane_pos(q_base)
    q_start = pick(starts, ends, q_pos + shift, starts) - shift
    last = q_base // TILE
    number = last - first // TILE + 1

    def step(i, carry):
        t = last - i
        k_pos = t * TILE + lax.broadcasted_iota(jnp.int32, (TILE, TILE), 0)
        bias[...] = jnp.where((k_pos >= q_start) & (k_pos <= q_pos), 0.0, NEG)
        body(t)
        return carry

    lax.fori_loop(0, number, step, 0)


def self_forward_kernel(sh, lens, order, *refs):
    halo, count, rows, n = sh.halo, sh.count, sh.rows, sh.piece
    toks = refs[: halo + 1]
    slots = refs[halo + 1 : halo + 1 + count]
    (*kept, ctx, ctx_t3, lse, vec) = refs[halo + 1 + count : halo + 10 + count]
    outs = refs[halo + 10 + count :]
    (q_ref, q_t3, k3, v3, k_t3, wq, wk, wv, vec_slots, v_t3, q_t, bias) = outs[:12]
    (m_ref, l_ref, acc, sems, q_sems, tile_sems) = outs[12:]
    z = lax.axis_index("seq")
    for s, slot in enumerate(slots):
        pltpu.make_async_copy(slot.at[pl.ds(3 * n, VROWS)], vec_slots.at[s], sems.at[3]).start()
    for i, w in enumerate((wq, wk, wv)):
        start_weight(sh, slots, i * n, n, w, sems.at[i])
    spread_zero(q_t)
    wait_all(vec_slots, sems.at[3])
    vec[...] = jnp.sum(vec_slots[...].astype(F32), axis=0)
    wait_all(wq, sems.at[0])
    tiles = rows // TILE

    def own_rows(i, carry):
        r = pl.ds(pl.multiple_of(i * TILE, TILE), TILE)
        q = (mm(toks[0][r, :], wq[...]) + vec[V_SQB : V_SQB + 1, :]).astype(BF)
        q = q * BF(HDIM**-0.5)
        q_ref[r, :] = q
        q_t3[i] = q.T
        return carry

    for i in range(tiles):
        own_rows(i, 0)
    q_copies = send_all((q_ref, q_t3), kept[:2], q_sems)
    wait_all(wk, sems.at[1])
    wait_all(wv, sems.at[2])

    def window_copies(t):
        return tile_copies(t, (k3, v3, k_t3), kept[2:], tile_sems)

    for k in range(halo + 1):

        def window_rows(i, carry, k=k):
            r = pl.ds(pl.multiple_of(i * TILE, TILE), TILE)
            t = (halo - k) * tiles + i
            x = toks[k][r, :]
            key = mm(x, wk[...]).astype(BF)
            val = (mm(x, wv[...]) + vec[V_SVB : V_SVB + 1, :]).astype(BF)
            k3[t] = key
            v3[t] = val
            k_t3[t] = key.T
            v_t3[t] = val.T
            for copy in window_copies(t):
                copy.start()
            return carry

        @pl.when(z >= k)
        def _(window_rows=window_rows):
            lax.fori_loop(0, tiles, window_rows, 0)

    def block(b, carry):
        spread_rows(q_t3.at[b], q_t)
        forward_start(m_ref, l_ref, acc)
        self_tiles(
            sh,
            lens,
            order,
            b,
            bias,
            lambda t: forward_tile(k3.at[t], v_t3.at[t], bias, q_t, m_ref, l_ref, acc),
        )
        forward_end(b, m_ref, l_ref, acc, ctx, ctx_t3, lse)
        return carry

    lax.fori_loop(0, sh.q_blocks, block, 0)
    for copy in q_copies:
        copy.wait()
    for k in range(halo + 1):

        @pl.when(z >= k)
        def _(k=k):
            for i in range(tiles):
                for copy in window_copies((halo - k) * tiles + i):
                    copy.wait()


SMEM_SPEC = pl.BlockSpec(memory_space=pltpu.SMEM)
VMEM_SPEC = pl.BlockSpec(memory_space=pltpu.VMEM)
ANY_SPEC = pl.BlockSpec(memory_space=pl.ANY)


def shape(dims, dtype):
    return jax.ShapeDtypeStruct(dims, dtype)


def call(body, name, inputs, specs, outs, scratch, micros, vmem=VMEM_BYTES, out_specs=None):
    moved = sum(a.size * a.dtype.itemsize for a in (*inputs, *outs))
    cost = pl.CostEstimate(
        flops=int(micros * 1e-6 * FLOPS_RATE), transcendentals=0, bytes_accessed=moved // 50
    )
    return pl.pallas_call(
        body,
        name=name,
        in_specs=specs,
        out_specs=out_specs or [VMEM_SPEC] * len(outs),
        out_shape=outs,
        scratch_shapes=scratch,
        cost_estimate=cost,
        compiler_params=pltpu.CompilerParams(vmem_limit_bytes=vmem),
    )(*inputs)


def pack_kernel(sh, *refs):
    small = refs[:V_EB]
    wide_bias = refs[V_EB]
    mats = refs[V_EB + 1 : V_EB + 11]
    own_a, own_b = refs[V_EB + 11 :]
    n, wide = sh.piece, sh.wide_piece
    (sq, sk, sv, so, cq, ck, cv, co, w1, w2) = mats
    for i, m in enumerate((sq, sk, sv)):
        own_a[pl.ds(i * n, n), :] = m[...]
    for i, m in enumerate((so, cq, ck, cv, co)):
        own_b[pl.ds(i * n, n), :] = m[...]
    for c in range(FFB):
        own_b[pl.ds((5 + c) * n, n), :] = w1[:, c * D : (c + 1) * D]
    own_b[pl.ds(9 * n, wide), :] = w2[...]
    index = lax.axis_index("fsdp")

    def spread(piece, size, offset):
        hot = lax.broadcasted_iota(jnp.int32, (size, D), 1) == offset + lax.broadcasted_iota(
            jnp.int32, (size, D), 0
        )
        return mm(piece, hot.astype(BF)).astype(BF)

    rows = jnp.concatenate([r[...].reshape(1, n) for r in small], axis=0)
    size = wide_bias.shape[0]
    flat = index * size
    line = spread(wide_bias[...].reshape(1, size), size, flat % D)
    row = lax.broadcasted_iota(jnp.int32, (FFB, D), 0)
    own_a[pl.ds(3 * n, VROWS), :] = jnp.concatenate(
        [
            spread(rows, n, index * n),
            jnp.where(row == flat // D, line, jnp.zeros((FFB, D), BF)),
            jnp.zeros((VROWS - V_EB - FFB, D), BF),
        ],
        axis=0,
    )


def pack(sh, small, wide_bias, mats):
    n, wide = sh.piece, sh.wide_piece
    outs = [shape((3 * n + VROWS, D), BF), shape((9 * n + wide, D), BF)]
    return call(
        lambda *refs: pack_kernel(sh, *refs),
        "pack",
        (*small, wide_bias, *mats),
        [VMEM_SPEC] * (V_EB + 1 + len(mats)),
        outs,
        [],
        2,
    )


def digit_bits(devices):
    return 3 if 7 * devices <= 256 else 1


def digits(value, bits):
    lane = lax.broadcasted_iota(jnp.int32, (1, D), 1)
    scale = jnp.full((1, D), 2.0**LOW_BITS, F32)
    for i in range(9):
        scale = scale * jnp.where((lane // 2**i) % 2 == 1, 2.0 ** -min(bits * 2**i, 140), 1.0)
    whole = jnp.floor(value * scale)
    return whole - 2.0**bits * jnp.floor(value * scale * 2.0**-bits)


def undigits(row, bits):
    lane = lax.broadcasted_iota(jnp.int32, (1, D), 1)
    scale = jnp.full((1, D), 2.0**-LOW_BITS, F32)
    for i in range(7):
        scale = scale * jnp.where(
            (lane // 2**i) % 2 == 1, 2.0 ** min(bits * 2**i, LOW_BITS + HIGH_BITS), 1.0
        )
    used = lane < (LOW_BITS + HIGH_BITS) // bits
    return jnp.sum(jnp.where(used, row * jnp.where(used, scale, 0.0), 0.0), axis=1, keepdims=True)


def finish_kernel(sh, mine, got, *outs):
    n = sh.piece
    mats, small, wide_bias, loss = outs[:3], outs[3 : 3 + V_EB], outs[3 + V_EB], outs[4 + V_EB]
    red = outs[5 + V_EB]
    odd = lax.axis_index("seq") % 2 == 1
    half = mine.shape[0]
    red[pl.ds(0, half), :] = jnp.where(odd, got[...], mine[...])
    red[pl.ds(half, half), :] = jnp.where(odd, mine[...], got[...])
    for i, m in enumerate(mats):
        m[...] = red[pl.ds(i * n, n), :].astype(F32)
    index = lax.axis_index("fsdp")
    vec = red[pl.ds(3 * n, VROWS), :]

    def cut(rows, size, offset):
        hot = lax.broadcasted_iota(jnp.int32, (D, size), 0) == offset + lax.broadcasted_iota(
            jnp.int32, (D, size), 1
        )
        return mm(rows, hot.astype(BF))

    parts = cut(vec, n, index * n)
    for i in range(V_EB):
        small[i][...] = parts[i : i + 1, :].reshape(n)
    size = wide_bias.shape[0]
    flat = index * size
    row = lax.broadcasted_iota(jnp.int32, (VROWS, D), 0)
    lines = jnp.where(row == V_EB + flat // D, vec.astype(F32), 0.0).astype(BF)
    wide_bias[...] = jnp.sum(cut(lines, size, flat % D), axis=0, keepdims=True).reshape(size)
    bits = digit_bits(sh.count * sh.split)
    error_sum = undigits(vec[V_LOSS : V_LOSS + 1, :].astype(F32), bits)
    live = undigits(vec[V_LIVE : V_LIVE + 1, :].astype(F32), bits)
    loss[...] = error_sum / (live * D)


def finish(sh, mine, got, bias_size):
    n = sh.piece
    outs = [shape((n, D), F32)] * 3 + [shape((n,), F32)] * V_EB
    outs += [shape((bias_size,), F32), shape((1, 1), F32)]
    return call(
        lambda *refs: finish_kernel(sh, *refs),
        "finish",
        (mine, got),
        [VMEM_SPEC] * 2,
        outs,
        [pltpu.VMEM((3 * n + VROWS, D), BF)],
        2,
    )


def self_forward(sh, lens, order, toks, slots):
    nb, nq = sh.k_blocks, sh.q_blocks
    outs = [
        shape((sh.rows, D), BF),
        shape((nq, D, TILE), BF),
        shape((nb, TILE, D), BF),
        shape((nb, TILE, D), BF),
        shape((nb, D, TILE), BF),
        shape((sh.rows, D), BF),
        shape((nq, D, TILE), F32),
        shape((nq, HEADS, TILE), F32),
        shape((VROWS, D), F32),
    ]
    scratch = [
        pltpu.VMEM((sh.rows, D), BF),
        pltpu.VMEM((nq, D, TILE), BF),
        pltpu.VMEM((nb, TILE, D), BF),
        pltpu.VMEM((nb, TILE, D), BF),
        pltpu.VMEM((nb, D, TILE), BF),
        pltpu.VMEM((D, D), BF),
        pltpu.VMEM((D, D), BF),
        pltpu.VMEM((D, D), BF),
        pltpu.VMEM((sh.count, VROWS, D), BF),
        pltpu.VMEM((nb, D, TILE), BF),
        pltpu.VMEM((HEADS, 2 * HDIM, TILE), BF),
        pltpu.VMEM((TILE, TILE), F32),
        pltpu.VMEM((HEADS, TILE), F32),
        pltpu.VMEM((HEADS, TILE), F32),
        pltpu.VMEM((D, TILE), F32),
        pltpu.SemaphoreType.DMA((4,)),
        pltpu.SemaphoreType.DMA((2,)),
        pltpu.SemaphoreType.DMA((3, nb)),
    ]
    specs = [SMEM_SPEC] * 2 + [VMEM_SPEC] * len(toks) + [ANY_SPEC] * len(slots)
    return call(
        lambda *refs: self_forward_kernel(sh, *refs),
        "self_forward",
        (lens, order, *toks, *slots),
        specs,
        outs,
        scratch,
        16,
        out_specs=[ANY_SPEC] * 5 + [VMEM_SPEC] * 4,
    )


def cross_tiles(sh, lens, order, mlens, b, bias, bounds, skip_pad, body):
    z = lax.axis_index("seq")
    starts, ends = doc_bounds(lens, order)
    for p in range(DOCS):
        bounds[0, p] = starts[p]
        bounds[1, p] = ends[p]
    base = z * sh.rows + b * TILE
    slots = [order[0, p] for p in range(DOCS)]
    pos = lane_pos(base)
    low = pick(starts, ends, pos, [s * MEM for s in slots])
    high = pick(starts, ends, pos, [s * MEM + mlens[0, s] for s in slots])

    def doc(p, carry):
        slot = order[0, p]
        seen = (bounds[0, p] < base + TILE) & (bounds[1, p] > base)
        if skip_pad:
            seen = seen & (slot != DOCS - 1)
        number = jnp.where(seen, (mlens[0, slot] + TILE - 1) // TILE, 0)

        def step(i, inner):
            t = slot * (MEM // TILE) + i
            k_pos = t * TILE + lax.broadcasted_iota(jnp.int32, (TILE, TILE), 0)
            bias[...] = jnp.where((k_pos >= low) & (k_pos < high), 0.0, NEG)
            body(t)
            return inner

        return lax.fori_loop(0, number, step, carry)

    lax.fori_loop(0, DOCS, doc, 0)


def touched_tile(sh, lens, order, mlens, t, bounds, skip_pad):
    z = lax.axis_index("seq")
    slot = t // (MEM // TILE)
    base = z * sh.rows
    seen = (bounds[2, slot] < base + sh.rows) & (bounds[3, slot] > base)
    seen = seen & (t % (MEM // TILE) * TILE < mlens[0, slot])
    if skip_pad:
        seen = seen & (slot != DOCS - 1)
    return seen


def slot_bounds(lens, order, bounds):
    starts, ends = doc_bounds(lens, order)
    for p in range(DOCS):
        bounds[2, order[0, p]] = starts[p]
        bounds[3, order[0, p]] = ends[p]


def cross_forward_kernel(sh, lens, order, mlens, *refs):
    count, rows, n, split = sh.count, sh.rows, sh.piece, sh.split
    tok, ctx, vec = refs[:3]
    mems = refs[3 : 3 + 2 * split - 1]
    slots = refs[2 + 2 * split : 2 + 2 * split + count]
    outs = refs[2 + 2 * split + count :]
    (n1_out, inv1, *early, mk_out, mv_out, mk_t_out, cctx, cctx_t3, lse) = outs[:11]
    kept = (mk_out, mv_out, mk_t_out)
    (n1, first_low, q_ref, q_t3) = outs[11:15]
    outs = outs[4:]
    (wo, wcq, wck, wcv, mem, mk3, mv3, mk_t3, mv_t3, q_t, bias, m_ref, l_ref, acc) = outs[11:25]
    (bounds, sems, mem_sems, tile_sems, row_sems) = outs[25:]
    for i, w in enumerate((wo, wcq, wck, wcv)):
        start_weight(sh, slots, i * n, n, w, sems.at[i])

    def wanted(t):
        return touched_tile(sh, lens, order, mlens, t, bounds, False)

    slot_bounds(lens, order, bounds)
    start_mems(sh, mems, mem, mem_sems, wanted)
    spread_zero(q_t)
    wait_all(wo, sems.at[0])
    wait_all(wcq, sems.at[1])

    def own_rows(i, carry):
        r = pl.ds(pl.multiple_of(i * TILE, TILE), TILE)
        v = tok[r, :].astype(F32) + (mm(ctx[r, :], wo[...]) + vec[V_SOB : V_SOB + 1, :])
        normal, inv = norm_stats(v)
        n1[r, :] = normal
        inv1[r, :] = inv
        low = (normal * vec[V_G1 : V_G1 + 1, :] + vec[V_S1 : V_S1 + 1, :]).astype(BF)
        first_low[r, :] = low
        q = (mm(low, wcq[...]) + vec[V_CQB : V_CQB + 1, :]).astype(BF)
        q = q * BF(HDIM**-0.5)
        q_ref[r, :] = q
        q_t3[i] = q.T
        return carry

    for i in range(rows // TILE):
        own_rows(i, 0)
    row_copies = send_all((n1, first_low, q_ref, q_t3), (n1_out, *early), row_sems)
    wait_all(wck, sems.at[2])
    wait_all(wcv, sems.at[3])

    def mem_tile(t, carry):
        @pl.when(wanted(t))
        def _():
            wait_mem(mem, t, mem_sems)
            x = mem[t]
            key = mm(x, wck[...]).astype(BF)
            val = (mm(x, wcv[...]) + vec[V_CVB : V_CVB + 1, :]).astype(BF)
            mk3[t] = key
            mv3[t] = val
            mk_t3[t] = key.T
            mv_t3[t] = val.T
            for copy in tile_copies(t, (mk3, mv3, mk_t3), kept, tile_sems):
                copy.start()

        return carry

    lax.fori_loop(0, sh.m_blocks, mem_tile, 0)

    def block(b, carry):
        spread_rows(q_t3.at[b], q_t)
        forward_start(m_ref, l_ref, acc)
        cross_tiles(
            sh,
            lens,
            order,
            mlens,
            b,
            bias,
            bounds,
            False,
            lambda t: forward_tile(mk3.at[t], mv_t3.at[t], bias, q_t, m_ref, l_ref, acc),
        )
        forward_end(b, m_ref, l_ref, acc, cctx, cctx_t3, lse)
        return carry

    lax.fori_loop(0, sh.q_blocks, block, 0)

    def settle(t, carry):
        @pl.when(wanted(t))
        def _():
            for copy in tile_copies(t, (mk3, mv3, mk_t3), kept, tile_sems):
                copy.wait()

        return carry

    lax.fori_loop(0, sh.m_blocks, settle, 0)
    for copy in row_copies:
        copy.wait()


def cross_forward(sh, lens, order, mlens, tok, ctx, vec, mems, slots):
    nm, nq = sh.m_blocks, sh.q_blocks
    outs = [
        shape((sh.rows, D), F32),
        shape((sh.rows, 1), F32),
        shape((sh.rows, D), BF),
        shape((sh.rows, D), BF),
        shape((nq, D, TILE), BF),
        shape((nm, TILE, D), BF),
        shape((nm, TILE, D), BF),
        shape((nm, D, TILE), BF),
        shape((sh.rows, D), BF),
        shape((nq, D, TILE), F32),
        shape((nq, HEADS, TILE), F32),
    ]
    scratch = [
        pltpu.VMEM((sh.rows, D), F32),
        pltpu.VMEM((sh.rows, D), BF),
        pltpu.VMEM((sh.rows, D), BF),
        pltpu.VMEM((nq, D, TILE), BF),
        pltpu.VMEM((D, D), BF),
        pltpu.VMEM((D, D), BF),
        pltpu.VMEM((D, D), BF),
        pltpu.VMEM((D, D), BF),
        pltpu.VMEM((nm, TILE, D), BF),
        pltpu.VMEM((nm, TILE, D), BF),
        pltpu.VMEM((nm, TILE, D), BF),
        pltpu.VMEM((nm, D, TILE), BF),
        pltpu.VMEM((nm, D, TILE), BF),
        pltpu.VMEM((HEADS, 2 * HDIM, TILE), BF),
        pltpu.VMEM((TILE, TILE), F32),
        pltpu.VMEM((HEADS, TILE), F32),
        pltpu.VMEM((HEADS, TILE), F32),
        pltpu.VMEM((D, TILE), F32),
        pltpu.SMEM((4, DOCS), jnp.int32),
        pltpu.SemaphoreType.DMA((4,)),
        pltpu.SemaphoreType.DMA((nm,)),
        pltpu.SemaphoreType.DMA((3, nm)),
        pltpu.SemaphoreType.DMA((4,)),
    ]
    specs = [SMEM_SPEC] * 3 + [VMEM_SPEC] * 3 + [ANY_SPEC] * (len(mems) + len(slots))
    return call(
        lambda *refs: cross_forward_kernel(sh, *refs),
        "cross_forward",
        (lens, order, mlens, tok, ctx, vec, *mems, *slots),
        specs,
        outs,
        scratch,
        21,
        out_specs=[ANY_SPEC, VMEM_SPEC] + [ANY_SPEC] * 6 + [VMEM_SPEC] * 3,
    )


def feed_kernel(sh, lens, order, *refs):
    count, rows, n, wide = sh.count, sh.rows, sh.piece, sh.wide_piece
    n1, cctx, targets, vec = refs[:4]
    slots = refs[4 : 4 + count]
    outs = refs[4 + count :]
    row_outs, vec_grad, grad_outs = outs[:4], outs[4], outs[5:7]
    (final_ref, g_second, g_cc, g_cc_t3, g_send, g_own) = outs[7:13]
    (sec_low, hid, feed_low, g_exp, g_cross) = outs[13:18]
    (wco, w1, w2, n2, dact, loss, stage, stage2, sems, out_sems) = outs[18:]
    z = lax.axis_index("seq")
    start_weight(sh, slots, 4 * n, n, wco, sems.at[0])
    for c in range(FFB):
        start_weight(sh, slots, (5 + c) * n, n, w1.at[c], sems.at[1 + c])
    start_weight(sh, slots, 9 * n, wide, w2, sems.at[5])
    vec_grad[...] = jnp.zeros(vec_grad.shape, F32)
    loss[...] = jnp.zeros(loss.shape, F32)
    starts, ends = doc_bounds(lens, order)
    pad_start, pad_end = jnp.int32(0), jnp.int32(0)
    for p in range(DOCS):
        is_pad = order[0, p] == DOCS - 1
        pad_start = jnp.where(is_pad, starts[p], pad_start)
        pad_end = jnp.where(is_pad, ends[p], pad_end)
    wait_all(wco, sems.at[0])

    def add_vec(row, value):
        vec_grad[row : row + 1, :] = vec_grad[row : row + 1, :] + value

    def chunk(i, carry):
        r = pl.ds(i * rows, rows)
        first = n1[r, :] * vec[V_G1 : V_G1 + 1, :] + vec[V_S1 : V_S1 + 1, :]
        v = first + (mm(cctx[r, :], wco[...]) + vec[V_COB : V_COB + 1, :])
        normal2, inv2 = norm_stats(v)
        n2[...] = normal2
        second = normal2 * vec[V_G2 : V_G2 + 1, :] + vec[V_S2 : V_S2 + 1, :]
        low = second.astype(BF)
        sec_low[r, :] = low
        feed = second + vec[V_CB : V_CB + 1, :]
        wide = range(FFB)

        if i == 0:
            for c in wide:
                wait_all(w1.at[c], sems.at[1 + c])
            wait_all(w2, sems.at[5])
        es = [mm(low, w1[c]) + vec[V_EB + c : V_EB + c + 1, :] for c in wide]
        sgs = [jax.nn.sigmoid(e) for e in es]
        hs = [(e * sg).astype(BF) for e, sg in zip(es, sgs)]
        for c in wide:
            hid[c, r, :] = hs[c]
            dact[c] = sgs[c] * (1.0 + es[c] * (1.0 - sgs[c]))
        for c in wide:
            feed = feed + mm(hs[c], w2[pl.ds(c * D, D), :])
        normal3, inv3 = norm_stats(feed)
        final = normal3 * vec[V_G3 : V_G3 + 1, :] + vec[V_S3 : V_S3 + 1, :]
        final_ref[r, :] = final.astype(BF)
        diff = final - targets[r, :].astype(F32)
        pos = z * rows + i * rows + lax.broadcasted_iota(jnp.int32, (rows, 1), 0)
        live = jnp.where((pos >= pad_start) & (pos < pad_end), 0.0, 1.0)
        g = live * diff
        loss[0:1, :] = loss[0:1, :] + col_sum(g * diff)
        add_vec(V_G3, col_sum(g * normal3))
        add_vec(V_S3, col_sum(g))
        g_third = norm_back(g, normal3, inv3, vec[V_G3 : V_G3 + 1, :])
        g_low = g_third.astype(BF)
        feed_low[r, :] = g_low
        add_vec(V_CB, col_sum(g_low))
        total = g_third
        ges = [(mm_nt(g_low, w2[pl.ds(c * D, D), :]) * dact[c]).astype(BF) for c in wide]
        for c in wide:
            total = total + mm_nt(ges[c], w1[c])
        for c in wide:
            g_exp[c, r, :] = ges[c]
            add_vec(V_EB + c, col_sum(ges[c]))
        normal2 = n2[...]
        add_vec(V_G2, col_sum(total * normal2))
        add_vec(V_S2, col_sum(total))
        gs = norm_back(total, normal2, inv2, vec[V_G2 : V_G2 + 1, :])
        g_second[r, :] = gs
        gc = gs.astype(BF)
        g_cross[r, :] = gc
        add_vec(V_COB, col_sum(gc))
        gcc = mm_nt(gc, wco[...]).astype(BF)
        g_cc[r, :] = gcc
        for b in range(rows // TILE):
            g_cc_t3[b] = gcc[b * TILE : (b + 1) * TILE, :].T
        return carry

    chunk(0, 0)
    live_count = jnp.int32(rows) - jnp.maximum(
        jnp.minimum(pad_end, (z + 1) * rows) - jnp.maximum(pad_start, z * rows), 0
    )
    bits = digit_bits(count * sh.split)
    error_sum = jnp.sum(loss[0:1, :], axis=1, keepdims=True)
    vec_grad[V_LOSS : V_LOSS + 1, :] = digits(error_sum, bits)
    vec_grad[V_LIVE : V_LIVE + 1, :] = digits(jnp.full((1, 1), live_count.astype(F32)), bits)
    copies = send_all((final_ref, g_second, g_cc, g_cc_t3), row_outs, out_sems)

    def send_grad(full, size, row):
        put_grad(sh, full, size, row, g_send, g_own)
        copies.extend(
            send_all(
                [ref.at[:, pl.ds(row, size)] for ref in (g_send, g_own)],
                [ref.at[:, pl.ds(row, size)] for ref in grad_outs],
                out_sems,
                len(copies),
            )
        )

    for c in range(FFB):
        stage2[pl.ds(c * D, D), :] = mm_tn(hid[c], feed_low[...]).astype(BF)
    send_grad(stage2, wide, 5 * n)
    for c in range(FFB):
        stage[...] = mm_tn(sec_low[...], g_exp[c]).astype(BF)
        send_grad(stage, n, (1 + c) * n)
    stage[...] = mm_tn(cctx[...], g_cross[...]).astype(BF)
    send_grad(stage, n, 0)
    for copy in copies:
        copy.wait()


def feed(sh, lens, order, n1, cctx, targets, vec, slots):
    rows, nq = sh.rows, sh.q_blocks
    block = 5 * sh.piece + sh.wide_piece
    outs = [
        shape((rows, D), BF),
        shape((rows, D), F32),
        shape((rows, D), BF),
        shape((nq, D, TILE), BF),
        shape((VROWS, D), F32),
        shape((sh.count // 2, block, D), BF),
        shape((sh.count // 2, block, D), BF),
    ]
    scratch = [
        pltpu.VMEM((rows, D), BF),
        pltpu.VMEM((rows, D), F32),
        pltpu.VMEM((rows, D), BF),
        pltpu.VMEM((nq, D, TILE), BF),
        pltpu.VMEM((sh.count // 2, block, D), BF),
        pltpu.VMEM((sh.count // 2, block, D), BF),
        pltpu.VMEM((rows, D), BF),
        pltpu.VMEM((FFB, rows, D), BF),
        pltpu.VMEM((rows, D), BF),
        pltpu.VMEM((FFB, rows, D), BF),
        pltpu.VMEM((rows, D), BF),
        pltpu.VMEM((D, D), BF),
        pltpu.VMEM((FFB, D, D), BF),
        pltpu.VMEM((FFB * D, D), BF),
        pltpu.VMEM((rows, D), F32),
        pltpu.VMEM((FFB, rows, D), F32),
        pltpu.VMEM((8, D), F32),
        pltpu.VMEM((D, D), BF),
        pltpu.VMEM((FFB * D, D), BF),
        pltpu.SemaphoreType.DMA((6,)),
        pltpu.SemaphoreType.DMA((4 + 2 * (FFB + 2),)),
    ]
    specs = [SMEM_SPEC] * 2 + [VMEM_SPEC] * 4 + [ANY_SPEC] * len(slots)
    return call(
        lambda *refs: feed_kernel(sh, *refs),
        "feed",
        (lens, order, n1, cctx, targets, vec, *slots),
        specs,
        outs,
        scratch,
        17,
        out_specs=[ANY_SPEC] * 4 + [VMEM_SPEC] + [ANY_SPEC] * 2,
    )


def mem_shard(z, slot, high):
    low, mid = z % 2, (z // 2) % 2
    low = low if slot % 2 else 1 - low
    mid = mid if slot >= 2 else 1 - mid
    return 4 * high + 2 * mid + low


def cross_backward_kernel(sh, lens, order, mlens, *refs):
    count, n = sh.count, sh.piece
    (q_ref, q_t3, *kept, cctx_t3, lse, g_cc, g_cc_t3) = refs[:9]
    slots = refs[9 : 9 + count]
    outs = refs[9 + count :]
    part_outs = outs[:4]
    (dq, *low_out) = outs[4:7]
    (wck, wcv, q_t, g_t, q_m, g_m, delta, bias, dk, dv, dq_t) = outs[7:18]
    (mk3, mv3, mk_t3, k_low3, v_low3, bounds, sems, tile_sems, low_sems) = outs[18:27]
    mem_parts, part_sems = outs[27:31], outs[31]
    for i, w in enumerate((wck, wcv)):
        start_weight(sh, slots, (2 + i) * n, n, w, sems.at[i])
    slot_bounds(lens, order, bounds)
    spread_zero(q_t)
    spread_zero(g_t)

    def each_wanted(body):
        def one(t, carry):
            @pl.when(touched_tile(sh, lens, order, mlens, t, bounds, True))
            def _():
                body(t)

            return carry

        lax.fori_loop(0, sh.m_blocks, one, 0)

    def fetch(t):
        for copy in tile_copies(t, kept, (mk3, mv3, mk_t3), tile_sems):
            copy.start()

    def clear(t):
        dk[t] = jnp.zeros((TILE, D), F32)
        dv[t] = jnp.zeros((TILE, D), F32)
        for copy in tile_copies(t, kept, (mk3, mv3, mk_t3), tile_sems):
            copy.wait()

    def low_copies(t):
        return tile_copies(t, (k_low3, v_low3), low_out, low_sems)

    each_wanted(fetch)
    each_wanted(clear)

    def block(b, carry):
        backward_start(b, q_t3, g_cc_t3, q_ref, g_cc, cctx_t3, q_t, g_t, q_m, g_m, delta, dq_t)
        cross_tiles(
            sh,
            lens,
            order,
            mlens,
            b,
            bias,
            bounds,
            True,
            lambda t: backward_tile(
                mk3.at[t],
                mv3.at[t],
                mk_t3.at[t],
                bias,
                q_t,
                g_t,
                q_m,
                g_m,
                lse.at[b],
                delta,
                dk.at[t],
                dv.at[t],
                dq_t,
            ),
        )
        r = pl.ds(pl.multiple_of(b * TILE, TILE), TILE)
        dq[r, :] = (dq_t[...] * HDIM**-0.5).T.astype(BF)
        return carry

    lax.fori_loop(0, sh.q_blocks, block, 0)
    wait_all(wck, sems.at[0])
    wait_all(wcv, sems.at[1])

    z = lax.axis_index("seq")
    tiles_per = sh.mem_rows // TILE

    def mem_tile(i, carry, slot, out):
        shard = mem_shard(z, slot, i // tiles_per)
        t = shard * tiles_per + i % tiles_per
        seen = touched_tile(sh, lens, order, mlens, t, bounds, True)

        @pl.when(seen)
        def _():
            k_low = dk[t].astype(BF)
            v_low = dv[t].astype(BF)
            k_low3[t] = k_low
            v_low3[t] = v_low
            for copy in low_copies(t):
                copy.start()
            out[i] = (mm_nt(k_low, wck[...]) + mm_nt(v_low, wcv[...])).astype(BF)

        @pl.when(jnp.logical_not(seen))
        def _():
            out[i] = jnp.zeros((TILE, D), BF)

        return carry

    copies = []
    for slot, out in enumerate(mem_parts):
        lax.fori_loop(
            0, sh.m_blocks // 4, lambda i, c, slot=slot, out=out: mem_tile(i, c, slot, out), 0
        )
        copies += send_all([out], [part_outs[slot]], part_sems, slot)
    for copy in copies:
        copy.wait()

    def settle(t):
        for copy in low_copies(t):
            copy.wait()

    each_wanted(settle)


def cross_backward(sh, lens, order, mlens, arrays, slots):
    rows, nm = sh.rows, sh.m_blocks
    outs = [shape((nm // 4, TILE, D), BF)] * 4 + [
        shape((rows, D), BF),
        shape((nm, TILE, D), BF),
        shape((nm, TILE, D), BF),
    ]
    scratch = [
        pltpu.VMEM((D, D), BF),
        pltpu.VMEM((D, D), BF),
        pltpu.VMEM((HEADS, 2 * HDIM, TILE), BF),
        pltpu.VMEM((HEADS, 2 * HDIM, TILE), BF),
        pltpu.VMEM((HEADS, TILE, 2 * HDIM), BF),
        pltpu.VMEM((HEADS, TILE, 2 * HDIM), BF),
        pltpu.VMEM((HEADS, TILE), F32),
        pltpu.VMEM((TILE, TILE), F32),
        pltpu.VMEM((nm, TILE, D), F32),
        pltpu.VMEM((nm, TILE, D), F32),
        pltpu.VMEM((D, TILE), F32),
        pltpu.VMEM((nm, TILE, D), BF),
        pltpu.VMEM((nm, TILE, D), BF),
        pltpu.VMEM((nm, D, TILE), BF),
        pltpu.VMEM((nm, TILE, D), BF),
        pltpu.VMEM((nm, TILE, D), BF),
        pltpu.SMEM((4, DOCS), jnp.int32),
        pltpu.SemaphoreType.DMA((2,)),
        pltpu.SemaphoreType.DMA((3, nm)),
        pltpu.SemaphoreType.DMA((2, nm)),
    ]
    scratch += [pltpu.VMEM((nm // 4, TILE, D), BF)] * 4 + [pltpu.SemaphoreType.DMA((4,))]
    specs = [SMEM_SPEC] * 3 + [VMEM_SPEC] * 2 + [ANY_SPEC] * 3 + [VMEM_SPEC] * 4
    specs += [ANY_SPEC] * len(slots)
    return call(
        lambda *refs: cross_backward_kernel(sh, *refs),
        "cross_backward",
        (lens, order, mlens, *arrays, *slots),
        specs,
        outs,
        scratch,
        15,
        out_specs=[ANY_SPEC] * 4 + [VMEM_SPEC] + [ANY_SPEC] * 2,
    )


def first_backward_kernel(sh, lens, order, mlens, *refs):
    count, rows, n = sh.count, sh.rows, sh.piece
    (dq, *low_in, g_second, n1, inv1, first_low, ctx, vec, vec_in) = refs[:10]
    mems = refs[10 : 9 + 2 * sh.split]
    slots = refs[9 + 2 * sh.split : 9 + 2 * sh.split + count]
    outs = refs[9 + 2 * sh.split + count :]
    (g_send, g_own, g_first, g_ctx, g_ctx_t3, vec_grad) = outs[:6]
    (wo, wcq, g_self, acc_k, acc_v, stage, mem, k_low3, v_low3, bounds) = outs[6:16]
    (sems, mem_sems, low_sems) = outs[16:]
    for i, w in enumerate((wo, wcq)):
        start_weight(sh, slots, i * n, n, w, sems.at[i])
    vec_grad[...] = vec_in[...]
    slot_bounds(lens, order, bounds)

    def wanted(t):
        return touched_tile(sh, lens, order, mlens, t, bounds, True)

    def fetch(t, carry):
        @pl.when(wanted(t))
        def _():
            for copy in tile_copies(t, low_in, (k_low3, v_low3), low_sems):
                copy.start()

        return carry

    lax.fori_loop(0, sh.m_blocks, fetch, 0)
    start_mems(sh, mems, mem, mem_sems, wanted)
    wait_all(wo, sems.at[0])
    wait_all(wcq, sems.at[1])

    def add_vec(row, value):
        vec_grad[row : row + 1, :] = vec_grad[row : row + 1, :] + value

    def own_rows(i, carry):
        r = pl.ds(pl.multiple_of(i * TILE, TILE), TILE)
        total = g_second[r, :] + mm_nt(dq[r, :], wcq[...])
        normal = n1[r, :]
        add_vec(V_G1, col_sum(total * normal))
        add_vec(V_S1, col_sum(total))
        gf = norm_back(total, normal, inv1[r, :], vec[V_G1 : V_G1 + 1, :])
        g_first[r, :] = gf
        low = gf.astype(BF)
        g_self[r, :] = low
        add_vec(V_SOB, col_sum(low))
        gc = mm_nt(low, wo[...]).astype(BF)
        g_ctx[r, :] = gc
        g_ctx_t3[i] = gc.T
        return carry

    lax.fori_loop(0, rows // TILE, own_rows, 0)
    acc_k[...] = jnp.zeros(acc_k.shape, F32)
    acc_v[...] = jnp.zeros(acc_v.shape, F32)

    def mem_tile(t, carry):
        @pl.when(wanted(t))
        def _():
            wait_mem(mem, t, mem_sems)
            for copy in tile_copies(t, low_in, (k_low3, v_low3), low_sems):
                copy.wait()
            k_low = k_low3[t]
            v_low = v_low3[t]
            x = mem[t]
            acc_k[...] = acc_k[...] + mm_tn(x, k_low)
            acc_v[...] = acc_v[...] + mm_tn(x, v_low)
            add_vec(V_CVB, col_sum(v_low))

        return carry

    lax.fori_loop(0, sh.m_blocks, mem_tile, 0)

    add_vec(V_CQB, col_sum(dq[...]))
    stage[...] = mm_tn(ctx[...], g_self[...]).astype(BF)
    put_grad(sh, stage, n, 0, g_send, g_own)
    stage[...] = mm_tn(first_low[...], dq[...]).astype(BF)
    put_grad(sh, stage, n, n, g_send, g_own)
    stage[...] = acc_k[...].astype(BF)
    put_grad(sh, stage, n, 2 * n, g_send, g_own)
    stage[...] = acc_v[...].astype(BF)
    put_grad(sh, stage, n, 3 * n, g_send, g_own)


def first_backward(sh, lens, order, mlens, arrays, mems, slots):
    rows, nq, n, nm = sh.rows, sh.q_blocks, sh.piece, sh.m_blocks
    outs = [
        shape((sh.count // 2, 4 * n, D), BF),
        shape((sh.count // 2, 4 * n, D), BF),
        shape((rows, D), F32),
        shape((rows, D), BF),
        shape((nq, D, TILE), BF),
        shape((VROWS, D), F32),
    ]
    scratch = [
        pltpu.VMEM((D, D), BF),
        pltpu.VMEM((D, D), BF),
        pltpu.VMEM((rows, D), BF),
        pltpu.VMEM((D, D), F32),
        pltpu.VMEM((D, D), F32),
        pltpu.VMEM((D, D), BF),
        pltpu.VMEM((nm, TILE, D), BF),
        pltpu.VMEM((nm, TILE, D), BF),
        pltpu.VMEM((nm, TILE, D), BF),
        pltpu.SMEM((4, DOCS), jnp.int32),
        pltpu.SemaphoreType.DMA((2,)),
        pltpu.SemaphoreType.DMA((nm,)),
        pltpu.SemaphoreType.DMA((2, nm)),
    ]
    specs = [SMEM_SPEC] * 3 + [VMEM_SPEC] + [ANY_SPEC] * 2 + [VMEM_SPEC] * 7
    specs += [ANY_SPEC] * (len(mems) + len(slots))
    return call(
        lambda *refs: first_backward_kernel(sh, *refs),
        "first_backward",
        (lens, order, mlens, *arrays, *mems, *slots),
        specs,
        outs,
        scratch,
        6,
    )


def self_backward_kernel(sh, lens, order, *refs):
    count, rows, n, halo = sh.count, sh.rows, sh.piece, sh.halo
    (q_ref, q_t3, k3, v3, k_t3, ctx_t3, lse, g_ctx, g_ctx_t3) = refs[:9]
    slots = refs[9 : 9 + count]
    outs = refs[9 + count :]
    (grad_halo, dq, k_low3, v_low3) = outs[:4]
    (wk, wv, q_t, g_t, q_m, g_m, delta, bias, dk, dv, dq_t, sems) = outs[4:]
    z = lax.axis_index("seq")
    for i, w in enumerate((wk, wv)):
        start_weight(sh, slots, (1 + i) * n, n, w, sems.at[i])
    spread_zero(q_t)
    spread_zero(g_t)

    def clear(t, carry):
        dk[t] = jnp.zeros((TILE, D), F32)
        dv[t] = jnp.zeros((TILE, D), F32)
        return carry

    lax.fori_loop(0, sh.k_blocks, clear, 0)

    def block(b, carry):
        backward_start(b, q_t3, g_ctx_t3, q_ref, g_ctx, ctx_t3, q_t, g_t, q_m, g_m, delta, dq_t)
        self_tiles(
            sh,
            lens,
            order,
            b,
            bias,
            lambda t: backward_tile(
                k3.at[t],
                v3.at[t],
                k_t3.at[t],
                bias,
                q_t,
                g_t,
                q_m,
                g_m,
                lse.at[b],
                delta,
                dk.at[t],
                dv.at[t],
                dq_t,
            ),
        )
        r = pl.ds(pl.multiple_of(b * TILE, TILE), TILE)
        dq[r, :] = (dq_t[...] * HDIM**-0.5).T.astype(BF)
        return carry

    lax.fori_loop(0, sh.q_blocks, block, 0)
    wait_all(wk, sems.at[0])
    wait_all(wv, sems.at[1])
    tiles = rows // TILE

    def lower(t, carry):
        k_low3[t] = dk[t].astype(BF)
        v_low3[t] = dv[t].astype(BF)
        return carry

    lax.fori_loop(0, sh.k_blocks, lower, 0)
    for k in range(halo, 0, -1):

        def window_rows(i, carry, k=k):
            r = pl.ds(pl.multiple_of(i * TILE, TILE), TILE)
            t = (halo - k) * tiles + i
            part = mm_nt(k_low3[t], wk[...]) + mm_nt(v_low3[t], wv[...])
            grad_halo[k - 1, r, :] = part.astype(BF)
            return carry

        @pl.when(z >= k)
        def _(window_rows=window_rows):
            lax.fori_loop(0, tiles, window_rows, 0)

        @pl.when(z < k)
        def _(k=k):
            grad_halo[k - 1] = jnp.zeros((rows, D), BF)


def self_backward(sh, lens, order, arrays, slots):
    rows, nb = sh.rows, sh.k_blocks
    outs = [
        shape((sh.halo, rows, D), BF),
        shape((rows, D), BF),
        shape((nb, TILE, D), BF),
        shape((nb, TILE, D), BF),
    ]
    scratch = [
        pltpu.VMEM((D, D), BF),
        pltpu.VMEM((D, D), BF),
        pltpu.VMEM((HEADS, 2 * HDIM, TILE), BF),
        pltpu.VMEM((HEADS, 2 * HDIM, TILE), BF),
        pltpu.VMEM((HEADS, TILE, 2 * HDIM), BF),
        pltpu.VMEM((HEADS, TILE, 2 * HDIM), BF),
        pltpu.VMEM((HEADS, TILE), F32),
        pltpu.VMEM((TILE, TILE), F32),
        pltpu.VMEM((nb, TILE, D), F32),
        pltpu.VMEM((nb, TILE, D), F32),
        pltpu.VMEM((D, TILE), F32),
        pltpu.SemaphoreType.DMA((2,)),
    ]
    specs = [SMEM_SPEC] * 2 + [VMEM_SPEC] * len(arrays) + [ANY_SPEC] * len(slots)
    return call(
        lambda *refs: self_backward_kernel(sh, *refs),
        "self_backward",
        (lens, order, *arrays, *slots),
        specs,
        outs,
        scratch,
        14,
    )


def self_weights_kernel(sh, *refs):
    count, rows, n, halo = sh.count, sh.rows, sh.piece, sh.halo
    (dq, k_low3, v_low3, g_first, vec_in) = refs[:5]
    toks = refs[5 : 6 + halo]
    slots = refs[6 + halo : 6 + halo + count]
    outs = refs[6 + halo + count :]
    (g_send, g_own, grad_own) = outs[:3]
    (wq, wk, wv, acc_k, acc_v, vec_grad, stage, sems) = outs[3:]
    z = lax.axis_index("seq")
    for i, w in enumerate((wq, wk, wv)):
        start_weight(sh, slots, i * n, n, w, sems.at[i])
    vec_grad[...] = vec_in[...]
    tiles = rows // TILE

    def add_vec(row, value):
        vec_grad[row : row + 1, :] = vec_grad[row : row + 1, :] + value

    acc_k[...] = jnp.zeros(acc_k.shape, F32)
    acc_v[...] = jnp.zeros(acc_v.shape, F32)
    for k in range(halo, -1, -1):

        def window_rows(i, carry, k=k):
            r = pl.ds(pl.multiple_of(i * TILE, TILE), TILE)
            t = (halo - k) * tiles + i
            x = toks[k][r, :]
            acc_k[...] = acc_k[...] + mm_tn(x, k_low3[t])
            acc_v[...] = acc_v[...] + mm_tn(x, v_low3[t])
            add_vec(V_SVB, col_sum(v_low3[t]))
            return carry

        @pl.when(z >= k)
        def _(window_rows=window_rows):
            lax.fori_loop(0, tiles, window_rows, 0)

    add_vec(V_SQB, col_sum(dq[...]))
    stage[...] = mm_tn(toks[0][...], dq[...]).astype(BF)
    put_grad(sh, stage, n, 0, g_send, g_own)
    stage[...] = acc_k[...].astype(BF)
    put_grad(sh, stage, n, n, g_send, g_own)
    stage[...] = acc_v[...].astype(BF)
    put_grad(sh, stage, n, 2 * n, g_send, g_own)
    vec_low = vec_grad[...].astype(BF)
    for s in range(count // 2):
        g_send[s, pl.ds(3 * n, VROWS), :] = vec_low
        g_own[s, pl.ds(3 * n, VROWS), :] = vec_low
    for i, w in enumerate((wq, wk, wv)):
        wait_all(w, sems.at[i])

    def own_rows(i, carry):
        r = pl.ds(pl.multiple_of(i * TILE, TILE), TILE)
        t = halo * tiles + i
        part = mm_nt(k_low3[t], wk[...]) + mm_nt(v_low3[t], wv[...])
        grad_own[r, :] = g_first[r, :] + part + mm_nt(dq[r, :], wq[...])
        return carry

    lax.fori_loop(0, tiles, own_rows, 0)


def self_weights(sh, arrays, toks, slots):
    rows, n = sh.rows, sh.piece
    outs = [
        shape((sh.count // 2, 3 * n + VROWS, D), BF),
        shape((sh.count // 2, 3 * n + VROWS, D), BF),
        shape((rows, D), F32),
    ]
    scratch = [
        pltpu.VMEM((D, D), BF),
        pltpu.VMEM((D, D), BF),
        pltpu.VMEM((D, D), BF),
        pltpu.VMEM((D, D), F32),
        pltpu.VMEM((D, D), F32),
        pltpu.VMEM((VROWS, D), F32),
        pltpu.VMEM((D, D), BF),
        pltpu.SemaphoreType.DMA((3,)),
    ]
    specs = [VMEM_SPEC] * (len(arrays) + len(toks)) + [ANY_SPEC] * len(slots)
    return call(
        lambda *refs: self_weights_kernel(sh, *refs),
        "self_weights",
        (*arrays, *toks, *slots),
        specs,
        outs,
        scratch,
        7,
    )


def shards(
    tokens,
    memory,
    targets,
    doc_lengths,
    doc_order,
    memory_lengths,
    self_query,
    self_query_bias,
    self_key,
    self_value,
    self_value_bias,
    self_output,
    self_output_bias,
    first_gain,
    first_shift,
    cross_query,
    cross_query_bias,
    cross_key,
    cross_value,
    cross_value_bias,
    cross_output,
    cross_output_bias,
    second_gain,
    second_shift,
    expand_weight,
    expand_bias,
    contract_weight,
    contract_bias,
    third_gain,
    third_shift,
):
    split = lax.axis_size("seq")
    count = lax.axis_size("fsdp")
    n = self_query.shape[0]
    wide = contract_weight.shape[0]
    sh = Shard(tokens.shape[0], memory.shape[0], count, split, n, wide)

    own_a, own_b = pack(
        sh,
        (
            self_query_bias,
            self_value_bias,
            self_output_bias,
            first_gain,
            first_shift,
            cross_query_bias,
            cross_value_bias,
            cross_output_bias,
            second_gain,
            second_shift,
            contract_bias,
            third_gain,
            third_shift,
        ),
        expand_bias,
        (
            self_query,
            self_key,
            self_value,
            self_output,
            cross_query,
            cross_key,
            cross_value,
            cross_output,
            expand_weight,
            contract_weight,
        ),
    )
    toks, downs = [tokens, seq_up(tokens, split)], [seq_down(memory, split)]
    swaps = [(i, i ^ 1) for i in range(count)]
    pairs = [step_pairs(count, index) for index in range(len(chip_steps(count)[0]))]
    slots_a, slots_b = [own_a], [own_b]
    own_b_first = [own_b]
    other_b = [lax.ppermute(own_b, "fsdp", swaps)]
    first = [lax.ppermute(own_a, "fsdp", p) for p in pairs]
    hold = (toks[1], downs[0], *first, *other_b)
    for _ in range(1, sh.halo):
        toks.append(seq_up(after(toks[-1], *hold), split))
    ups = [seq_up(after(memory, *hold), split)]
    held_b = after(own_b, *hold)
    second = [lax.ppermute(held_b, "fsdp", p) for p in pairs]
    for index, p in enumerate(pairs):
        slots_a += [first[index]] + [lax.ppermute(after(a, *hold), "fsdp", p) for a in slots_a[1:]]
    hold = (toks[-1], ups[0], *second, *slots_a[3:])
    for index, p in enumerate(pairs):
        slots_b += [second[index]] + [lax.ppermute(after(a, *hold), "fsdp", p) for a in slots_b[1:]]
    slots_a = slots_a + [lax.ppermute(after(a, *hold), "fsdp", swaps) for a in slots_a]
    for k in range(2, split):
        if k == split - 1:
            last = after(memory, *hold)
            ends = lax.ppermute(last, "seq", [(0, split - 1), (split - 1, 0)])
            ups.append(ends)
            downs.append(ends)
        else:
            ups.append(seq_up(after(ups[-1], *hold), split))
            downs.append(seq_down(after(downs[-1], *hold), split))
    mems = [memory]
    for up, down in zip(ups, downs):
        mems += [up, down]

    near = [lax.ppermute(after(a, *hold), "fsdp", swaps) for a in second]
    first_tok = after(tokens, *hold, *near)
    (q, q_t3, k3, v3, k_t3, ctx, ctx_t3, lse, vec) = self_forward(
        sh, doc_lengths, doc_order, [first_tok] + toks[1:], slots_a
    )
    swapped = {id(a): b for a, b in zip(own_b_first + second, other_b + near)}
    late = (ctx, *ups, *downs)
    slots_b = slots_b + [
        swapped[id(a)] if id(a) in swapped else lax.ppermute(after(a, *late), "fsdp", swaps)
        for a in slots_b
    ]
    (n1, inv1, first_low, cq, cq_t3, mk3, mv3, mk_t3, cctx, cctx_t3, clse) = cross_forward(
        sh, doc_lengths, doc_order, memory_lengths, tokens, ctx, vec, mems, slots_b
    )
    feed_out = feed(sh, doc_lengths, doc_order, n1, cctx, targets, vec, slots_b)
    (final_low, g_second, g_cc, g_cc_t3, vec_grad, send_c, own_c) = feed_out
    sum_c = Reduction(send_c, own_c, count, split)
    sum_c.step()
    cq = after(cq, sum_c.send)
    sum_c.step()
    *mem_parts, dcq, k_low3, v_low3 = cross_backward(
        sh,
        doc_lengths,
        doc_order,
        memory_lengths,
        (cq, cq_t3, mk3, mv3, mk_t3, cctx_t3, clse, g_cc, g_cc_t3),
        slots_b,
    )
    dcq = after(dcq, sum_c.send)
    sum_c.step(dcq)
    swap = [(i, i ^ 1) for i in range(split)]
    mem_got = lax.ppermute(mem_parts[0], "seq", swap)
    (send_b, own_b, g_first, g_ctx, g_ctx_t3, vec_grad) = first_backward(
        sh,
        doc_lengths,
        doc_order,
        memory_lengths,
        (dcq, k_low3, v_low3, g_second, n1, inv1, first_low, ctx, vec, vec_grad),
        mems,
        slots_b,
    )
    mem_away = add_low(after(mem_parts[1], g_first), mem_got)
    sum_b = Reduction(send_b, own_b, count, split)
    g_ctx = after(g_ctx, sum_c.send, mem_away)
    sum_c.step(g_ctx)
    sum_b.step(g_ctx)
    mem_got = lax.ppermute(after(mem_parts[2], g_ctx), "seq", swap)
    mem_far = lax.ppermute(after(mem_away, g_ctx), "seq", [(i, i ^ 2) for i in range(split)])
    (grad_halo, dq, sk_low3, sv_low3) = self_backward(
        sh,
        doc_lengths,
        doc_order,
        (q, q_t3, k3, v3, k_t3, ctx_t3, lse, g_ctx, g_ctx_t3),
        slots_a,
    )
    dq = after(dq, mem_got, mem_far, sum_c.send, sum_b.send)
    back = seq_down(after(grad_halo[sh.halo - 1], dq), split)
    sum_b.step(dq)
    sum_c.step(dq)
    (send_a, own_a, grad_own) = self_weights(
        sh,
        (dq, sk_low3, sv_low3, g_first, vec_grad),
        toks,
        slots_a,
    )
    send_a = after(send_a, sum_b.send, sum_c.send)
    sum_a = Reduction(send_a, own_a, count, split)
    sum_a.step()
    sum_b.step(send_a)
    sum_c.step(send_a)
    for k in range(sh.halo - 1, 0, -1):
        back = seq_down(after(add_low(grad_halo[k - 1], back), send_a), split)
    sum_a.step()
    ready, held = sum_a.send, (sum_b.send, sum_c.send)
    while [a for a, _ in sum_a.plan].count("fsdp"):
        sum_a.step()
    sum_b.step(ready)
    ready = sum_a.send
    sum_a.step(back, *held)
    sum_b.step(ready)
    input_grad = grad_own + back.astype(F32)
    mem_last = after(mem_parts[3], sum_a.send)
    mem_here = mem_last.astype(F32) + mem_got.astype(F32) + mem_far.astype(F32)
    memory_grad = seq_rest(mem_here.reshape(split // 4, sh.mem_rows, D), split)[0]
    sum_a.finish()
    red_b, red_c = sum_b.finish(), sum_c.finish()

    def rows_of(array, start, size):
        return array[start : start + size].astype(F32)

    done = finish(sh, sum_a.parts[0], sum_a.got, expand_bias.shape[0])
    small_grad = done[3 : 3 + V_EB]
    expand_bias_grad = done[3 + V_EB]
    loss_value = done[4 + V_EB].reshape(())
    expand_grad = jnp.concatenate(
        [rows_of(red_c, (1 + c) * n, n) for c in range(FFB)], axis=1
    )
    return (
        final_low,
        loss_value,
        input_grad,
        memory_grad,
        done[0],
        small_grad[V_SQB],
        done[1],
        done[2],
        small_grad[V_SVB],
        rows_of(red_b, 0, n),
        small_grad[V_SOB],
        small_grad[V_G1],
        small_grad[V_S1],
        rows_of(red_b, n, n),
        small_grad[V_CQB],
        rows_of(red_b, 2 * n, n),
        rows_of(red_b, 3 * n, n),
        small_grad[V_CVB],
        rows_of(red_c, 0, n),
        small_grad[V_COB],
        small_grad[V_G2],
        small_grad[V_S2],
        expand_grad,
        expand_bias_grad,
        rows_of(red_c, 5 * n, wide),
        small_grad[V_CB],
        small_grad[V_G3],
        small_grad[V_S3],
    )


def solution(mesh):
    rows = P(("fsdp", "seq"), None)
    matrix = P("fsdp", None)
    vector = P("fsdp")
    kinds = (
        "mvmmvmvvvmvmmvmvvvmvmvvv"
    )
    weights = tuple(matrix if kind == "m" else vector for kind in kinds)
    return jax.shard_map(
        shards,
        mesh=mesh,
        in_specs=(rows, rows, rows, matrix, matrix, matrix) + weights,
        out_specs=(rows, P(), rows, rows) + weights,
        check_vma=False,
    )
```

```python
import jax
import jax.numpy as jnp
from jax import lax
from jax.experimental import pallas as pl
from jax.experimental.pallas import tpu as pltpu
from jax.sharding import PartitionSpec as P

D = 512
HDIM = 64
HEADS = D // HDIM
DOCS = 4
MEM = 512
FFB = 4
TILE = 256
GROUP = 4
VROWS = 32
NEG = -1e30
BF = jnp.bfloat16
F32 = jnp.float32
VMEM_BYTES = 60 * 1024 * 1024
FLOPS_RATE = 3e13

(
    V_SQB,
    V_SVB,
    V_SOB,
    V_G1,
    V_S1,
    V_CQB,
    V_CVB,
    V_COB,
    V_G2,
    V_S2,
    V_CB,
    V_G3,
    V_S3,
    V_EB,
) = range(14)
V_LOSS = V_EB + FFB
V_LIVE = V_LOSS + 1
LOW_BITS = 36
HIGH_BITS = 36


def mm(a, b):
    return jnp.dot(a, b, preferred_element_type=F32)


def mm_nt(a, b):
    return lax.dot_general(a, b, (((1,), (1,)), ((), ())), preferred_element_type=F32)


def mm_tn(a, b):
    return lax.dot_general(a, b, (((0,), (0,)), ((), ())), preferred_element_type=F32)


def col_sum(v):
    return jnp.sum(v.astype(F32), axis=0, keepdims=True)


def chip_steps(count):
    bits = []
    bit = 2
    while bit < count:
        bits.append(bit)
        bit *= 2
    return bits, bits[::-1]


def gather_masks(count):
    result = []
    for steps in chip_steps(count):
        masks = [0]
        for step in steps:
            masks = masks + [m ^ step for m in masks]
        result.append(masks)
    own0, own1 = result
    return [own0 + [m ^ 1 for m in own1], own1 + [m ^ 1 for m in own0]]


def reduce_masks(count):
    result = []
    for steps in chip_steps(count):
        masks = [0]
        for step in steps[::-1]:
            masks = masks + [m ^ step for m in masks]
        result.append(masks)
    return result


def step_pairs(count, index):
    orders = chip_steps(count)
    return [(i, i ^ orders[i & 1][index]) for i in range(count)]


def fsdp_gather_parts(own, count):
    have = [own]
    for index in range(len(chip_steps(count)[0])):
        pairs = step_pairs(count, index)
        have = have + [lax.ppermute(a, "fsdp", pairs) for a in have]
    return have, [(i, i ^ 1) for i in range(count)]


def fsdp_gather(own, count):
    have, swap = fsdp_gather_parts(own, count)
    return have + [lax.ppermute(a, "fsdp", swap) for a in have]


def add_low(a, b):
    return (a.astype(F32) + b.astype(F32)).astype(BF)


def after(value, *others):
    return lax.optimization_barrier((value, *others))[0]


def sum_low(parts):
    total = parts[0].astype(F32)
    for part in parts[1:]:
        total = total + part.astype(F32)
    return total.astype(BF)


class Reduction:
    def __init__(self, send, own, count, split):
        self.send, self.parts = send, [own]
        self.odd = (lax.axis_index("seq") % 2) == 1
        self.got = None
        self.plan = [("fsdp", [(i, i ^ 1) for i in range(count)])]
        for index in range(len(chip_steps(count)[0])):
            self.plan.append(("fsdp", step_pairs(count, index)))
        bits = [1 << k for k in range(split.bit_length() - 1)]
        for bit in bits + [1]:
            self.plan.append(("seq", [(i, i ^ bit) for i in range(split)]))

    def start(self, *others):
        send = after(self.send, *others) if others else self.send
        self.axis, pairs = self.plan.pop(0)
        self.got = lax.ppermute(send, self.axis, pairs)

    def end(self, *others):
        if others:
            self.parts[0] = after(self.parts[0], *others)
        left = sum(1 for axis, _ in self.plan if axis == "fsdp")
        if self.axis == "fsdp":
            self.parts.append(self.got)
            if left > 0:
                half = self.got.shape[0] // 2
                self.send = sum_low([part[half:] for part in self.parts])
                self.parts = [part[:half] for part in self.parts]
            else:
                total = sum_low([part[0] for part in self.parts])
                half = total.shape[0] // 2
                self.send = jnp.where(self.odd, total[:half], total[half:])
                self.parts = [jnp.where(self.odd, total[half:], total[:half])]
        elif self.plan:
            self.send = sum_low([self.parts[0], self.got])
            self.parts = [self.send]
        else:
            mine, got = self.parts[0], self.got
            self.send = jnp.where(
                self.odd, jnp.concatenate([got, mine]), jnp.concatenate([mine, got])
            )

    def step(self, *others):
        self.start(*others)
        self.end()

    def finish(self):
        while self.plan:
            self.step()
        return self.send


def seq_rest(parts, split):
    z = lax.axis_index("seq")
    bit = 4
    while bit < split:
        pairs = parts.reshape(parts.shape[0] // 2, 2, *parts.shape[1:])
        odd = (z // bit) % 2 == 1
        got = lax.ppermute(
            jnp.where(odd, pairs[:, 0], pairs[:, 1]), "seq", [(i, i ^ bit) for i in range(split)]
        )
        parts = jnp.where(odd, pairs[:, 1], pairs[:, 0]) + got
        bit *= 2
    return parts


def seq_up(a, count):
    return lax.ppermute(a, "seq", [(i, i + 1) for i in range(count - 1)])


def seq_down(a, count):
    return lax.ppermute(a, "seq", [(i + 1, i) for i in range(count - 1)])


def slot_place(index, masks, slot):
    return jnp.where(index % 2 == 0, index ^ masks[0][slot], index ^ masks[1][slot])


class Shard:
    def __init__(self, rows, mem_rows, count, split, piece, wide_piece):
        self.rows = rows
        self.mem_rows = mem_rows
        self.count = count
        self.split = split
        self.piece = piece
        self.wide_piece = wide_piece
        self.group_rows = rows * split
        self.group_mem = mem_rows * split
        self.halo = min(-(-(self.group_rows // 2 - 1) // rows), split - 1)
        self.window = rows * (self.halo + 1)
        self.q_blocks = rows // TILE
        self.k_blocks = self.window // TILE
        self.m_blocks = self.group_mem // TILE
        self.gather = gather_masks(count)
        self.reduce = reduce_masks(count)


def start_weight(sh, slots, row, n, target, sem):
    index = lax.axis_index("fsdp")
    for s, slot in enumerate(slots):
        place = pl.multiple_of(slot_place(index, sh.gather, s) * n, n)
        pltpu.make_async_copy(slot.at[pl.ds(row, n)], target.at[pl.ds(place, n)], sem).start()


def wait_all(target, sem):
    pltpu.make_async_copy(target, target, sem).wait()


def send_all(sources, targets, sems, first=0):
    copies = [
        pltpu.make_async_copy(source, target, sems.at[first + i])
        for i, (source, target) in enumerate(zip(sources, targets))
    ]
    for copy in copies:
        copy.start()
    return copies


def tile_copies(t, sources, targets, sems):
    return [
        pltpu.make_async_copy(source.at[t], target.at[t], sems.at[i, t])
        for i, (source, target) in enumerate(zip(sources, targets))
    ]


def start_mems(sh, mems, target, sems, wanted):
    z = lax.axis_index("seq")
    tiles_per = sh.mem_rows // TILE

    def place(source, shard):
        for i in range(tiles_per):
            t = shard * tiles_per + i

            @pl.when(wanted(t))
            def _(i=i, t=t):
                pltpu.make_async_copy(
                    source.at[pl.ds(i * TILE, TILE)], target.at[t], sems.at[t]
                ).start()

    place(mems[0], z)
    for k in range(1, sh.split):
        up, down = mems[2 * k - 1], mems[2 * k]

        @pl.when(z >= k)
        def _(up=up, k=k):
            place(up, z - k)

        @pl.when(z + k < sh.split)
        def _(down=down, k=k):
            place(down, z + k)


def wait_mem(target, t, sems):
    pltpu.make_async_copy(target.at[t], target.at[t], sems.at[t]).wait()


def put_grad(sh, full, n, row, send_ref, own_ref):
    index = lax.axis_index("fsdp")
    partner = index ^ 1
    for s in range(sh.count // 2):
        mine = pl.multiple_of(slot_place(index, sh.reduce, s) * n, n)
        theirs = pl.multiple_of(slot_place(partner, sh.reduce, s) * n, n)
        own_ref[s, pl.ds(row, n), :] = full[pl.ds(mine, n), :]
        send_ref[s, pl.ds(row, n), :] = full[pl.ds(theirs, n), :]


def doc_bounds(lens, order):
    starts, ends = [], []
    total = jnp.int32(0)
    for p in range(DOCS):
        starts.append(total)
        total = total + lens[0, order[0, p]]
        ends.append(total)
    return starts, ends


def pick(starts, ends, pos, values):
    out = jnp.zeros_like(pos)
    for p in range(DOCS):
        out = jnp.where((pos >= starts[p]) & (pos < ends[p]), values[p], out)
    return out


def lane_pos(base):
    return base + lax.broadcasted_iota(jnp.int32, (1, TILE), 1)


def norm_stats(v):
    mean = jnp.mean(v, axis=1, keepdims=True)
    c = v - mean
    inv = lax.rsqrt(jnp.mean(c * c, axis=1, keepdims=True) + 1e-05)
    return c * inv, inv


def norm_back(dy, n, inv, gain):
    e = dy * gain
    return inv * (
        e - jnp.mean(e, axis=1, keepdims=True) - n * jnp.mean(e * n, axis=1, keepdims=True)
    )


def head_rows(h):
    return slice(h * HDIM, (h + 1) * HDIM)


def pair_lanes(h):
    j = h // 2
    return slice(j * 2 * HDIM, (j + 1) * 2 * HDIM)


def spread_rows(source, target):
    for h in range(HEADS):
        o = (h % 2) * HDIM
        target[h, pl.ds(o, HDIM), :] = source[head_rows(h), :]


def spread_zero(target):
    for h in range(HEADS):
        o = (1 - h % 2) * HDIM
        target[h, pl.ds(o, HDIM), :] = jnp.zeros((HDIM, TILE), BF)


def spread_lanes(source, target):
    lane = lax.broadcasted_iota(jnp.int32, (TILE, 2 * HDIM), 1)
    for h in range(HEADS):
        part = source[:, pair_lanes(h)]
        keep = (lane >= HDIM) if h % 2 else (lane < HDIM)
        target[h] = jnp.where(keep, part, jnp.zeros_like(part))


def forward_tile(keys, vals_t, bias, q_t, m_ref, l_ref, acc_ref):
    heads = range(HEADS)
    mask = bias[...]
    m_old, l_old = m_ref[...], l_ref[...]
    scores = [mm(keys[:, pair_lanes(h)], q_t[h]) + mask for h in heads]
    tops = [
        jnp.maximum(m_old[h : h + 1], jnp.max(scores[h], axis=0, keepdims=True)) for h in heads
    ]
    probs = [jnp.exp(scores[h] - tops[h]) for h in heads]
    alphas = [jnp.exp(m_old[h : h + 1] - tops[h]) for h in heads]
    sums = [
        alphas[h] * l_old[h : h + 1] + jnp.sum(probs[h], axis=0, keepdims=True) for h in heads
    ]
    outs = [mm(vals_t[head_rows(h), :], probs[h].astype(BF)) for h in heads]
    for h in heads:
        acc_ref[head_rows(h), :] = acc_ref[head_rows(h), :] * alphas[h] + outs[h]
    m_ref[...] = jnp.concatenate(tops, axis=0)
    l_ref[...] = jnp.concatenate(sums, axis=0)


def forward_start(m_ref, l_ref, acc_ref):
    m_ref[...] = jnp.full(m_ref.shape, NEG, F32)
    l_ref[...] = jnp.zeros(l_ref.shape, F32)
    acc_ref[...] = jnp.zeros(acc_ref.shape, F32)


def forward_end(b, m_ref, l_ref, acc_ref, ctx_ref, ctx_t_ref, lse_ref):
    lse_ref[b] = m_ref[...] + jnp.log(l_ref[...])
    for h in range(HEADS):
        acc_ref[head_rows(h), :] = acc_ref[head_rows(h), :] / l_ref[h : h + 1, :]
    ctx_t_ref[b] = acc_ref[...]
    ctx_ref[pl.ds(pl.multiple_of(b * TILE, TILE), TILE), :] = acc_ref[...].T.astype(BF)


def backward_tile(keys, vals, keys_t, bias, q_t, g_t, q_m, g_m, lse, delta, dk, dv, dq_t):
    mask = bias[...]
    for first in range(0, HEADS, GROUP):
        heads = range(first, first + GROUP)
        scores = [mm(keys[:, pair_lanes(h)], q_t[h]) for h in heads]
        probs = [jnp.exp(s + mask - lse[h : h + 1, :]) for h, s in zip(heads, scores)]
        dvs = [mm(p.astype(BF), g_m[h]) for h, p in zip(heads, probs)]
        dps = [mm(vals[:, pair_lanes(h)], g_t[h]) for h in heads]
        dss = [
            (p * (dp - delta[h : h + 1, :])).astype(BF) for h, p, dp in zip(heads, probs, dps)
        ]
        dks = [mm(ds, q_m[h]) for h, ds in zip(heads, dss)]
        dqs = [mm(keys_t[head_rows(h), :], ds) for h, ds in zip(heads, dss)]
        for i in range(0, GROUP, 2):
            lanes = pair_lanes(first + i)
            dv[:, lanes] = dv[:, lanes] + dvs[i] + dvs[i + 1]
            dk[:, lanes] = dk[:, lanes] + dks[i] + dks[i + 1]
        for h, dq in zip(heads, dqs):
            dq_t[head_rows(h), :] = dq_t[head_rows(h), :] + dq


def backward_start(b, q_t3, g_t3, q, g, ctx_t3, q_t, g_t, q_m, g_m, delta, dq_t):
    rows = pl.ds(pl.multiple_of(b * TILE, TILE), TILE)
    spread_rows(q_t3.at[b], q_t)
    spread_rows(g_t3.at[b], g_t)
    spread_lanes(q[rows, :], q_m)
    spread_lanes(g[rows, :], g_m)
    prod = g_t3[b].astype(F32) * ctx_t3[b]
    for h in range(HEADS):
        delta[h : h + 1, :] = jnp.sum(prod[head_rows(h), :], axis=0, keepdims=True)
    dq_t[...] = jnp.zeros(dq_t.shape, F32)


def self_tiles(sh, lens, order, b, bias, body):
    z = lax.axis_index("seq")
    starts, ends = doc_bounds(lens, order)
    shift = (z - sh.halo) * sh.rows
    q_base = sh.halo * sh.rows + b * TILE
    first = pick(starts, ends, q_base + shift, starts) - shift
    q_pos = lane_pos(q_base)
    q_start = pick(starts, ends, q_pos + shift, starts) - shift
    last = q_base // TILE
    number = last - first // TILE + 1

    def step(i, carry):
        t = last - i
        k_pos = t * TILE + lax.broadcasted_iota(jnp.int32, (TILE, TILE), 0)
        bias[...] = jnp.where((k_pos >= q_start) & (k_pos <= q_pos), 0.0, NEG)
        body(t)
        return carry

    lax.fori_loop(0, number, step, 0)


def self_forward_kernel(sh, lens, order, *refs):
    halo, count, rows, n = sh.halo, sh.count, sh.rows, sh.piece
    toks = refs[: halo + 1]
    slots = refs[halo + 1 : halo + 1 + count]
    (*kept, ctx, ctx_t3, lse, vec) = refs[halo + 1 + count : halo + 10 + count]
    outs = refs[halo + 10 + count :]
    (q_ref, q_t3, k3, v3, k_t3, wq, wk, wv, vec_slots, v_t3, q_t, bias) = outs[:12]
    (m_ref, l_ref, acc, sems, q_sems, tile_sems) = outs[12:]
    z = lax.axis_index("seq")
    for s, slot in enumerate(slots):
        pltpu.make_async_copy(slot.at[pl.ds(3 * n, VROWS)], vec_slots.at[s], sems.at[3]).start()
    for i, w in enumerate((wq, wk, wv)):
        start_weight(sh, slots, i * n, n, w, sems.at[i])
    spread_zero(q_t)
    wait_all(vec_slots, sems.at[3])
    vec[...] = jnp.sum(vec_slots[...].astype(F32), axis=0)
    wait_all(wq, sems.at[0])
    tiles = rows // TILE

    q = (mm(toks[0][...], wq[...]) + vec[V_SQB : V_SQB + 1, :]).astype(BF)
    q = q * BF(HDIM**-0.5)
    q_ref[...] = q
    for i in range(tiles):
        q_t3[i] = q[i * TILE : (i + 1) * TILE, :].T
    q_copies = send_all((q_ref, q_t3), kept[:2], q_sems)
    wait_all(wk, sems.at[1])
    wait_all(wv, sems.at[2])

    def window_copies(t):
        return tile_copies(t, (k3, v3, k_t3), kept[2:], tile_sems)

    for k in range(halo + 1):

        @pl.when(z >= k)
        def _(k=k):
            x = toks[k][...]
            keys = mm(x, wk[...]).astype(BF)
            vals = (mm(x, wv[...]) + vec[V_SVB : V_SVB + 1, :]).astype(BF)
            for i in range(tiles):
                t = (halo - k) * tiles + i
                key = keys[i * TILE : (i + 1) * TILE, :]
                val = vals[i * TILE : (i + 1) * TILE, :]
                k3[t] = key
                v3[t] = val
                k_t3[t] = key.T
                v_t3[t] = val.T
                for copy in window_copies(t):
                    copy.start()

    def block(b, carry):
        spread_rows(q_t3.at[b], q_t)
        forward_start(m_ref, l_ref, acc)
        self_tiles(
            sh,
            lens,
            order,
            b,
            bias,
            lambda t: forward_tile(k3.at[t], v_t3.at[t], bias, q_t, m_ref, l_ref, acc),
        )
        forward_end(b, m_ref, l_ref, acc, ctx, ctx_t3, lse)
        return carry

    lax.fori_loop(0, sh.q_blocks, block, 0)
    for copy in q_copies:
        copy.wait()
    for k in range(halo + 1):

        @pl.when(z >= k)
        def _(k=k):
            for i in range(tiles):
                for copy in window_copies((halo - k) * tiles + i):
                    copy.wait()


SMEM_SPEC = pl.BlockSpec(memory_space=pltpu.SMEM)
VMEM_SPEC = pl.BlockSpec(memory_space=pltpu.VMEM)
ANY_SPEC = pl.BlockSpec(memory_space=pl.ANY)


def shape(dims, dtype):
    return jax.ShapeDtypeStruct(dims, dtype)


def call(body, name, inputs, specs, outs, scratch, micros, vmem=VMEM_BYTES, out_specs=None):
    moved = sum(a.size * a.dtype.itemsize for a in (*inputs, *outs))
    cost = pl.CostEstimate(
        flops=int(micros * 1e-6 * FLOPS_RATE), transcendentals=0, bytes_accessed=moved // 50
    )
    return pl.pallas_call(
        body,
        name=name,
        in_specs=specs,
        out_specs=out_specs or [VMEM_SPEC] * len(outs),
        out_shape=outs,
        scratch_shapes=scratch,
        cost_estimate=cost,
        compiler_params=pltpu.CompilerParams(vmem_limit_bytes=vmem),
    )(*inputs)


def pack_kernel(sh, *refs):
    small = refs[:V_EB]
    wide_bias = refs[V_EB]
    mats = refs[V_EB + 1 : V_EB + 11]
    own_a, own_b = refs[V_EB + 11 :]
    n, wide = sh.piece, sh.wide_piece
    (sq, sk, sv, so, cq, ck, cv, co, w1, w2) = mats
    for i, m in enumerate((sq, sk, sv)):
        own_a[pl.ds(i * n, n), :] = m[...]
    for i, m in enumerate((so, cq, ck, cv, co)):
        own_b[pl.ds(i * n, n), :] = m[...]
    for c in range(FFB):
        own_b[pl.ds((5 + c) * n, n), :] = w1[:, c * D : (c + 1) * D]
    own_b[pl.ds(9 * n, wide), :] = w2[...]
    index = lax.axis_index("fsdp")

    def spread(piece, size, offset):
        hot = lax.broadcasted_iota(jnp.int32, (size, D), 1) == offset + lax.broadcasted_iota(
            jnp.int32, (size, D), 0
        )
        return mm(piece, hot.astype(BF)).astype(BF)

    rows = jnp.concatenate([r[...].reshape(1, n) for r in small], axis=0)
    size = wide_bias.shape[0]
    flat = index * size
    line = spread(wide_bias[...].reshape(1, size), size, flat % D)
    row = lax.broadcasted_iota(jnp.int32, (FFB, D), 0)
    own_a[pl.ds(3 * n, VROWS), :] = jnp.concatenate(
        [
            spread(rows, n, index * n),
            jnp.where(row == flat // D, line, jnp.zeros((FFB, D), BF)),
            jnp.zeros((VROWS - V_EB - FFB, D), BF),
        ],
        axis=0,
    )


def pack(sh, small, wide_bias, mats):
    n, wide = sh.piece, sh.wide_piece
    outs = [shape((3 * n + VROWS, D), BF), shape((9 * n + wide, D), BF)]
    return call(
        lambda *refs: pack_kernel(sh, *refs),
        "pack",
        (*small, wide_bias, *mats),
        [VMEM_SPEC] * (V_EB + 1 + len(mats)),
        outs,
        [],
        2,
    )


def digit_bits(devices):
    return 3 if 7 * devices <= 256 else 1


def digits(value, bits):
    lane = lax.broadcasted_iota(jnp.int32, (1, D), 1)
    scale = jnp.full((1, D), 2.0**LOW_BITS, F32)
    for i in range(9):
        scale = scale * jnp.where((lane // 2**i) % 2 == 1, 2.0 ** -min(bits * 2**i, 140), 1.0)
    whole = jnp.floor(value * scale)
    return whole - 2.0**bits * jnp.floor(value * scale * 2.0**-bits)


def undigits(row, bits):
    lane = lax.broadcasted_iota(jnp.int32, (1, D), 1)
    scale = jnp.full((1, D), 2.0**-LOW_BITS, F32)
    for i in range(7):
        scale = scale * jnp.where(
            (lane // 2**i) % 2 == 1, 2.0 ** min(bits * 2**i, LOW_BITS + HIGH_BITS), 1.0
        )
    used = lane < (LOW_BITS + HIGH_BITS) // bits
    return jnp.sum(jnp.where(used, row * jnp.where(used, scale, 0.0), 0.0), axis=1, keepdims=True)


def finish_kernel(sh, mine, got, *outs):
    n = sh.piece
    mats, small, wide_bias, loss = outs[:3], outs[3 : 3 + V_EB], outs[3 + V_EB], outs[4 + V_EB]
    red = outs[5 + V_EB]
    odd = lax.axis_index("seq") % 2 == 1
    half = mine.shape[0]
    red[pl.ds(0, half), :] = jnp.where(odd, got[...], mine[...])
    red[pl.ds(half, half), :] = jnp.where(odd, mine[...], got[...])
    for i, m in enumerate(mats):
        m[...] = red[pl.ds(i * n, n), :].astype(F32)
    index = lax.axis_index("fsdp")
    vec = red[pl.ds(3 * n, VROWS), :]

    def cut(rows, size, offset):
        hot = lax.broadcasted_iota(jnp.int32, (D, size), 0) == offset + lax.broadcasted_iota(
            jnp.int32, (D, size), 1
        )
        return mm(rows, hot.astype(BF))

    parts = cut(vec, n, index * n)
    for i in range(V_EB):
        small[i][...] = parts[i : i + 1, :].reshape(n)
    size = wide_bias.shape[0]
    flat = index * size
    row = lax.broadcasted_iota(jnp.int32, (VROWS, D), 0)
    lines = jnp.where(row == V_EB + flat // D, vec.astype(F32), 0.0).astype(BF)
    wide_bias[...] = jnp.sum(cut(lines, size, flat % D), axis=0, keepdims=True).reshape(size)
    bits = digit_bits(sh.count * sh.split)
    error_sum = undigits(vec[V_LOSS : V_LOSS + 1, :].astype(F32), bits)
    live = undigits(vec[V_LIVE : V_LIVE + 1, :].astype(F32), bits)
    loss[...] = error_sum / (live * D)


def finish(sh, mine, got, bias_size):
    n = sh.piece
    outs = [shape((n, D), F32)] * 3 + [shape((n,), F32)] * V_EB
    outs += [shape((bias_size,), F32), shape((1, 1), F32)]
    return call(
        lambda *refs: finish_kernel(sh, *refs),
        "finish",
        (mine, got),
        [VMEM_SPEC] * 2,
        outs,
        [pltpu.VMEM((3 * n + VROWS, D), BF)],
        2,
    )


def self_forward(sh, lens, order, toks, slots):
    nb, nq = sh.k_blocks, sh.q_blocks
    outs = [
        shape((sh.rows, D), BF),
        shape((nq, D, TILE), BF),
        shape((nb, TILE, D), BF),
        shape((nb, TILE, D), BF),
        shape((nb, D, TILE), BF),
        shape((sh.rows, D), BF),
        shape((nq, D, TILE), F32),
        shape((nq, HEADS, TILE), F32),
        shape((VROWS, D), F32),
    ]
    scratch = [
        pltpu.VMEM((sh.rows, D), BF),
        pltpu.VMEM((nq, D, TILE), BF),
        pltpu.VMEM((nb, TILE, D), BF),
        pltpu.VMEM((nb, TILE, D), BF),
        pltpu.VMEM((nb, D, TILE), BF),
        pltpu.VMEM((D, D), BF),
        pltpu.VMEM((D, D), BF),
        pltpu.VMEM((D, D), BF),
        pltpu.VMEM((sh.count, VROWS, D), BF),
        pltpu.VMEM((nb, D, TILE), BF),
        pltpu.VMEM((HEADS, 2 * HDIM, TILE), BF),
        pltpu.VMEM((TILE, TILE), F32),
        pltpu.VMEM((HEADS, TILE), F32),
        pltpu.VMEM((HEADS, TILE), F32),
        pltpu.VMEM((D, TILE), F32),
        pltpu.SemaphoreType.DMA((4,)),
        pltpu.SemaphoreType.DMA((2,)),
        pltpu.SemaphoreType.DMA((3, nb)),
    ]
    specs = [SMEM_SPEC] * 2 + [VMEM_SPEC] * len(toks) + [ANY_SPEC] * len(slots)
    return call(
        lambda *refs: self_forward_kernel(sh, *refs),
        "self_forward",
        (lens, order, *toks, *slots),
        specs,
        outs,
        scratch,
        16,
        out_specs=[ANY_SPEC] * 5 + [VMEM_SPEC] * 4,
    )


def cross_tiles(sh, lens, order, mlens, b, bias, bounds, skip_pad, body):
    z = lax.axis_index("seq")
    starts, ends = doc_bounds(lens, order)
    for p in range(DOCS):
        bounds[0, p] = starts[p]
        bounds[1, p] = ends[p]
    base = z * sh.rows + b * TILE
    slots = [order[0, p] for p in range(DOCS)]
    pos = lane_pos(base)
    low = pick(starts, ends, pos, [s * MEM for s in slots])
    high = pick(starts, ends, pos, [s * MEM + mlens[0, s] for s in slots])

    def doc(p, carry):
        slot = order[0, p]
        seen = (bounds[0, p] < base + TILE) & (bounds[1, p] > base)
        if skip_pad:
            seen = seen & (slot != DOCS - 1)
        number = jnp.where(seen, (mlens[0, slot] + TILE - 1) // TILE, 0)

        def step(i, inner):
            t = slot * (MEM // TILE) + i
            k_pos = t * TILE + lax.broadcasted_iota(jnp.int32, (TILE, TILE), 0)
            bias[...] = jnp.where((k_pos >= low) & (k_pos < high), 0.0, NEG)
            body(t)
            return inner

        return lax.fori_loop(0, number, step, carry)

    lax.fori_loop(0, DOCS, doc, 0)


def touched_tile(sh, lens, order, mlens, t, bounds, skip_pad):
    z = lax.axis_index("seq")
    slot = t // (MEM // TILE)
    base = z * sh.rows
    seen = (bounds[2, slot] < base + sh.rows) & (bounds[3, slot] > base)
    seen = seen & (t % (MEM // TILE) * TILE < mlens[0, slot])
    if skip_pad:
        seen = seen & (slot != DOCS - 1)
    return seen


def slot_bounds(lens, order, bounds):
    starts, ends = doc_bounds(lens, order)
    for p in range(DOCS):
        bounds[2, order[0, p]] = starts[p]
        bounds[3, order[0, p]] = ends[p]


def cross_forward_kernel(sh, lens, order, mlens, *refs):
    count, rows, n, split = sh.count, sh.rows, sh.piece, sh.split
    tok, ctx, vec = refs[:3]
    mems = refs[3 : 3 + 2 * split - 1]
    slots = refs[2 + 2 * split : 2 + 2 * split + count]
    outs = refs[2 + 2 * split + count :]
    (n1_out, inv1, *early, mk_out, mv_out, mk_t_out, cctx, cctx_t3, lse) = outs[:11]
    kept = (mk_out, mv_out, mk_t_out)
    (n1, first_low, q_ref, q_t3) = outs[11:15]
    outs = outs[4:]
    (wo, wcq, wck, wcv, mem, mk3, mv3, mk_t3, mv_t3, q_t, bias, m_ref, l_ref, acc) = outs[11:25]
    (bounds, sems, mem_sems, tile_sems, row_sems) = outs[25:]
    for i, w in enumerate((wo, wcq, wck, wcv)):
        start_weight(sh, slots, i * n, n, w, sems.at[i])

    def wanted(t):
        return touched_tile(sh, lens, order, mlens, t, bounds, False)

    slot_bounds(lens, order, bounds)
    start_mems(sh, mems, mem, mem_sems, wanted)
    spread_zero(q_t)
    wait_all(wo, sems.at[0])
    wait_all(wcq, sems.at[1])

    v = tok[...].astype(F32) + (mm(ctx[...], wo[...]) + vec[V_SOB : V_SOB + 1, :])
    normal, inv = norm_stats(v)
    n1[...] = normal
    inv1[...] = inv
    low = (normal * vec[V_G1 : V_G1 + 1, :] + vec[V_S1 : V_S1 + 1, :]).astype(BF)
    first_low[...] = low
    q = (mm(low, wcq[...]) + vec[V_CQB : V_CQB + 1, :]).astype(BF)
    q = q * BF(HDIM**-0.5)
    q_ref[...] = q
    for i in range(rows // TILE):
        q_t3[i] = q[i * TILE : (i + 1) * TILE, :].T
    row_copies = send_all((n1, first_low, q_ref, q_t3), (n1_out, *early), row_sems)
    wait_all(wck, sems.at[2])
    wait_all(wcv, sems.at[3])

    def mem_tile(t, carry):
        @pl.when(wanted(t))
        def _():
            wait_mem(mem, t, mem_sems)
            x = mem[t]
            key = mm(x, wck[...]).astype(BF)
            val = (mm(x, wcv[...]) + vec[V_CVB : V_CVB + 1, :]).astype(BF)
            mk3[t] = key
            mv3[t] = val
            mk_t3[t] = key.T
            mv_t3[t] = val.T
            for copy in tile_copies(t, (mk3, mv3, mk_t3), kept, tile_sems):
                copy.start()

        return carry

    lax.fori_loop(0, sh.m_blocks, mem_tile, 0)

    def block(b, carry):
        spread_rows(q_t3.at[b], q_t)
        forward_start(m_ref, l_ref, acc)
        cross_tiles(
            sh,
            lens,
            order,
            mlens,
            b,
            bias,
            bounds,
            False,
            lambda t: forward_tile(mk3.at[t], mv_t3.at[t], bias, q_t, m_ref, l_ref, acc),
        )
        forward_end(b, m_ref, l_ref, acc, cctx, cctx_t3, lse)
        return carry

    lax.fori_loop(0, sh.q_blocks, block, 0)

    def settle(t, carry):
        @pl.when(wanted(t))
        def _():
            for copy in tile_copies(t, (mk3, mv3, mk_t3), kept, tile_sems):
                copy.wait()

        return carry

    lax.fori_loop(0, sh.m_blocks, settle, 0)
    for copy in row_copies:
        copy.wait()


def cross_forward(sh, lens, order, mlens, tok, ctx, vec, mems, slots):
    nm, nq = sh.m_blocks, sh.q_blocks
    outs = [
        shape((sh.rows, D), F32),
        shape((sh.rows, 1), F32),
        shape((sh.rows, D), BF),
        shape((sh.rows, D), BF),
        shape((nq, D, TILE), BF),
        shape((nm, TILE, D), BF),
        shape((nm, TILE, D), BF),
        shape((nm, D, TILE), BF),
        shape((sh.rows, D), BF),
        shape((nq, D, TILE), F32),
        shape((nq, HEADS, TILE), F32),
    ]
    scratch = [
        pltpu.VMEM((sh.rows, D), F32),
        pltpu.VMEM((sh.rows, D), BF),
        pltpu.VMEM((sh.rows, D), BF),
        pltpu.VMEM((nq, D, TILE), BF),
        pltpu.VMEM((D, D), BF),
        pltpu.VMEM((D, D), BF),
        pltpu.VMEM((D, D), BF),
        pltpu.VMEM((D, D), BF),
        pltpu.VMEM((nm, TILE, D), BF),
        pltpu.VMEM((nm, TILE, D), BF),
        pltpu.VMEM((nm, TILE, D), BF),
        pltpu.VMEM((nm, D, TILE), BF),
        pltpu.VMEM((nm, D, TILE), BF),
        pltpu.VMEM((HEADS, 2 * HDIM, TILE), BF),
        pltpu.VMEM((TILE, TILE), F32),
        pltpu.VMEM((HEADS, TILE), F32),
        pltpu.VMEM((HEADS, TILE), F32),
        pltpu.VMEM((D, TILE), F32),
        pltpu.SMEM((4, DOCS), jnp.int32),
        pltpu.SemaphoreType.DMA((4,)),
        pltpu.SemaphoreType.DMA((nm,)),
        pltpu.SemaphoreType.DMA((3, nm)),
        pltpu.SemaphoreType.DMA((4,)),
    ]
    specs = [SMEM_SPEC] * 3 + [VMEM_SPEC] * 3 + [ANY_SPEC] * (len(mems) + len(slots))
    return call(
        lambda *refs: cross_forward_kernel(sh, *refs),
        "cross_forward",
        (lens, order, mlens, tok, ctx, vec, *mems, *slots),
        specs,
        outs,
        scratch,
        21,
        out_specs=[ANY_SPEC, VMEM_SPEC] + [ANY_SPEC] * 6 + [VMEM_SPEC] * 3,
    )


def feed_kernel(sh, lens, order, *refs):
    count, rows, n, wide = sh.count, sh.rows, sh.piece, sh.wide_piece
    n1, cctx, targets, vec = refs[:4]
    slots = refs[4 : 4 + count]
    outs = refs[4 + count :]
    row_outs, vec_grad, grad_outs = outs[:4], outs[4], outs[5:7]
    (final_ref, g_second, g_cc, g_cc_t3, g_send, g_own) = outs[7:13]
    (sec_low, hid, feed_low, g_exp, g_cross) = outs[13:18]
    (wco, w1, w2, n2, dact, loss, stage, stage2, sems, out_sems) = outs[18:]
    z = lax.axis_index("seq")
    start_weight(sh, slots, 4 * n, n, wco, sems.at[0])
    for c in range(FFB):
        start_weight(sh, slots, (5 + c) * n, n, w1.at[c], sems.at[1 + c])
    start_weight(sh, slots, 9 * n, wide, w2, sems.at[5])
    vec_grad[...] = jnp.zeros(vec_grad.shape, F32)
    loss[...] = jnp.zeros(loss.shape, F32)
    starts, ends = doc_bounds(lens, order)
    pad_start, pad_end = jnp.int32(0), jnp.int32(0)
    for p in range(DOCS):
        is_pad = order[0, p] == DOCS - 1
        pad_start = jnp.where(is_pad, starts[p], pad_start)
        pad_end = jnp.where(is_pad, ends[p], pad_end)
    wait_all(wco, sems.at[0])

    def add_vec(row, value):
        vec_grad[row : row + 1, :] = vec_grad[row : row + 1, :] + value

    def chunk(i, carry):
        r = pl.ds(i * rows, rows)
        first = n1[r, :] * vec[V_G1 : V_G1 + 1, :] + vec[V_S1 : V_S1 + 1, :]
        v = first + (mm(cctx[r, :], wco[...]) + vec[V_COB : V_COB + 1, :])
        normal2, inv2 = norm_stats(v)
        n2[...] = normal2
        second = normal2 * vec[V_G2 : V_G2 + 1, :] + vec[V_S2 : V_S2 + 1, :]
        low = second.astype(BF)
        sec_low[r, :] = low
        feed = second + vec[V_CB : V_CB + 1, :]
        wide = range(FFB)

        if i == 0:
            for c in wide:
                wait_all(w1.at[c], sems.at[1 + c])
            wait_all(w2, sems.at[5])
        es = [mm(low, w1[c]) + vec[V_EB + c : V_EB + c + 1, :] for c in wide]
        sgs = [jax.nn.sigmoid(e) for e in es]
        hs = [(e * sg).astype(BF) for e, sg in zip(es, sgs)]
        for c in wide:
            hid[c, r, :] = hs[c]
            dact[c] = sgs[c] * (1.0 + es[c] * (1.0 - sgs[c]))
        for c in wide:
            feed = feed + mm(hs[c], w2[pl.ds(c * D, D), :])
        normal3, inv3 = norm_stats(feed)
        final = normal3 * vec[V_G3 : V_G3 + 1, :] + vec[V_S3 : V_S3 + 1, :]
        final_ref[r, :] = final.astype(BF)
        diff = final - targets[r, :].astype(F32)
        pos = z * rows + i * rows + lax.broadcasted_iota(jnp.int32, (rows, 1), 0)
        live = jnp.where((pos >= pad_start) & (pos < pad_end), 0.0, 1.0)
        g = live * diff
        loss[0:1, :] = loss[0:1, :] + col_sum(g * diff)
        add_vec(V_G3, col_sum(g * normal3))
        add_vec(V_S3, col_sum(g))
        g_third = norm_back(g, normal3, inv3, vec[V_G3 : V_G3 + 1, :])
        g_low = g_third.astype(BF)
        feed_low[r, :] = g_low
        add_vec(V_CB, col_sum(g_low))
        total = g_third
        ges = [(mm_nt(g_low, w2[pl.ds(c * D, D), :]) * dact[c]).astype(BF) for c in wide]
        for c in wide:
            total = total + mm_nt(ges[c], w1[c])
        for c in wide:
            g_exp[c, r, :] = ges[c]
            add_vec(V_EB + c, col_sum(ges[c]))
        normal2 = n2[...]
        add_vec(V_G2, col_sum(total * normal2))
        add_vec(V_S2, col_sum(total))
        gs = norm_back(total, normal2, inv2, vec[V_G2 : V_G2 + 1, :])
        g_second[r, :] = gs
        gc = gs.astype(BF)
        g_cross[r, :] = gc
        add_vec(V_COB, col_sum(gc))
        gcc = mm_nt(gc, wco[...]).astype(BF)
        g_cc[r, :] = gcc
        for b in range(rows // TILE):
            g_cc_t3[b] = gcc[b * TILE : (b + 1) * TILE, :].T
        return carry

    chunk(0, 0)
    live_count = jnp.int32(rows) - jnp.maximum(
        jnp.minimum(pad_end, (z + 1) * rows) - jnp.maximum(pad_start, z * rows), 0
    )
    bits = digit_bits(count * sh.split)
    error_sum = jnp.sum(loss[0:1, :], axis=1, keepdims=True)
    vec_grad[V_LOSS : V_LOSS + 1, :] = digits(error_sum, bits)
    vec_grad[V_LIVE : V_LIVE + 1, :] = digits(jnp.full((1, 1), live_count.astype(F32)), bits)
    copies = send_all((final_ref, g_second, g_cc, g_cc_t3), row_outs, out_sems)

    def send_grad(full, size, row):
        put_grad(sh, full, size, row, g_send, g_own)
        copies.extend(
            send_all(
                [ref.at[:, pl.ds(row, size)] for ref in (g_send, g_own)],
                [ref.at[:, pl.ds(row, size)] for ref in grad_outs],
                out_sems,
                len(copies),
            )
        )

    for c in range(FFB):
        stage2[pl.ds(c * D, D), :] = mm_tn(hid[c], feed_low[...]).astype(BF)
    send_grad(stage2, wide, 5 * n)
    for c in range(FFB):
        stage[...] = mm_tn(sec_low[...], g_exp[c]).astype(BF)
        send_grad(stage, n, (1 + c) * n)
    stage[...] = mm_tn(cctx[...], g_cross[...]).astype(BF)
    send_grad(stage, n, 0)
    for copy in copies:
        copy.wait()


def feed(sh, lens, order, n1, cctx, targets, vec, slots):
    rows, nq = sh.rows, sh.q_blocks
    block = 5 * sh.piece + sh.wide_piece
    outs = [
        shape((rows, D), BF),
        shape((rows, D), F32),
        shape((rows, D), BF),
        shape((nq, D, TILE), BF),
        shape((VROWS, D), F32),
        shape((sh.count // 2, block, D), BF),
        shape((sh.count // 2, block, D), BF),
    ]
    scratch = [
        pltpu.VMEM((rows, D), BF),
        pltpu.VMEM((rows, D), F32),
        pltpu.VMEM((rows, D), BF),
        pltpu.VMEM((nq, D, TILE), BF),
        pltpu.VMEM((sh.count // 2, block, D), BF),
        pltpu.VMEM((sh.count // 2, block, D), BF),
        pltpu.VMEM((rows, D), BF),
        pltpu.VMEM((FFB, rows, D), BF),
        pltpu.VMEM((rows, D), BF),
        pltpu.VMEM((FFB, rows, D), BF),
        pltpu.VMEM((rows, D), BF),
        pltpu.VMEM((D, D), BF),
        pltpu.VMEM((FFB, D, D), BF),
        pltpu.VMEM((FFB * D, D), BF),
        pltpu.VMEM((rows, D), F32),
        pltpu.VMEM((FFB, rows, D), F32),
        pltpu.VMEM((8, D), F32),
        pltpu.VMEM((D, D), BF),
        pltpu.VMEM((FFB * D, D), BF),
        pltpu.SemaphoreType.DMA((6,)),
        pltpu.SemaphoreType.DMA((4 + 2 * (FFB + 2),)),
    ]
    specs = [SMEM_SPEC] * 2 + [VMEM_SPEC] * 4 + [ANY_SPEC] * len(slots)
    return call(
        lambda *refs: feed_kernel(sh, *refs),
        "feed",
        (lens, order, n1, cctx, targets, vec, *slots),
        specs,
        outs,
        scratch,
        17,
        out_specs=[ANY_SPEC] * 4 + [VMEM_SPEC] + [ANY_SPEC] * 2,
    )


def mem_shard(z, slot, high):
    low, mid = z % 2, (z // 2) % 2
    low = low if slot % 2 else 1 - low
    mid = mid if slot >= 2 else 1 - mid
    return 4 * high + 2 * mid + low


def cross_backward_kernel(sh, lens, order, mlens, *refs):
    count, n = sh.count, sh.piece
    (q_ref, q_t3, *kept, cctx_t3, lse, g_cc, g_cc_t3) = refs[:9]
    slots = refs[9 : 9 + count]
    outs = refs[9 + count :]
    part_outs = outs[:4]
    (dq, *low_out) = outs[4:7]
    (wck, wcv, q_t, g_t, q_m, g_m, delta, bias, dk, dv, dq_t) = outs[7:18]
    (mk3, mv3, mk_t3, k_low3, v_low3, bounds, sems, tile_sems, low_sems) = outs[18:27]
    mem_parts, part_sems = outs[27:31], outs[31]
    for i, w in enumerate((wck, wcv)):
        start_weight(sh, slots, (2 + i) * n, n, w, sems.at[i])
    slot_bounds(lens, order, bounds)
    spread_zero(q_t)
    spread_zero(g_t)

    def each_wanted(body):
        def one(t, carry):
            @pl.when(touched_tile(sh, lens, order, mlens, t, bounds, True))
            def _():
                body(t)

            return carry

        lax.fori_loop(0, sh.m_blocks, one, 0)

    def fetch(t):
        for copy in tile_copies(t, kept, (mk3, mv3, mk_t3), tile_sems):
            copy.start()

    def clear(t):
        dk[t] = jnp.zeros((TILE, D), F32)
        dv[t] = jnp.zeros((TILE, D), F32)
        for copy in tile_copies(t, kept, (mk3, mv3, mk_t3), tile_sems):
            copy.wait()

    def low_copies(t):
        return tile_copies(t, (k_low3, v_low3), low_out, low_sems)

    each_wanted(fetch)
    each_wanted(clear)

    def block(b, carry):
        backward_start(b, q_t3, g_cc_t3, q_ref, g_cc, cctx_t3, q_t, g_t, q_m, g_m, delta, dq_t)
        cross_tiles(
            sh,
            lens,
            order,
            mlens,
            b,
            bias,
            bounds,
            True,
            lambda t: backward_tile(
                mk3.at[t],
                mv3.at[t],
                mk_t3.at[t],
                bias,
                q_t,
                g_t,
                q_m,
                g_m,
                lse.at[b],
                delta,
                dk.at[t],
                dv.at[t],
                dq_t,
            ),
        )
        r = pl.ds(pl.multiple_of(b * TILE, TILE), TILE)
        dq[r, :] = (dq_t[...] * HDIM**-0.5).T.astype(BF)
        return carry

    lax.fori_loop(0, sh.q_blocks, block, 0)
    wait_all(wck, sems.at[0])
    wait_all(wcv, sems.at[1])

    z = lax.axis_index("seq")
    tiles_per = sh.mem_rows // TILE

    def mem_tile(i, carry, slot, out):
        shard = mem_shard(z, slot, i // tiles_per)
        t = shard * tiles_per + i % tiles_per
        seen = touched_tile(sh, lens, order, mlens, t, bounds, True)

        @pl.when(seen)
        def _():
            k_low = dk[t].astype(BF)
            v_low = dv[t].astype(BF)
            k_low3[t] = k_low
            v_low3[t] = v_low
            for copy in low_copies(t):
                copy.start()
            out[i] = (mm_nt(k_low, wck[...]) + mm_nt(v_low, wcv[...])).astype(BF)

        @pl.when(jnp.logical_not(seen))
        def _():
            out[i] = jnp.zeros((TILE, D), BF)

        return carry

    copies = []
    for slot, out in enumerate(mem_parts):
        lax.fori_loop(
            0, sh.m_blocks // 4, lambda i, c, slot=slot, out=out: mem_tile(i, c, slot, out), 0
        )
        copies += send_all([out], [part_outs[slot]], part_sems, slot)
    for copy in copies:
        copy.wait()

    def settle(t):
        for copy in low_copies(t):
            copy.wait()

    each_wanted(settle)


def cross_backward(sh, lens, order, mlens, arrays, slots):
    rows, nm = sh.rows, sh.m_blocks
    outs = [shape((nm // 4, TILE, D), BF)] * 4 + [
        shape((rows, D), BF),
        shape((nm, TILE, D), BF),
        shape((nm, TILE, D), BF),
    ]
    scratch = [
        pltpu.VMEM((D, D), BF),
        pltpu.VMEM((D, D), BF),
        pltpu.VMEM((HEADS, 2 * HDIM, TILE), BF),
        pltpu.VMEM((HEADS, 2 * HDIM, TILE), BF),
        pltpu.VMEM((HEADS, TILE, 2 * HDIM), BF),
        pltpu.VMEM((HEADS, TILE, 2 * HDIM), BF),
        pltpu.VMEM((HEADS, TILE), F32),
        pltpu.VMEM((TILE, TILE), F32),
        pltpu.VMEM((nm, TILE, D), F32),
        pltpu.VMEM((nm, TILE, D), F32),
        pltpu.VMEM((D, TILE), F32),
        pltpu.VMEM((nm, TILE, D), BF),
        pltpu.VMEM((nm, TILE, D), BF),
        pltpu.VMEM((nm, D, TILE), BF),
        pltpu.VMEM((nm, TILE, D), BF),
        pltpu.VMEM((nm, TILE, D), BF),
        pltpu.SMEM((4, DOCS), jnp.int32),
        pltpu.SemaphoreType.DMA((2,)),
        pltpu.SemaphoreType.DMA((3, nm)),
        pltpu.SemaphoreType.DMA((2, nm)),
    ]
    scratch += [pltpu.VMEM((nm // 4, TILE, D), BF)] * 4 + [pltpu.SemaphoreType.DMA((4,))]
    specs = [SMEM_SPEC] * 3 + [VMEM_SPEC] * 2 + [ANY_SPEC] * 3 + [VMEM_SPEC] * 4
    specs += [ANY_SPEC] * len(slots)
    return call(
        lambda *refs: cross_backward_kernel(sh, *refs),
        "cross_backward",
        (lens, order, mlens, *arrays, *slots),
        specs,
        outs,
        scratch,
        15,
        out_specs=[ANY_SPEC] * 4 + [VMEM_SPEC] + [ANY_SPEC] * 2,
    )


def first_backward_kernel(sh, lens, order, mlens, *refs):
    count, rows, n = sh.count, sh.rows, sh.piece
    (dq, *low_in, g_second, n1, inv1, first_low, ctx, vec, vec_in) = refs[:10]
    mems = refs[10 : 9 + 2 * sh.split]
    slots = refs[9 + 2 * sh.split : 9 + 2 * sh.split + count]
    outs = refs[9 + 2 * sh.split + count :]
    (g_send, g_own, g_first, g_ctx, g_ctx_t3, vec_grad) = outs[:6]
    (wo, wcq, g_self, acc_k, acc_v, stage, mem, k_low3, v_low3, bounds) = outs[6:16]
    (sems, mem_sems, low_sems) = outs[16:]
    for i, w in enumerate((wo, wcq)):
        start_weight(sh, slots, i * n, n, w, sems.at[i])
    vec_grad[...] = vec_in[...]
    slot_bounds(lens, order, bounds)

    def wanted(t):
        return touched_tile(sh, lens, order, mlens, t, bounds, True)

    def fetch(t, carry):
        @pl.when(wanted(t))
        def _():
            for copy in tile_copies(t, low_in, (k_low3, v_low3), low_sems):
                copy.start()

        return carry

    lax.fori_loop(0, sh.m_blocks, fetch, 0)
    start_mems(sh, mems, mem, mem_sems, wanted)
    wait_all(wo, sems.at[0])
    wait_all(wcq, sems.at[1])

    def add_vec(row, value):
        vec_grad[row : row + 1, :] = vec_grad[row : row + 1, :] + value

    def own_rows(i, carry):
        r = pl.ds(pl.multiple_of(i * TILE, TILE), TILE)
        total = g_second[r, :] + mm_nt(dq[r, :], wcq[...])
        normal = n1[r, :]
        add_vec(V_G1, col_sum(total * normal))
        add_vec(V_S1, col_sum(total))
        gf = norm_back(total, normal, inv1[r, :], vec[V_G1 : V_G1 + 1, :])
        g_first[r, :] = gf
        low = gf.astype(BF)
        g_self[r, :] = low
        add_vec(V_SOB, col_sum(low))
        gc = mm_nt(low, wo[...]).astype(BF)
        g_ctx[r, :] = gc
        g_ctx_t3[i] = gc.T
        return carry

    lax.fori_loop(0, rows // TILE, own_rows, 0)
    acc_k[...] = jnp.zeros(acc_k.shape, F32)
    acc_v[...] = jnp.zeros(acc_v.shape, F32)

    def mem_tile(t, carry):
        @pl.when(wanted(t))
        def _():
            wait_mem(mem, t, mem_sems)
            for copy in tile_copies(t, low_in, (k_low3, v_low3), low_sems):
                copy.wait()
            k_low = k_low3[t]
            v_low = v_low3[t]
            x = mem[t]
            acc_k[...] = acc_k[...] + mm_tn(x, k_low)
            acc_v[...] = acc_v[...] + mm_tn(x, v_low)
            add_vec(V_CVB, col_sum(v_low))

        return carry

    lax.fori_loop(0, sh.m_blocks, mem_tile, 0)

    add_vec(V_CQB, col_sum(dq[...]))
    stage[...] = mm_tn(ctx[...], g_self[...]).astype(BF)
    put_grad(sh, stage, n, 0, g_send, g_own)
    stage[...] = mm_tn(first_low[...], dq[...]).astype(BF)
    put_grad(sh, stage, n, n, g_send, g_own)
    stage[...] = acc_k[...].astype(BF)
    put_grad(sh, stage, n, 2 * n, g_send, g_own)
    stage[...] = acc_v[...].astype(BF)
    put_grad(sh, stage, n, 3 * n, g_send, g_own)


def first_backward(sh, lens, order, mlens, arrays, mems, slots):
    rows, nq, n, nm = sh.rows, sh.q_blocks, sh.piece, sh.m_blocks
    outs = [
        shape((sh.count // 2, 4 * n, D), BF),
        shape((sh.count // 2, 4 * n, D), BF),
        shape((rows, D), F32),
        shape((rows, D), BF),
        shape((nq, D, TILE), BF),
        shape((VROWS, D), F32),
    ]
    scratch = [
        pltpu.VMEM((D, D), BF),
        pltpu.VMEM((D, D), BF),
        pltpu.VMEM((rows, D), BF),
        pltpu.VMEM((D, D), F32),
        pltpu.VMEM((D, D), F32),
        pltpu.VMEM((D, D), BF),
        pltpu.VMEM((nm, TILE, D), BF),
        pltpu.VMEM((nm, TILE, D), BF),
        pltpu.VMEM((nm, TILE, D), BF),
        pltpu.SMEM((4, DOCS), jnp.int32),
        pltpu.SemaphoreType.DMA((2,)),
        pltpu.SemaphoreType.DMA((nm,)),
        pltpu.SemaphoreType.DMA((2, nm)),
    ]
    specs = [SMEM_SPEC] * 3 + [VMEM_SPEC] + [ANY_SPEC] * 2 + [VMEM_SPEC] * 7
    specs += [ANY_SPEC] * (len(mems) + len(slots))
    return call(
        lambda *refs: first_backward_kernel(sh, *refs),
        "first_backward",
        (lens, order, mlens, *arrays, *mems, *slots),
        specs,
        outs,
        scratch,
        6,
    )


def self_backward_kernel(sh, lens, order, *refs):
    count, rows, n, halo = sh.count, sh.rows, sh.piece, sh.halo
    (q_ref, q_t3, k3, v3, k_t3, ctx_t3, lse, g_ctx, g_ctx_t3) = refs[:9]
    slots = refs[9 : 9 + count]
    outs = refs[9 + count :]
    (grad_halo, dq, k_low3, v_low3) = outs[:4]
    (wk, wv, q_t, g_t, q_m, g_m, delta, bias, dk, dv, dq_t, sems) = outs[4:]
    z = lax.axis_index("seq")
    for i, w in enumerate((wk, wv)):
        start_weight(sh, slots, (1 + i) * n, n, w, sems.at[i])
    spread_zero(q_t)
    spread_zero(g_t)

    def clear(t, carry):
        dk[t] = jnp.zeros((TILE, D), F32)
        dv[t] = jnp.zeros((TILE, D), F32)
        return carry

    lax.fori_loop(0, sh.k_blocks, clear, 0)

    def block(b, carry):
        backward_start(b, q_t3, g_ctx_t3, q_ref, g_ctx, ctx_t3, q_t, g_t, q_m, g_m, delta, dq_t)
        self_tiles(
            sh,
            lens,
            order,
            b,
            bias,
            lambda t: backward_tile(
                k3.at[t],
                v3.at[t],
                k_t3.at[t],
                bias,
                q_t,
                g_t,
                q_m,
                g_m,
                lse.at[b],
                delta,
                dk.at[t],
                dv.at[t],
                dq_t,
            ),
        )
        r = pl.ds(pl.multiple_of(b * TILE, TILE), TILE)
        dq[r, :] = (dq_t[...] * HDIM**-0.5).T.astype(BF)
        return carry

    lax.fori_loop(0, sh.q_blocks, block, 0)
    wait_all(wk, sems.at[0])
    wait_all(wv, sems.at[1])
    tiles = rows // TILE

    def lower(t, carry):
        k_low3[t] = dk[t].astype(BF)
        v_low3[t] = dv[t].astype(BF)
        return carry

    lax.fori_loop(0, sh.k_blocks, lower, 0)
    for k in range(halo, 0, -1):

        def window_rows(i, carry, k=k):
            r = pl.ds(pl.multiple_of(i * TILE, TILE), TILE)
            t = (halo - k) * tiles + i
            part = mm_nt(k_low3[t], wk[...]) + mm_nt(v_low3[t], wv[...])
            grad_halo[k - 1, r, :] = part.astype(BF)
            return carry

        @pl.when(z >= k)
        def _(window_rows=window_rows):
            lax.fori_loop(0, tiles, window_rows, 0)

        @pl.when(z < k)
        def _(k=k):
            grad_halo[k - 1] = jnp.zeros((rows, D), BF)


def self_backward(sh, lens, order, arrays, slots):
    rows, nb = sh.rows, sh.k_blocks
    outs = [
        shape((sh.halo, rows, D), BF),
        shape((rows, D), BF),
        shape((nb, TILE, D), BF),
        shape((nb, TILE, D), BF),
    ]
    scratch = [
        pltpu.VMEM((D, D), BF),
        pltpu.VMEM((D, D), BF),
        pltpu.VMEM((HEADS, 2 * HDIM, TILE), BF),
        pltpu.VMEM((HEADS, 2 * HDIM, TILE), BF),
        pltpu.VMEM((HEADS, TILE, 2 * HDIM), BF),
        pltpu.VMEM((HEADS, TILE, 2 * HDIM), BF),
        pltpu.VMEM((HEADS, TILE), F32),
        pltpu.VMEM((TILE, TILE), F32),
        pltpu.VMEM((nb, TILE, D), F32),
        pltpu.VMEM((nb, TILE, D), F32),
        pltpu.VMEM((D, TILE), F32),
        pltpu.SemaphoreType.DMA((2,)),
    ]
    specs = [SMEM_SPEC] * 2 + [VMEM_SPEC] * len(arrays) + [ANY_SPEC] * len(slots)
    return call(
        lambda *refs: self_backward_kernel(sh, *refs),
        "self_backward",
        (lens, order, *arrays, *slots),
        specs,
        outs,
        scratch,
        14,
    )


def self_weights_kernel(sh, *refs):
    count, rows, n, halo = sh.count, sh.rows, sh.piece, sh.halo
    (dq, k_low3, v_low3, g_first, vec_in) = refs[:5]
    toks = refs[5 : 6 + halo]
    slots = refs[6 + halo : 6 + halo + count]
    outs = refs[6 + halo + count :]
    (g_send, g_own, grad_own) = outs[:3]
    (wq, wk, wv, acc_k, acc_v, vec_grad, stage, sems) = outs[3:]
    z = lax.axis_index("seq")
    for i, w in enumerate((wq, wk, wv)):
        start_weight(sh, slots, i * n, n, w, sems.at[i])
    vec_grad[...] = vec_in[...]
    tiles = rows // TILE

    def add_vec(row, value):
        vec_grad[row : row + 1, :] = vec_grad[row : row + 1, :] + value

    acc_k[...] = jnp.zeros(acc_k.shape, F32)
    acc_v[...] = jnp.zeros(acc_v.shape, F32)
    for k in range(halo, -1, -1):

        def window_rows(i, carry, k=k):
            r = pl.ds(pl.multiple_of(i * TILE, TILE), TILE)
            t = (halo - k) * tiles + i
            x = toks[k][r, :]
            acc_k[...] = acc_k[...] + mm_tn(x, k_low3[t])
            acc_v[...] = acc_v[...] + mm_tn(x, v_low3[t])
            add_vec(V_SVB, col_sum(v_low3[t]))
            return carry

        @pl.when(z >= k)
        def _(window_rows=window_rows):
            lax.fori_loop(0, tiles, window_rows, 0)

    add_vec(V_SQB, col_sum(dq[...]))
    stage[...] = mm_tn(toks[0][...], dq[...]).astype(BF)
    put_grad(sh, stage, n, 0, g_send, g_own)
    stage[...] = acc_k[...].astype(BF)
    put_grad(sh, stage, n, n, g_send, g_own)
    stage[...] = acc_v[...].astype(BF)
    put_grad(sh, stage, n, 2 * n, g_send, g_own)
    vec_low = vec_grad[...].astype(BF)
    for s in range(count // 2):
        g_send[s, pl.ds(3 * n, VROWS), :] = vec_low
        g_own[s, pl.ds(3 * n, VROWS), :] = vec_low
    for i, w in enumerate((wq, wk, wv)):
        wait_all(w, sems.at[i])

    def own_rows(i, carry):
        r = pl.ds(pl.multiple_of(i * TILE, TILE), TILE)
        t = halo * tiles + i
        part = mm_nt(k_low3[t], wk[...]) + mm_nt(v_low3[t], wv[...])
        grad_own[r, :] = g_first[r, :] + part + mm_nt(dq[r, :], wq[...])
        return carry

    lax.fori_loop(0, tiles, own_rows, 0)


def self_weights(sh, arrays, toks, slots):
    rows, n = sh.rows, sh.piece
    outs = [
        shape((sh.count // 2, 3 * n + VROWS, D), BF),
        shape((sh.count // 2, 3 * n + VROWS, D), BF),
        shape((rows, D), F32),
    ]
    scratch = [
        pltpu.VMEM((D, D), BF),
        pltpu.VMEM((D, D), BF),
        pltpu.VMEM((D, D), BF),
        pltpu.VMEM((D, D), F32),
        pltpu.VMEM((D, D), F32),
        pltpu.VMEM((VROWS, D), F32),
        pltpu.VMEM((D, D), BF),
        pltpu.SemaphoreType.DMA((3,)),
    ]
    specs = [VMEM_SPEC] * (len(arrays) + len(toks)) + [ANY_SPEC] * len(slots)
    return call(
        lambda *refs: self_weights_kernel(sh, *refs),
        "self_weights",
        (*arrays, *toks, *slots),
        specs,
        outs,
        scratch,
        7,
    )


def shards(
    tokens,
    memory,
    targets,
    doc_lengths,
    doc_order,
    memory_lengths,
    self_query,
    self_query_bias,
    self_key,
    self_value,
    self_value_bias,
    self_output,
    self_output_bias,
    first_gain,
    first_shift,
    cross_query,
    cross_query_bias,
    cross_key,
    cross_value,
    cross_value_bias,
    cross_output,
    cross_output_bias,
    second_gain,
    second_shift,
    expand_weight,
    expand_bias,
    contract_weight,
    contract_bias,
    third_gain,
    third_shift,
):
    split = lax.axis_size("seq")
    count = lax.axis_size("fsdp")
    n = self_query.shape[0]
    wide = contract_weight.shape[0]
    sh = Shard(tokens.shape[0], memory.shape[0], count, split, n, wide)

    own_a, own_b = pack(
        sh,
        (
            self_query_bias,
            self_value_bias,
            self_output_bias,
            first_gain,
            first_shift,
            cross_query_bias,
            cross_value_bias,
            cross_output_bias,
            second_gain,
            second_shift,
            contract_bias,
            third_gain,
            third_shift,
        ),
        expand_bias,
        (
            self_query,
            self_key,
            self_value,
            self_output,
            cross_query,
            cross_key,
            cross_value,
            cross_output,
            expand_weight,
            contract_weight,
        ),
    )
    toks, downs = [tokens, seq_up(tokens, split)], [seq_down(memory, split)]
    swaps = [(i, i ^ 1) for i in range(count)]
    pairs = [step_pairs(count, index) for index in range(len(chip_steps(count)[0]))]
    slots_a, slots_b = [own_a], [own_b]
    own_b_first = [own_b]
    other_b = [lax.ppermute(own_b, "fsdp", swaps)]
    first = [lax.ppermute(own_a, "fsdp", p) for p in pairs]
    hold = (toks[1], downs[0], *first, *other_b)
    for _ in range(1, sh.halo):
        toks.append(seq_up(after(toks[-1], *hold), split))
    ups = [seq_up(after(memory, *hold), split)]
    held_b = after(own_b, *hold)
    second = [lax.ppermute(held_b, "fsdp", p) for p in pairs]
    for index, p in enumerate(pairs):
        slots_a += [first[index]] + [lax.ppermute(after(a, *hold), "fsdp", p) for a in slots_a[1:]]
    hold = (toks[-1], ups[0], *second, *slots_a[3:])
    for index, p in enumerate(pairs):
        slots_b += [second[index]] + [lax.ppermute(after(a, *hold), "fsdp", p) for a in slots_b[1:]]
    slots_a = slots_a + [lax.ppermute(after(a, *hold), "fsdp", swaps) for a in slots_a]
    for k in range(2, split):
        if k == split - 1:
            last = after(memory, *hold)
            ends = lax.ppermute(last, "seq", [(0, split - 1), (split - 1, 0)])
            ups.append(ends)
            downs.append(ends)
        else:
            ups.append(seq_up(after(ups[-1], *hold), split))
            downs.append(seq_down(after(downs[-1], *hold), split))
    mems = [memory]
    for up, down in zip(ups, downs):
        mems += [up, down]

    near = [lax.ppermute(after(a, *hold), "fsdp", swaps) for a in second]
    first_tok = after(tokens, *hold, *near)
    (q, q_t3, k3, v3, k_t3, ctx, ctx_t3, lse, vec) = self_forward(
        sh, doc_lengths, doc_order, [first_tok] + toks[1:], slots_a
    )
    swapped = {id(a): b for a, b in zip(own_b_first + second, other_b + near)}
    late = (ctx, *ups, *downs)
    slots_b = slots_b + [
        swapped[id(a)] if id(a) in swapped else lax.ppermute(after(a, *late), "fsdp", swaps)
        for a in slots_b
    ]
    (n1, inv1, first_low, cq, cq_t3, mk3, mv3, mk_t3, cctx, cctx_t3, clse) = cross_forward(
        sh, doc_lengths, doc_order, memory_lengths, tokens, ctx, vec, mems, slots_b
    )
    feed_out = feed(sh, doc_lengths, doc_order, n1, cctx, targets, vec, slots_b)
    (final_low, g_second, g_cc, g_cc_t3, vec_grad, send_c, own_c) = feed_out
    sum_c = Reduction(send_c, own_c, count, split)
    sum_c.step()
    cq = after(cq, sum_c.send)
    sum_c.step()
    *mem_parts, dcq, k_low3, v_low3 = cross_backward(
        sh,
        doc_lengths,
        doc_order,
        memory_lengths,
        (cq, cq_t3, mk3, mv3, mk_t3, cctx_t3, clse, g_cc, g_cc_t3),
        slots_b,
    )
    dcq = after(dcq, sum_c.send)
    sum_c.step(dcq)
    swap = [(i, i ^ 1) for i in range(split)]
    mem_got = lax.ppermute(mem_parts[0], "seq", swap)
    (send_b, own_b, g_first, g_ctx, g_ctx_t3, vec_grad) = first_backward(
        sh,
        doc_lengths,
        doc_order,
        memory_lengths,
        (dcq, k_low3, v_low3, g_second, n1, inv1, first_low, ctx, vec, vec_grad),
        mems,
        slots_b,
    )
    mem_away = add_low(after(mem_parts[1], g_first), mem_got)
    sum_b = Reduction(send_b, own_b, count, split)
    g_ctx = after(g_ctx, sum_c.send, mem_away)
    sum_c.step(g_ctx)
    sum_b.step(g_ctx)
    mem_got = lax.ppermute(after(mem_parts[2], g_ctx), "seq", swap)
    mem_far = lax.ppermute(after(mem_away, g_ctx), "seq", [(i, i ^ 2) for i in range(split)])
    (grad_halo, dq, sk_low3, sv_low3) = self_backward(
        sh,
        doc_lengths,
        doc_order,
        (q, q_t3, k3, v3, k_t3, ctx_t3, lse, g_ctx, g_ctx_t3),
        slots_a,
    )
    dq = after(dq, mem_got, mem_far, sum_c.send, sum_b.send)
    back = seq_down(after(grad_halo[sh.halo - 1], dq), split)
    sum_b.step(dq)
    sum_c.step(dq)
    (send_a, own_a, grad_own) = self_weights(
        sh,
        (dq, sk_low3, sv_low3, g_first, vec_grad),
        toks,
        slots_a,
    )
    send_a = after(send_a, sum_b.send, sum_c.send)
    sum_a = Reduction(send_a, own_a, count, split)
    sum_a.step()
    sum_b.step(send_a)
    sum_c.step(send_a)
    for k in range(sh.halo - 1, 0, -1):
        back = seq_down(after(add_low(grad_halo[k - 1], back), send_a), split)
    sum_a.step()
    ready, held = sum_a.send, (sum_b.send, sum_c.send)
    while [a for a, _ in sum_a.plan].count("fsdp"):
        sum_a.step()
    sum_b.step(ready)
    ready = sum_a.send
    sum_a.step(back, *held)
    sum_b.step(ready)
    input_grad = grad_own + back.astype(F32)
    mem_last = after(mem_parts[3], sum_a.send)
    mem_here = mem_last.astype(F32) + mem_got.astype(F32) + mem_far.astype(F32)
    memory_grad = seq_rest(mem_here.reshape(split // 4, sh.mem_rows, D), split)[0]
    sum_a.finish()
    red_b, red_c = sum_b.finish(), sum_c.finish()

    def rows_of(array, start, size):
        return array[start : start + size].astype(F32)

    done = finish(sh, sum_a.parts[0], sum_a.got, expand_bias.shape[0])
    small_grad = done[3 : 3 + V_EB]
    expand_bias_grad = done[3 + V_EB]
    loss_value = done[4 + V_EB].reshape(())
    expand_grad = jnp.concatenate(
        [rows_of(red_c, (1 + c) * n, n) for c in range(FFB)], axis=1
    )
    return (
        final_low,
        loss_value,
        input_grad,
        memory_grad,
        done[0],
        small_grad[V_SQB],
        done[1],
        done[2],
        small_grad[V_SVB],
        rows_of(red_b, 0, n),
        small_grad[V_SOB],
        small_grad[V_G1],
        small_grad[V_S1],
        rows_of(red_b, n, n),
        small_grad[V_CQB],
        rows_of(red_b, 2 * n, n),
        rows_of(red_b, 3 * n, n),
        small_grad[V_CVB],
        rows_of(red_c, 0, n),
        small_grad[V_COB],
        small_grad[V_G2],
        small_grad[V_S2],
        expand_grad,
        expand_bias_grad,
        rows_of(red_c, 5 * n, wide),
        small_grad[V_CB],
        small_grad[V_G3],
        small_grad[V_S3],
    )


def solution(mesh):
    rows = P(("fsdp", "seq"), None)
    matrix = P("fsdp", None)
    vector = P("fsdp")
    kinds = (
        "mvmmvmvvvmvmmvmvvvmvmvvv"
    )
    weights = tuple(matrix if kind == "m" else vector for kind in kinds)
    return jax.shard_map(
        shards,
        mesh=mesh,
        in_specs=(rows, rows, rows, matrix, matrix, matrix) + weights,
        out_specs=(rows, P(), rows, rows) + weights,
        check_vma=False,
    )
```
